32 devices in a mesh: group: 4 (over y, x), replica: 8 (over z, core).
Axes of the slice: x: 2, y: 2, z: 4, core: 2. Of those that a mesh axis runs over, the one named last changes fastest.
Arguments:
- tokens_in: bfloat16 [16, 1024, 768], P('replica', 'group'), may hold values from -6 to 6
- doc_ids: int32 [16, 1024], P('replica', 'group'), may hold values from 0 to 3, never falling along the last dimension, each value on 1 to 512 neighbouring positions
- out_grad: bfloat16 [16, 1024, 768], P('replica', 'group'), may hold values from -6 to 6
- w_query: bfloat16 [768, 768], P('group'), may hold values from -0.21875 to 0.21875
- w_key: bfloat16 [768, 768], P('group'), may hold values from -0.21875 to 0.21875
- w_value: bfloat16 [768, 768], P('group'), may hold values from -0.21875 to 0.21875
- w_out: bfloat16 [768, 768], P('group'), may hold values from -0.875 to 0.875
- w_up: bfloat16 [768, 3072], P('group'), may hold values from -0.21875 to 0.21875
- w_down: bfloat16 [3072, 768], P('group'), may hold values from -0.109375 to 0.109375
- b_query: bfloat16 [768], P('group'), may hold values from -2 to 2
- b_value: bfloat16 [768], P('group'), may hold values from -2 to 2
- b_out: bfloat16 [768], P('group'), may hold values from -2 to 2
- gain_attn: bfloat16 [768], P('group'), may hold values from 0.5 to 1.5
- shift_attn: bfloat16 [768], P('group'), may hold values from -2 to 2
- b_up: bfloat16 [3072], P('group'), may hold values from -2 to 2
- b_down: bfloat16 [768], P('group'), may hold values from -2 to 2
- gain_ffn: bfloat16 [768], P('group'), may hold values from 0.5 to 1.5
- shift_ffn: bfloat16 [768], P('group'), may hold values from -2 to 2
Outputs:
- layer_out: bfloat16 [16, 1024, 768], P('replica', 'group')
- grad_input: float32 [16, 1024, 768], P('replica', 'group')
- grad_w_query: float32 [768, 768], P('group')
- grad_w_key: float32 [768, 768], P('group')
- grad_w_value: float32 [768, 768], P('group')
- grad_w_out: float32 [768, 768], P('group')
- grad_w_up: float32 [768, 3072], P('group')
- grad_w_down: float32 [3072, 768], P('group')
- grad_b_query: float32 [768], P('group')
- grad_b_value: float32 [768], P('group')
- grad_b_out: float32 [768], P('group')
- grad_gain_attn: float32 [768], P('group')
- grad_shift_attn: float32 [768], P('group')
- grad_b_up: float32 [3072], P('group')
- grad_b_down: float32 [768], P('group')
- grad_gain_ffn: float32 [768], P('group')
- grad_shift_ffn: float32 [768], P('group')
The draws below stay inside these ranges and needn't reach their ends.
Inputs may be any that keep to these rules, and one draw needn't show every extreme that they name: `doc_ids`: along each sequence the document numbers never fall; every document has 1 to 512 tokens, and one has exactly 512.
All inputs are finite; a program needn't handle non-finite values.
Results may differ from the reference program's by a relative error of at most 0.03.
Values may be sent and summed in bfloat16 or wider, within the bound.
A program may use at most 256 MiB of HBM per device.

```python
import math
import jax
import jax.numpy as jnp
import numpy as np
from jax import lax

D = 768
HEADS = 12
HEAD_DIM = 64
FF = 3072
SEQ = 1024
SEQS = 16
DOCS = 4
DOC_MAX = 512


def block_levels(own_key, shape, pieces, least, largest):
    def one(axis_at, shards_of):
        steps = jax.random.uniform(jax.random.fold_in(jax.random.fold_in(own_key, 6), axis_at), (shards_of,), jnp.float32, least / len(pieces), largest / len(pieces))
        return jnp.repeat(jnp.exp(steps), shape[axis_at] // shards_of).reshape((-1,) + (1,) * (len(shape) - axis_at - 1))

    factor_of = one(*pieces[0])
    for cut in pieces[1:]:
        factor_of = factor_of * one(*cut)
    return factor_of


def length_profile(number_of, total, reach, skew):
    portions = [(1 << 20) // math.isqrt(standing ** skew) + 1 for standing in range(2, number_of + 1)]
    surplus, counts = total - reach - (number_of - 1), [1] * (number_of - 1)
    while surplus > 0:
        free = [i for i in range(number_of - 1) if counts[i] < reach]
        mass, left = sum([portions[i] for i in free]), surplus
        for i in free:
            extra = min(reach - counts[i], max(1, left * portions[i] // mass), surplus)
            counts[i] = counts[i] + extra
            surplus = surplus - extra
    return np.array([reach] + counts)


def uneven(own_key, count, total, most, skew):
    if count == 2:
        one = jax.random.randint(own_key, (), max(1, total - most), min(most, total - 1) + 1)
        return jnp.stack([one, total - one])
    sizes = jnp.asarray(length_profile(count, total, most, skew), jnp.int32)
    twos = (count - 1) // 2
    donor, taker = sizes[1:1 + 2 * twos:2], sizes[2:2 + 2 * twos:2]
    room = jnp.minimum(donor - 1, most - taker)
    shifted = jax.random.randint(jax.random.fold_in(own_key, 1), (twos,), 0, 1 << 20) % (room + 1)
    sizes = sizes.at[1:1 + 2 * twos:2].set(donor - shifted).at[2:2 + 2 * twos:2].set(taker + shifted)
    return sizes[jax.random.permutation(jax.random.fold_in(own_key, 2), count)]


def normal_values(stream_key, extent, scale, bound, cuts=(), held_as=jnp.bfloat16):
    level = block_levels(stream_key, extent, cuts, -0.22, 0.18) if cuts else 1.0
    entries = jax.random.normal(stream_key, extent, jnp.float32) * scale * level
    return jnp.minimum(jnp.maximum(entries, -bound), bound).astype(held_as)


def setup_inputs(seed: int = 0) -> dict:
    arg_keys = jax.random.split(jax.random.key(seed), 19)
    tokens_in = normal_values(arg_keys[0], (SEQS, SEQ, D), 1.0, 6.0, ((0, 8), (1, 4)))
    doc_ids = jax.vmap(lambda own: jnp.searchsorted(jnp.cumsum(uneven(own, DOCS, SEQ, DOC_MAX, 2)), jnp.arange(SEQ), side="right"))(jax.random.split(arg_keys[1], SEQS)).reshape((SEQS, SEQ)).astype(jnp.int32)
    out_grad = normal_values(arg_keys[2], (SEQS, SEQ, D), 1.0, 6.0, ((0, 8), (1, 4)))
    w_query = normal_values(arg_keys[3], (D, D), D ** -0.5, 0.21875, ((0, 4),))
    w_key = normal_values(arg_keys[4], (D, D), D ** -0.5, 0.21875, ((0, 4),))
    w_value = normal_values(arg_keys[5], (D, D), D ** -0.5, 0.21875, ((0, 4),))
    w_out = normal_values(arg_keys[6], (D, D), (D // 16) ** -0.5, 0.875, ((0, 4),))
    w_up = normal_values(arg_keys[7], (D, FF), D ** -0.5, 0.21875, ((0, 4),))
    w_down = normal_values(arg_keys[8], (FF, D), FF ** -0.5, 0.109375, ((0, 4),))
    b_query = normal_values(arg_keys[9], (D,), 0.3, 2.0, ((0, 4),))
    b_value = normal_values(arg_keys[10], (D,), 0.3, 2.0, ((0, 4),))
    b_out = normal_values(arg_keys[11], (D,), 0.3, 2.0, ((0, 4),))
    gain_attn = jnp.clip(1.0 + 0.1 * jax.random.normal(arg_keys[12], (D,), jnp.float32), 0.5, 1.5).astype(jnp.bfloat16)
    shift_attn = normal_values(arg_keys[13], (D,), 0.3, 2.0, ((0, 4),))
    b_up = normal_values(arg_keys[14], (FF,), 0.3, 2.0, ((0, 4),))
    b_down = normal_values(arg_keys[15], (D,), 0.3, 2.0, ((0, 4),))
    gain_ffn = jnp.clip(1.0 + 0.1 * jax.random.normal(arg_keys[16], (D,), jnp.float32), 0.5, 1.5).astype(jnp.bfloat16)
    shift_ffn = normal_values(arg_keys[17], (D,), 0.3, 2.0, ((0, 4),))
    return {"tokens_in": tokens_in, "doc_ids": doc_ids, "out_grad": out_grad, "w_query": w_query, "w_key": w_key, "w_value": w_value, "w_out": w_out, "w_up": w_up, "w_down": w_down, "b_query": b_query, "b_value": b_value, "b_out": b_out, "gain_attn": gain_attn, "shift_attn": shift_attn, "b_up": b_up, "b_down": b_down, "gain_ffn": gain_ffn, "shift_ffn": shift_ffn}


EPSILON = 1e-05
NEGATIVE = -1e+30
HIGHEST = lax.Precision.HIGHEST

@jax.custom_vjp
def low(v):
    return lax.optimization_barrier(v.astype(jnp.bfloat16)).astype(jnp.float32)

@jax.custom_vjp
def low_back(v):
    return v

def low_keep(v):
    return (low(v), None)

def low_pass(kept, grad):
    return (grad,)

def back_keep(v):
    return (v, None)

def back_low(kept, grad):
    return (low(grad),)
low.defvjp(low_keep, low_pass)
low_back.defvjp(back_keep, back_low)

def layer_norm(values, gain, shift):
    centre = values - lax.optimization_barrier(jnp.mean(values, axis=-1, keepdims=True))
    spread = lax.optimization_barrier(jnp.mean(centre * centre, axis=-1, keepdims=True))
    return centre * lax.rsqrt(spread + EPSILON) * gain + shift

def product(left, right):
    return jnp.dot(left, right, precision=HIGHEST, preferred_element_type=jnp.float32)

def rounded_both(values):
    return low(low_back(values))

def one_sequence(params, inputs, segment):
    w_query, w_key, w_value, w_out, w_up, w_down, b_query, b_value, b_out, gain_attn, shift_attn, b_up, b_down, gain_ffn, shift_ffn = params
    length = inputs.shape[0]
    rows = min(512, length)
    nblocks = length // rows
    scaling = HEAD_DIM ** (-0.5)
    query = rounded_both(product(inputs, w_query) + b_query)
    keys = rounded_both(product(inputs, w_key)).reshape(length, HEADS, HEAD_DIM)
    values = rounded_both(product(inputs, w_value) + b_value).reshape(length, HEADS, HEAD_DIM)

    def attend(pair):
        query_rows, seg_rows = pair
        scores = jnp.einsum('qhd,khd->hqk', query_rows, keys, precision=HIGHEST) * scaling
        scores = low_back(scores)
        allowed = seg_rows[:, None] == segment[None, :]
        scores = jnp.where(allowed[None], scores, NEGATIVE)
        row_max = lax.optimization_barrier(jnp.max(scores, axis=-1, keepdims=True))
        exponent = jnp.exp(scores - row_max)
        probs = low(exponent / lax.optimization_barrier(jnp.sum(exponent, axis=-1, keepdims=True)))
        joined = jnp.einsum('hqk,khd->qhd', probs, values, precision=HIGHEST)
        return joined.reshape(rows, HEADS * HEAD_DIM)
    attended = lax.map(jax.checkpoint(attend), (query.reshape(nblocks, rows, HEADS, HEAD_DIM), segment.reshape(nblocks, rows)))
    attended = rounded_both(attended.reshape(length, HEADS * HEAD_DIM))
    branch = low_back(product(attended, w_out) + b_out)
    normed = layer_norm(inputs + branch, gain_attn, shift_attn)
    hidden = low_back(product(low(normed), w_up) + b_up)
    activated = low(jax.nn.gelu(hidden, approximate=False))
    ffn_out = low_back(product(activated, w_down) + b_down)
    return layer_norm(normed + ffn_out, gain_ffn, shift_ffn)

def reference(tokens_in, doc_ids, out_grad, w_query, w_key, w_value, w_out, w_up, w_down, b_query, b_value, b_out, gain_attn, shift_attn, b_up, b_down, gain_ffn, shift_ffn):
    params = tuple((member.astype(jnp.float32) for member in (w_query, w_key, w_value, w_out, w_up, w_down, b_query, b_value, b_out, gain_attn, shift_attn, b_up, b_down, gain_ffn, shift_ffn)))
    inputs = tokens_in.astype(jnp.float32)

    def forward(all_inputs, all_params):

        def per_sequence(pair):
            return one_sequence(all_params, pair[0], pair[1])
        return lax.map(jax.checkpoint(per_sequence), (all_inputs, doc_ids))
    layer_out, pullback = jax.vjp(forward, inputs, params)
    grad_input, grads = pullback(out_grad.astype(jnp.float32))
    return (layer_out.astype(jnp.bfloat16), grad_input, grads[0], grads[1], grads[2], grads[3], grads[4], grads[5], grads[6], grads[7], grads[8], grads[9], grads[10], grads[11], grads[12], grads[13], grads[14])
```

```python
import functools

import jax
import jax.numpy as jnp
from jax import lax
from jax.experimental import pallas as pl
from jax.experimental.pallas import tpu as pltpu
from jax.sharding import PartitionSpec as P

HEADS = 12
HEAD_DIM = 64
EPSILON = 1e-05
NEGATIVE = -1e30
F32 = jnp.float32
BF16 = jnp.bfloat16
MESH = pl.DeviceIdType.MESH
ANY = pl.BlockSpec(memory_space=pl.ANY)


class Place:
    def __init__(self):
        self.g = lax.axis_index("group")
        self.r = lax.axis_index("replica")
        self.c = self.r % 2
        self.z = self.r // 2
        self.gx = self.g + 1 - 2 * (self.g % 2)
        self.gy = self.g + 2 - 4 * (self.g // 2)
        self.gd = 3 - self.g
        self.rp = self.r + 1 - 2 * self.c


def remote(src, dst, send, recv, device):
    return pltpu.make_async_remote_copy(
        src_ref=src, dst_ref=dst, send_sem=send, recv_sem=recv, device_id=device, device_id_type=MESH
    )


def plane_barrier(place, extra=()):
    barrier = pltpu.get_barrier_semaphore()
    for g in (place.g, place.gx, place.gy, place.gd):
        for r in (place.r, place.rp):
            if g is place.g and r is place.r:
                continue
            pl.semaphore_signal(barrier, inc=1, device_id=(g, r), device_id_type=MESH)
    return barrier


def dot(a, b):
    return jnp.dot(a, b, preferred_element_type=F32)


def norm_parts(values):
    centre = values - jnp.mean(values, axis=-1, keepdims=True)
    spread = jnp.mean(centre * centre, axis=-1, keepdims=True)
    inverse = lax.rsqrt(spread + EPSILON)
    return centre * inverse, inverse


GROUPS = 6


def half_of(W, k, r, core, part=None):
    if k < 4:
        lo, hi = ((0, 3), (3, 4), (4, 6), (6, 8))[k]
        start, size = 192 * r + 96 * core, 96
        if part is not None:
            start, size = start + 48 * part, 48
        return W.at[lo:hi, pl.ds(pl.multiple_of(start, 16), size), :]
    start, size = 384 * (k - 4) + 192 * core, 192
    if part is not None:
        start, size = start + 96 * part, 96
    return W.at[8 + r, pl.ds(pl.multiple_of(start, 16), size), :]


def forward_kernel(
    tok, docs_in, og, wq, wk, wv, wo, wup, wdn, pack,
    Wo, Xo, Qo, KVo, Mo, Lo, ATo, ATTo, R1o, NLo, ACo, GPo, R2o, Go, PFo,
    W, X, D, PK, PF, Q, KV, MASK, LSE, AT, ATT, R1, NL, R2, ACT, GP,
    lsem, osem, ags, agr, xs, xr, ds_, dr, ps, pr, gs, gr, kvs, kvr, los, lor,
):
    me = Place()
    g, r, c, z = me.g, me.r, me.c, me.z
    gx, gy, gd, rp = me.gx, me.gy, me.gd, me.rp

    local = []
    for w, ref in enumerate((wq, wk, wv, wo)):
        local.append((ref, W.at[w, pl.ds(pl.multiple_of(192 * g, 16), 192), :]))
    for u in range(4):
        local.append((wup.at[:, 768 * u : 768 * u + 768], W.at[4 + u, pl.ds(pl.multiple_of(192 * g, 16), 192), :]))
    local.append((wdn, W.at[8 + g]))
    local.append((pack, PK.at[g]))
    local = [pltpu.make_async_copy(a, b, lsem.at[i]) for i, (a, b) in enumerate(local)]
    for copy in local:
        copy.start()

    barrier = plane_barrier(me)
    pl.semaphore_wait(barrier, 7)

    def reshard(src, dst_of, ssem, rsem):
        for m in range(2):
            t, e = 2 * c + m, g // 2
            b = g % 2
            here = (t == g) & (e == c)
            src_m = src.at[m]
            dst_b = dst_of(b)

            @pl.when(jnp.logical_not(here))
            def _():
                remote(src_m, dst_b, ssem.at[m], rsem.at[b], (t, 2 * z + e)).start()

            @pl.when(here)
            def _():
                pltpu.make_async_copy(src_m, dst_b, rsem.at[b]).start()

    def reshard_wait(src, dst_of, ssem, rsem, b):
        remote(src.at[0], dst_of(b), ssem.at[0], rsem.at[b], (g, r)).wait_recv()

    def reshard_drain(src, dst_of, ssem, rsem):
        for m in range(2):
            t, e = 2 * c + m, g // 2
            here = (t == g) & (e == c)

            @pl.when(jnp.logical_not(here))
            def _():
                remote(src.at[m], dst_of(0), ssem.at[m], rsem.at[0], (t, 2 * z + e)).wait_send()

    def x_rows(b):
        if isinstance(b, int):
            return X.at[256 * b : 256 * b + 256, :]
        return X.at[pl.ds(pl.multiple_of(256 * b, 256), 256), :]

    def g_rows(b):
        if isinstance(b, int):
            return Go.at[256 * b : 256 * b + 256, :]
        return Go.at[pl.ds(pl.multiple_of(256 * b, 256), 256), :]

    reshard(tok, x_rows, xs, xr)

    for m in range(2):
        for e in range(2):
            t = 2 * c + m
            here = (t == g) & (c == e)

            @pl.when(jnp.logical_not(here))
            def _():
                remote(docs_in.at[m], D.at[g], ds_.at[2 * m + e], dr.at[g], (t, 2 * z + e)).start()

            @pl.when(here)
            def _():
                pltpu.make_async_copy(docs_in.at[m], D.at[g], dr.at[g]).start()

    def own_send(k):
        piece = half_of(W, k, g, c)
        remote(piece, piece, ags.at[k, 0], agr.at[k, 0], (gx, r)).start()
        remote(piece, piece, ags.at[k, 1], agr.at[k, 1], (gy, r)).start()

    def to_partner(k, slot, piece):
        remote(piece, piece, ags.at[k, slot], agr.at[k, slot], (g, rp)).start()

    def landed(k, slot, piece):
        remote(piece, piece, ags.at[k, slot], agr.at[k, slot], (g, rp)).wait_recv()

    def relay(k):
        piece = half_of(W, k, gx, c)
        landed(k, 0, piece)
        part = half_of(W, k, gx, c, 0)
        remote(part, part, ags.at[k, 2], agr.at[k, 2], (gy, r)).start()
        to_partner(k, 4, piece)
        piece = half_of(W, k, gy, c)
        landed(k, 1, piece)
        part = half_of(W, k, gy, c, 1)
        remote(part, part, ags.at[k, 3], agr.at[k, 3], (gx, r)).start()
        to_partner(k, 5, piece)

    def diagonal(k):
        landed(k, 2, half_of(W, k, gd, c, 0))
        landed(k, 3, half_of(W, k, gd, c, 1))
        to_partner(k, 6, half_of(W, k, gd, c))

    def complete(k):
        landed(k, 4, half_of(W, k, gx, 1 - c))
        landed(k, 5, half_of(W, k, gy, 1 - c))
        landed(k, 6, half_of(W, k, gd, 1 - c))

    def gather_drain(k):
        for slot, piece in (
            (0, half_of(W, k, g, c)), (1, half_of(W, k, g, c)),
            (2, half_of(W, k, gx, c, 0)), (3, half_of(W, k, gy, c, 1)),
            (4, half_of(W, k, gx, c)), (5, half_of(W, k, gy, c)), (6, half_of(W, k, gd, c)),
        ):
            remote(piece, piece, ags.at[k, slot], agr.at[k, slot], (g, rp)).wait_send()

    for i in range(3):
        local[i].wait()
    own_send(0)
    for i in range(3, 10):
        local[i].wait()
    own_send(1)
    for slot, chip in enumerate((gx, gy, gd)):
        remote(PK.at[g], PK.at[g], ps.at[slot], pr.at[slot], (chip, r)).start()
    relay(0)
    own_send(2)

    for slot, chip in enumerate((gx, gy, gd)):
        remote(PK.at[chip], PK.at[chip], ps.at[slot], pr.at[slot], (chip, r)).wait_recv()
    PF[...] = PK[0].astype(F32) + PK[1].astype(F32) + PK[2].astype(F32) + PK[3].astype(F32)
    for i in range(4):
        remote(docs_in.at[0], D.at[i], ds_.at[0], dr.at[i], (g, r)).wait_recv()
    for i in range(4):
        keys = D[i].astype(F32).T[:, 0:1]
        for b in range(2):
            rows = D[2 * c + b].astype(F32)[0:1, :]
            MASK[256 * i : 256 * i + 256, 256 * b : 256 * b + 256] = jnp.where(keys == rows, 0.0, NEGATIVE)
    for b in range(2):
        reshard_wait(tok, x_rows, xs, xr, b)
    remote(X, Xo.at[c], los.at[0], lor.at[0], (g, rp)).start()
    outs = [
        (X, Xo.at[c]), (PF, PFo), (MASK, Mo),
    ]
    out_copies = []

    def emit(pairs):
        for a, b in pairs:
            copy = pltpu.make_async_copy(a, b, osem.at[len(out_copies)])
            copy.start()
            out_copies.append(copy)

    emit(outs)
    diagonal(0)
    complete(0)
    own_rows = pl.ds(pl.multiple_of(512 * c, 512), 512)

    def project(w, t, dst):
        cols = pl.ds(pl.multiple_of(256 * t, 256), 256)
        out = dot(X[...], W[w, :, cols]) + PF[pl.ds(w, 1), cols]
        return cols, out.astype(BF16)

    @pl.loop(0, 6)
    def _(i):
        w = i // 3
        cols, out = project(1 + w, i % 3, None)
        KV[w, own_rows, cols] = out

    for w in range(2):
        piece = KV.at[w, own_rows, :]
        remote(piece, piece, kvs.at[w], kvr.at[w], (g, rp)).start()
    relay(1)
    own_send(3)

    @pl.loop(0, 3)
    def _(i):
        cols, out = project(0, i, None)
        Q[:, cols] = out

    diagonal(1)
    complete(1)
    for w in range(2):
        piece = KV.at[w, pl.ds(pl.multiple_of(512 * (1 - c), 512), 512), :]
        remote(piece, piece, kvs.at[w], kvr.at[w], (g, rp)).wait_recv()
    emit([(Q, Qo), (KV, KVo)])

    @pl.loop(0, 12)
    def _(i):
        pair, b = i // 2, i % 2
        lanes = pl.ds(pl.multiple_of(128 * pair, 128), 128)
        cols = pl.ds(pl.multiple_of(256 * b, 256), 256)
        qt = (Q[cols, lanes].astype(F32) * (HEAD_DIM ** -0.5)).T
        kp = KV[0, :, lanes]
        vt = KV[1, :, lanes].astype(F32).T.astype(BF16)
        top = lax.broadcasted_iota(jnp.int32, (128, 256), 0) < 64
        pieces = []
        for hh in range(2):
            qh = jnp.where(top if hh == 0 else jnp.logical_not(top), qt, 0.0).astype(BF16)
            s = dot(kp, qh) + MASK[:, cols]
            peak = jnp.max(s, axis=0, keepdims=True)
            e = jnp.exp(s - peak)
            total = jnp.sum(e, axis=0, keepdims=True)
            o = dot(vt[64 * hh : 64 * hh + 64, :], e.astype(BF16)) / total
            LSE[pl.ds(2 * pair + hh, 1), cols] = peak + jnp.log(total)
            pieces.append(o)
        ot = jnp.concatenate(pieces, axis=0)
        ATT[lanes, cols] = ot.astype(BF16)
        AT[cols, lanes] = ot.T.astype(BF16)

        @pl.when(i == 2)
        def _():
            relay(2)
            own_send(4)

        @pl.when(i == 5)
        def _():
            relay(3)
            own_send(5)
            diagonal(2)

        @pl.when(i == 9)
        def _():
            relay(4)
            diagonal(3)

    remote(AT, ATo.at[c], los.at[1], lor.at[1], (g, rp)).start()
    emit([(AT, ATo.at[c]), (ATT, ATTo), (LSE, Lo)])

    @pl.loop(0, 2)
    def _(i):
        rows = pl.ds(pl.multiple_of(256 * i, 256), 256)
        first = X[rows, :].astype(F32) + dot(AT[rows, :], W[3]) + PF[3:4, :]
        R1[rows, :] = first
        shape, _ = norm_parts(first)
        normed = shape * PF[4:5, :] + PF[5:6, :]
        R2[rows, :] = normed + PF[6:7, :]
        NL[rows, :] = normed.astype(BF16)

    remote(NL, NLo.at[c], los.at[2], lor.at[2], (g, rp)).start()
    emit([(R1, R1o), (NL, NLo.at[c])])
    relay(5)
    reshard(og, g_rows, gs, gr)
    complete(2)
    complete(3)

    def up(t):
        u, tt = t // 3, t % 3
        cols = pl.ds(pl.multiple_of(256 * tt, 256), 256)
        wide = pl.ds(pl.multiple_of(256 * t, 256), 256)
        h = dot(NL[...], W[4 + u, :, cols]) + PF[pl.ds(12 + u, 1), cols]
        cdf = 0.5 * (1.0 + lax.erf(h * (0.5 ** 0.5)))
        ACT[:, wide] = (h * cdf).astype(BF16)
        GP[:, wide] = (cdf + h * jnp.exp(-0.5 * h * h) * 0.3989422804014327).astype(BF16)

    @pl.loop(0, 12)
    def _(t):
        up(t)

        @pl.when(t == 8)
        def _():
            diagonal(4)

    diagonal(5)
    remote(ACT, ACo.at[c], los.at[3], lor.at[3], (g, rp)).start()
    emit([(ACT, ACo.at[c]), (GP, GPo)])
    complete(4)
    complete(5)

    @pl.loop(0, 12)
    def _(t):
        k, tt = t // 3, t % 3
        cols = pl.ds(pl.multiple_of(256 * tt, 256), 256)
        deep = pl.ds(pl.multiple_of(768 * k, 256), 768)
        R2[:, cols] += dot(ACT[:, deep], W[8 + k, :, cols])

    emit([(W, Wo), (R2, R2o)])

    for b in range(2):
        reshard_wait(og, g_rows, gs, gr, b)
    reshard_drain(tok, x_rows, xs, xr)
    reshard_drain(og, g_rows, gs, gr)
    for m in range(2):
        for e in range(2):
            t = 2 * c + m
            here = (t == g) & (c == e)

            @pl.when(jnp.logical_not(here))
            def _():
                remote(docs_in.at[m], D.at[g], ds_.at[2 * m + e], dr.at[g], (t, 2 * z + e)).wait_send()
    for slot, chip in enumerate((gx, gy, gd)):
        remote(PK.at[g], PK.at[g], ps.at[slot], pr.at[slot], (chip, r)).wait_send()
    for k in range(GROUPS):
        gather_drain(k)
    for w in range(2):
        piece = KV.at[w, own_rows, :]
        remote(piece, piece, kvs.at[w], kvr.at[w], (g, rp)).wait_send()
    for i, (a, o) in enumerate(((X, Xo), (AT, ATo), (NL, NLo), (ACT, ACo))):
        copy = remote(a, o.at[c], los.at[i], lor.at[i], (g, rp))
        copy.wait_send()
        remote(a, o.at[1 - c], los.at[i], lor.at[i], (g, rp)).wait_recv()
    for copy in out_copies:
        copy.wait()


def sds(shape, dtype=BF16):
    return jax.ShapeDtypeStruct(shape, dtype)


def forward(tok, docs_in, og, wq, wk, wv, wo, wup, wdn, pack):
    out = [
        sds((12, 768, 768)), sds((2, 512, 768)), sds((512, 768)), sds((2, 1024, 768)),
        sds((1024, 512), F32), sds((16, 512), F32), sds((2, 512, 768)), sds((768, 512)),
        sds((512, 768), F32), sds((2, 512, 768)), sds((2, 512, 3072)), sds((512, 3072)),
        sds((512, 768), F32), sds((512, 768)), sds((16, 768), F32),
    ]
    dma = pltpu.SemaphoreType.DMA
    v = pltpu.VMEM
    return pl.pallas_call(
        forward_kernel,
        out_shape=out,
        in_specs=[ANY] * 10,
        out_specs=[ANY] * len(out),
        scratch_shapes=[
            v((12, 768, 768), BF16), v((512, 768), BF16), v((4, 8, 256), jnp.int32), v((4, 16, 768), BF16),
            v((16, 768), F32), v((512, 768), BF16), v((2, 1024, 768), BF16), v((1024, 512), F32), v((16, 512), F32),
            v((512, 768), BF16), v((768, 512), BF16), v((512, 768), F32), v((512, 768), BF16), v((512, 768), F32),
            v((512, 3072), BF16), v((512, 3072), BF16),
            dma((10,)), dma((16,)), dma((6, 7)), dma((6, 7)), dma((2,)), dma((2,)), dma((4,)), dma((4,)),
            dma((3,)), dma((3,)), dma((2,)), dma((2,)), dma((2,)), dma((2,)), dma((4,)), dma((4,)),
        ],
        compiler_params=pltpu.CompilerParams(
            collective_id=0, has_side_effects=True, vmem_limit_bytes=66000000
        ),
    )(tok, docs_in, og, wq, wk, wv, wo, wup, wdn, pack)


def pack_small(g, b_query, b_value, b_out, gain_attn, shift_attn, b_down, gain_ffn, shift_ffn, b_up):
    zero = jnp.zeros_like(b_query)
    rows = jnp.stack(
        [b_query, zero, b_value, b_out, gain_attn, shift_attn, b_down, gain_ffn, shift_ffn, zero, zero, zero]
    )
    wide = jnp.tile(rows, (1, 4))
    lane = lax.broadcasted_iota(jnp.int32, wide.shape, 1) // 192
    wide = jnp.where(lane == g, wide, jnp.zeros_like(wide))
    tall = jnp.broadcast_to(b_up[None], (4, 768))
    tall = jnp.where(lax.broadcasted_iota(jnp.int32, tall.shape, 0) == g, tall, jnp.zeros_like(tall))
    return jnp.concatenate([wide, tall], axis=0)


def dot_nt(a, b):
    return lax.dot_general(a, b, (((1,), (1,)), ((), ())), preferred_element_type=F32)


def dot_tn(a, b):
    return lax.dot_general(a, b, (((0,), (0,)), ((), ())), preferred_element_type=F32)


def columns(values):
    return jnp.sum(values, axis=0, keepdims=True)


CHUNKS = 12


def backward_kernel(
    Wi, Xi, Qi, KVi, Mi, Li, ATi, ATTi, R1i, NLi, ACi, GPi, R2i, Gi, PFi,
    LOo, GIo, To, BTo,
    W, P1, P2, ZR, ACT, GP, DHP, Q, KV, MASK, LSE, ATT, R1, R2, G, PF,
    DF, DFP, DB, DBP, DATT, DQ, DQP, DKV, DKVO, DKVS, DKVR, DKP, LO, ACC, BG, BR, BS, BZ, BT,
    lsem, p1s, p1r, p2s, p2r, zs, zr, ts, tr, xs_, xr_, los, lor, gis, gir, b1s, b1r, b2s, b2r, osem,
):
    me = Place()
    g, r, c, z = me.g, me.r, me.c, me.z
    gx, gy, gd, rp = me.gx, me.gy, me.gd, me.rp
    outer = (z == 0) | (z == 3)
    inner = jnp.logical_not(outer)

    loads = {}

    def load(name, src, dst):
        copy = pltpu.make_async_copy(src, dst, lsem.at[len(loads)])
        copy.start()
        loads[name] = copy

    load("r2", R2i, R2)
    load("g", Gi, G)
    load("pf", PFi, PF)
    load("down", Wi.at[8:12], W.at[8:12])
    load("gp", GPi, GP)
    load("act", ACi, ACT)
    load("up", Wi.at[4:8], W.at[4:8])
    load("r1", R1i, R1)
    load("small", Wi.at[0:4], W.at[0:4])
    load("q", Qi, Q)
    load("kv", KVi, KV)
    load("mask", Mi, MASK)
    load("lse", Li, LSE)
    load("att_t", ATTi, ATT)
    BG[...] = jnp.zeros_like(BG)

    barrier = plane_barrier(me)
    zin, zout, zother = 1 + z // 3, 3 * (z - 1), 3 - z

    def zdev(zz):
        return (g, 2 * zz + c)

    for step in range(1, 4):
        pl.semaphore_signal(barrier, inc=1, device_id=zdev((z + step) % 4), device_id_type=MESH)
    pl.semaphore_wait(barrier, 10)

    def grad(j, q, part=None):
        start, size = 0, 192
        if part is not None:
            start, size = 96 * part, 96
        if j < 4:
            return W.at[8 + q // 2, pl.ds(192 * j + start, size), pl.ds(pl.multiple_of(384 * (q % 2), 128), 384)]
        rows = pl.ds(pl.multiple_of(192 * q + start, 16), size)
        if j < 8:
            return W.at[10 + (j - 4) // 2, rows, 384 * (j % 2) : 384 * (j % 2) + 384]
        return W.at[4 + (j - 8) // 2, rows, 384 * (j % 2) : 384 * (j % 2) + 384]

    def first(j):
        remote(grad(j, gd, 0), P1.at[j, 0], p1s.at[j, 0], p1r.at[j, 0], (gy, r)).start()
        remote(grad(j, gd, 1), P1.at[j, 1], p1s.at[j, 1], p1r.at[j, 1], (gx, r)).start()

    def plain(j):
        remote(grad(j, gx, 1), P2.at[j, 0, 96:192], p2s.at[j, 0], p2r.at[j, 0], (gx, r)).start()
        remote(grad(j, gy, 0), P2.at[j, 1, 0:96], p2s.at[j, 1], p2r.at[j, 1], (gy, r)).start()

    def passed(j):
        for side, (chip, slot, rows) in enumerate(((gx, 0, slice(0, 96)), (gy, 1, slice(96, 192)))):
            mine = grad(j, chip, side)
            remote(mine, P1.at[j, side], p1s.at[j, side], p1r.at[j, side], (chip, r)).wait_recv()
            mine[...] = (mine[...].astype(F32) + P1[j, side].astype(F32)).astype(BF16)
            remote(mine, P2.at[j, slot, rows], p2s.at[j, 2 + side], p2r.at[j, 2 + side], (chip, r)).start()

    def own(j):
        for slot, rows, k in ((0, slice(96, 192), 0), (1, slice(0, 96), 1), (0, slice(0, 96), 2), (1, slice(96, 192), 3)):
            dst = P2.at[j, slot, rows]
            remote(dst, dst, p2s.at[j, k], p2r.at[j, k], (gx, r)).wait_recv()
        mine = grad(j, g)
        total = mine[...].astype(F32) + P2[j, 0].astype(F32) + P2[j, 1].astype(F32)
        P2[j, 0] = total.astype(BF16)

        @pl.when(outer)
        def _():
            remote(P2.at[j, 0], ZR.at[j, 0], zs.at[j, 0], zr.at[j, 0], zdev(zin)).start()

    def chain(j):
        @pl.when(inner)
        def _():
            remote(P2.at[j, 0], ZR.at[j, 0], zs.at[j, 0], zr.at[j, 0], zdev(zother)).wait_recv()
            P2[j, 0] = (P2[j, 0].astype(F32) + ZR[j, 0].astype(F32)).astype(BF16)
            remote(P2.at[j, 0], ZR.at[j, 1], zs.at[j, 1], zr.at[j, 1], zdev(zother)).start()

    def finish(j):
        @pl.when(inner)
        def _():
            remote(P2.at[j, 0], ZR.at[j, 1], zs.at[j, 1], zr.at[j, 1], zdev(zother)).wait_recv()
            P2[j, 1] = (P2[j, 0].astype(F32) + ZR[j, 1].astype(F32)).astype(BF16)
            remote(P2.at[j, 1], ZR.at[j, 0], zs.at[j, 0], zr.at[j, 0], zdev(zout)).start()

        @pl.when(outer)
        def _():
            remote(P2.at[j, 1], ZR.at[j, 0], zs.at[j, 0], zr.at[j, 0], zdev(zin)).wait_recv()
            P2[j, 1] = ZR[j, 0]

        remote(P2.at[j, 1], To.at[c, j], ts.at[j], tr.at[j], (g, rp)).start()
        pltpu.make_async_copy(P2.at[j, 1], To.at[c, j], osem.at[j]).start()

    def drain(j):
        for side in range(2):
            remote(P1.at[j, side], P1.at[j, side], p1s.at[j, side], p1r.at[j, side], (gx, r)).wait_send()
        for k in range(4):
            remote(P1.at[j, 0], P1.at[j, 0], p2s.at[j, k], p2r.at[j, k], (gx, r)).wait_send()
        remote(P2.at[j, 0], ZR.at[j, 0], zs.at[j, 0], zr.at[j, 0], zdev(zother)).wait_send()

        @pl.when(inner)
        def _():
            remote(P2.at[j, 0], ZR.at[j, 1], zs.at[j, 1], zr.at[j, 1], zdev(zother)).wait_send()

        piece = remote(P2.at[j, 1], To.at[1 - c, j], ts.at[j], tr.at[j], (g, rp))
        piece.wait_send()
        piece.wait_recv()
        pltpu.make_async_copy(P2.at[j, 1], To.at[c, j], osem.at[j]).wait()

    def give_back(src, out, ssem, rsem):
        for b in range(2):
            t, e = 2 * c + b, g // 2
            here = (t == g) & (e == c)
            src_b = src.at[256 * b : 256 * b + 256, :]
            dst = out.at[g % 2]

            @pl.when(jnp.logical_not(here))
            def _():
                remote(src_b, dst, ssem.at[b], rsem.at[g % 2], (t, 2 * z + e)).start()

            @pl.when(here)
            def _():
                pltpu.make_async_copy(src_b, dst, rsem.at[g % 2]).start()

    def give_back_drain(src, out, ssem, rsem):
        for b in range(2):
            t, e = 2 * c + b, g // 2
            here = (t == g) & (e == c)
            src_b = src.at[256 * b : 256 * b + 256, :]

            @pl.when(jnp.logical_not(here))
            def _():
                remote(src_b, out.at[0], ssem.at[b], rsem.at[0], (t, 2 * z + e)).wait_send()

            remote(src_b, out.at[b], ssem.at[b], rsem.at[b], (g, rp)).wait_recv()

    def exchange(slot, src, dst):
        remote(src, dst, xs_.at[slot], xr_.at[slot], (g, rp)).start()

    def exchanged(slot, dst):
        remote(dst, dst, xs_.at[slot], xr_.at[slot], (g, rp)).wait_recv()

    def exchange_drain(slot, dst):
        remote(dst, dst, xs_.at[slot], xr_.at[slot], (g, rp)).wait_send()

    mine384 = pl.ds(pl.multiple_of(384 * c, 128), 384)
    theirs384 = pl.ds(pl.multiple_of(384 * (1 - c), 128), 384)

    def norm_back(values, gain, grad_out):
        shape, inverse = norm_parts(values)
        pulled = grad_out * gain
        d = inverse * (
            pulled
            - jnp.mean(pulled, axis=-1, keepdims=True)
            - shape * jnp.mean(pulled * shape, axis=-1, keepdims=True)
        )
        return shape, d

    for name in ("r2", "g", "pf"):
        loads[name].wait()

    @pl.loop(0, 4)
    def _(i):
        rows = pl.ds(pl.multiple_of(128 * i, 128), 128)
        up = G[rows, :].astype(F32)
        shape, d = norm_back(R2[rows, :], PF[7:8, :], up)
        LO[rows, :] = (shape * PF[7:8, :] + PF[8:9, :]).astype(BF16)
        R2[rows, :] = d
        low = d.astype(BF16)
        DF[rows, :] = low
        BG[7:8, :] += columns(up * shape)
        BG[8:9, :] += columns(up)
        BG[6:7, :] += columns(low.astype(F32))

    exchange(0, DF.at[:, theirs384], DFP)
    give_back(LO, LOo, los, lor)
    loads["down"].wait()
    loads["gp"].wait()

    def d_hidden(i):
        t = (i + 6 * (1 - c)) % 12
        tt = t % 3
        wide = pl.ds(pl.multiple_of(256 * t, 256), 256)
        back = dot_nt(DF[...], W[8 + t // 3, pl.ds(pl.multiple_of(256 * tt, 256), 256), :])
        low = (back * GP[:, wide].astype(F32)).astype(BF16)
        GP[:, wide] = low
        BG[pl.ds(12 + t // 3, 1), pl.ds(pl.multiple_of(256 * tt, 256), 256)] = columns(low.astype(F32))

    @pl.loop(0, 6)
    def _(i):
        d_hidden(i)

    exchange(1, GP.at[:, pl.ds(pl.multiple_of(1536 * (1 - c), 128), 1536)], DHP)

    @pl.loop(6, 12)
    def _(i):
        d_hidden(i)

    loads["act"].wait()
    exchanged(0, DFP)

    def pair_tn(left, lanes, own_right, their_right):
        return dot_tn(left[c, :, lanes], own_right) + dot_tn(left[1 - c, :, lanes], their_right)

    def down_quarter(q):
        @pl.loop(0, 3)
        def _(i):
            lanes = pl.ds(pl.multiple_of(768 * q + 256 * i, 256), 256)
            out = pair_tn(ACT, lanes, DF[:, mine384], DFP[...])
            W[8 + q // 2, pl.ds(pl.multiple_of(256 * i, 256), 256), pl.ds(pl.multiple_of(384 * (q % 2), 128), 384)] = (
                out.astype(BF16)
            )

    down_quarter(gd)
    for j in range(4):
        first(j)
    down_quarter(gx)
    down_quarter(gy)
    for j in range(4):
        plain(j)
    down_quarter(g)
    load("nl", NLi, ACT.at[:, :, 0:768])
    load("att", ATi, ACT.at[:, :, 768:1536])
    load("x", Xi, ACT.at[:, :, 1536:2304])

    loads["up"].wait()

    @pl.loop(0, 3)
    def _(i):
        cols = pl.ds(pl.multiple_of(256 * i, 256), 256)
        total = R2[:, cols]
        for u in range(4):
            total = total + dot_nt(GP[:, 768 * u : 768 * u + 768], W[4 + u, cols, :])
        R2[:, cols] = total

    passed(0)
    passed(1)
    loads["r1"].wait()

    @pl.loop(0, 4)
    def _(i):
        rows = pl.ds(pl.multiple_of(128 * i, 128), 128)
        up = R2[rows, :]
        shape, d = norm_back(R1[rows, :], PF[4:5, :], up)
        R2[rows, :] = d
        low = d.astype(BF16)
        DB[rows, :] = low
        BG[4:5, :] += columns(up * shape)
        BG[5:6, :] += columns(up)
        BG[3:4, :] += columns(low.astype(F32))

    exchange(2, DB.at[:, theirs384], DBP)
    passed(2)
    passed(3)
    exchanged(1, DHP)
    loads["nl"].wait()

    for j in range(4, 8):
        jj = j - 4
        own_cols = pl.ds(pl.multiple_of(1536 * c + 384 * jj, 128), 384)

        @pl.loop(0, 3)
        def _(i):
            lanes = pl.ds(pl.multiple_of(256 * i, 256), 256)
            out = pair_tn(ACT, lanes, GP[:, own_cols], DHP[:, 384 * jj : 384 * jj + 384])
            W[10 + jj // 2, lanes, 384 * (jj % 2) : 384 * (jj % 2) + 384] = out.astype(BF16)

        first(j)
        plain(j)

    loads["small"].wait()

    @pl.loop(0, 3)
    def _(i):
        cols = pl.ds(pl.multiple_of(256 * i, 256), 256)
        DATT[:, cols] = dot_nt(DB[...], W[3, cols, :]).astype(BF16)

    exchanged(2, DBP)
    loads["att"].wait()

    def square_grad(j, offset, own_right, their_right):
        @pl.loop(0, 3)
        def _(i):
            lanes = pl.ds(pl.multiple_of(offset + 256 * i, 256), 256)
            out = pair_tn(ACT, lanes, own_right[:, mine384], their_right[...])
            W[4 + (j - 8) // 2, pl.ds(pl.multiple_of(256 * i, 256), 256), 384 * (j % 2) : 384 * (j % 2) + 384] = (
                out.astype(BF16)
            )

        first(j)
        plain(j)

    square_grad(8, 768, DB, DBP)

    for name in ("q", "kv", "mask", "lse", "att_t"):
        loads[name].wait()
    own_rows = pl.ds(pl.multiple_of(512 * c, 512), 512)
    their_rows = pl.ds(pl.multiple_of(512 * (1 - c), 512), 512)

    services = {
        0: [(passed, 4), (passed, 5)],
        1: [(passed, 6), (passed, 7), (own, 0)],
        2: [(own, 1), (chain, 0)],
        3: [(own, 2), (chain, 1), (passed, 8)],
        4: [(own, 3), (chain, 2), (finish, 0)],
        5: [(chain, 3), (finish, 1)],
        6: [(own, 4), (finish, 2)],
        7: [(own, 5), (chain, 4), (finish, 3)],
        8: [(own, 6), (chain, 5)],
        9: [(own, 7), (chain, 6), (finish, 4)],
        10: [(chain, 7), (finish, 5), (own, 8)],
        11: [(finish, 6), (chain, 8)],
    }

    @pl.loop(0, 12)
    def _(i):
        pair, b = i // 2, i % 2
        lanes = pl.ds(pl.multiple_of(128 * pair, 128), 128)
        cols = pl.ds(pl.multiple_of(256 * b, 256), 256)
        qs = Q[cols, lanes].astype(F32) * (HEAD_DIM ** -0.5)
        do = DATT[cols, lanes].astype(F32)
        qt, dot_t = qs.T, do.T
        kp = KV[0, :, lanes]
        vp = KV[1, :, lanes]
        kt = kp.astype(F32).T.astype(BF16)
        weigh = dot_t * ATT[lanes, cols].astype(F32)
        top = lax.broadcasted_iota(jnp.int32, (128, 256), 0) < 64
        left = lax.broadcasted_iota(jnp.int32, (256, 128), 1) < 64
        dk = dv = None
        pieces = []
        for hh in range(2):
            rows_in = top if hh == 0 else jnp.logical_not(top)
            lanes_in = left if hh == 0 else jnp.logical_not(left)
            s = dot(kp, jnp.where(rows_in, qt, 0.0).astype(BF16)) + MASK[:, cols]
            p = jnp.exp(s - LSE[pl.ds(2 * pair + hh, 1), cols])
            dp = dot(vp, jnp.where(rows_in, dot_t, 0.0).astype(BF16))
            ds = (p * (dp - columns(weigh[64 * hh : 64 * hh + 64, :]))).astype(BF16)
            dv_h = dot(p.astype(BF16), jnp.where(lanes_in, do, 0.0).astype(BF16))
            dk_h = dot(ds, jnp.where(lanes_in, qs, 0.0).astype(BF16))
            dv = dv_h if dv is None else dv + dv_h
            dk = dk_h if dk is None else dk + dk_h
            pieces.append(dot(kt[64 * hh : 64 * hh + 64, :], ds))
        DQ[cols, lanes] = (jnp.concatenate(pieces, axis=0).T * (HEAD_DIM ** -0.5)).astype(BF16)

        @pl.when(b == 0)
        def _():
            ACC[0] = dk
            ACC[1] = dv

        @pl.when(b == 1)
        def _():
            ACC[0] += dk
            ACC[1] += dv
            for w in range(2):
                DKVO[w, :, lanes] = ACC[w, own_rows, :]
                DKVS[w, :, lanes] = ACC[w, their_rows, :].astype(BF16)

        for k, todo in services.items():
            @pl.when(i == k)
            def _():
                for f, j in todo:
                    f(j)

    exchange(3, DKVS, DKVR)
    exchange(4, DQ.at[:, theirs384], DQP)
    BG[0:1, :] = columns(DQ[...].astype(F32))

    def input_part(w, left):
        @pl.loop(0, 3)
        def _(i):
            cols = pl.ds(pl.multiple_of(256 * i, 256), 256)
            R2[:, cols] += dot_nt(left[...], W[w, cols, :])

    loads["x"].wait()
    input_part(0, DQ)
    exchanged(4, DQP)
    square_grad(9, 1536, DQ, DQP)
    exchanged(3, DKVR)

    @pl.loop(0, 4)
    def _(i):
        rows = pl.ds(pl.multiple_of(128 * i, 128), 128)
        for w in range(2):
            DKV[w, rows, :] = (DKVO[w, rows, :] + DKVR[w, rows, :].astype(F32)).astype(BF16)

    exchange(5, DKV.at[:, :, theirs384], DKP)
    BG[2:3, :] = columns(DKV[1].astype(F32))

    BS[...] = BG[...].astype(BF16)
    others = [(gg, rr, k) for k, (gg, rr) in enumerate(
        ((g, rp), (gx, r), (gx, rp), (gy, r), (gy, rp), (gd, r), (gd, rp)))]
    slot_of = 2 * g + c
    for gg, rr, k in others:
        remote(BS, BR.at[slot_of], b1s.at[k], b1r.at[k], (gg, rr)).start()
    BR[slot_of] = BS[...]

    finish(7)
    exchanged(5, DKP)
    square_grad(10, 1536, DKV.at[0], DKP.at[0])
    square_grad(11, 1536, DKV.at[1], DKP.at[1])
    passed(9)
    input_part(1, DKV.at[0])
    input_part(2, DKV.at[1])
    LO2 = DF
    exchange_drain(0, DFP)
    LO2[...] = R2[...].astype(BF16)
    passed(10)
    passed(11)
    give_back(LO2, GIo, gis, gir)
    finish(8)

    for gg, rr, k in others:
        src = (2 * gg + rr % 2)
        remote(BS, BR.at[src], b1s.at[k], b1r.at[k], (gg, rr)).wait_recv()
    total = BR[0].astype(F32)
    for k in range(1, 8):
        total = total + BR[k].astype(F32)
    BZ[z] = total.astype(BF16)
    for step in range(1, 4):
        zz = (z + step) % 4
        remote(BZ.at[z], BZ.at[z], b2s.at[step - 1], b2r.at[step - 1], zdev(zz)).start()

    own(9)
    own(10)
    chain(9)
    own(11)
    chain(10)
    finish(9)
    chain(11)
    finish(10)
    for step in range(1, 4):
        zz = (z + 4 - step) % 4
        remote(BZ.at[zz], BZ.at[zz], b2s.at[step - 1], b2r.at[step - 1], zdev(zz)).wait_recv()
    BT[...] = (BZ[0].astype(F32) + BZ[1].astype(F32)) + (BZ[2].astype(F32) + BZ[3].astype(F32))
    bt_copy = pltpu.make_async_copy(BT, BTo, osem.at[CHUNKS])
    bt_copy.start()
    finish(11)

    for j in range(CHUNKS):
        drain(j)
    for slot, dst in ((1, DHP), (2, DBP), (3, DKVR), (4, DQP), (5, DKP)):
        exchange_drain(slot, dst)
    give_back_drain(LO, LOo, los, lor)
    give_back_drain(LO2, GIo, gis, gir)
    for gg, rr, k in others:
        remote(BS, BR.at[0], b1s.at[k], b1r.at[k], (gg, rr)).wait_send()
    for step in range(1, 4):
        remote(BZ.at[z], BZ.at[z], b2s.at[step - 1], b2r.at[step - 1], zdev(z)).wait_send()
    bt_copy.wait()


def backward(saved):
    out = [
        sds((2, 256, 768)), sds((2, 256, 768)), sds((2, CHUNKS, 192, 384)), sds((16, 768), F32),
    ]
    dma = pltpu.SemaphoreType.DMA
    v = pltpu.VMEM
    return pl.pallas_call(
        backward_kernel,
        out_shape=out,
        in_specs=[ANY] * 15,
        out_specs=[ANY] * len(out),
        scratch_shapes=[
            v((12, 768, 768), BF16), v((CHUNKS, 2, 96, 384), BF16), v((CHUNKS, 2, 192, 384), BF16),
            v((CHUNKS, 2, 192, 384), BF16),
            v((2, 512, 3072), BF16), v((512, 3072), BF16), v((512, 1536), BF16), v((512, 768), BF16),
            v((2, 1024, 768), BF16), v((1024, 512), F32), v((16, 512), F32), v((768, 512), BF16),
            v((512, 768), F32), v((512, 768), F32), v((512, 768), BF16), v((16, 768), F32),
            v((512, 768), BF16), v((512, 384), BF16), v((512, 768), BF16), v((512, 384), BF16),
            v((512, 768), BF16), v((512, 768), BF16), v((512, 384), BF16), v((2, 512, 768), BF16),
            v((2, 512, 768), F32), v((2, 512, 768), BF16), v((2, 512, 768), BF16), v((2, 512, 384), BF16),
            v((512, 768), BF16), v((2, 1024, 128), F32), v((16, 768), F32), v((8, 16, 768), BF16),
            v((16, 768), BF16), v((4, 16, 768), BF16), v((16, 768), F32),
            dma((20,)), dma((CHUNKS, 2)), dma((CHUNKS, 2)), dma((CHUNKS, 4)), dma((CHUNKS, 4)),
            dma((CHUNKS, 2)), dma((CHUNKS, 2)), dma((CHUNKS,)), dma((CHUNKS,)), dma((6,)), dma((6,)),
            dma((2,)), dma((2,)), dma((2,)), dma((2,)), dma((7,)), dma((7,)), dma((3,)), dma((3,)),
            dma((CHUNKS + 1,)),
        ],
        compiler_params=pltpu.CompilerParams(
            collective_id=1, has_side_effects=True, vmem_limit_bytes=67043328
        ),
    )(*saved)


def fits(mesh):
    return dict(mesh.shape) == {"group": 4, "replica": 8}


def fast(
    tokens_in, doc_ids, out_grad, w_query, w_key, w_value, w_out, w_up, w_down, b_query, b_value, b_out,
    gain_attn, shift_attn, b_up, b_down, gain_ffn, shift_ffn,
):
    g = lax.axis_index("group")
    pack = pack_small(
        g, b_query, b_value, b_out, gain_attn, shift_attn, b_down, gain_ffn, shift_ffn, b_up
    )
    docs = jnp.broadcast_to(doc_ids[:, None, :], (2, 8, 256))
    saved = forward(tokens_in, docs, out_grad, w_query, w_key, w_value, w_out, w_up, w_down, pack)
    layer_out, grad_input, totals, small = backward(saved)
    totals = totals.astype(F32)

    def square(j):
        return jnp.concatenate([totals[0, j], totals[1, j]], axis=1)

    g_up = jnp.concatenate([totals[e, 4 + j] for e in range(2) for j in range(4)], axis=1)
    g_down = jnp.concatenate([square(j) for j in range(4)], axis=0)
    piece = lax.dynamic_slice(small, (0, 192 * g), (16, 192))
    up_piece = lax.dynamic_slice(small, (12 + g, 0), (1, 768))[0]
    return (
        layer_out, grad_input.astype(F32), square(9), square(10), square(11), square(8), g_up, g_down,
        piece[0], piece[2], piece[3], piece[4], piece[5], up_piece, piece[6], piece[7], piece[8],
    )


def layer_norm(values, gain, shift):
    centre = values - jnp.mean(values, axis=-1, keepdims=True)
    spread = jnp.mean(centre * centre, axis=-1, keepdims=True)
    return centre * lax.rsqrt(spread + EPSILON) * gain + shift


def norm_pull(values, gain, shift, grad):
    result, pullback = jax.vjp(
        layer_norm, values, gain.astype(jnp.float32), shift.astype(jnp.float32)
    )
    return (result, pullback(grad))


def exact_gelu(values):
    return jax.nn.gelu(values, approximate=False)


def project(inputs, weight, bias):
    return jnp.dot(inputs, weight, preferred_element_type=jnp.float32) + bias.astype(jnp.float32)


def contract_rows(left, right):
    return lax.dot_general(
        left, right, (((0,), (0,)), ((), ())), preferred_element_type=jnp.float32
    )


def against_rows(grad, weight):
    return lax.dot_general(
        grad, weight, (((1,), (1,)), ((), ())), preferred_element_type=jnp.float32
    )


def column_sum(values):
    return jnp.sum(values.astype(jnp.float32), axis=0)


def add_pair(first, second):
    return first + second


def scores_of(query, keys_all, allowed):
    rows = query.shape[0]
    length = keys_all.shape[0]
    scaling = HEAD_DIM ** (-0.5)
    scores = (
        jnp.einsum(
            "qhd,khd->hqk",
            query.reshape(rows, HEADS, HEAD_DIM),
            keys_all.reshape(length, HEADS, HEAD_DIM),
            preferred_element_type=jnp.float32,
        )
        * scaling
    )
    return jnp.where(allowed[None], scores, NEGATIVE)


def attention_forward(query, keys_all, values_all, allowed):
    rows = query.shape[0]
    length = keys_all.shape[0]
    scores = scores_of(query, keys_all, allowed)
    row_max = jnp.max(scores, axis=-1, keepdims=True)
    exponent = jnp.exp(scores - row_max)
    total = jnp.sum(exponent, axis=-1, keepdims=True)
    probs = (exponent / total).astype(jnp.bfloat16)
    log_total = row_max[..., 0] + jnp.log(total[..., 0])
    joined = jnp.einsum(
        "hqk,khd->qhd",
        probs,
        values_all.reshape(length, HEADS, HEAD_DIM),
        preferred_element_type=jnp.float32,
    )
    return (joined.reshape(rows, HEADS * HEAD_DIM), log_total)


def score_grads(query, keys_all, values_all, allowed, log_total, d_attended):
    rows = query.shape[0]
    length = keys_all.shape[0]
    scores = scores_of(query, keys_all, allowed)
    probs = jnp.exp(scores - log_total[..., None])
    d_heads = d_attended.reshape(rows, HEADS, HEAD_DIM)
    d_probs = jnp.einsum(
        "qhd,khd->hqk",
        d_heads,
        values_all.reshape(length, HEADS, HEAD_DIM),
        preferred_element_type=jnp.float32,
    )
    row_term = jnp.sum(probs * d_probs, axis=-1)
    d_scores = (probs * (d_probs - row_term[..., None])).astype(jnp.bfloat16)
    return (probs, d_scores, row_term)


def attention_backward(query, keys_all, values_all, allowed, log_total, d_attended):
    rows = query.shape[0]
    length = keys_all.shape[0]
    scaling = HEAD_DIM ** (-0.5)
    probs, d_scores, row_term = score_grads(
        query, keys_all, values_all, allowed, log_total, d_attended
    )
    d_heads = d_attended.reshape(rows, HEADS, HEAD_DIM)
    d_values_part = jnp.einsum(
        "hqk,qhd->khd", probs.astype(jnp.bfloat16), d_heads, preferred_element_type=jnp.float32
    ).reshape(length, HEADS * HEAD_DIM)
    d_query = (
        jnp.einsum(
            "hqk,khd->qhd",
            d_scores,
            keys_all.reshape(length, HEADS, HEAD_DIM),
            preferred_element_type=jnp.float32,
        ).reshape(rows, HEADS * HEAD_DIM)
        * scaling
    )
    d_keys_part = (
        jnp.einsum(
            "hqk,qhd->khd",
            d_scores,
            query.reshape(rows, HEADS, HEAD_DIM),
            preferred_element_type=jnp.float32,
        ).reshape(length, HEADS * HEAD_DIM)
        * scaling
    )
    return (d_query, d_keys_part, d_values_part, row_term)


def owner_sum(grads):
    return (
        lax.psum_scatter(
            grads[0].astype(jnp.bfloat16), "group", scatter_dimension=0, tiled=True
        ).astype(jnp.float32),
        lax.psum_scatter(
            grads[1].astype(jnp.bfloat16), "group", scatter_dimension=0, tiled=True
        ).astype(jnp.float32),
        lax.psum_scatter(
            grads[2].astype(jnp.bfloat16), "group", scatter_dimension=0, tiled=True
        ).astype(jnp.float32),
        lax.psum_scatter(
            grads[3].astype(jnp.bfloat16), "group", scatter_dimension=0, tiled=True
        ).astype(jnp.float32),
        lax.psum_scatter(
            grads[4].astype(jnp.bfloat16), "group", scatter_dimension=0, tiled=True
        ).astype(jnp.float32),
        lax.psum_scatter(
            grads[5].astype(jnp.bfloat16), "group", scatter_dimension=0, tiled=True
        ).astype(jnp.float32),
        lax.psum_scatter(
            grads[6].astype(jnp.bfloat16), "group", scatter_dimension=0, tiled=True
        ).astype(jnp.float32),
        lax.psum_scatter(
            grads[7].astype(jnp.bfloat16), "group", scatter_dimension=0, tiled=True
        ).astype(jnp.float32),
        lax.psum_scatter(
            grads[8].astype(jnp.bfloat16), "group", scatter_dimension=0, tiled=True
        ).astype(jnp.float32),
        lax.psum_scatter(
            grads[9].astype(jnp.bfloat16), "group", scatter_dimension=0, tiled=True
        ).astype(jnp.float32),
        lax.psum_scatter(
            grads[10].astype(jnp.bfloat16), "group", scatter_dimension=0, tiled=True
        ).astype(jnp.float32),
        lax.psum_scatter(
            grads[11].astype(jnp.bfloat16), "group", scatter_dimension=0, tiled=True
        ).astype(jnp.float32),
        lax.psum_scatter(
            grads[12].astype(jnp.bfloat16), "group", scatter_dimension=0, tiled=True
        ).astype(jnp.float32),
        lax.psum_scatter(
            grads[13].astype(jnp.bfloat16), "group", scatter_dimension=0, tiled=True
        ).astype(jnp.float32),
        lax.psum_scatter(
            grads[14].astype(jnp.bfloat16), "group", scatter_dimension=0, tiled=True
        ).astype(jnp.float32),
    )


def shards(
    tokens_in,
    doc_ids,
    out_grad,
    w_query,
    w_key,
    w_value,
    w_out,
    w_up,
    w_down,
    b_query,
    b_value,
    b_out,
    gain_attn,
    shift_attn,
    b_up,
    b_down,
    gain_ffn,
    shift_ffn,
):
    gathered = (
        lax.all_gather(w_query, "group", axis=0, tiled=True),
        lax.all_gather(w_key, "group", axis=0, tiled=True),
        lax.all_gather(w_value, "group", axis=0, tiled=True),
        lax.all_gather(w_out, "group", axis=0, tiled=True),
        lax.all_gather(w_up, "group", axis=0, tiled=True),
        lax.all_gather(w_down, "group", axis=0, tiled=True),
        lax.all_gather(b_query, "group", axis=0, tiled=True),
        lax.all_gather(b_value, "group", axis=0, tiled=True),
        lax.all_gather(b_out, "group", axis=0, tiled=True),
        lax.all_gather(gain_attn, "group", axis=0, tiled=True),
        lax.all_gather(shift_attn, "group", axis=0, tiled=True),
        lax.all_gather(b_up, "group", axis=0, tiled=True),
        lax.all_gather(b_down, "group", axis=0, tiled=True),
        lax.all_gather(gain_ffn, "group", axis=0, tiled=True),
        lax.all_gather(shift_ffn, "group", axis=0, tiled=True),
    )
    (
        query_weight,
        key_weight,
        value_weight,
        out_weight,
        up_weight,
        down_weight,
        query_bias,
        value_bias,
        out_bias,
        attn_gain,
        attn_shift,
        up_bias,
        down_bias,
        ffn_gain,
        ffn_shift,
    ) = gathered
    micros = tokens_in.shape[0]
    outputs = []
    stored = []
    for micro in range(micros):
        inputs = tokens_in[micro]
        segment = doc_ids[micro]
        query = project(inputs, query_weight, query_bias).astype(jnp.bfloat16)
        keys = jnp.dot(inputs, key_weight, preferred_element_type=jnp.float32).astype(jnp.bfloat16)
        values = project(inputs, value_weight, value_bias).astype(jnp.bfloat16)
        keys_all, values_all, seg_all = (
            lax.all_gather(keys, "group", axis=0, tiled=True),
            lax.all_gather(values, "group", axis=0, tiled=True),
            lax.all_gather(segment, "group", axis=0, tiled=True),
        )
        allowed = segment[:, None] == seg_all[None, :]
        attended, log_total = attention_forward(query, keys_all, values_all, allowed)
        attended = attended.astype(jnp.bfloat16)
        resid_one = inputs.astype(jnp.float32) + project(attended, out_weight, out_bias)
        normed = layer_norm(
            resid_one, attn_gain.astype(jnp.float32), attn_shift.astype(jnp.float32)
        )
        hidden = project(normed.astype(jnp.bfloat16), up_weight, up_bias)
        activated = exact_gelu(hidden).astype(jnp.bfloat16)
        resid_two = normed + project(activated, down_weight, down_bias)
        result = layer_norm(resid_two, ffn_gain.astype(jnp.float32), ffn_shift.astype(jnp.float32))
        outputs.append(result.astype(jnp.bfloat16))
        stored.append((query, keys, values, log_total, attended, resid_one, hidden, resid_two))
    gathered = (
        lax.all_gather(w_query, "group", axis=0, tiled=True),
        lax.all_gather(w_key, "group", axis=0, tiled=True),
        lax.all_gather(w_value, "group", axis=0, tiled=True),
        lax.all_gather(w_out, "group", axis=0, tiled=True),
        lax.all_gather(w_up, "group", axis=0, tiled=True),
        lax.all_gather(w_down, "group", axis=0, tiled=True),
        lax.all_gather(b_query, "group", axis=0, tiled=True),
        lax.all_gather(b_value, "group", axis=0, tiled=True),
        lax.all_gather(b_out, "group", axis=0, tiled=True),
        lax.all_gather(gain_attn, "group", axis=0, tiled=True),
        lax.all_gather(shift_attn, "group", axis=0, tiled=True),
        lax.all_gather(b_up, "group", axis=0, tiled=True),
        lax.all_gather(b_down, "group", axis=0, tiled=True),
        lax.all_gather(gain_ffn, "group", axis=0, tiled=True),
        lax.all_gather(shift_ffn, "group", axis=0, tiled=True),
    )
    (
        query_weight,
        key_weight,
        value_weight,
        out_weight,
        up_weight,
        down_weight,
        query_bias,
        value_bias,
        out_bias,
        attn_gain,
        attn_shift,
        up_bias,
        down_bias,
        ffn_gain,
        ffn_shift,
    ) = gathered
    totals = tuple((jnp.zeros(member.shape, jnp.float32) for member in gathered))
    input_grads = []
    for micro in range(micros):
        inputs = tokens_in[micro]
        segment = doc_ids[micro]
        query, keys, values, log_total, attended, resid_one, hidden, resid_two = stored[micro]
        upstream = out_grad[micro].astype(jnp.float32)
        unused_out, (d_resid_two, g_ffn_gain, g_ffn_shift) = norm_pull(
            resid_two, ffn_gain, ffn_shift, upstream
        )
        d_ffn = d_resid_two.astype(jnp.bfloat16)
        activated, gelu_pull = jax.vjp(exact_gelu, hidden)
        activated = activated.astype(jnp.bfloat16)
        g_down_w = contract_rows(activated, d_ffn)
        g_down_b = column_sum(d_ffn)
        d_activated = against_rows(d_ffn, down_weight)
        d_hidden = gelu_pull(d_activated)[0].astype(jnp.bfloat16)
        normed = layer_norm(
            resid_one, attn_gain.astype(jnp.float32), attn_shift.astype(jnp.float32)
        )
        normed_low = normed.astype(jnp.bfloat16)
        g_up_w = contract_rows(normed_low, d_hidden)
        g_up_b = column_sum(d_hidden)
        d_normed = against_rows(d_hidden, up_weight) + d_resid_two
        unused_norm, (d_resid_one, g_attn_gain, g_attn_shift) = norm_pull(
            resid_one, attn_gain, attn_shift, d_normed
        )
        d_branch = d_resid_one.astype(jnp.bfloat16)
        g_out_w = contract_rows(attended, d_branch)
        g_out_b = column_sum(d_branch)
        d_attended = against_rows(d_branch, out_weight).astype(jnp.bfloat16)
        keys_all, values_all, seg_all = (
            lax.all_gather(keys, "group", axis=0, tiled=True),
            lax.all_gather(values, "group", axis=0, tiled=True),
            lax.all_gather(segment, "group", axis=0, tiled=True),
        )
        allowed = segment[:, None] == seg_all[None, :]
        d_query, d_keys_part, d_values_part, row_term = attention_backward(
            query, keys_all, values_all, allowed, log_total, d_attended
        )
        d_keys, d_values = (
            lax.psum_scatter(
                d_keys_part.astype(jnp.bfloat16), "group", scatter_dimension=0, tiled=True
            ).astype(jnp.float32),
            lax.psum_scatter(
                d_values_part.astype(jnp.bfloat16), "group", scatter_dimension=0, tiled=True
            ).astype(jnp.float32),
        )
        d_query = d_query.astype(jnp.bfloat16)
        d_keys = d_keys.astype(jnp.bfloat16)
        d_values = d_values.astype(jnp.bfloat16)
        g_query_w = contract_rows(inputs, d_query)
        g_key_w = contract_rows(inputs, d_keys)
        g_value_w = contract_rows(inputs, d_values)
        g_query_b = column_sum(d_query)
        g_value_b = column_sum(d_values)
        input_grad = (
            d_resid_one
            + against_rows(d_query, query_weight)
            + against_rows(d_keys, key_weight)
            + against_rows(d_values, value_weight)
        )
        input_grads.append(input_grad)
        micro_grads = (
            g_query_w,
            g_key_w,
            g_value_w,
            g_out_w,
            g_up_w,
            g_down_w,
            g_query_b,
            g_value_b,
            g_out_b,
            g_attn_gain,
            g_attn_shift,
            g_up_b,
            g_down_b,
            g_ffn_gain,
            g_ffn_shift,
        )
        totals = jax.tree.map(add_pair, totals, micro_grads)
    totals = tuple(owner_sum(totals))
    summed = (
        lax.psum(totals[0].astype(jnp.bfloat16), "replica").astype(jnp.float32),
        lax.psum(totals[1].astype(jnp.bfloat16), "replica").astype(jnp.float32),
        lax.psum(totals[2].astype(jnp.bfloat16), "replica").astype(jnp.float32),
        lax.psum(totals[3].astype(jnp.bfloat16), "replica").astype(jnp.float32),
        lax.psum(totals[4].astype(jnp.bfloat16), "replica").astype(jnp.float32),
        lax.psum(totals[5].astype(jnp.bfloat16), "replica").astype(jnp.float32),
        lax.psum(totals[6].astype(jnp.bfloat16), "replica").astype(jnp.float32),
        lax.psum(totals[7].astype(jnp.bfloat16), "replica").astype(jnp.float32),
        lax.psum(totals[8].astype(jnp.bfloat16), "replica").astype(jnp.float32),
        lax.psum(totals[9].astype(jnp.bfloat16), "replica").astype(jnp.float32),
        lax.psum(totals[10].astype(jnp.bfloat16), "replica").astype(jnp.float32),
        lax.psum(totals[11].astype(jnp.bfloat16), "replica").astype(jnp.float32),
        lax.psum(totals[12].astype(jnp.bfloat16), "replica").astype(jnp.float32),
        lax.psum(totals[13].astype(jnp.bfloat16), "replica").astype(jnp.float32),
        lax.psum(totals[14].astype(jnp.bfloat16), "replica").astype(jnp.float32),
    )
    layer_out = jnp.stack(outputs)
    grad_input = jnp.stack(input_grads)
    return (
        layer_out,
        grad_input,
        summed[0],
        summed[1],
        summed[2],
        summed[3],
        summed[4],
        summed[5],
        summed[6],
        summed[7],
        summed[8],
        summed[9],
        summed[10],
        summed[11],
        summed[12],
        summed[13],
        summed[14],
    )


def solution(mesh):
    return jax.shard_map(
        shards if not fits(mesh) else fast,
        mesh=mesh,
        in_specs=(
            P("replica", "group", None),
            P("replica", "group"),
            P("replica", "group", None),
            P("group", None),
            P("group", None),
            P("group", None),
            P("group", None),
            P("group", None),
            P("group", None),
            P("group"),
            P("group"),
            P("group"),
            P("group"),
            P("group"),
            P("group"),
            P("group"),
            P("group"),
            P("group"),
        ),
        out_specs=(
            P("replica", "group", None),
            P("replica", "group", None),
            P("group", None),
            P("group", None),
            P("group", None),
            P("group", None),
            P("group", None),
            P("group", None),
            P("group"),
            P("group"),
            P("group"),
            P("group"),
            P("group"),
            P("group"),
            P("group"),
            P("group"),
            P("group"),
        ),
        check_vma=False,
    )
```

```python
import functools

import jax
import jax.numpy as jnp
from jax import lax
from jax.experimental import pallas as pl
from jax.experimental.pallas import tpu as pltpu
from jax.sharding import PartitionSpec as P

HEADS = 12
HEAD_DIM = 64
EPSILON = 1e-05
NEGATIVE = -1e30
F32 = jnp.float32
BF16 = jnp.bfloat16
MESH = pl.DeviceIdType.MESH
ANY = pl.BlockSpec(memory_space=pl.ANY)


class Place:
    def __init__(self):
        self.g = lax.axis_index("group")
        self.r = lax.axis_index("replica")
        self.c = self.r % 2
        self.z = self.r // 2
        self.gx = self.g + 1 - 2 * (self.g % 2)
        self.gy = self.g + 2 - 4 * (self.g // 2)
        self.gd = 3 - self.g
        self.rp = self.r + 1 - 2 * self.c


def remote(src, dst, send, recv, device):
    return pltpu.make_async_remote_copy(
        src_ref=src, dst_ref=dst, send_sem=send, recv_sem=recv, device_id=device, device_id_type=MESH
    )


def plane_barrier(place, extra=()):
    barrier = pltpu.get_barrier_semaphore()
    for g in (place.g, place.gx, place.gy, place.gd):
        for r in (place.r, place.rp):
            if g is place.g and r is place.r:
                continue
            pl.semaphore_signal(barrier, inc=1, device_id=(g, r), device_id_type=MESH)
    return barrier


def dot(a, b):
    return jnp.dot(a, b, preferred_element_type=F32)


def norm_parts(values):
    centre = values - jnp.mean(values, axis=-1, keepdims=True)
    spread = jnp.mean(centre * centre, axis=-1, keepdims=True)
    inverse = lax.rsqrt(spread + EPSILON)
    return centre * inverse, inverse


GROUPS = 6


def half_of(W, k, r, core, part=None):
    if k < 4:
        lo, hi = ((0, 3), (3, 4), (4, 6), (6, 8))[k]
        start, size = 192 * r + 96 * core, 96
        if part is not None:
            start, size = start + 48 * part, 48
        return W.at[lo:hi, pl.ds(pl.multiple_of(start, 16), size), :]
    start, size = 384 * (k - 4) + 192 * core, 192
    if part is not None:
        start, size = start + 96 * part, 96
    return W.at[8 + r, pl.ds(pl.multiple_of(start, 16), size), :]


def forward_kernel(
    tok, docs_in, og, wq, wk, wv, wo, wup, wdn,
    bq, bv, bo, ga, sa, bd, gf, sf, bu,
    Wo, Xo, Qo, KVo, Mo, Lo, ATo, ATTo, R1o, NLo, ACo, GPo, R2o, Go, PFo,
    W, X, D, PK, PF, Q, KV, MASK, LSE, AT, ATT, R1, NL, R2, ACT, GP,
    lsem, osem, ags, agr, xs, xr, ds_, dr, ps, pr, gs, gr, kvs, kvr, los, lor,
):
    me = Place()
    g, r, c, z = me.g, me.r, me.c, me.z
    gx, gy, gd, rp = me.gx, me.gy, me.gd, me.rp

    local = []
    for w, ref in enumerate((wq, wk, wv, wo)):
        local.append((ref, W.at[w, pl.ds(pl.multiple_of(192 * g, 16), 192), :]))
    for u in range(4):
        local.append((wup.at[:, 768 * u : 768 * u + 768], W.at[4 + u, pl.ds(pl.multiple_of(192 * g, 16), 192), :]))
    local.append((wdn, W.at[8 + g]))
    local = [pltpu.make_async_copy(a, b, lsem.at[i]) for i, (a, b) in enumerate(local)]
    for copy in local:
        copy.start()

    own_lane = lax.broadcasted_iota(jnp.int32, (1, 768), 1) // 192 == g
    for row, ref in ((0, bq), (2, bv), (3, bo), (4, ga), (5, sa), (6, bd), (7, gf), (8, sf)):
        piece = ref[...].astype(F32).reshape(1, 192)
        PF[row : row + 1, :] = jnp.where(own_lane, jnp.concatenate([piece] * 4, axis=1), 0.0)
    for row in (1, 9, 10, 11):
        PF[row : row + 1, :] = jnp.zeros((1, 768), F32)
    tall = lax.broadcasted_iota(jnp.int32, (4, 768), 0) == g
    PF[12:16, :] = jnp.where(tall, bu[...].astype(F32).reshape(1, 768), 0.0)
    PK[g] = PF[...].astype(BF16)

    barrier = plane_barrier(me)
    pl.semaphore_wait(barrier, 7)

    def reshard(src, dst_of, ssem, rsem):
        for m in range(2):
            t, e = 2 * c + m, g // 2
            b = g % 2
            here = (t == g) & (e == c)
            src_m = src.at[m]
            dst_b = dst_of(b)

            @pl.when(jnp.logical_not(here))
            def _():
                remote(src_m, dst_b, ssem.at[m], rsem.at[b], (t, 2 * z + e)).start()

            @pl.when(here)
            def _():
                pltpu.make_async_copy(src_m, dst_b, rsem.at[b]).start()

    def reshard_wait(src, dst_of, ssem, rsem, b):
        remote(src.at[0], dst_of(b), ssem.at[0], rsem.at[b], (g, r)).wait_recv()

    def reshard_drain(src, dst_of, ssem, rsem):
        for m in range(2):
            t, e = 2 * c + m, g // 2
            here = (t == g) & (e == c)

            @pl.when(jnp.logical_not(here))
            def _():
                remote(src.at[m], dst_of(0), ssem.at[m], rsem.at[0], (t, 2 * z + e)).wait_send()

    def x_rows(b):
        if isinstance(b, int):
            return X.at[256 * b : 256 * b + 256, :]
        return X.at[pl.ds(pl.multiple_of(256 * b, 256), 256), :]

    def g_rows(b):
        if isinstance(b, int):
            return Go.at[256 * b : 256 * b + 256, :]
        return Go.at[pl.ds(pl.multiple_of(256 * b, 256), 256), :]

    reshard(tok, x_rows, xs, xr)

    for m in range(2):
        for e in range(2):
            t = 2 * c + m
            here = (t == g) & (c == e)

            @pl.when(jnp.logical_not(here))
            def _():
                remote(docs_in, D.at[g], ds_.at[2 * m + e], dr.at[g], (t, 2 * z + e)).start()

            @pl.when(here)
            def _():
                pltpu.make_async_copy(docs_in, D.at[g], dr.at[g]).start()

    def own_send(k):
        piece = half_of(W, k, g, c)
        remote(piece, piece, ags.at[k, 0], agr.at[k, 0], (gx, r)).start()
        remote(piece, piece, ags.at[k, 1], agr.at[k, 1], (gy, r)).start()

    def to_partner(k, slot, piece):
        remote(piece, piece, ags.at[k, slot], agr.at[k, slot], (g, rp)).start()

    def landed(k, slot, piece):
        remote(piece, piece, ags.at[k, slot], agr.at[k, slot], (g, rp)).wait_recv()

    def relay(k):
        piece = half_of(W, k, gx, c)
        landed(k, 0, piece)
        part = half_of(W, k, gx, c, 0)
        remote(part, part, ags.at[k, 2], agr.at[k, 2], (gy, r)).start()
        to_partner(k, 4, piece)
        piece = half_of(W, k, gy, c)
        landed(k, 1, piece)
        part = half_of(W, k, gy, c, 1)
        remote(part, part, ags.at[k, 3], agr.at[k, 3], (gx, r)).start()
        to_partner(k, 5, piece)

    def diagonal(k):
        landed(k, 2, half_of(W, k, gd, c, 0))
        landed(k, 3, half_of(W, k, gd, c, 1))
        to_partner(k, 6, half_of(W, k, gd, c))

    def complete(k):
        landed(k, 4, half_of(W, k, gx, 1 - c))
        landed(k, 5, half_of(W, k, gy, 1 - c))
        landed(k, 6, half_of(W, k, gd, 1 - c))

    def gather_drain(k):
        for slot, piece in (
            (0, half_of(W, k, g, c)), (1, half_of(W, k, g, c)),
            (2, half_of(W, k, gx, c, 0)), (3, half_of(W, k, gy, c, 1)),
            (4, half_of(W, k, gx, c)), (5, half_of(W, k, gy, c)), (6, half_of(W, k, gd, c)),
        ):
            remote(piece, piece, ags.at[k, slot], agr.at[k, slot], (g, rp)).wait_send()

    for i in range(3):
        local[i].wait()
    own_send(0)
    for i in range(3, 9):
        local[i].wait()
    own_send(1)
    for slot, chip in enumerate((gx, gy, gd)):
        remote(PK.at[g], PK.at[g], ps.at[slot], pr.at[slot], (chip, r)).start()
    relay(0)
    own_send(2)

    for slot, chip in enumerate((gx, gy, gd)):
        remote(PK.at[chip], PK.at[chip], ps.at[slot], pr.at[slot], (chip, r)).wait_recv()
    PF[...] = PK[0].astype(F32) + PK[1].astype(F32) + PK[2].astype(F32) + PK[3].astype(F32)
    for i in range(4):
        remote(docs_in, D.at[i], ds_.at[0], dr.at[i], (g, r)).wait_recv()
    for i in range(4):
        keys = jnp.broadcast_to(D[i, pl.ds(g % 2, 1), :].astype(F32), (8, 256)).T[:, 0:1]
        for b in range(2):
            rows = D[2 * c + b, pl.ds(g % 2, 1), :].astype(F32)
            MASK[256 * i : 256 * i + 256, 256 * b : 256 * b + 256] = jnp.where(keys == rows, 0.0, NEGATIVE)
    for b in range(2):
        reshard_wait(tok, x_rows, xs, xr, b)
    remote(X, Xo.at[c], los.at[0], lor.at[0], (g, rp)).start()
    outs = [
        (X, Xo.at[c]), (PF, PFo), (MASK, Mo),
    ]
    out_copies = []

    def emit(pairs):
        for a, b in pairs:
            copy = pltpu.make_async_copy(a, b, osem.at[len(out_copies)])
            copy.start()
            out_copies.append(copy)

    emit(outs)
    diagonal(0)
    complete(0)
    own_rows = pl.ds(pl.multiple_of(512 * c, 512), 512)

    def project(w, t, dst):
        cols = pl.ds(pl.multiple_of(256 * t, 256), 256)
        out = dot(X[...], W[w, :, cols]) + PF[pl.ds(w, 1), cols]
        return cols, out.astype(BF16)

    @pl.loop(0, 6)
    def _(i):
        w = i // 3
        cols, out = project(1 + w, i % 3, None)
        KV[w, own_rows, cols] = out

    for w in range(2):
        piece = KV.at[w, own_rows, :]
        remote(piece, piece, kvs.at[w], kvr.at[w], (g, rp)).start()
    relay(1)
    own_send(3)

    @pl.loop(0, 3)
    def _(i):
        cols, out = project(0, i, None)
        Q[:, cols] = out

    diagonal(1)
    complete(1)
    for w in range(2):
        piece = KV.at[w, pl.ds(pl.multiple_of(512 * (1 - c), 512), 512), :]
        remote(piece, piece, kvs.at[w], kvr.at[w], (g, rp)).wait_recv()
    emit([(Q, Qo), (KV, KVo)])

    @pl.loop(0, 12)
    def _(i):
        pair, b = i // 2, i % 2
        lanes = pl.ds(pl.multiple_of(128 * pair, 128), 128)
        cols = pl.ds(pl.multiple_of(256 * b, 256), 256)
        qt = (Q[cols, lanes].astype(F32) * (HEAD_DIM ** -0.5)).T
        kp = KV[0, :, lanes]
        vt = KV[1, :, lanes].astype(F32).T.astype(BF16)
        top = lax.broadcasted_iota(jnp.int32, (128, 256), 0) < 64
        pieces = []
        for hh in range(2):
            qh = jnp.where(top if hh == 0 else jnp.logical_not(top), qt, 0.0).astype(BF16)
            s = dot(kp, qh) + MASK[:, cols]
            peak = jnp.max(s, axis=0, keepdims=True)
            e = jnp.exp(s - peak)
            total = jnp.sum(e, axis=0, keepdims=True)
            o = dot(vt[64 * hh : 64 * hh + 64, :], e.astype(BF16)) / total
            LSE[pl.ds(2 * pair + hh, 1), cols] = peak + jnp.log(total)
            pieces.append(o)
        ot = jnp.concatenate(pieces, axis=0)
        ATT[lanes, cols] = ot.astype(BF16)
        AT[cols, lanes] = ot.T.astype(BF16)

        @pl.when(i == 2)
        def _():
            relay(2)
            own_send(4)

        @pl.when(i == 5)
        def _():
            relay(3)
            own_send(5)
            diagonal(2)

        @pl.when(i == 9)
        def _():
            relay(4)
            diagonal(3)

    remote(AT, ATo.at[c], los.at[1], lor.at[1], (g, rp)).start()
    emit([(AT, ATo.at[c]), (ATT, ATTo), (LSE, Lo)])

    @pl.loop(0, 2)
    def _(i):
        rows = pl.ds(pl.multiple_of(256 * i, 256), 256)
        first = X[rows, :].astype(F32) + dot(AT[rows, :], W[3]) + PF[3:4, :]
        R1[rows, :] = first
        shape, _ = norm_parts(first)
        normed = shape * PF[4:5, :] + PF[5:6, :]
        R2[rows, :] = normed + PF[6:7, :]
        NL[rows, :] = normed.astype(BF16)

    remote(NL, NLo.at[c], los.at[2], lor.at[2], (g, rp)).start()
    emit([(R1, R1o), (NL, NLo.at[c])])
    relay(5)
    reshard(og, g_rows, gs, gr)
    complete(2)
    complete(3)

    def up(t):
        u, tt = t // 3, t % 3
        cols = pl.ds(pl.multiple_of(256 * tt, 256), 256)
        wide = pl.ds(pl.multiple_of(256 * t, 256), 256)
        h = dot(NL[...], W[4 + u, :, cols]) + PF[pl.ds(12 + u, 1), cols]
        cdf = 0.5 * (1.0 + lax.erf(h * (0.5 ** 0.5)))
        ACT[:, wide] = (h * cdf).astype(BF16)
        GP[:, wide] = (cdf + h * jnp.exp(-0.5 * h * h) * 0.3989422804014327).astype(BF16)

    @pl.loop(0, 12)
    def _(t):
        up(t)

        @pl.when(t == 8)
        def _():
            diagonal(4)

    diagonal(5)
    remote(ACT, ACo.at[c], los.at[3], lor.at[3], (g, rp)).start()
    emit([(ACT, ACo.at[c]), (GP, GPo)])
    complete(4)
    complete(5)

    @pl.loop(0, 12)
    def _(t):
        k, tt = t // 3, t % 3
        cols = pl.ds(pl.multiple_of(256 * tt, 256), 256)
        deep = pl.ds(pl.multiple_of(768 * k, 256), 768)
        R2[:, cols] += dot(ACT[:, deep], W[8 + k, :, cols])

    emit([(W, Wo), (R2, R2o)])

    for b in range(2):
        reshard_wait(og, g_rows, gs, gr, b)
    reshard_drain(tok, x_rows, xs, xr)
    reshard_drain(og, g_rows, gs, gr)
    for m in range(2):
        for e in range(2):
            t = 2 * c + m
            here = (t == g) & (c == e)

            @pl.when(jnp.logical_not(here))
            def _():
                remote(docs_in, D.at[g], ds_.at[2 * m + e], dr.at[g], (t, 2 * z + e)).wait_send()
    for slot, chip in enumerate((gx, gy, gd)):
        remote(PK.at[g], PK.at[g], ps.at[slot], pr.at[slot], (chip, r)).wait_send()
    for k in range(GROUPS):
        gather_drain(k)
    for w in range(2):
        piece = KV.at[w, own_rows, :]
        remote(piece, piece, kvs.at[w], kvr.at[w], (g, rp)).wait_send()
    for i, (a, o) in enumerate(((X, Xo), (AT, ATo), (NL, NLo), (ACT, ACo))):
        copy = remote(a, o.at[c], los.at[i], lor.at[i], (g, rp))
        copy.wait_send()
        remote(a, o.at[1 - c], los.at[i], lor.at[i], (g, rp)).wait_recv()
    for copy in out_copies:
        copy.wait()


def sds(shape, dtype=BF16):
    return jax.ShapeDtypeStruct(shape, dtype)


def forward(*args):
    out = [
        sds((12, 768, 768)), sds((2, 512, 768)), sds((512, 768)), sds((2, 1024, 768)),
        sds((1024, 512), F32), sds((16, 512), F32), sds((2, 512, 768)), sds((768, 512)),
        sds((512, 768), F32), sds((2, 512, 768)), sds((2, 512, 3072)), sds((512, 3072)),
        sds((512, 768), F32), sds((512, 768)), sds((16, 768), F32),
    ]
    dma = pltpu.SemaphoreType.DMA
    v = pltpu.VMEM
    return pl.pallas_call(
        forward_kernel,
        out_shape=out,
        in_specs=[ANY] * 9 + [pl.BlockSpec(memory_space=pltpu.VMEM)] * 9,
        out_specs=[ANY] * len(out),
        scratch_shapes=[
            v((12, 768, 768), BF16), v((512, 768), BF16), v((4, 2, 256), jnp.int32), v((4, 16, 768), BF16),
            v((16, 768), F32), v((512, 768), BF16), v((2, 1024, 768), BF16), v((1024, 512), F32), v((16, 512), F32),
            v((512, 768), BF16), v((768, 512), BF16), v((512, 768), F32), v((512, 768), BF16), v((512, 768), F32),
            v((512, 3072), BF16), v((512, 3072), BF16),
            dma((10,)), dma((16,)), dma((6, 7)), dma((6, 7)), dma((2,)), dma((2,)), dma((4,)), dma((4,)),
            dma((3,)), dma((3,)), dma((2,)), dma((2,)), dma((2,)), dma((2,)), dma((4,)), dma((4,)),
        ],
        compiler_params=pltpu.CompilerParams(
            collective_id=0, has_side_effects=True, vmem_limit_bytes=66000000
        ),
    )(*args)


def dot_nt(a, b):
    return lax.dot_general(a, b, (((1,), (1,)), ((), ())), preferred_element_type=F32)


def dot_tn(a, b):
    return lax.dot_general(a, b, (((0,), (0,)), ((), ())), preferred_element_type=F32)


def columns(values):
    return jnp.sum(values, axis=0, keepdims=True)


CHUNKS = 12


def backward_kernel(
    Wi, Xi, Qi, KVi, Mi, Li, ATi, ATTi, R1i, NLi, ACi, GPi, R2i, Gi, PFi,
    LOo, GIo, To, BTo,
    W, P1, P2, ZR, ACT, GP, DHP, Q, KV, MASK, LSE, ATT, R1, R2, G, PF,
    DF, DFP, DB, DBP, DATT, DQ, DQP, DKS, DKR, DKF, DKP, LO, LO2, ACC, BG, BR, BS, BZ, BT,
    lsem, p1s, p1r, p2s, p2r, zs, zr, ts, tr, xs_, xr_, los, lor, gis, gir, b1s, b1r, b2s, b2r, osem,
):
    me = Place()
    g, r, c, z = me.g, me.r, me.c, me.z
    gx, gy, gd, rp = me.gx, me.gy, me.gd, me.rp
    outer = (z == 0) | (z == 3)
    inner = jnp.logical_not(outer)

    loads = {}

    def load(name, src, dst):
        copy = pltpu.make_async_copy(src, dst, lsem.at[len(loads)])
        copy.start()
        loads[name] = copy

    load("r2", R2i, R2)
    load("g", Gi, G)
    load("pf", PFi, PF)
    load("down", Wi.at[8:12], W.at[8:12])
    load("gp", GPi, GP)
    load("act", ACi, ACT)
    load("up", Wi.at[4:8], W.at[4:8])
    load("r1", R1i, R1)
    load("small", Wi.at[0:4], W.at[0:4])
    load("q", Qi, Q)
    load("kv", KVi, KV)
    load("mask", Mi, MASK)
    load("lse", Li, LSE)
    load("att_t", ATTi, ATT)
    BG[...] = jnp.zeros_like(BG)

    barrier = plane_barrier(me)
    zin, zout, zother = 1 + z // 3, 3 * (z - 1), 3 - z

    def zdev(zz):
        return (g, 2 * zz + c)

    for step in range(1, 4):
        pl.semaphore_signal(barrier, inc=1, device_id=zdev((z + step) % 4), device_id_type=MESH)
    pl.semaphore_wait(barrier, 10)

    def grad(j, q, part=None):
        start, size = 0, 192
        if part is not None:
            start, size = 96 * part, 96
        if j < 4:
            return W.at[8 + q // 2, pl.ds(192 * j + start, size), pl.ds(pl.multiple_of(384 * (q % 2), 128), 384)]
        rows = pl.ds(pl.multiple_of(192 * q + start, 16), size)
        if j < 8:
            return W.at[10 + (j - 4) // 2, rows, 384 * (j % 2) : 384 * (j % 2) + 384]
        return W.at[4 + (j - 8) // 2, rows, 384 * (j % 2) : 384 * (j % 2) + 384]

    def first(j):
        remote(grad(j, gd, 0), P1.at[j, 0], p1s.at[j, 0], p1r.at[j, 0], (gy, r)).start()
        remote(grad(j, gd, 1), P1.at[j, 1], p1s.at[j, 1], p1r.at[j, 1], (gx, r)).start()

    def plain(j):
        remote(grad(j, gx, 1), P2.at[j, 0, 96:192], p2s.at[j, 0], p2r.at[j, 0], (gx, r)).start()
        remote(grad(j, gy, 0), P2.at[j, 1, 0:96], p2s.at[j, 1], p2r.at[j, 1], (gy, r)).start()

    def passed(j):
        for side, (chip, slot, rows) in enumerate(((gx, 0, slice(0, 96)), (gy, 1, slice(96, 192)))):
            mine = grad(j, chip, side)
            remote(mine, P1.at[j, side], p1s.at[j, side], p1r.at[j, side], (chip, r)).wait_recv()
            mine[...] = (mine[...].astype(F32) + P1[j, side].astype(F32)).astype(BF16)
            remote(mine, P2.at[j, slot, rows], p2s.at[j, 2 + side], p2r.at[j, 2 + side], (chip, r)).start()

    def own(j):
        for slot, rows, k in ((0, slice(96, 192), 0), (1, slice(0, 96), 1), (0, slice(0, 96), 2), (1, slice(96, 192), 3)):
            dst = P2.at[j, slot, rows]
            remote(dst, dst, p2s.at[j, k], p2r.at[j, k], (gx, r)).wait_recv()
        mine = grad(j, g)
        total = mine[...].astype(F32) + P2[j, 0].astype(F32) + P2[j, 1].astype(F32)
        P2[j, 0] = total.astype(BF16)

        @pl.when(outer)
        def _():
            remote(P2.at[j, 0], ZR.at[j, 0], zs.at[j, 0], zr.at[j, 0], zdev(zin)).start()

    def chain(j):
        @pl.when(inner)
        def _():
            remote(P2.at[j, 0], ZR.at[j, 0], zs.at[j, 0], zr.at[j, 0], zdev(zother)).wait_recv()
            P2[j, 0] = (P2[j, 0].astype(F32) + ZR[j, 0].astype(F32)).astype(BF16)
            remote(P2.at[j, 0], ZR.at[j, 1], zs.at[j, 1], zr.at[j, 1], zdev(zother)).start()

    def hand_over(j):
        remote(P2.at[j, 1], To.at[c, j], ts.at[j], tr.at[j], (g, rp)).start()
        pltpu.make_async_copy(P2.at[j, 1], To.at[c, j], osem.at[j]).start()

    def fin_in(j):
        @pl.when(inner)
        def _():
            remote(P2.at[j, 0], ZR.at[j, 1], zs.at[j, 1], zr.at[j, 1], zdev(zother)).wait_recv()
            P2[j, 1] = (P2[j, 0].astype(F32) + ZR[j, 1].astype(F32)).astype(BF16)
            remote(P2.at[j, 1], ZR.at[j, 0], zs.at[j, 0], zr.at[j, 0], zdev(zout)).start()
            hand_over(j)

    def fin_out(j):
        @pl.when(outer)
        def _():
            remote(P2.at[j, 1], ZR.at[j, 0], zs.at[j, 0], zr.at[j, 0], zdev(zin)).wait_recv()
            P2[j, 1] = ZR[j, 0]
            hand_over(j)

    def drain(j):
        for side in range(2):
            remote(P1.at[j, side], P1.at[j, side], p1s.at[j, side], p1r.at[j, side], (gx, r)).wait_send()
        for k in range(4):
            remote(P1.at[j, 0], P1.at[j, 0], p2s.at[j, k], p2r.at[j, k], (gx, r)).wait_send()
        remote(P2.at[j, 0], ZR.at[j, 0], zs.at[j, 0], zr.at[j, 0], zdev(zother)).wait_send()

        @pl.when(inner)
        def _():
            remote(P2.at[j, 0], ZR.at[j, 1], zs.at[j, 1], zr.at[j, 1], zdev(zother)).wait_send()

        piece = remote(P2.at[j, 1], To.at[1 - c, j], ts.at[j], tr.at[j], (g, rp))
        piece.wait_send()
        piece.wait_recv()
        pltpu.make_async_copy(P2.at[j, 1], To.at[c, j], osem.at[j]).wait()

    def give_back(src, out, ssem, rsem):
        for b in range(2):
            t, e = 2 * c + b, g // 2
            here = (t == g) & (e == c)
            src_b = src.at[256 * b : 256 * b + 256, :]
            dst = out.at[g % 2]

            @pl.when(jnp.logical_not(here))
            def _():
                remote(src_b, dst, ssem.at[b], rsem.at[g % 2], (t, 2 * z + e)).start()

            @pl.when(here)
            def _():
                pltpu.make_async_copy(src_b, dst, rsem.at[g % 2]).start()

    def give_back_drain(src, out, ssem, rsem):
        for b in range(2):
            t, e = 2 * c + b, g // 2
            here = (t == g) & (e == c)
            src_b = src.at[256 * b : 256 * b + 256, :]

            @pl.when(jnp.logical_not(here))
            def _():
                remote(src_b, out.at[0], ssem.at[b], rsem.at[0], (t, 2 * z + e)).wait_send()

            remote(src_b, out.at[b], ssem.at[b], rsem.at[b], (g, rp)).wait_recv()

    def exchange(slot, src, dst):
        remote(src, dst, xs_.at[slot], xr_.at[slot], (g, rp)).start()

    def exchanged(slot, dst):
        remote(dst, dst, xs_.at[slot], xr_.at[slot], (g, rp)).wait_recv()

    def exchange_drain(slot, dst):
        remote(dst, dst, xs_.at[slot], xr_.at[slot], (g, rp)).wait_send()

    mine384 = pl.ds(pl.multiple_of(384 * c, 128), 384)
    theirs384 = pl.ds(pl.multiple_of(384 * (1 - c), 128), 384)

    def norm_back(values, gain, grad_out):
        shape, inverse = norm_parts(values)
        pulled = grad_out * gain
        d = inverse * (
            pulled
            - jnp.mean(pulled, axis=-1, keepdims=True)
            - shape * jnp.mean(pulled * shape, axis=-1, keepdims=True)
        )
        return shape, d

    for name in ("r2", "g", "pf"):
        loads[name].wait()

    @pl.loop(0, 4)
    def _(i):
        rows = pl.ds(pl.multiple_of(128 * i, 128), 128)
        up = G[rows, :].astype(F32)
        shape, d = norm_back(R2[rows, :], PF[7:8, :], up)
        LO[rows, :] = (shape * PF[7:8, :] + PF[8:9, :]).astype(BF16)
        R2[rows, :] = d
        low = d.astype(BF16)
        DF[rows, :] = low
        BG[7:8, :] += columns(up * shape)
        BG[8:9, :] += columns(up)
        BG[6:7, :] += columns(low.astype(F32))

    exchange(0, DF.at[:, theirs384], DFP)
    give_back(LO, LOo, los, lor)
    loads["down"].wait()
    loads["gp"].wait()

    def d_hidden(i):
        t = (i + 6 * (1 - c)) % 12
        tt = t % 3
        wide = pl.ds(pl.multiple_of(256 * t, 256), 256)
        back = dot_nt(DF[...], W[8 + t // 3, pl.ds(pl.multiple_of(256 * tt, 256), 256), :])
        low = (back * GP[:, wide].astype(F32)).astype(BF16)
        GP[:, wide] = low
        BG[pl.ds(12 + t // 3, 1), pl.ds(pl.multiple_of(256 * tt, 256), 256)] = columns(low.astype(F32))

    @pl.loop(0, 6)
    def _(i):
        d_hidden(i)

    exchange(1, GP.at[:, pl.ds(pl.multiple_of(1536 * (1 - c), 128), 1536)], DHP)

    @pl.loop(6, 12)
    def _(i):
        d_hidden(i)

    loads["act"].wait()
    exchanged(0, DFP)

    def pair_tn(left, lanes, own_right, their_right):
        return dot_tn(left[c, :, lanes], own_right) + dot_tn(left[1 - c, :, lanes], their_right)

    def down_quarter(q):
        @pl.loop(0, 3)
        def _(i):
            lanes = pl.ds(pl.multiple_of(768 * q + 256 * i, 256), 256)
            out = pair_tn(ACT, lanes, DF[:, mine384], DFP[...])
            W[8 + q // 2, pl.ds(pl.multiple_of(256 * i, 256), 256), pl.ds(pl.multiple_of(384 * (q % 2), 128), 384)] = (
                out.astype(BF16)
            )

    down_quarter(gd)
    for j in range(4):
        first(j)
    down_quarter(gx)
    down_quarter(gy)
    for j in range(4):
        plain(j)
    down_quarter(g)
    load("nl", NLi, ACT.at[:, :, 0:768])
    load("att", ATi, ACT.at[:, :, 768:1536])
    load("x", Xi, ACT.at[:, :, 1536:2304])

    loads["up"].wait()

    @pl.loop(0, 3)
    def _(i):
        cols = pl.ds(pl.multiple_of(256 * i, 256), 256)
        total = R2[:, cols]
        for u in range(4):
            total = total + dot_nt(GP[:, 768 * u : 768 * u + 768], W[4 + u, cols, :])
        R2[:, cols] = total

    passed(0)
    passed(1)
    loads["r1"].wait()

    @pl.loop(0, 4)
    def _(i):
        rows = pl.ds(pl.multiple_of(128 * i, 128), 128)
        up = R2[rows, :]
        shape, d = norm_back(R1[rows, :], PF[4:5, :], up)
        R2[rows, :] = d
        low = d.astype(BF16)
        DB[rows, :] = low
        BG[4:5, :] += columns(up * shape)
        BG[5:6, :] += columns(up)
        BG[3:4, :] += columns(low.astype(F32))

    exchange(2, DB.at[:, theirs384], DBP)
    passed(2)
    passed(3)
    exchanged(1, DHP)
    loads["nl"].wait()

    for j in range(4, 8):
        jj = j - 4
        own_cols = pl.ds(pl.multiple_of(1536 * c + 384 * jj, 128), 384)

        @pl.loop(0, 3)
        def _(i):
            lanes = pl.ds(pl.multiple_of(256 * i, 256), 256)
            out = pair_tn(ACT, lanes, GP[:, own_cols], DHP[:, 384 * jj : 384 * jj + 384])
            W[10 + jj // 2, lanes, 384 * (jj % 2) : 384 * (jj % 2) + 384] = out.astype(BF16)

        first(j)
        plain(j)

    loads["small"].wait()

    @pl.loop(0, 3)
    def _(i):
        cols = pl.ds(pl.multiple_of(256 * i, 256), 256)
        DATT[:, cols] = dot_nt(DB[...], W[3, cols, :]).astype(BF16)

    exchanged(2, DBP)
    loads["att"].wait()

    def square_grad(j, offset, own_right, their_right):
        @pl.loop(0, 3)
        def _(i):
            lanes = pl.ds(pl.multiple_of(offset + 256 * i, 256), 256)
            out = pair_tn(ACT, lanes, own_right[...], their_right[...])
            W[4 + (j - 8) // 2, pl.ds(pl.multiple_of(256 * i, 256), 256), 384 * (j % 2) : 384 * (j % 2) + 384] = (
                out.astype(BF16)
            )

        first(j)
        plain(j)

    square_grad(8, 768, DB.at[:, mine384], DBP)

    for name in ("q", "kv", "mask", "lse", "att_t"):
        loads[name].wait()
    own_rows = pl.ds(pl.multiple_of(512 * c, 512), 512)
    their_rows = pl.ds(pl.multiple_of(512 * (1 - c), 512), 512)

    services = {
        1: [(own, 0)],
        2: [(own, 1)],
        3: [(own, 2)],
        4: [(own, 3), (passed, 4)],
        5: [(chain, 0)],
        6: [(chain, 1), (passed, 5)],
        7: [(chain, 2)],
        8: [(chain, 3), (passed, 6), (fin_in, 0)],
        9: [(fin_in, 1)],
        10: [(passed, 7), (fin_in, 2)],
        11: [(fin_in, 3), (fin_out, 0), (passed, 8)],
    }

    @pl.loop(0, 12)
    def _(i):
        pair, b = (i // 2 + 3 * (1 - c)) % 6, i % 2
        lanes = pl.ds(pl.multiple_of(128 * pair, 128), 128)
        half_lanes = pl.ds(pl.multiple_of(128 * (pair % 3), 128), 128)
        cols = pl.ds(pl.multiple_of(256 * b, 256), 256)
        qs = Q[cols, lanes].astype(F32) * (HEAD_DIM ** -0.5)
        do = DATT[cols, lanes].astype(F32)
        qt, dot_t = qs.T, do.T
        kp = KV[0, :, lanes]
        vp = KV[1, :, lanes]
        kt = kp.astype(F32).T.astype(BF16)
        weigh = dot_t * ATT[lanes, cols].astype(F32)
        top = lax.broadcasted_iota(jnp.int32, (128, 256), 0) < 64
        left = lax.broadcasted_iota(jnp.int32, (256, 128), 1) < 64
        dk = dv = None
        pieces = []
        for hh in range(2):
            rows_in = top if hh == 0 else jnp.logical_not(top)
            lanes_in = left if hh == 0 else jnp.logical_not(left)
            s = dot(kp, jnp.where(rows_in, qt, 0.0).astype(BF16)) + MASK[:, cols]
            p = jnp.exp(s - LSE[pl.ds(2 * pair + hh, 1), cols])
            dp = dot(vp, jnp.where(rows_in, dot_t, 0.0).astype(BF16))
            ds = (p * (dp - columns(weigh[64 * hh : 64 * hh + 64, :]))).astype(BF16)
            dv_h = dot(p.astype(BF16), jnp.where(lanes_in, do, 0.0).astype(BF16))
            dk_h = dot(ds, jnp.where(lanes_in, qs, 0.0).astype(BF16))
            dv = dv_h if dv is None else dv + dv_h
            dk = dk_h if dk is None else dk + dk_h
            pieces.append(dot(kt[64 * hh : 64 * hh + 64, :], ds))
        DQ[cols, lanes] = (jnp.concatenate(pieces, axis=0).T * (HEAD_DIM ** -0.5)).astype(BF16)

        @pl.when(b == 0)
        def _():
            ACC[0] = dk
            ACC[1] = dv

        @pl.when(i == 7)
        def _():
            exchanged(3, DKR)

        @pl.when((b == 1) & (i < 6))
        def _():
            DKS[0, :, half_lanes] = (ACC[0] + dk).astype(BF16)
            DKS[1, :, half_lanes] = (ACC[1] + dv).astype(BF16)

        @pl.when((b == 1) & (i > 6))
        def _():
            DKF[0, :, half_lanes] = (ACC[0] + dk + DKR[0, :, half_lanes].astype(F32)).astype(BF16)
            DKF[1, :, half_lanes] = (ACC[1] + dv + DKR[1, :, half_lanes].astype(F32)).astype(BF16)

        @pl.when(i == 5)
        def _():
            exchange(3, DKS, DKR)
            exchange(4, DQ.at[:, theirs384], DQP)

        for k, todo in services.items():
            @pl.when(i == k)
            def _():
                for f, j in todo:
                    f(j)

    exchange(5, DKF.at[:, their_rows, :], DKP)
    BG[0:1, :] = columns(DQ[...].astype(F32))
    BG[2:3, mine384] = columns(DKF[1].astype(F32))

    BS[...] = BG[...].astype(BF16)
    others = [(gg, rr, k) for k, (gg, rr) in enumerate(
        ((g, rp), (gx, r), (gx, rp), (gy, r), (gy, rp), (gd, r), (gd, rp)))]
    slot_of = 2 * g + c
    for gg, rr, k in others:
        remote(BS, BR.at[slot_of], b1s.at[k], b1r.at[k], (gg, rr)).start()
    BR[slot_of] = BS[...]

    loads["x"].wait()
    exchanged(4, DQP)
    square_grad(9, 1536, DQ.at[:, mine384], DQP)
    own(4)
    square_grad(10, 1536, DKF.at[0, own_rows, :], DKF.at[0, their_rows, :])
    own(5)
    own(6)
    square_grad(11, 1536, DKF.at[1, own_rows, :], DKF.at[1, their_rows, :])
    own(7)
    passed(9)

    exchanged(5, DKP)

    @pl.loop(0, 3)
    def _(i):
        cols = pl.ds(pl.multiple_of(256 * i, 256), 256)
        total = R2[:, cols] + dot_nt(DQ[...], W[0, cols, :])
        for w in range(2):
            total = total + dot_nt(DKF[w, own_rows, :], W[1 + w, cols, mine384])
            total = total + dot_nt(DKP[w], W[1 + w, cols, theirs384])
        LO2[:, cols] = total.astype(BF16)

    chain(4)
    chain(5)
    own(8)
    passed(10)
    chain(6)
    fin_in(4)
    for gg, rr, k in others:
        src = 2 * gg + rr % 2
        remote(BS, BR.at[src], b1s.at[k], b1r.at[k], (gg, rr)).wait_recv()
    total = BR[0].astype(F32)
    for k in range(1, 8):
        total = total + BR[k].astype(F32)
    BZ[z] = total.astype(BF16)
    for step in range(1, 4):
        zz = (z + step) % 4
        remote(BZ.at[z], BZ.at[z], b2s.at[step - 1], b2r.at[step - 1], zdev(zz)).start()
    passed(11)
    give_back(LO2, GIo, gis, gir)
    for f, j in (
        (chain, 7), (fin_in, 5), (chain, 8), (fin_out, 1), (fin_out, 2), (fin_out, 3), (fin_in, 6), (own, 9),
        (fin_out, 4), (fin_in, 7), (own, 10), (fin_out, 5), (chain, 9), (fin_in, 8), (fin_out, 6), (own, 11),
        (fin_out, 7), (chain, 10), (fin_in, 9), (fin_out, 8), (chain, 11), (fin_in, 10), (fin_out, 9),
        (fin_in, 11), (fin_out, 10), (fin_out, 11),
    ):
        f(j)
    for step in range(1, 4):
        zz = (z + 4 - step) % 4
        remote(BZ.at[zz], BZ.at[zz], b2s.at[step - 1], b2r.at[step - 1], zdev(zz)).wait_recv()
    BT[...] = (BZ[0].astype(F32) + BZ[1].astype(F32)) + (BZ[2].astype(F32) + BZ[3].astype(F32))
    bt_copy = pltpu.make_async_copy(BT, BTo, osem.at[CHUNKS])
    bt_copy.start()

    for j in range(CHUNKS):
        drain(j)
    for slot, dst in ((0, DFP), (1, DHP), (2, DBP), (3, DKR), (4, DQP), (5, DKP)):
        exchange_drain(slot, dst)
    give_back_drain(LO, LOo, los, lor)
    give_back_drain(LO2, GIo, gis, gir)
    for gg, rr, k in others:
        remote(BS, BR.at[0], b1s.at[k], b1r.at[k], (gg, rr)).wait_send()
    for step in range(1, 4):
        remote(BZ.at[z], BZ.at[z], b2s.at[step - 1], b2r.at[step - 1], zdev(z)).wait_send()
    bt_copy.wait()


def backward(saved):
    out = [
        sds((2, 256, 768)), sds((2, 256, 768)), sds((2, CHUNKS, 192, 384)), sds((16, 768), F32),
    ]
    dma = pltpu.SemaphoreType.DMA
    v = pltpu.VMEM
    return pl.pallas_call(
        backward_kernel,
        out_shape=out,
        in_specs=[ANY] * 15,
        out_specs=[ANY] * len(out),
        scratch_shapes=[
            v((12, 768, 768), BF16), v((CHUNKS, 2, 96, 384), BF16), v((CHUNKS, 2, 192, 384), BF16),
            v((CHUNKS, 2, 192, 384), BF16),
            v((2, 512, 3072), BF16), v((512, 3072), BF16), v((512, 1536), BF16), v((512, 768), BF16),
            v((2, 1024, 768), BF16), v((1024, 512), F32), v((16, 512), F32), v((768, 512), BF16),
            v((512, 768), F32), v((512, 768), F32), v((512, 768), BF16), v((16, 768), F32),
            v((512, 768), BF16), v((512, 384), BF16), v((512, 768), BF16), v((512, 384), BF16),
            v((512, 768), BF16), v((512, 768), BF16), v((512, 384), BF16), v((2, 1024, 384), BF16),
            v((2, 1024, 384), BF16), v((2, 1024, 384), BF16), v((2, 512, 384), BF16),
            v((512, 768), BF16), v((512, 768), BF16), v((2, 1024, 128), F32), v((16, 768), F32), v((8, 16, 768), BF16),
            v((16, 768), BF16), v((4, 16, 768), BF16), v((16, 768), F32),
            dma((20,)), dma((CHUNKS, 2)), dma((CHUNKS, 2)), dma((CHUNKS, 4)), dma((CHUNKS, 4)),
            dma((CHUNKS, 2)), dma((CHUNKS, 2)), dma((CHUNKS,)), dma((CHUNKS,)), dma((6,)), dma((6,)),
            dma((2,)), dma((2,)), dma((2,)), dma((2,)), dma((7,)), dma((7,)), dma((3,)), dma((3,)),
            dma((CHUNKS + 1,)),
        ],
        compiler_params=pltpu.CompilerParams(
            collective_id=1, has_side_effects=True, vmem_limit_bytes=67043328
        ),
    )(*saved)


def spread_kernel(
    Ti, GIi, LOi, BTi,
    LOo, GIo, WQo, WKo, WVo, WOo, WUo, WDo, BQo, BVo, BOo, GAo, SAo, BUo, BDo, GFo, SFo,
    T, GI, LO, OUT, GIF, sem, osem,
):
    g = lax.axis_index("group")
    order = (0, 1, 2, 3, 4, 5, 6, 7, 8, 9, 10, 11)
    loads = []
    for j in order:
        loads.append(pltpu.make_async_copy(Ti.at[:, j], T.at[:, j], sem.at[j]))
    loads.append(pltpu.make_async_copy(GIi, GI, sem.at[12]))
    loads.append(pltpu.make_async_copy(LOi, LO, sem.at[13]))
    for copy in loads:
        copy.start()
    stores = []

    def store(src, dst):
        copy = pltpu.make_async_copy(src, dst, osem.at[len(stores)])
        copy.start()
        stores.append(copy)

    for j in order:
        loads[j].wait()
        for e in range(2):
            OUT[j, :, 384 * e : 384 * e + 384] = T[e, j].astype(F32)
        if j < 4:
            store(OUT.at[j], WDo.at[192 * j : 192 * j + 192, :])
        elif j < 8:
            for e in range(2):
                start = 1536 * e + 384 * (j - 4)
                store(OUT.at[j, :, 384 * e : 384 * e + 384], WUo.at[:, start : start + 384])
        else:
            store(OUT.at[j], (WOo, WQo, WKo, WVo)[j - 8])
    loads[12].wait()
    GIF[...] = GI[...].astype(F32)
    store(GIF, GIo)
    loads[13].wait()
    store(LO, LOo)
    moved = pltpu.roll(BTi[...], (768 - 192 * g) % 768, 1)
    for row, ref in ((0, BQo), (2, BVo), (3, BOo), (4, GAo), (5, SAo), (6, BDo), (7, GFo), (8, SFo)):
        ref[...] = moved[row, 0:192]
    up = BTi[pl.ds(12 + g, 1), :]
    BUo[...] = up[0, :]
    for copy in stores:
        copy.wait()


def spread(totals, grad_input, layer_out, small):
    square = sds((192, 768), F32)
    short = sds((192,), F32)
    whole = pl.BlockSpec(memory_space=pltpu.VMEM)
    dma = pltpu.SemaphoreType.DMA
    return pl.pallas_call(
        spread_kernel,
        out_shape=[
            sds((2, 256, 768)), sds((2, 256, 768), F32), square, square, square, square,
            sds((192, 3072), F32), sds((768, 768), F32),
            short, short, short, short, short, sds((768,), F32), short, short, short,
        ],
        in_specs=[ANY, ANY, ANY, whole],
        out_specs=[ANY] * 8 + [whole] * 9,
        scratch_shapes=[
            pltpu.VMEM((2, CHUNKS, 192, 384), BF16), pltpu.VMEM((2, 256, 768), BF16), pltpu.VMEM((2, 256, 768), BF16),
            pltpu.VMEM((CHUNKS, 192, 768), F32), pltpu.VMEM((2, 256, 768), F32), dma((14,)), dma((20,)),
        ],
        compiler_params=pltpu.CompilerParams(vmem_limit_bytes=66000000),
    )(totals, grad_input, layer_out, small)


def fits(mesh):
    return dict(mesh.shape) == {"group": 4, "replica": 8}


def fast(
    tokens_in, doc_ids, out_grad, w_query, w_key, w_value, w_out, w_up, w_down, b_query, b_value, b_out,
    gain_attn, shift_attn, b_up, b_down, gain_ffn, shift_ffn,
):
    saved = forward(
        tokens_in, doc_ids, out_grad, w_query, w_key, w_value, w_out, w_up, w_down,
        b_query, b_value, b_out, gain_attn, shift_attn, b_down, gain_ffn, shift_ffn, b_up,
    )
    layer_out, grad_input, totals, small = backward(saved)
    return tuple(spread(totals, grad_input, layer_out, small))


def layer_norm(values, gain, shift):
    centre = values - jnp.mean(values, axis=-1, keepdims=True)
    spread = jnp.mean(centre * centre, axis=-1, keepdims=True)
    return centre * lax.rsqrt(spread + EPSILON) * gain + shift


def norm_pull(values, gain, shift, grad):
    result, pullback = jax.vjp(
        layer_norm, values, gain.astype(jnp.float32), shift.astype(jnp.float32)
    )
    return (result, pullback(grad))


def exact_gelu(values):
    return jax.nn.gelu(values, approximate=False)


def project(inputs, weight, bias):
    return jnp.dot(inputs, weight, preferred_element_type=jnp.float32) + bias.astype(jnp.float32)


def contract_rows(left, right):
    return lax.dot_general(
        left, right, (((0,), (0,)), ((), ())), preferred_element_type=jnp.float32
    )


def against_rows(grad, weight):
    return lax.dot_general(
        grad, weight, (((1,), (1,)), ((), ())), preferred_element_type=jnp.float32
    )


def column_sum(values):
    return jnp.sum(values.astype(jnp.float32), axis=0)


def add_pair(first, second):
    return first + second


def scores_of(query, keys_all, allowed):
    rows = query.shape[0]
    length = keys_all.shape[0]
    scaling = HEAD_DIM ** (-0.5)
    scores = (
        jnp.einsum(
            "qhd,khd->hqk",
            query.reshape(rows, HEADS, HEAD_DIM),
            keys_all.reshape(length, HEADS, HEAD_DIM),
            preferred_element_type=jnp.float32,
        )
        * scaling
    )
    return jnp.where(allowed[None], scores, NEGATIVE)


def attention_forward(query, keys_all, values_all, allowed):
    rows = query.shape[0]
    length = keys_all.shape[0]
    scores = scores_of(query, keys_all, allowed)
    row_max = jnp.max(scores, axis=-1, keepdims=True)
    exponent = jnp.exp(scores - row_max)
    total = jnp.sum(exponent, axis=-1, keepdims=True)
    probs = (exponent / total).astype(jnp.bfloat16)
    log_total = row_max[..., 0] + jnp.log(total[..., 0])
    joined = jnp.einsum(
        "hqk,khd->qhd",
        probs,
        values_all.reshape(length, HEADS, HEAD_DIM),
        preferred_element_type=jnp.float32,
    )
    return (joined.reshape(rows, HEADS * HEAD_DIM), log_total)


def score_grads(query, keys_all, values_all, allowed, log_total, d_attended):
    rows = query.shape[0]
    length = keys_all.shape[0]
    scores = scores_of(query, keys_all, allowed)
    probs = jnp.exp(scores - log_total[..., None])
    d_heads = d_attended.reshape(rows, HEADS, HEAD_DIM)
    d_probs = jnp.einsum(
        "qhd,khd->hqk",
        d_heads,
        values_all.reshape(length, HEADS, HEAD_DIM),
        preferred_element_type=jnp.float32,
    )
    row_term = jnp.sum(probs * d_probs, axis=-1)
    d_scores = (probs * (d_probs - row_term[..., None])).astype(jnp.bfloat16)
    return (probs, d_scores, row_term)


def attention_backward(query, keys_all, values_all, allowed, log_total, d_attended):
    rows = query.shape[0]
    length = keys_all.shape[0]
    scaling = HEAD_DIM ** (-0.5)
    probs, d_scores, row_term = score_grads(
        query, keys_all, values_all, allowed, log_total, d_attended
    )
    d_heads = d_attended.reshape(rows, HEADS, HEAD_DIM)
    d_values_part = jnp.einsum(
        "hqk,qhd->khd", probs.astype(jnp.bfloat16), d_heads, preferred_element_type=jnp.float32
    ).reshape(length, HEADS * HEAD_DIM)
    d_query = (
        jnp.einsum(
            "hqk,khd->qhd",
            d_scores,
            keys_all.reshape(length, HEADS, HEAD_DIM),
            preferred_element_type=jnp.float32,
        ).reshape(rows, HEADS * HEAD_DIM)
        * scaling
    )
    d_keys_part = (
        jnp.einsum(
            "hqk,qhd->khd",
            d_scores,
            query.reshape(rows, HEADS, HEAD_DIM),
            preferred_element_type=jnp.float32,
        ).reshape(length, HEADS * HEAD_DIM)
        * scaling
    )
    return (d_query, d_keys_part, d_values_part, row_term)


def owner_sum(grads):
    return (
        lax.psum_scatter(
            grads[0].astype(jnp.bfloat16), "group", scatter_dimension=0, tiled=True
        ).astype(jnp.float32),
        lax.psum_scatter(
            grads[1].astype(jnp.bfloat16), "group", scatter_dimension=0, tiled=True
        ).astype(jnp.float32),
        lax.psum_scatter(
            grads[2].astype(jnp.bfloat16), "group", scatter_dimension=0, tiled=True
        ).astype(jnp.float32),
        lax.psum_scatter(
            grads[3].astype(jnp.bfloat16), "group", scatter_dimension=0, tiled=True
        ).astype(jnp.float32),
        lax.psum_scatter(
            grads[4].astype(jnp.bfloat16), "group", scatter_dimension=0, tiled=True
        ).astype(jnp.float32),
        lax.psum_scatter(
            grads[5].astype(jnp.bfloat16), "group", scatter_dimension=0, tiled=True
        ).astype(jnp.float32),
        lax.psum_scatter(
            grads[6].astype(jnp.bfloat16), "group", scatter_dimension=0, tiled=True
        ).astype(jnp.float32),
        lax.psum_scatter(
            grads[7].astype(jnp.bfloat16), "group", scatter_dimension=0, tiled=True
        ).astype(jnp.float32),
        lax.psum_scatter(
            grads[8].astype(jnp.bfloat16), "group", scatter_dimension=0, tiled=True
        ).astype(jnp.float32),
        lax.psum_scatter(
            grads[9].astype(jnp.bfloat16), "group", scatter_dimension=0, tiled=True
        ).astype(jnp.float32),
        lax.psum_scatter(
            grads[10].astype(jnp.bfloat16), "group", scatter_dimension=0, tiled=True
        ).astype(jnp.float32),
        lax.psum_scatter(
            grads[11].astype(jnp.bfloat16), "group", scatter_dimension=0, tiled=True
        ).astype(jnp.float32),
        lax.psum_scatter(
            grads[12].astype(jnp.bfloat16), "group", scatter_dimension=0, tiled=True
        ).astype(jnp.float32),
        lax.psum_scatter(
            grads[13].astype(jnp.bfloat16), "group", scatter_dimension=0, tiled=True
        ).astype(jnp.float32),
        lax.psum_scatter(
            grads[14].astype(jnp.bfloat16), "group", scatter_dimension=0, tiled=True
        ).astype(jnp.float32),
    )


def shards(
    tokens_in,
    doc_ids,
    out_grad,
    w_query,
    w_key,
    w_value,
    w_out,
    w_up,
    w_down,
    b_query,
    b_value,
    b_out,
    gain_attn,
    shift_attn,
    b_up,
    b_down,
    gain_ffn,
    shift_ffn,
):
    gathered = (
        lax.all_gather(w_query, "group", axis=0, tiled=True),
        lax.all_gather(w_key, "group", axis=0, tiled=True),
        lax.all_gather(w_value, "group", axis=0, tiled=True),
        lax.all_gather(w_out, "group", axis=0, tiled=True),
        lax.all_gather(w_up, "group", axis=0, tiled=True),
        lax.all_gather(w_down, "group", axis=0, tiled=True),
        lax.all_gather(b_query, "group", axis=0, tiled=True),
        lax.all_gather(b_value, "group", axis=0, tiled=True),
        lax.all_gather(b_out, "group", axis=0, tiled=True),
        lax.all_gather(gain_attn, "group", axis=0, tiled=True),
        lax.all_gather(shift_attn, "group", axis=0, tiled=True),
        lax.all_gather(b_up, "group", axis=0, tiled=True),
        lax.all_gather(b_down, "group", axis=0, tiled=True),
        lax.all_gather(gain_ffn, "group", axis=0, tiled=True),
        lax.all_gather(shift_ffn, "group", axis=0, tiled=True),
    )
    (
        query_weight,
        key_weight,
        value_weight,
        out_weight,
        up_weight,
        down_weight,
        query_bias,
        value_bias,
        out_bias,
        attn_gain,
        attn_shift,
        up_bias,
        down_bias,
        ffn_gain,
        ffn_shift,
    ) = gathered
    micros = tokens_in.shape[0]
    outputs = []
    stored = []
    for micro in range(micros):
        inputs = tokens_in[micro]
        segment = doc_ids[micro]
        query = project(inputs, query_weight, query_bias).astype(jnp.bfloat16)
        keys = jnp.dot(inputs, key_weight, preferred_element_type=jnp.float32).astype(jnp.bfloat16)
        values = project(inputs, value_weight, value_bias).astype(jnp.bfloat16)
        keys_all, values_all, seg_all = (
            lax.all_gather(keys, "group", axis=0, tiled=True),
            lax.all_gather(values, "group", axis=0, tiled=True),
            lax.all_gather(segment, "group", axis=0, tiled=True),
        )
        allowed = segment[:, None] == seg_all[None, :]
        attended, log_total = attention_forward(query, keys_all, values_all, allowed)
        attended = attended.astype(jnp.bfloat16)
        resid_one = inputs.astype(jnp.float32) + project(attended, out_weight, out_bias)
        normed = layer_norm(
            resid_one, attn_gain.astype(jnp.float32), attn_shift.astype(jnp.float32)
        )
        hidden = project(normed.astype(jnp.bfloat16), up_weight, up_bias)
        activated = exact_gelu(hidden).astype(jnp.bfloat16)
        resid_two = normed + project(activated, down_weight, down_bias)
        result = layer_norm(resid_two, ffn_gain.astype(jnp.float32), ffn_shift.astype(jnp.float32))
        outputs.append(result.astype(jnp.bfloat16))
        stored.append((query, keys, values, log_total, attended, resid_one, hidden, resid_two))
    gathered = (
        lax.all_gather(w_query, "group", axis=0, tiled=True),
        lax.all_gather(w_key, "group", axis=0, tiled=True),
        lax.all_gather(w_value, "group", axis=0, tiled=True),
        lax.all_gather(w_out, "group", axis=0, tiled=True),
        lax.all_gather(w_up, "group", axis=0, tiled=True),
        lax.all_gather(w_down, "group", axis=0, tiled=True),
        lax.all_gather(b_query, "group", axis=0, tiled=True),
        lax.all_gather(b_value, "group", axis=0, tiled=True),
        lax.all_gather(b_out, "group", axis=0, tiled=True),
        lax.all_gather(gain_attn, "group", axis=0, tiled=True),
        lax.all_gather(shift_attn, "group", axis=0, tiled=True),
        lax.all_gather(b_up, "group", axis=0, tiled=True),
        lax.all_gather(b_down, "group", axis=0, tiled=True),
        lax.all_gather(gain_ffn, "group", axis=0, tiled=True),
        lax.all_gather(shift_ffn, "group", axis=0, tiled=True),
    )
    (
        query_weight,
        key_weight,
        value_weight,
        out_weight,
        up_weight,
        down_weight,
        query_bias,
        value_bias,
        out_bias,
        attn_gain,
        attn_shift,
        up_bias,
        down_bias,
        ffn_gain,
        ffn_shift,
    ) = gathered
    totals = tuple((jnp.zeros(member.shape, jnp.float32) for member in gathered))
    input_grads = []
    for micro in range(micros):
        inputs = tokens_in[micro]
        segment = doc_ids[micro]
        query, keys, values, log_total, attended, resid_one, hidden, resid_two = stored[micro]
        upstream = out_grad[micro].astype(jnp.float32)
        unused_out, (d_resid_two, g_ffn_gain, g_ffn_shift) = norm_pull(
            resid_two, ffn_gain, ffn_shift, upstream
        )
        d_ffn = d_resid_two.astype(jnp.bfloat16)
        activated, gelu_pull = jax.vjp(exact_gelu, hidden)
        activated = activated.astype(jnp.bfloat16)
        g_down_w = contract_rows(activated, d_ffn)
        g_down_b = column_sum(d_ffn)
        d_activated = against_rows(d_ffn, down_weight)
        d_hidden = gelu_pull(d_activated)[0].astype(jnp.bfloat16)
        normed = layer_norm(
            resid_one, attn_gain.astype(jnp.float32), attn_shift.astype(jnp.float32)
        )
        normed_low = normed.astype(jnp.bfloat16)
        g_up_w = contract_rows(normed_low, d_hidden)
        g_up_b = column_sum(d_hidden)
        d_normed = against_rows(d_hidden, up_weight) + d_resid_two
        unused_norm, (d_resid_one, g_attn_gain, g_attn_shift) = norm_pull(
            resid_one, attn_gain, attn_shift, d_normed
        )
        d_branch = d_resid_one.astype(jnp.bfloat16)
        g_out_w = contract_rows(attended, d_branch)
        g_out_b = column_sum(d_branch)
        d_attended = against_rows(d_branch, out_weight).astype(jnp.bfloat16)
        keys_all, values_all, seg_all = (
            lax.all_gather(keys, "group", axis=0, tiled=True),
            lax.all_gather(values, "group", axis=0, tiled=True),
            lax.all_gather(segment, "group", axis=0, tiled=True),
        )
        allowed = segment[:, None] == seg_all[None, :]
        d_query, d_keys_part, d_values_part, row_term = attention_backward(
            query, keys_all, values_all, allowed, log_total, d_attended
        )
        d_keys, d_values = (
            lax.psum_scatter(
                d_keys_part.astype(jnp.bfloat16), "group", scatter_dimension=0, tiled=True
            ).astype(jnp.float32),
            lax.psum_scatter(
                d_values_part.astype(jnp.bfloat16), "group", scatter_dimension=0, tiled=True
            ).astype(jnp.float32),
        )
        d_query = d_query.astype(jnp.bfloat16)
        d_keys = d_keys.astype(jnp.bfloat16)
        d_values = d_values.astype(jnp.bfloat16)
        g_query_w = contract_rows(inputs, d_query)
        g_key_w = contract_rows(inputs, d_keys)
        g_value_w = contract_rows(inputs, d_values)
        g_query_b = column_sum(d_query)
        g_value_b = column_sum(d_values)
        input_grad = (
            d_resid_one
            + against_rows(d_query, query_weight)
            + against_rows(d_keys, key_weight)
            + against_rows(d_values, value_weight)
        )
        input_grads.append(input_grad)
        micro_grads = (
            g_query_w,
            g_key_w,
            g_value_w,
            g_out_w,
            g_up_w,
            g_down_w,
            g_query_b,
            g_value_b,
            g_out_b,
            g_attn_gain,
            g_attn_shift,
            g_up_b,
            g_down_b,
            g_ffn_gain,
            g_ffn_shift,
        )
        totals = jax.tree.map(add_pair, totals, micro_grads)
    totals = tuple(owner_sum(totals))
    summed = (
        lax.psum(totals[0].astype(jnp.bfloat16), "replica").astype(jnp.float32),
        lax.psum(totals[1].astype(jnp.bfloat16), "replica").astype(jnp.float32),
        lax.psum(totals[2].astype(jnp.bfloat16), "replica").astype(jnp.float32),
        lax.psum(totals[3].astype(jnp.bfloat16), "replica").astype(jnp.float32),
        lax.psum(totals[4].astype(jnp.bfloat16), "replica").astype(jnp.float32),
        lax.psum(totals[5].astype(jnp.bfloat16), "replica").astype(jnp.float32),
        lax.psum(totals[6].astype(jnp.bfloat16), "replica").astype(jnp.float32),
        lax.psum(totals[7].astype(jnp.bfloat16), "replica").astype(jnp.float32),
        lax.psum(totals[8].astype(jnp.bfloat16), "replica").astype(jnp.float32),
        lax.psum(totals[9].astype(jnp.bfloat16), "replica").astype(jnp.float32),
        lax.psum(totals[10].astype(jnp.bfloat16), "replica").astype(jnp.float32),
        lax.psum(totals[11].astype(jnp.bfloat16), "replica").astype(jnp.float32),
        lax.psum(totals[12].astype(jnp.bfloat16), "replica").astype(jnp.float32),
        lax.psum(totals[13].astype(jnp.bfloat16), "replica").astype(jnp.float32),
        lax.psum(totals[14].astype(jnp.bfloat16), "replica").astype(jnp.float32),
    )
    layer_out = jnp.stack(outputs)
    grad_input = jnp.stack(input_grads)
    return (
        layer_out,
        grad_input,
        summed[0],
        summed[1],
        summed[2],
        summed[3],
        summed[4],
        summed[5],
        summed[6],
        summed[7],
        summed[8],
        summed[9],
        summed[10],
        summed[11],
        summed[12],
        summed[13],
        summed[14],
    )


def solution(mesh):
    return jax.shard_map(
        shards if not fits(mesh) else fast,
        mesh=mesh,
        in_specs=(
            P("replica", "group", None),
            P("replica", "group"),
            P("replica", "group", None),
            P("group", None),
            P("group", None),
            P("group", None),
            P("group", None),
            P("group", None),
            P("group", None),
            P("group"),
            P("group"),
            P("group"),
            P("group"),
            P("group"),
            P("group"),
            P("group"),
            P("group"),
            P("group"),
        ),
        out_specs=(
            P("replica", "group", None),
            P("replica", "group", None),
            P("group", None),
            P("group", None),
            P("group", None),
            P("group", None),
            P("group", None),
            P("group", None),
            P("group"),
            P("group"),
            P("group"),
            P("group"),
            P("group"),
            P("group"),
            P("group"),
            P("group"),
            P("group"),
        ),
        check_vma=False,
    )
```

```python
import functools

import jax
import jax.numpy as jnp
from jax import lax
from jax.experimental import pallas as pl
from jax.experimental.pallas import tpu as pltpu
from jax.sharding import PartitionSpec as P

HEADS = 12
HEAD_DIM = 64
EPSILON = 1e-05
NEGATIVE = -1e30
F32 = jnp.float32
BF16 = jnp.bfloat16
MESH = pl.DeviceIdType.MESH
ANY = pl.BlockSpec(memory_space=pl.ANY)


class Place:
    def __init__(self):
        self.g = lax.axis_index("group")
        self.r = lax.axis_index("replica")
        self.c = self.r % 2
        self.z = self.r // 2
        self.gx = self.g + 1 - 2 * (self.g % 2)
        self.gy = self.g + 2 - 4 * (self.g // 2)
        self.gd = 3 - self.g
        self.rp = self.r + 1 - 2 * self.c


def remote(src, dst, send, recv, device):
    return pltpu.make_async_remote_copy(
        src_ref=src, dst_ref=dst, send_sem=send, recv_sem=recv, device_id=device, device_id_type=MESH
    )


def plane_barrier(place, extra=()):
    barrier = pltpu.get_barrier_semaphore()
    for g in (place.g, place.gx, place.gy, place.gd):
        for r in (place.r, place.rp):
            if g is place.g and r is place.r:
                continue
            pl.semaphore_signal(barrier, inc=1, device_id=(g, r), device_id_type=MESH)
    return barrier


def dot(a, b):
    return jnp.dot(a, b, preferred_element_type=F32)


def norm_parts(values):
    centre = values - jnp.mean(values, axis=-1, keepdims=True)
    spread = jnp.mean(centre * centre, axis=-1, keepdims=True)
    inverse = lax.rsqrt(spread + EPSILON)
    return centre * inverse, inverse


def dot_nt(a, b):
    return lax.dot_general(a, b, (((1,), (1,)), ((), ())), preferred_element_type=F32)


def dot_tn(a, b):
    return lax.dot_general(a, b, (((0,), (0,)), ((), ())), preferred_element_type=F32)


def columns(values):
    return jnp.sum(values, axis=0, keepdims=True)


CHUNKS = 12


SCHEDULE = {
    ("normed",): (
        ("passed", 0), ("passed", 1), ("passed", 2),
    ),
    ("ln1",): (
        ("passed", 3),
    ),
    ("sq", 8): (
        ("own", 0),
    ),
    ("a", 0): (
        ("own", 1), ("own", 2),
    ),
    ("a", 1): (
        ("own", 3),
    ),
    ("a", 2): (
        ("passed", 4), ("chain", 0),
    ),
    ("a", 3): (
        ("passed", 5), ("chain", 1),
    ),
    ("a", 5): (
        ("passed", 6), ("chain", 2), ("fin_in", 0),
    ),
    ("a", 7): (
        ("passed", 7), ("chain", 3), ("fin_in", 1),
    ),
    ("a", 8): (
        ("passed", 8), ("fin_in", 2), ("fin_out", 0),
    ),
    ("a", 10): (
        ("own", 4), ("own", 5), ("fin_in", 3),
    ),
    ("a", 11): (
        ("own", 6), ("fin_out", 1), ("fin_out", 2),
    ),
    ("sq", 9): (
        ("own", 7), ("own", 8), ("chain", 4),
    ),
    ("sq", 10): (
        ("chain", 5), ("fin_out", 3),
    ),
    ("sq", 11): (
        ("passed", 9), ("chain", 6),
    ),
    ("inp",): (
        ("passed", 10), ("fin_in", 4), ("chain", 7),
    ),
    ("tail",): (
        ("fin_in", 5), ("passed", 11), ("gi", 0), ("chain", 8),
        ("fin_in", 6), ("own", 9), ("fin_out", 4), ("own", 10),
        ("fin_in", 7), ("own", 11), ("fin_out", 5), ("chain", 9),
        ("fin_in", 8), ("fin_out", 6), ("chain", 10), ("fin_in", 9),
        ("fin_out", 7), ("chain", 11), ("fin_in", 10), ("fin_out", 8),
        ("fin_in", 11), ("fin_out", 9), ("fin_out", 10), ("fin_out", 11),
    ),
}

GROUPS = 6


def piece_of(W, k, chip, core, first=0, count=3):
    if k < 4:
        lo, hi = ((0, 3), (3, 4), (4, 6), (6, 8))[k]
        return W.at[lo:hi, pl.ds(pl.multiple_of(192 * chip + 96 * core + 32 * first, 16), 32 * count), :]
    start = 384 * (k - 4) + 192 * core + 64 * first
    return W.at[8 + chip, pl.ds(pl.multiple_of(start, 16), 64 * count), :]


def layer_kernel(
    tok, docs_in, og, wq, wk, wv, wo, wup, wdn,
    bq, bv, bo, ga, sa, bd, gf, sf, bu,
    LOo, GIo, To, BTo, Xo, ATo, NLo,
    W, P1, P2, ZR, ACT, GP, DHP, Q, KV, MASK, LSE, R1, R2, G, PF,
    DF, DFP, DB, DBP, DATT, DQ, DQP, DKS, DKR, DKF, DKP, LO, LO2, ACC, BG, BR, BS, BZ, BT,
    X, AT, NL, SA, SB, PA, PB, DC, DR, LC, D, PK,
    lsem, p1s, p1r, p2s, p2r, zs, zr, ts, tr, xs_, xr_, los, lor, gis, gir, b1s, b1r, b2s, b2r, osem,
    ags, agr, xs, xr, ds_, dr, ps, pr, gs, gr, kvs, kvr, lls, llr,
):
    me = Place()
    g, r, c, z = me.g, me.r, me.c, me.z
    gx, gy, gd, rp = me.gx, me.gy, me.gd, me.rp
    outer = (z == 0) | (z == 3)
    inner = jnp.logical_not(outer)
    zin, zout, zother = 1 + z // 3, 3 * (z - 1), 3 - z
    zp = z % 2
    rz = r + 2 - 4 * zp

    def zdev(zz):
        return (g, 2 * zz + c)

    barrier = plane_barrier(me)
    for step in range(1, 4):
        pl.semaphore_signal(barrier, inc=1, device_id=zdev((z + step) % 4), device_id_type=MESH)

    local = []
    for w, ref in enumerate((wq, wk, wv, wo)):
        local.append((ref, W.at[w, pl.ds(pl.multiple_of(192 * g, 16), 192), :]))
    for u in range(4):
        local.append((wup.at[:, 768 * u : 768 * u + 768], W.at[4 + u, pl.ds(pl.multiple_of(192 * g, 16), 192), :]))
    local.append((wdn, W.at[8 + g]))
    local = [pltpu.make_async_copy(a, b, lsem.at[i]) for i, (a, b) in enumerate(local)]
    for copy in local:
        copy.start()

    own_lane = lax.broadcasted_iota(jnp.int32, (1, 768), 1) // 192 == g
    for row, ref in ((0, bq), (2, bv), (3, bo), (4, ga), (5, sa), (6, bd), (7, gf), (8, sf)):
        piece = ref[...].astype(F32).reshape(1, 192)
        PF[row : row + 1, :] = jnp.where(own_lane, jnp.concatenate([piece] * 4, axis=1), 0.0)
    for row in (1, 9, 10, 11):
        PF[row : row + 1, :] = jnp.zeros((1, 768), F32)
    tall = lax.broadcasted_iota(jnp.int32, (4, 768), 0) == g
    PF[12:16, :] = jnp.where(tall, bu[...].astype(F32).reshape(1, 768), 0.0)
    PK[g] = PF[...].astype(BF16)

    BG[...] = jnp.zeros_like(BG)
    pl.semaphore_wait(barrier, 10)

    def reshard(src, dst_of, ssem, rsem, blocks=(0, 1)):
        for m in blocks:
            t, e = 2 * c + m, g // 2
            b = g % 2
            here = (t == g) & (e == c)
            src_m = src.at[m]
            dst_b = dst_of(b)

            @pl.when(jnp.logical_not(here))
            def _():
                remote(src_m, dst_b, ssem.at[m], rsem.at[b], (t, 2 * z + e)).start()

            @pl.when(here)
            def _():
                pltpu.make_async_copy(src_m, dst_b, rsem.at[b]).start()

    def reshard_wait(src, dst_of, ssem, rsem, b):
        remote(src.at[0], dst_of(b), ssem.at[0], rsem.at[b], (g, r)).wait_recv()

    def reshard_drain(src, dst_of, ssem, rsem):
        for m in range(2):
            t, e = 2 * c + m, g // 2
            here = (t == g) & (e == c)

            @pl.when(jnp.logical_not(here))
            def _():
                remote(src.at[m], dst_of(0), ssem.at[m], rsem.at[0], (t, 2 * z + e)).wait_send()

    def x_rows(b):
        if isinstance(b, int):
            return X.at[256 * b : 256 * b + 256, :]
        return X.at[pl.ds(pl.multiple_of(256 * b, 256), 256), :]

    def g_rows(b):
        if isinstance(b, int):
            return G.at[256 * b : 256 * b + 256, :]
        return G.at[pl.ds(pl.multiple_of(256 * b, 256), 256), :]

    for m in range(2):
        for e in range(2):
            t = 2 * c + m
            here = (t == g) & (c == e)

            @pl.when(jnp.logical_not(here))
            def _():
                remote(docs_in, D.at[g], ds_.at[2 * m + e], dr.at[g], (t, 2 * z + e)).start()

            @pl.when(here)
            def _():
                pltpu.make_async_copy(docs_in, D.at[g], dr.at[g]).start()

    def own_send(k):
        part = piece_of(W, k, g, c, zp, 2)
        remote(part, part, ags.at[k, 0], agr.at[k, 0], (gx, r)).start()
        remote(part, part, ags.at[k, 1], agr.at[k, 1], (gy, r)).start()

    def pass_on(k, slot, part, device):
        remote(part, part, ags.at[k, slot], agr.at[k, slot], device).start()

    def landed(k, slot, part):
        remote(part, part, ags.at[k, slot], agr.at[k, slot], (g, rp)).wait_recv()

    def relay(k):
        landed(k, 0, piece_of(W, k, gx, c, zp, 2))
        pass_on(k, 2, piece_of(W, k, gx, c, zp, 1), (gy, r))
        pass_on(k, 7, piece_of(W, k, gx, c, 2 * zp, 1), (g, rz))
        landed(k, 1, piece_of(W, k, gy, c, zp, 2))
        pass_on(k, 3, piece_of(W, k, gy, c, zp + 1, 1), (gx, r))
        pass_on(k, 8, piece_of(W, k, gy, c, 2 * zp, 1), (g, rz))

    def diagonal(k):
        landed(k, 2, piece_of(W, k, gd, c, zp, 1))
        landed(k, 3, piece_of(W, k, gd, c, zp + 1, 1))
        pass_on(k, 9, piece_of(W, k, gd, c, 2 * zp, 1), (g, rz))

    def join(k, slots=(0, 1, 2)):
        for slot in slots:
            chip = (gx, gy, gd)[slot]
            landed(k, 7 + slot, piece_of(W, k, chip, c, 2 - 2 * zp, 1))
            pass_on(k, 4 + slot, piece_of(W, k, chip, c), (g, rp))

    def complete(k, slots=(0, 1, 2)):
        for slot in slots:
            landed(k, 4 + slot, piece_of(W, k, (gx, gy, gd)[slot], 1 - c))

    def gather_drain(k):
        two, one, all_three = piece_of(W, k, g, c, 0, 2), piece_of(W, k, g, c, 0, 1), piece_of(W, k, g, c)
        for slot, part in enumerate((two, two, one, one, all_three, all_three, all_three, one, one, one)):
            remote(part, part, ags.at[k, slot], agr.at[k, slot], (g, rp)).wait_send()

    for slot, chip in enumerate((gx, gy, gd)):
        remote(PK.at[g], PK.at[g], ps.at[slot], pr.at[slot], (chip, r)).start()
    for i in range(3):
        local[i].wait()
    own_send(0)
    reshard(tok, x_rows, xs, xr, (0,))
    for i in range(3, 9):
        local[i].wait()

    for slot, chip in enumerate((gx, gy, gd)):
        remote(PK.at[chip], PK.at[chip], ps.at[slot], pr.at[slot], (chip, r)).wait_recv()
    PF[...] = PK[0].astype(F32) + PK[1].astype(F32) + PK[2].astype(F32) + PK[3].astype(F32)
    for i in range(4):
        remote(docs_in, D.at[i], ds_.at[0], dr.at[i], (g, r)).wait_recv()
    for b in range(2):
        row = jnp.broadcast_to(D[2 * c + b, pl.ds(g % 2, 1), :].astype(F32), (128, 256))
        DC[256 * b : 256 * b + 256, :] = row.T
    for i in range(4):
        DR[:, 256 * i : 256 * i + 256] = jnp.broadcast_to(D[i, pl.ds(g % 2, 1), :].astype(F32), (8, 256))
    for i in range(4):
        keys = jnp.broadcast_to(D[i, pl.ds(g % 2, 1), :].astype(F32), (8, 256)).T[:, 0:1]
        for b in range(2):
            rows = D[2 * c + b, pl.ds(g % 2, 1), :].astype(F32)
            MASK[256 * i : 256 * i + 256, 256 * b : 256 * b + 256] = jnp.where(keys == rows, 0.0, NEGATIVE)
    relay(0)
    reshard(tok, x_rows, xs, xr, (1,))
    own_send(1)
    own_send(2)
    diagonal(0)
    for b in range(2):
        reshard_wait(tok, x_rows, xs, xr, b)
    remote(X, Xo, lls.at[0], llr.at[0], (g, rp)).start()
    join(0)
    complete(0)
    relay(1)
    own_send(3)
    own_rows = pl.ds(pl.multiple_of(512 * c, 512), 512)
    their_rows = pl.ds(pl.multiple_of(512 * (1 - c), 512), 512)

    def project(w, t, dst):
        cols = pl.ds(pl.multiple_of(256 * t, 256), 256)
        out = dot(X[...], W[w, :, cols]) + PF[pl.ds(w, 1), cols]
        return cols, out.astype(BF16)

    @pl.loop(0, 6)
    def _(i):
        w = i // 3
        cols, out = project(1 + w, i % 3, None)
        KV[w, own_rows, cols] = out

    for w in range(2):
        piece = KV.at[w, own_rows, :]
        remote(piece, piece, kvs.at[w], kvr.at[w], (g, rp)).start()
    @pl.loop(0, 3)
    def _(i):
        cols, out = project(0, i, None)
        Q[:, cols] = out

    for w in range(2):
        part = KV.at[w, their_rows, :]
        remote(part, part, kvs.at[w], kvr.at[w], (g, rp)).wait_recv()

    def at_step(i):
        pair, b = i // 2, i % 2
        return pair, pl.ds(pl.multiple_of(128 * pair, 128), 128), pl.ds(pl.multiple_of(256 * b, 256), 256)

    left_lanes = lax.broadcasted_iota(jnp.int32, (256, 128), 1) < 64

    def score(i, hh, S, peaks):
        pair, lanes, rows = at_step(i)
        q = Q[rows, lanes].astype(F32) * (HEAD_DIM ** -0.5)
        qh = jnp.where(left_lanes if hh == 0 else jnp.logical_not(left_lanes), q, 0.0).astype(BF16)
        s = dot_nt(qh, KV[0, :, lanes])
        s = jnp.where(DC[rows, 0:1] == DR[0:1, :], s, NEGATIVE)
        S[...] = s
        peaks[...] = jnp.broadcast_to(jnp.max(s, axis=1, keepdims=True), (256, 128))

    def soften(i, hh, S, peaks, vp):
        pair, lanes, rows = at_step(i)
        peak = peaks[...]
        e = jnp.exp(S[...] - peak[:, 0:1])
        total = jnp.sum(e, axis=1, keepdims=True)
        lane = lax.broadcasted_iota(jnp.int32, (256, 128), 1)
        LC[rows, :] = jnp.where(lane == 2 * pair + hh, peak + jnp.log(total), LC[rows, :])
        return dot(e.astype(BF16), vp) / total

    LC[...] = jnp.zeros_like(LC)
    score(0, 0, SA, PA)

    @pl.loop(0, 12)
    def _(i):
        pair, lanes, rows = at_step(i)
        vp = KV[1, :, lanes]
        score(i, 1, SB, PB)
        out0 = soften(i, 0, SA, PA, vp)
        score((i + 1) % 12, 0, SA, PA)
        out1 = soften(i, 1, SB, PB, vp)
        AT[rows, lanes] = jnp.where(left_lanes, out0, out1).astype(BF16)

        def at(k, *todo):
            @pl.when(i == k)
            def _():
                for f, j in todo:
                    f(j)

        at(0, (relay, 2), (own_send, 4))
        at(1, (diagonal, 1))
        at(5, (relay, 3), (own_send, 5))
        at(7, (diagonal, 2), (join, 1))
        at(11, (relay, 4))

    LSE[...] = LC[...].T[0:16, :]
    remote(AT, ATo, lls.at[1], llr.at[1], (g, rp)).start()
    join(2)
    complete(1)

    @pl.loop(0, 2)
    def _(i):
        rows = pl.ds(pl.multiple_of(256 * i, 256), 256)
        first = X[rows, :].astype(F32) + dot(AT[rows, :], W[3]) + PF[3:4, :]
        R1[rows, :] = first
        shape, _ = norm_parts(first)
        normed = shape * PF[4:5, :] + PF[5:6, :]
        R2[rows, :] = normed + PF[6:7, :]
        NL[rows, :] = normed.astype(BF16)

    remote(NL, NLo, lls.at[2], llr.at[2], (g, rp)).start()
    diagonal(3)
    join(3)
    relay(5)
    reshard(og, g_rows, gs, gr)
    complete(2)
    complete(3)

    def up(t):
        u, tt = t // 3, t % 3
        cols = pl.ds(pl.multiple_of(256 * tt, 256), 256)
        wide = pl.ds(pl.multiple_of(256 * t, 256), 256)
        h = dot(NL[...], W[4 + u, :, cols]) + PF[pl.ds(12 + u, 1), cols]
        cdf = 0.5 * (1.0 + lax.erf(h * (0.5 ** 0.5)))
        ACT[c, :, wide] = (h * cdf).astype(BF16)
        GP[:, wide] = (cdf + h * jnp.exp(-0.5 * h * h) * 0.3989422804014327).astype(BF16)

    @pl.loop(0, 12)
    def _(t):
        up(t)

        @pl.when(t == 3)
        def _():
            diagonal(4)

        @pl.when(t == 9)
        def _():
            diagonal(5)

    remote(ACT.at[c], ACT.at[c], lls.at[3], llr.at[3], (g, rp)).start()

    def down(k):
        deep = pl.ds(pl.multiple_of(768 * k, 256), 768)

        @pl.loop(0, 3)
        def _(tt):
            cols = pl.ds(pl.multiple_of(256 * tt, 256), 256)
            R2[:, cols] += dot(ACT[c, :, deep], W[8 + k, :, cols])

    down(g)
    join(4)
    join(5, (0, 1))
    complete(4)
    complete(5, (0, 1))
    down(gx)
    down(gy)
    join(5, (2,))
    complete(5, (2,))
    down(gd)

    def forward_drain():
        reshard_drain(tok, x_rows, xs, xr)
        reshard_drain(og, g_rows, gs, gr)
        for m in range(2):
            for e in range(2):
                t = 2 * c + m
                here = (t == g) & (c == e)

                @pl.when(jnp.logical_not(here))
                def _():
                    remote(docs_in, D.at[g], ds_.at[2 * m + e], dr.at[g], (t, 2 * z + e)).wait_send()
        for slot, chip in enumerate((gx, gy, gd)):
            remote(PK.at[g], PK.at[g], ps.at[slot], pr.at[slot], (chip, r)).wait_send()
        for w in range(2):
            part = KV.at[w, own_rows, :]
            remote(part, part, kvs.at[w], kvr.at[w], (g, rp)).wait_send()
        for i, (src, dst) in enumerate(((X, Xo), (AT, ATo), (NL, NLo), (ACT.at[c], ACT.at[c]))):
            remote(src, dst, lls.at[i], llr.at[i], (g, rp)).wait_send()

    loads = {}

    def load(name, slot, dst):
        src = {"x": Xo, "att": ATo, "nl": NLo}[name]
        remote(src, src, lls.at[slot], llr.at[slot], (g, rp)).wait_recv()
        copy = pltpu.make_async_copy(src, dst, lsem.at[9 + slot])
        copy.start()
        loads[name] = copy

    def grad(j, q, part=None):
        start, size = 0, 192
        if part is not None:
            start, size = 96 * part, 96
        if j < 4:
            return W.at[8 + q // 2, pl.ds(192 * j + start, size), pl.ds(pl.multiple_of(384 * (q % 2), 128), 384)]
        rows = pl.ds(pl.multiple_of(192 * q + start, 16), size)
        if j < 8:
            return W.at[10 + (j - 4) // 2, rows, 384 * (j % 2) : 384 * (j % 2) + 384]
        return W.at[4 + (j - 8) // 2, rows, 384 * (j % 2) : 384 * (j % 2) + 384]

    def first(j):
        remote(grad(j, gd, 0), P1.at[j, 0], p1s.at[j, 0], p1r.at[j, 0], (gy, r)).start()
        remote(grad(j, gd, 1), P1.at[j, 1], p1s.at[j, 1], p1r.at[j, 1], (gx, r)).start()

    def plain(j):
        remote(grad(j, gx, 1), P2.at[j, 0, 96:192], p2s.at[j, 0], p2r.at[j, 0], (gx, r)).start()
        remote(grad(j, gy, 0), P2.at[j, 1, 0:96], p2s.at[j, 1], p2r.at[j, 1], (gy, r)).start()

    def passed(j):
        for side, (chip, slot, rows) in enumerate(((gx, 0, slice(0, 96)), (gy, 1, slice(96, 192)))):
            mine = grad(j, chip, side)
            remote(mine, P1.at[j, side], p1s.at[j, side], p1r.at[j, side], (chip, r)).wait_recv()
            mine[...] = (mine[...].astype(F32) + P1[j, side].astype(F32)).astype(BF16)
            remote(mine, P2.at[j, slot, rows], p2s.at[j, 2 + side], p2r.at[j, 2 + side], (chip, r)).start()

    def own(j):
        for slot, rows, k in ((0, slice(96, 192), 0), (1, slice(0, 96), 1), (0, slice(0, 96), 2), (1, slice(96, 192), 3)):
            dst = P2.at[j, slot, rows]
            remote(dst, dst, p2s.at[j, k], p2r.at[j, k], (gx, r)).wait_recv()
        mine = grad(j, g)
        total = mine[...].astype(F32) + P2[j, 0].astype(F32) + P2[j, 1].astype(F32)
        P2[j, 0] = total.astype(BF16)

        @pl.when(outer)
        def _():
            remote(P2.at[j, 0], ZR.at[j, 0], zs.at[j, 0], zr.at[j, 0], zdev(zin)).start()

    def chain(j):
        @pl.when(inner)
        def _():
            remote(P2.at[j, 0], ZR.at[j, 0], zs.at[j, 0], zr.at[j, 0], zdev(zother)).wait_recv()
            P2[j, 0] = (P2[j, 0].astype(F32) + ZR[j, 0].astype(F32)).astype(BF16)
            remote(P2.at[j, 0], ZR.at[j, 1], zs.at[j, 1], zr.at[j, 1], zdev(zother)).start()

    def hand_over(j):
        remote(P2.at[j, 1], To.at[c, j], ts.at[j], tr.at[j], (g, rp)).start()
        pltpu.make_async_copy(P2.at[j, 1], To.at[c, j], osem.at[j]).start()

    def fin_in(j):
        @pl.when(inner)
        def _():
            remote(P2.at[j, 0], ZR.at[j, 1], zs.at[j, 1], zr.at[j, 1], zdev(zother)).wait_recv()
            P2[j, 1] = (P2[j, 0].astype(F32) + ZR[j, 1].astype(F32)).astype(BF16)
            remote(P2.at[j, 1], ZR.at[j, 0], zs.at[j, 0], zr.at[j, 0], zdev(zout)).start()
            hand_over(j)

    def fin_out(j):
        @pl.when(outer)
        def _():
            remote(P2.at[j, 1], ZR.at[j, 0], zs.at[j, 0], zr.at[j, 0], zdev(zin)).wait_recv()
            P2[j, 1] = ZR[j, 0]
            hand_over(j)

    def drain(j):
        for side in range(2):
            remote(P1.at[j, side], P1.at[j, side], p1s.at[j, side], p1r.at[j, side], (gx, r)).wait_send()
        for k in range(4):
            remote(P1.at[j, 0], P1.at[j, 0], p2s.at[j, k], p2r.at[j, k], (gx, r)).wait_send()
        remote(P2.at[j, 0], ZR.at[j, 0], zs.at[j, 0], zr.at[j, 0], zdev(zother)).wait_send()

        @pl.when(inner)
        def _():
            remote(P2.at[j, 0], ZR.at[j, 1], zs.at[j, 1], zr.at[j, 1], zdev(zother)).wait_send()

        piece = remote(P2.at[j, 1], To.at[1 - c, j], ts.at[j], tr.at[j], (g, rp))
        piece.wait_send()
        piece.wait_recv()
        pltpu.make_async_copy(P2.at[j, 1], To.at[c, j], osem.at[j]).wait()

    def serve(*slot):
        for name, j in SCHEDULE.get(slot, ()):
            services[name](j)

    def give_back(src, out, ssem, rsem):
        for b in range(2):
            t, e = 2 * c + b, g // 2
            here = (t == g) & (e == c)
            src_b = src.at[256 * b : 256 * b + 256, :]
            dst = out.at[g % 2]

            @pl.when(jnp.logical_not(here))
            def _():
                remote(src_b, dst, ssem.at[b], rsem.at[g % 2], (t, 2 * z + e)).start()

            @pl.when(here)
            def _():
                pltpu.make_async_copy(src_b, dst, rsem.at[g % 2]).start()

    def give_back_drain(src, out, ssem, rsem):
        for b in range(2):
            t, e = 2 * c + b, g // 2
            here = (t == g) & (e == c)
            src_b = src.at[256 * b : 256 * b + 256, :]

            @pl.when(jnp.logical_not(here))
            def _():
                remote(src_b, out.at[0], ssem.at[b], rsem.at[0], (t, 2 * z + e)).wait_send()

            remote(src_b, out.at[b], ssem.at[b], rsem.at[b], (g, rp)).wait_recv()

    services = {
        "passed": passed, "own": own, "chain": chain, "fin_in": fin_in, "fin_out": fin_out,
        "gi": lambda j: give_back(LO2, GIo, gis, gir),
    }

    def exchange(slot, src, dst):
        remote(src, dst, xs_.at[slot], xr_.at[slot], (g, rp)).start()

    def exchanged(slot, dst):
        remote(dst, dst, xs_.at[slot], xr_.at[slot], (g, rp)).wait_recv()

    def exchange_drain(slot, dst):
        remote(dst, dst, xs_.at[slot], xr_.at[slot], (g, rp)).wait_send()

    mine384 = pl.ds(pl.multiple_of(384 * c, 128), 384)
    theirs384 = pl.ds(pl.multiple_of(384 * (1 - c), 128), 384)

    def norm_back(values, gain, grad_out):
        shape, inverse = norm_parts(values)
        pulled = grad_out * gain
        d = inverse * (
            pulled
            - jnp.mean(pulled, axis=-1, keepdims=True)
            - shape * jnp.mean(pulled * shape, axis=-1, keepdims=True)
        )
        return shape, d

    for b in range(2):
        reshard_wait(og, g_rows, gs, gr, b)

    @pl.loop(0, 4)
    def _(i):
        rows = pl.ds(pl.multiple_of(128 * i, 128), 128)
        up = G[rows, :].astype(F32)
        shape, d = norm_back(R2[rows, :], PF[7:8, :], up)
        LO[rows, :] = (shape * PF[7:8, :] + PF[8:9, :]).astype(BF16)
        R2[rows, :] = d
        low = d.astype(BF16)
        DF[rows, :] = low
        BG[7:8, :] += columns(up * shape)
        BG[8:9, :] += columns(up)
        BG[6:7, :] += columns(low.astype(F32))

    exchange(0, DF.at[:, theirs384], DFP)
    give_back(LO, LOo, los, lor)

    def d_hidden(i):
        t = (i + 6 * (1 - c)) % 12
        tt = t % 3
        wide = pl.ds(pl.multiple_of(256 * t, 256), 256)
        back = dot_nt(DF[...], W[8 + t // 3, pl.ds(pl.multiple_of(256 * tt, 256), 256), :])
        low = (back * GP[:, wide].astype(F32)).astype(BF16)
        GP[:, wide] = low
        BG[pl.ds(12 + t // 3, 1), pl.ds(pl.multiple_of(256 * tt, 256), 256)] = columns(low.astype(F32))

    @pl.loop(0, 6)
    def _(i):
        d_hidden(i)

    exchange(1, GP.at[:, pl.ds(pl.multiple_of(1536 * (1 - c), 128), 1536)], DHP)

    @pl.loop(6, 12)
    def _(i):
        d_hidden(i)

    remote(ACT.at[1 - c], ACT.at[1 - c], lls.at[3], llr.at[3], (g, rp)).wait_recv()
    forward_drain()
    for k in range(GROUPS):
        gather_drain(k)
    exchanged(0, DFP)

    def pair_tn(own_left, their_left, own_right, their_right):
        return dot_tn(own_left, own_right) + dot_tn(their_left, their_right)

    def down_quarter(q):
        @pl.loop(0, 3)
        def _(i):
            lanes = pl.ds(pl.multiple_of(768 * q + 256 * i, 256), 256)
            out = pair_tn(ACT[c, :, lanes], ACT[1 - c, :, lanes], DF[:, mine384], DFP[...])
            W[8 + q // 2, pl.ds(pl.multiple_of(256 * i, 256), 256), pl.ds(pl.multiple_of(384 * (q % 2), 128), 384)] = (
                out.astype(BF16)
            )

    down_quarter(gd)
    for j in range(4):
        first(j)
    down_quarter(gx)
    down_quarter(gy)
    for j in range(4):
        plain(j)
    down_quarter(g)
    load("nl", 2, ACT.at[0, :, 0:768])
    load("att", 1, ACT.at[0, :, 768:1536])
    load("x", 0, ACT.at[0, :, 1536:2304])

    @pl.loop(0, 3)
    def _(i):
        cols = pl.ds(pl.multiple_of(256 * i, 256), 256)
        total = R2[:, cols]
        for u in range(4):
            total = total + dot_nt(GP[:, 768 * u : 768 * u + 768], W[4 + u, cols, :])
        R2[:, cols] = total

    serve("normed")

    @pl.loop(0, 4)
    def _(i):
        rows = pl.ds(pl.multiple_of(128 * i, 128), 128)
        up = R2[rows, :]
        shape, d = norm_back(R1[rows, :], PF[4:5, :], up)
        R2[rows, :] = d
        low = d.astype(BF16)
        DB[rows, :] = low
        BG[4:5, :] += columns(up * shape)
        BG[5:6, :] += columns(up)
        BG[3:4, :] += columns(low.astype(F32))

    exchange(2, DB.at[:, theirs384], DBP)
    serve("ln1")
    exchanged(1, DHP)
    loads["nl"].wait()

    for j in range(4, 8):
        jj = j - 4
        own_cols = pl.ds(pl.multiple_of(1536 * c + 384 * jj, 128), 384)

        @pl.loop(0, 3)
        def _(i):
            lanes = pl.ds(pl.multiple_of(256 * i, 256), 256)
            out = pair_tn(NL[:, lanes], ACT[0, :, lanes], GP[:, own_cols], DHP[:, 384 * jj : 384 * jj + 384])
            W[10 + jj // 2, lanes, 384 * (jj % 2) : 384 * (jj % 2) + 384] = out.astype(BF16)

        first(j)
        plain(j)
        serve("up", j)

    @pl.loop(0, 3)
    def _(i):
        cols = pl.ds(pl.multiple_of(256 * i, 256), 256)
        DATT[:, cols] = dot_nt(DB[...], W[3, cols, :]).astype(BF16)

    serve("datt")
    exchanged(2, DBP)
    loads["att"].wait()

    def square_grad(j, offset, own_left, own_right, their_right):
        @pl.loop(0, 3)
        def _(i):
            lanes = pl.ds(pl.multiple_of(offset + 256 * i, 256), 256)
            cols = pl.ds(pl.multiple_of(256 * i, 256), 256)
            out = pair_tn(own_left[:, cols], ACT[0, :, lanes], own_right[...], their_right[...])
            W[4 + (j - 8) // 2, cols, 384 * (j % 2) : 384 * (j % 2) + 384] = (
                out.astype(BF16)
            )

        first(j)
        plain(j)

    square_grad(8, 768, AT, DB.at[:, mine384], DBP)
    serve("sq", 8)

    @pl.loop(0, 12)
    def _(i):
        pair, b = (i // 2 + 3 * (1 - c)) % 6, i % 2
        lanes = pl.ds(pl.multiple_of(128 * pair, 128), 128)
        half_lanes = pl.ds(pl.multiple_of(128 * (pair % 3), 128), 128)
        cols = pl.ds(pl.multiple_of(256 * b, 256), 256)
        qs = Q[cols, lanes].astype(F32) * (HEAD_DIM ** -0.5)
        do = DATT[cols, lanes].astype(F32)
        qt, dot_t = qs.T, do.T
        kp = KV[0, :, lanes]
        vp = KV[1, :, lanes]
        kt = kp.astype(F32).T.astype(BF16)
        weigh = (do * AT[cols, lanes].astype(F32)).T
        top = lax.broadcasted_iota(jnp.int32, (128, 256), 0) < 64
        left = lax.broadcasted_iota(jnp.int32, (256, 128), 1) < 64
        dk = dv = None
        pieces = []
        for hh in range(2):
            rows_in = top if hh == 0 else jnp.logical_not(top)
            lanes_in = left if hh == 0 else jnp.logical_not(left)
            s = dot(kp, jnp.where(rows_in, qt, 0.0).astype(BF16)) + MASK[:, cols]
            p = jnp.exp(s - LSE[pl.ds(2 * pair + hh, 1), cols])
            dp = dot(vp, jnp.where(rows_in, dot_t, 0.0).astype(BF16))
            ds = (p * (dp - columns(weigh[64 * hh : 64 * hh + 64, :]))).astype(BF16)
            dv_h = dot(p.astype(BF16), jnp.where(lanes_in, do, 0.0).astype(BF16))
            dk_h = dot(ds, jnp.where(lanes_in, qs, 0.0).astype(BF16))
            dv = dv_h if dv is None else dv + dv_h
            dk = dk_h if dk is None else dk + dk_h
            pieces.append(dot(kt[64 * hh : 64 * hh + 64, :], ds))
        DQ[cols, lanes] = (jnp.concatenate(pieces, axis=0).T * (HEAD_DIM ** -0.5)).astype(BF16)

        @pl.when(b == 0)
        def _():
            ACC[0] = dk
            ACC[1] = dv

        @pl.when(i == 7)
        def _():
            exchanged(3, DKR)

        @pl.when((b == 1) & (i < 6))
        def _():
            DKS[0, :, half_lanes] = (ACC[0] + dk).astype(BF16)
            DKS[1, :, half_lanes] = (ACC[1] + dv).astype(BF16)

        @pl.when((b == 1) & (i > 6))
        def _():
            DKF[0, :, half_lanes] = (ACC[0] + dk + DKR[0, :, half_lanes].astype(F32)).astype(BF16)
            DKF[1, :, half_lanes] = (ACC[1] + dv + DKR[1, :, half_lanes].astype(F32)).astype(BF16)

        @pl.when(i == 5)
        def _():
            exchange(3, DKS, DKR)
            exchange(4, DQ.at[:, theirs384], DQP)

        for k in range(12):
            if ("a", k) in SCHEDULE:
                @pl.when(i == k)
                def _():
                    serve("a", k)

    exchange(5, DKF.at[:, their_rows, :], DKP)
    BG[0:1, :] = columns(DQ[...].astype(F32))
    BG[2:3, mine384] = columns(DKF[1].astype(F32))

    BS[...] = BG[...].astype(BF16)
    others = [(gg, rr, k) for k, (gg, rr) in enumerate(
        ((g, rp), (gx, r), (gx, rp), (gy, r), (gy, rp), (gd, r), (gd, rp)))]
    slot_of = 2 * g + c
    for gg, rr, k in others:
        remote(BS, BR.at[slot_of], b1s.at[k], b1r.at[k], (gg, rr)).start()
    BR[slot_of] = BS[...]

    loads["x"].wait()
    exchanged(4, DQP)
    square_grad(9, 1536, X, DQ.at[:, mine384], DQP)
    serve("sq", 9)
    square_grad(10, 1536, X, DKF.at[0, own_rows, :], DKF.at[0, their_rows, :])
    serve("sq", 10)
    square_grad(11, 1536, X, DKF.at[1, own_rows, :], DKF.at[1, their_rows, :])
    serve("sq", 11)

    exchanged(5, DKP)

    @pl.loop(0, 3)
    def _(i):
        cols = pl.ds(pl.multiple_of(256 * i, 256), 256)
        total = R2[:, cols] + dot_nt(DQ[...], W[0, cols, :])
        for w in range(2):
            total = total + dot_nt(DKF[w, own_rows, :], W[1 + w, cols, mine384])
            total = total + dot_nt(DKP[w], W[1 + w, cols, theirs384])
        LO2[:, cols] = total.astype(BF16)

    serve("inp")
    for gg, rr, k in others:
        src = 2 * gg + rr % 2
        remote(BS, BR.at[src], b1s.at[k], b1r.at[k], (gg, rr)).wait_recv()
    total = BR[0].astype(F32)
    for k in range(1, 8):
        total = total + BR[k].astype(F32)
    BZ[z] = total.astype(BF16)
    for step in range(1, 4):
        zz = (z + step) % 4
        remote(BZ.at[z], BZ.at[z], b2s.at[step - 1], b2r.at[step - 1], zdev(zz)).start()
    serve("tail")
    for step in range(1, 4):
        zz = (z + 4 - step) % 4
        remote(BZ.at[zz], BZ.at[zz], b2s.at[step - 1], b2r.at[step - 1], zdev(zz)).wait_recv()
    BT[...] = (BZ[0].astype(F32) + BZ[1].astype(F32)) + (BZ[2].astype(F32) + BZ[3].astype(F32))
    bt_copy = pltpu.make_async_copy(BT, BTo, osem.at[CHUNKS])
    bt_copy.start()

    for j in range(CHUNKS):
        drain(j)
    for slot, dst in ((0, DFP), (1, DHP), (2, DBP), (3, DKR), (4, DQP), (5, DKP)):
        exchange_drain(slot, dst)
    give_back_drain(LO, LOo, los, lor)
    give_back_drain(LO2, GIo, gis, gir)
    for gg, rr, k in others:
        remote(BS, BR.at[0], b1s.at[k], b1r.at[k], (gg, rr)).wait_send()
    for step in range(1, 4):
        remote(BZ.at[z], BZ.at[z], b2s.at[step - 1], b2r.at[step - 1], zdev(z)).wait_send()
    bt_copy.wait()


def sds(shape, dtype=BF16):
    return jax.ShapeDtypeStruct(shape, dtype)


def layer(*args):
    out = [
        sds((2, 256, 768)), sds((2, 256, 768)), sds((2, CHUNKS, 192, 384)), sds((16, 768), F32),
        sds((512, 768)), sds((512, 768)), sds((512, 768)),
    ]
    dma = pltpu.SemaphoreType.DMA
    v = pltpu.VMEM
    return pl.pallas_call(
        layer_kernel,
        out_shape=out,
        in_specs=[ANY] * 9 + [pl.BlockSpec(memory_space=pltpu.VMEM)] * 9,
        out_specs=[ANY] * len(out),
        scratch_shapes=[
            v((12, 768, 768), BF16), v((CHUNKS, 2, 96, 384), BF16), v((CHUNKS, 2, 192, 384), BF16),
            v((CHUNKS, 2, 192, 384), BF16),
            v((2, 512, 3072), BF16), v((512, 3072), BF16), v((512, 1536), BF16), v((512, 768), BF16),
            v((2, 1024, 768), BF16), v((1024, 512), F32), v((16, 512), F32),
            v((512, 768), F32), v((512, 768), F32), v((512, 768), BF16), v((16, 768), F32),
            v((512, 768), BF16), v((512, 384), BF16), v((512, 768), BF16), v((512, 384), BF16),
            v((512, 768), BF16), v((512, 768), BF16), v((512, 384), BF16), v((2, 1024, 384), BF16),
            v((2, 1024, 384), BF16), v((2, 1024, 384), BF16), v((2, 512, 384), BF16),
            v((512, 768), BF16), v((512, 768), BF16), v((2, 1024, 128), F32), v((16, 768), F32), v((8, 16, 768), BF16),
            v((16, 768), BF16), v((4, 16, 768), BF16), v((16, 768), F32),
            v((512, 768), BF16), v((512, 768), BF16), v((512, 768), BF16), v((256, 1024), F32), v((256, 1024), F32),
            v((256, 128), F32), v((256, 128), F32), v((512, 128), F32), v((8, 1024), F32), v((512, 128), F32),
            v((4, 2, 256), jnp.int32), v((4, 16, 768), BF16),
            dma((12,)), dma((CHUNKS, 2)), dma((CHUNKS, 2)), dma((CHUNKS, 4)), dma((CHUNKS, 4)),
            dma((CHUNKS, 2)), dma((CHUNKS, 2)), dma((CHUNKS,)), dma((CHUNKS,)), dma((6,)), dma((6,)),
            dma((2,)), dma((2,)), dma((2,)), dma((2,)), dma((7,)), dma((7,)), dma((3,)), dma((3,)),
            dma((CHUNKS + 1,)),
            dma((GROUPS, 10)), dma((GROUPS, 10)), dma((2,)), dma((2,)), dma((4,)), dma((4,)),
            dma((3,)), dma((3,)), dma((2,)), dma((2,)), dma((2,)), dma((2,)), dma((4,)), dma((4,)),
        ],
        compiler_params=pltpu.CompilerParams(
            collective_id=0, has_side_effects=True, vmem_limit_bytes=67043328
        ),
    )(*args)


def spread_kernel(
    Ti, GIi, LOi, BTi,
    LOo, GIo, WQo, WKo, WVo, WOo, WUo, WDo, BQo, BVo, BOo, GAo, SAo, BUo, BDo, GFo, SFo,
    T, GI, LO, OUT, GIF, sem, osem,
):
    g = lax.axis_index("group")
    order = (0, 1, 2, 3, 4, 5, 6, 7, 8, 9, 10, 11)
    loads = []
    for j in order:
        loads.append(pltpu.make_async_copy(Ti.at[:, j], T.at[:, j], sem.at[j]))
    loads.append(pltpu.make_async_copy(GIi, GI, sem.at[12]))
    loads.append(pltpu.make_async_copy(LOi, LO, sem.at[13]))
    for copy in loads:
        copy.start()
    stores = []

    def store(src, dst):
        copy = pltpu.make_async_copy(src, dst, osem.at[len(stores)])
        copy.start()
        stores.append(copy)

    for j in order:
        loads[j].wait()
        for e in range(2):
            OUT[j, :, 384 * e : 384 * e + 384] = T[e, j].astype(F32)
        if j < 4:
            store(OUT.at[j], WDo.at[192 * j : 192 * j + 192, :])
        elif j < 8:
            for e in range(2):
                start = 1536 * e + 384 * (j - 4)
                store(OUT.at[j, :, 384 * e : 384 * e + 384], WUo.at[:, start : start + 384])
        else:
            store(OUT.at[j], (WOo, WQo, WKo, WVo)[j - 8])
    loads[12].wait()
    GIF[...] = GI[...].astype(F32)
    store(GIF, GIo)
    loads[13].wait()
    store(LO, LOo)
    moved = pltpu.roll(BTi[...], (768 - 192 * g) % 768, 1)
    for row, ref in ((0, BQo), (2, BVo), (3, BOo), (4, GAo), (5, SAo), (6, BDo), (7, GFo), (8, SFo)):
        ref[...] = moved[row, 0:192]
    up = BTi[pl.ds(12 + g, 1), :]
    BUo[...] = up[0, :]
    for copy in stores:
        copy.wait()


def spread(totals, grad_input, layer_out, small):
    square = sds((192, 768), F32)
    short = sds((192,), F32)
    whole = pl.BlockSpec(memory_space=pltpu.VMEM)
    dma = pltpu.SemaphoreType.DMA
    return pl.pallas_call(
        spread_kernel,
        out_shape=[
            sds((2, 256, 768)), sds((2, 256, 768), F32), square, square, square, square,
            sds((192, 3072), F32), sds((768, 768), F32),
            short, short, short, short, short, sds((768,), F32), short, short, short,
        ],
        in_specs=[ANY, ANY, ANY, whole],
        out_specs=[ANY] * 8 + [whole] * 9,
        scratch_shapes=[
            pltpu.VMEM((2, CHUNKS, 192, 384), BF16), pltpu.VMEM((2, 256, 768), BF16), pltpu.VMEM((2, 256, 768), BF16),
            pltpu.VMEM((CHUNKS, 192, 768), F32), pltpu.VMEM((2, 256, 768), F32), dma((14,)), dma((20,)),
        ],
        compiler_params=pltpu.CompilerParams(vmem_limit_bytes=66000000),
    )(totals, grad_input, layer_out, small)


def fits(mesh):
    return dict(mesh.shape) == {"group": 4, "replica": 8}


def fast(
    tokens_in, doc_ids, out_grad, w_query, w_key, w_value, w_out, w_up, w_down, b_query, b_value, b_out,
    gain_attn, shift_attn, b_up, b_down, gain_ffn, shift_ffn,
):
    layer_out, grad_input, totals, small, *_ = layer(
        tokens_in, doc_ids, out_grad, w_query, w_key, w_value, w_out, w_up, w_down,
        b_query, b_value, b_out, gain_attn, shift_attn, b_down, gain_ffn, shift_ffn, b_up,
    )
    return tuple(spread(totals, grad_input, layer_out, small))


def layer_norm(values, gain, shift):
    centre = values - jnp.mean(values, axis=-1, keepdims=True)
    spread = jnp.mean(centre * centre, axis=-1, keepdims=True)
    return centre * lax.rsqrt(spread + EPSILON) * gain + shift


def norm_pull(values, gain, shift, grad):
    result, pullback = jax.vjp(
        layer_norm, values, gain.astype(jnp.float32), shift.astype(jnp.float32)
    )
    return (result, pullback(grad))


def exact_gelu(values):
    return jax.nn.gelu(values, approximate=False)


def project(inputs, weight, bias):
    return jnp.dot(inputs, weight, preferred_element_type=jnp.float32) + bias.astype(jnp.float32)


def contract_rows(left, right):
    return lax.dot_general(
        left, right, (((0,), (0,)), ((), ())), preferred_element_type=jnp.float32
    )


def against_rows(grad, weight):
    return lax.dot_general(
        grad, weight, (((1,), (1,)), ((), ())), preferred_element_type=jnp.float32
    )


def column_sum(values):
    return jnp.sum(values.astype(jnp.float32), axis=0)


def add_pair(first, second):
    return first + second


def scores_of(query, keys_all, allowed):
    rows = query.shape[0]
    length = keys_all.shape[0]
    scaling = HEAD_DIM ** (-0.5)
    scores = (
        jnp.einsum(
            "qhd,khd->hqk",
            query.reshape(rows, HEADS, HEAD_DIM),
            keys_all.reshape(length, HEADS, HEAD_DIM),
            preferred_element_type=jnp.float32,
        )
        * scaling
    )
    return jnp.where(allowed[None], scores, NEGATIVE)


def attention_forward(query, keys_all, values_all, allowed):
    rows = query.shape[0]
    length = keys_all.shape[0]
    scores = scores_of(query, keys_all, allowed)
    row_max = jnp.max(scores, axis=-1, keepdims=True)
    exponent = jnp.exp(scores - row_max)
    total = jnp.sum(exponent, axis=-1, keepdims=True)
    probs = (exponent / total).astype(jnp.bfloat16)
    log_total = row_max[..., 0] + jnp.log(total[..., 0])
    joined = jnp.einsum(
        "hqk,khd->qhd",
        probs,
        values_all.reshape(length, HEADS, HEAD_DIM),
        preferred_element_type=jnp.float32,
    )
    return (joined.reshape(rows, HEADS * HEAD_DIM), log_total)


def score_grads(query, keys_all, values_all, allowed, log_total, d_attended):
    rows = query.shape[0]
    length = keys_all.shape[0]
    scores = scores_of(query, keys_all, allowed)
    probs = jnp.exp(scores - log_total[..., None])
    d_heads = d_attended.reshape(rows, HEADS, HEAD_DIM)
    d_probs = jnp.einsum(
        "qhd,khd->hqk",
        d_heads,
        values_all.reshape(length, HEADS, HEAD_DIM),
        preferred_element_type=jnp.float32,
    )
    row_term = jnp.sum(probs * d_probs, axis=-1)
    d_scores = (probs * (d_probs - row_term[..., None])).astype(jnp.bfloat16)
    return (probs, d_scores, row_term)


def attention_backward(query, keys_all, values_all, allowed, log_total, d_attended):
    rows = query.shape[0]
    length = keys_all.shape[0]
    scaling = HEAD_DIM ** (-0.5)
    probs, d_scores, row_term = score_grads(
        query, keys_all, values_all, allowed, log_total, d_attended
    )
    d_heads = d_attended.reshape(rows, HEADS, HEAD_DIM)
    d_values_part = jnp.einsum(
        "hqk,qhd->khd", probs.astype(jnp.bfloat16), d_heads, preferred_element_type=jnp.float32
    ).reshape(length, HEADS * HEAD_DIM)
    d_query = (
        jnp.einsum(
            "hqk,khd->qhd",
            d_scores,
            keys_all.reshape(length, HEADS, HEAD_DIM),
            preferred_element_type=jnp.float32,
        ).reshape(rows, HEADS * HEAD_DIM)
        * scaling
    )
    d_keys_part = (
        jnp.einsum(
            "hqk,qhd->khd",
            d_scores,
            query.reshape(rows, HEADS, HEAD_DIM),
            preferred_element_type=jnp.float32,
        ).reshape(length, HEADS * HEAD_DIM)
        * scaling
    )
    return (d_query, d_keys_part, d_values_part, row_term)


def owner_sum(grads):
    return (
        lax.psum_scatter(
            grads[0].astype(jnp.bfloat16), "group", scatter_dimension=0, tiled=True
        ).astype(jnp.float32),
        lax.psum_scatter(
            grads[1].astype(jnp.bfloat16), "group", scatter_dimension=0, tiled=True
        ).astype(jnp.float32),
        lax.psum_scatter(
            grads[2].astype(jnp.bfloat16), "group", scatter_dimension=0, tiled=True
        ).astype(jnp.float32),
        lax.psum_scatter(
            grads[3].astype(jnp.bfloat16), "group", scatter_dimension=0, tiled=True
        ).astype(jnp.float32),
        lax.psum_scatter(
            grads[4].astype(jnp.bfloat16), "group", scatter_dimension=0, tiled=True
        ).astype(jnp.float32),
        lax.psum_scatter(
            grads[5].astype(jnp.bfloat16), "group", scatter_dimension=0, tiled=True
        ).astype(jnp.float32),
        lax.psum_scatter(
            grads[6].astype(jnp.bfloat16), "group", scatter_dimension=0, tiled=True
        ).astype(jnp.float32),
        lax.psum_scatter(
            grads[7].astype(jnp.bfloat16), "group", scatter_dimension=0, tiled=True
        ).astype(jnp.float32),
        lax.psum_scatter(
            grads[8].astype(jnp.bfloat16), "group", scatter_dimension=0, tiled=True
        ).astype(jnp.float32),
        lax.psum_scatter(
            grads[9].astype(jnp.bfloat16), "group", scatter_dimension=0, tiled=True
        ).astype(jnp.float32),
        lax.psum_scatter(
            grads[10].astype(jnp.bfloat16), "group", scatter_dimension=0, tiled=True
        ).astype(jnp.float32),
        lax.psum_scatter(
            grads[11].astype(jnp.bfloat16), "group", scatter_dimension=0, tiled=True
        ).astype(jnp.float32),
        lax.psum_scatter(
            grads[12].astype(jnp.bfloat16), "group", scatter_dimension=0, tiled=True
        ).astype(jnp.float32),
        lax.psum_scatter(
            grads[13].astype(jnp.bfloat16), "group", scatter_dimension=0, tiled=True
        ).astype(jnp.float32),
        lax.psum_scatter(
            grads[14].astype(jnp.bfloat16), "group", scatter_dimension=0, tiled=True
        ).astype(jnp.float32),
    )


def shards(
    tokens_in,
    doc_ids,
    out_grad,
    w_query,
    w_key,
    w_value,
    w_out,
    w_up,
    w_down,
    b_query,
    b_value,
    b_out,
    gain_attn,
    shift_attn,
    b_up,
    b_down,
    gain_ffn,
    shift_ffn,
):
    gathered = (
        lax.all_gather(w_query, "group", axis=0, tiled=True),
        lax.all_gather(w_key, "group", axis=0, tiled=True),
        lax.all_gather(w_value, "group", axis=0, tiled=True),
        lax.all_gather(w_out, "group", axis=0, tiled=True),
        lax.all_gather(w_up, "group", axis=0, tiled=True),
        lax.all_gather(w_down, "group", axis=0, tiled=True),
        lax.all_gather(b_query, "group", axis=0, tiled=True),
        lax.all_gather(b_value, "group", axis=0, tiled=True),
        lax.all_gather(b_out, "group", axis=0, tiled=True),
        lax.all_gather(gain_attn, "group", axis=0, tiled=True),
        lax.all_gather(shift_attn, "group", axis=0, tiled=True),
        lax.all_gather(b_up, "group", axis=0, tiled=True),
        lax.all_gather(b_down, "group", axis=0, tiled=True),
        lax.all_gather(gain_ffn, "group", axis=0, tiled=True),
        lax.all_gather(shift_ffn, "group", axis=0, tiled=True),
    )
    (
        query_weight,
        key_weight,
        value_weight,
        out_weight,
        up_weight,
        down_weight,
        query_bias,
        value_bias,
        out_bias,
        attn_gain,
        attn_shift,
        up_bias,
        down_bias,
        ffn_gain,
        ffn_shift,
    ) = gathered
    micros = tokens_in.shape[0]
    outputs = []
    stored = []
    for micro in range(micros):
        inputs = tokens_in[micro]
        segment = doc_ids[micro]
        query = project(inputs, query_weight, query_bias).astype(jnp.bfloat16)
        keys = jnp.dot(inputs, key_weight, preferred_element_type=jnp.float32).astype(jnp.bfloat16)
        values = project(inputs, value_weight, value_bias).astype(jnp.bfloat16)
        keys_all, values_all, seg_all = (
            lax.all_gather(keys, "group", axis=0, tiled=True),
            lax.all_gather(values, "group", axis=0, tiled=True),
            lax.all_gather(segment, "group", axis=0, tiled=True),
        )
        allowed = segment[:, None] == seg_all[None, :]
        attended, log_total = attention_forward(query, keys_all, values_all, allowed)
        attended = attended.astype(jnp.bfloat16)
        resid_one = inputs.astype(jnp.float32) + project(attended, out_weight, out_bias)
        normed = layer_norm(
            resid_one, attn_gain.astype(jnp.float32), attn_shift.astype(jnp.float32)
        )
        hidden = project(normed.astype(jnp.bfloat16), up_weight, up_bias)
        activated = exact_gelu(hidden).astype(jnp.bfloat16)
        resid_two = normed + project(activated, down_weight, down_bias)
        result = layer_norm(resid_two, ffn_gain.astype(jnp.float32), ffn_shift.astype(jnp.float32))
        outputs.append(result.astype(jnp.bfloat16))
        stored.append((query, keys, values, log_total, attended, resid_one, hidden, resid_two))
    gathered = (
        lax.all_gather(w_query, "group", axis=0, tiled=True),
        lax.all_gather(w_key, "group", axis=0, tiled=True),
        lax.all_gather(w_value, "group", axis=0, tiled=True),
        lax.all_gather(w_out, "group", axis=0, tiled=True),
        lax.all_gather(w_up, "group", axis=0, tiled=True),
        lax.all_gather(w_down, "group", axis=0, tiled=True),
        lax.all_gather(b_query, "group", axis=0, tiled=True),
        lax.all_gather(b_value, "group", axis=0, tiled=True),
        lax.all_gather(b_out, "group", axis=0, tiled=True),
        lax.all_gather(gain_attn, "group", axis=0, tiled=True),
        lax.all_gather(shift_attn, "group", axis=0, tiled=True),
        lax.all_gather(b_up, "group", axis=0, tiled=True),
        lax.all_gather(b_down, "group", axis=0, tiled=True),
        lax.all_gather(gain_ffn, "group", axis=0, tiled=True),
        lax.all_gather(shift_ffn, "group", axis=0, tiled=True),
    )
    (
        query_weight,
        key_weight,
        value_weight,
        out_weight,
        up_weight,
        down_weight,
        query_bias,
        value_bias,
        out_bias,
        attn_gain,
        attn_shift,
        up_bias,
        down_bias,
        ffn_gain,
        ffn_shift,
    ) = gathered
    totals = tuple((jnp.zeros(member.shape, jnp.float32) for member in gathered))
    input_grads = []
    for micro in range(micros):
        inputs = tokens_in[micro]
        segment = doc_ids[micro]
        query, keys, values, log_total, attended, resid_one, hidden, resid_two = stored[micro]
        upstream = out_grad[micro].astype(jnp.float32)
        unused_out, (d_resid_two, g_ffn_gain, g_ffn_shift) = norm_pull(
            resid_two, ffn_gain, ffn_shift, upstream
        )
        d_ffn = d_resid_two.astype(jnp.bfloat16)
        activated, gelu_pull = jax.vjp(exact_gelu, hidden)
        activated = activated.astype(jnp.bfloat16)
        g_down_w = contract_rows(activated, d_ffn)
        g_down_b = column_sum(d_ffn)
        d_activated = against_rows(d_ffn, down_weight)
        d_hidden = gelu_pull(d_activated)[0].astype(jnp.bfloat16)
        normed = layer_norm(
            resid_one, attn_gain.astype(jnp.float32), attn_shift.astype(jnp.float32)
        )
        normed_low = normed.astype(jnp.bfloat16)
        g_up_w = contract_rows(normed_low, d_hidden)
        g_up_b = column_sum(d_hidden)
        d_normed = against_rows(d_hidden, up_weight) + d_resid_two
        unused_norm, (d_resid_one, g_attn_gain, g_attn_shift) = norm_pull(
            resid_one, attn_gain, attn_shift, d_normed
        )
        d_branch = d_resid_one.astype(jnp.bfloat16)
        g_out_w = contract_rows(attended, d_branch)
        g_out_b = column_sum(d_branch)
        d_attended = against_rows(d_branch, out_weight).astype(jnp.bfloat16)
        keys_all, values_all, seg_all = (
            lax.all_gather(keys, "group", axis=0, tiled=True),
            lax.all_gather(values, "group", axis=0, tiled=True),
            lax.all_gather(segment, "group", axis=0, tiled=True),
        )
        allowed = segment[:, None] == seg_all[None, :]
        d_query, d_keys_part, d_values_part, row_term = attention_backward(
            query, keys_all, values_all, allowed, log_total, d_attended
        )
        d_keys, d_values = (
            lax.psum_scatter(
                d_keys_part.astype(jnp.bfloat16), "group", scatter_dimension=0, tiled=True
            ).astype(jnp.float32),
            lax.psum_scatter(
                d_values_part.astype(jnp.bfloat16), "group", scatter_dimension=0, tiled=True
            ).astype(jnp.float32),
        )
        d_query = d_query.astype(jnp.bfloat16)
        d_keys = d_keys.astype(jnp.bfloat16)
        d_values = d_values.astype(jnp.bfloat16)
        g_query_w = contract_rows(inputs, d_query)
        g_key_w = contract_rows(inputs, d_keys)
        g_value_w = contract_rows(inputs, d_values)
        g_query_b = column_sum(d_query)
        g_value_b = column_sum(d_values)
        input_grad = (
            d_resid_one
            + against_rows(d_query, query_weight)
            + against_rows(d_keys, key_weight)
            + against_rows(d_values, value_weight)
        )
        input_grads.append(input_grad)
        micro_grads = (
            g_query_w,
            g_key_w,
            g_value_w,
            g_out_w,
            g_up_w,
            g_down_w,
            g_query_b,
            g_value_b,
            g_out_b,
            g_attn_gain,
            g_attn_shift,
            g_up_b,
            g_down_b,
            g_ffn_gain,
            g_ffn_shift,
        )
        totals = jax.tree.map(add_pair, totals, micro_grads)
    totals = tuple(owner_sum(totals))
    summed = (
        lax.psum(totals[0].astype(jnp.bfloat16), "replica").astype(jnp.float32),
        lax.psum(totals[1].astype(jnp.bfloat16), "replica").astype(jnp.float32),
        lax.psum(totals[2].astype(jnp.bfloat16), "replica").astype(jnp.float32),
        lax.psum(totals[3].astype(jnp.bfloat16), "replica").astype(jnp.float32),
        lax.psum(totals[4].astype(jnp.bfloat16), "replica").astype(jnp.float32),
        lax.psum(totals[5].astype(jnp.bfloat16), "replica").astype(jnp.float32),
        lax.psum(totals[6].astype(jnp.bfloat16), "replica").astype(jnp.float32),
        lax.psum(totals[7].astype(jnp.bfloat16), "replica").astype(jnp.float32),
        lax.psum(totals[8].astype(jnp.bfloat16), "replica").astype(jnp.float32),
        lax.psum(totals[9].astype(jnp.bfloat16), "replica").astype(jnp.float32),
        lax.psum(totals[10].astype(jnp.bfloat16), "replica").astype(jnp.float32),
        lax.psum(totals[11].astype(jnp.bfloat16), "replica").astype(jnp.float32),
        lax.psum(totals[12].astype(jnp.bfloat16), "replica").astype(jnp.float32),
        lax.psum(totals[13].astype(jnp.bfloat16), "replica").astype(jnp.float32),
        lax.psum(totals[14].astype(jnp.bfloat16), "replica").astype(jnp.float32),
    )
    layer_out = jnp.stack(outputs)
    grad_input = jnp.stack(input_grads)
    return (
        layer_out,
        grad_input,
        summed[0],
        summed[1],
        summed[2],
        summed[3],
        summed[4],
        summed[5],
        summed[6],
        summed[7],
        summed[8],
        summed[9],
        summed[10],
        summed[11],
        summed[12],
        summed[13],
        summed[14],
    )


def solution(mesh):
    return jax.shard_map(
        shards if not fits(mesh) else fast,
        mesh=mesh,
        in_specs=(
            P("replica", "group", None),
            P("replica", "group"),
            P("replica", "group", None),
            P("group", None),
            P("group", None),
            P("group", None),
            P("group", None),
            P("group", None),
            P("group", None),
            P("group"),
            P("group"),
            P("group"),
            P("group"),
            P("group"),
            P("group"),
            P("group"),
            P("group"),
            P("group"),
        ),
        out_specs=(
            P("replica", "group", None),
            P("replica", "group", None),
            P("group", None),
            P("group", None),
            P("group", None),
            P("group", None),
            P("group", None),
            P("group", None),
            P("group"),
            P("group"),
            P("group"),
            P("group"),
            P("group"),
            P("group"),
            P("group"),
            P("group"),
            P("group"),
        ),
        check_vma=False,
    )
```

```python
import functools

import jax
import jax.numpy as jnp
from jax import lax
from jax.experimental import pallas as pl
from jax.experimental.pallas import tpu as pltpu
from jax.sharding import PartitionSpec as P

HEADS = 12
HEAD_DIM = 64
EPSILON = 1e-05
NEGATIVE = -1e30
F32 = jnp.float32
BF16 = jnp.bfloat16
MESH = pl.DeviceIdType.MESH
ANY = pl.BlockSpec(memory_space=pl.ANY)


class Place:
    def __init__(self):
        self.g = lax.axis_index("group")
        self.r = lax.axis_index("replica")
        self.c = self.r % 2
        self.z = self.r // 2
        self.gx = self.g + 1 - 2 * (self.g % 2)
        self.gy = self.g + 2 - 4 * (self.g // 2)
        self.gd = 3 - self.g
        self.rp = self.r + 1 - 2 * self.c


def remote(src, dst, send, recv, device):
    return pltpu.make_async_remote_copy(
        src_ref=src, dst_ref=dst, send_sem=send, recv_sem=recv, device_id=device, device_id_type=MESH
    )


def plane_barrier(place, extra=()):
    barrier = pltpu.get_barrier_semaphore()
    for g in (place.g, place.gx, place.gy, place.gd):
        for r in (place.r, place.rp):
            if g is place.g and r is place.r:
                continue
            pl.semaphore_signal(barrier, inc=1, device_id=(g, r), device_id_type=MESH)
    return barrier


def dot(a, b):
    return jnp.dot(a, b, preferred_element_type=F32)


def norm_parts(values):
    centre = values - jnp.mean(values, axis=-1, keepdims=True)
    spread = jnp.mean(centre * centre, axis=-1, keepdims=True)
    inverse = lax.rsqrt(spread + EPSILON)
    return centre * inverse, inverse


def dot_nt(a, b):
    return lax.dot_general(a, b, (((1,), (1,)), ((), ())), preferred_element_type=F32)


def dot_tn(a, b):
    return lax.dot_general(a, b, (((0,), (0,)), ((), ())), preferred_element_type=F32)


def columns(values):
    return jnp.sum(values, axis=0, keepdims=True)


CHUNKS = 12


SHARED = (2, 3, 5, 7,)
SCHEDULE = {
    ("down", 0): (
        ("first", 0), ("first", 1),
    ),
    ("down", 1): (
        ("plain", 0), ("plain", 1), ("share", 2), ("share", 3),
    ),
    ("down", 2): (
        ("passed", 0),
    ),
    ("normed",): (
        ("passed", 1), ("shared", 2), ("first", 2), ("plain", 2),
    ),
    ("up", 4): (
        ("first", 4), ("plain", 4), ("own", 0), ("shared", 3),
        ("first", 3), ("plain", 3),
    ),
    ("up", 5): (
        ("share", 5), ("own", 1), ("passed", 2),
    ),
    ("up", 6): (
        ("first", 6), ("plain", 6),
    ),
    ("up", 7): (
        ("share", 7), ("passed", 4),
    ),
    ("datt",): (
        ("chain", 0),
    ),
    ("sq", 8): (
        ("first", 8), ("plain", 8), ("passed", 3), ("shared", 5),
        ("first", 5), ("plain", 5),
    ),
    ("a", 0): (
        ("own", 2),
    ),
    ("a", 1): (
        ("chain", 1), ("fin_in", 0), ("passed", 6),
    ),
    ("a", 2): (
        ("own", 4), ("shared", 7), ("first", 7), ("plain", 7),
    ),
    ("a", 3): (
        ("first", 9), ("plain", 9), ("own", 3), ("chain", 2),
        ("fin_in", 1),
    ),
    ("a", 4): (
        ("chain", 4), ("fin_out", 0), ("passed", 5),
    ),
    ("a", 5): (
        ("own", 6), ("passed", 7), ("passed", 8),
    ),
    ("a", 6): (
        ("chain", 3), ("fin_in", 2), ("fin_out", 1),
    ),
    ("a", 7): (
        ("first", 10), ("plain", 10), ("own", 5), ("own", 7),
        ("chain", 6),
    ),
    ("a", 8): (
        ("own", 8), ("fin_in", 3), ("fin_in", 4),
    ),
    ("a", 9): (
        ("chain", 5), ("fin_out", 2), ("passed", 9),
    ),
    ("a", 10): (
        ("fin_in", 6), ("passed", 10), ("chain", 7),
    ),
    ("a", 11): (
        ("first", 11), ("plain", 11), ("own", 9), ("own", 10),
        ("chain", 8),
    ),
    ("end",): (
        ("fin_in", 5), ("fin_out", 3), ("fin_out", 4),
    ),
    ("inp",): (
        ("chain", 9), ("fin_in", 7), ("fin_out", 6), ("passed", 11),
    ),
    ("tail",): (
        ("fin_in", 8), ("gi", 0), ("small_chain", 0), ("chain", 10),
        ("fin_out", 5), ("own", 11), ("small_in", 0), ("fin_in", 9),
        ("fin_out", 7), ("chain", 11), ("fin_in", 10), ("fin_out", 8),
        ("fin_out", 9), ("fin_in", 11), ("fin_out", 10), ("fin_out", 11),
        ("small_out", 0),
    ),
}

GATHER = {
    ("pre",): (
        ("relay", 0), ("x1", 0), ("diagonal", 0), ("own", 1),
        ("jn", 0), ("jf", 0), ("own", 2), ("relay", 1),
    ),
    ("kv",): (
        ("own", 3),
    ),
    ("q",): (
        ("jn", 1), ("relay", 2),
    ),
    ("a", 0): (
        ("diagonal", 1),
    ),
    ("a", 1): (
        ("own", 4),
    ),
    ("a", 4): (
        ("relay", 3), ("jn", 2),
    ),
    ("a", 5): (
        ("jf", 1),
    ),
    ("a", 6): (
        ("diagonal", 2),
    ),
    ("a", 8): (
        ("own", 5),
    ),
    ("a", 10): (
        ("relay", 4), ("jn", 3),
    ),
    ("up",): (
        ("diagonal", 3), ("jf", 2), ("relay", 5), ("g", 0),
        ("jn", 4), ("diagonal", 4), ("jf", 3),
    ),
    ("u", 1): (
        ("diagonal", 5),
    ),
    ("u", 7): (
        ("jn", 5),
    ),
    ("df",): (
        ("jf", 4), ("jf", 5),
    ),
}


GROUPS = 6


def piece_of(W, k, chip, core, first=0, count=3):
    if k < 4:
        lo, hi = ((0, 3), (3, 4), (4, 6), (6, 8))[k]
        return W.at[lo:hi, pl.ds(pl.multiple_of(192 * chip + 96 * core + 32 * first, 16), 32 * count), :]
    start = 384 * (k - 4) + 192 * core + 64 * first
    return W.at[8 + chip, pl.ds(pl.multiple_of(start, 16), 64 * count), :]


def layer_kernel(
    tok, docs_in, og, wq, wk, wv, wo, wup, wdn,
    bq_in, bv_in, bo_in, ga_in, sa_in, bd_in, gf_in, sf_in, bu_in,
    LOo, GIo, To, BTo, Xo, ATo, NLo,
    W, P1, P2, ZR, ACT, GP, DHP, Q, KV, MASK, LSE, R1, R2, G, PF,
    DF, DFP, DB, DBP, DQ, DQP, DKS, DKR, DKF, DKP, LO, ACC, BG, BR, BS, BZ, BT,
    X, AT, NL, SA, SB, PA, PB, DC, DR, LC, D, PK, ZF, RC, bq, bv, bo, ga, sa, bd, gf, sf, bu,
    lsem, vsem, hops, p1r, p2r, zs, zr, zfr, ts, tr, xs_, xr_, los, lor, gis, gir, b1s, b1r, osem,
    ags, agr, xs, xr, ds_, dr, ps, pr, gs, gr, kvs, kvr, lls, llr,
):
    DATT, LO2 = G, NL
    me = Place()
    g, r, c, z = me.g, me.r, me.c, me.z
    gx, gy, gd, rp = me.gx, me.gy, me.gd, me.rp
    outer = (z == 0) | (z == 3)
    inner = jnp.logical_not(outer)
    zin, zout, zother = 1 + z // 3, 3 * (z - 1), 3 - z
    zp = z % 2
    rz = r + 2 - 4 * zp

    def zdev(zz):
        return (g, 2 * zz + c)

    barrier = plane_barrier(me)
    pl.semaphore_signal(barrier, inc=1, device_id=(g, rz), device_id_type=MESH)

    @pl.when(inner)
    def _():
        pl.semaphore_signal(barrier, inc=1, device_id=zdev(zother), device_id_type=MESH)

    vectors = []
    for i, (src, dst) in enumerate((
        (bq_in, bq), (bv_in, bv), (bo_in, bo), (ga_in, ga), (sa_in, sa), (bd_in, bd), (gf_in, gf), (sf_in, sf), (bu_in, bu),
    )):
        vectors.append(pltpu.make_async_copy(src, dst, vsem.at[i]))
        vectors[-1].start()

    local = []
    for w, ref in enumerate((wq, wk, wv, wo)):
        local.append((ref, W.at[w, pl.ds(pl.multiple_of(192 * g, 16), 192), :]))
    for u in range(4):
        local.append((wup.at[:, 768 * u : 768 * u + 768], W.at[4 + u, pl.ds(pl.multiple_of(192 * g, 16), 192), :]))
    local.append((wdn, W.at[8 + g]))
    local = [pltpu.make_async_copy(a, b, lsem.at[i]) for i, (a, b) in enumerate(local)]
    for copy in local:
        copy.start()

    own_lane = lax.broadcasted_iota(jnp.int32, (1, 768), 1) // 192 == g
    for copy in vectors:
        copy.wait()
    for row, ref in ((0, bq), (2, bv), (3, bo), (4, ga), (5, sa), (6, bd), (7, gf), (8, sf)):
        piece = ref[...].astype(F32).reshape(1, 192)
        PF[row : row + 1, :] = jnp.where(own_lane, jnp.concatenate([piece] * 4, axis=1), 0.0)
    for row in (1, 9, 10, 11):
        PF[row : row + 1, :] = jnp.zeros((1, 768), F32)
    tall = lax.broadcasted_iota(jnp.int32, (4, 768), 0) == g
    PF[12:16, :] = jnp.where(tall, bu[...].astype(F32).reshape(1, 768), 0.0)
    PK[g] = PF[...].astype(BF16)

    BG[...] = jnp.zeros_like(BG)
    pl.semaphore_wait(barrier, 9 - z // 3 - (3 - z) // 3)

    def reshard(src, dst_of, ssem, rsem, blocks=(0, 1)):
        for m in blocks:
            t, e = 2 * c + m, g // 2
            b = g % 2
            here = (t == g) & (e == c)
            src_m = src.at[m]
            dst_b = dst_of(b)

            @pl.when(jnp.logical_not(here))
            def _():
                remote(src_m, dst_b, ssem.at[m], rsem.at[b], (t, 2 * z + e)).start()

            @pl.when(here)
            def _():
                pltpu.make_async_copy(src_m, dst_b, rsem.at[b]).start()

    def reshard_wait(src, dst_of, ssem, rsem, b):
        remote(src.at[0], dst_of(b), ssem.at[0], rsem.at[b], (g, r)).wait_recv()

    def reshard_drain(src, dst_of, ssem, rsem):
        for m in range(2):
            t, e = 2 * c + m, g // 2
            here = (t == g) & (e == c)

            @pl.when(jnp.logical_not(here))
            def _():
                remote(src.at[m], dst_of(0), ssem.at[m], rsem.at[0], (t, 2 * z + e)).wait_send()

    def x_rows(b):
        if isinstance(b, int):
            return X.at[256 * b : 256 * b + 256, :]
        return X.at[pl.ds(pl.multiple_of(256 * b, 256), 256), :]

    def g_rows(b):
        if isinstance(b, int):
            return G.at[256 * b : 256 * b + 256, :]
        return G.at[pl.ds(pl.multiple_of(256 * b, 256), 256), :]

    for m in range(2):
        for e in range(2):
            t = 2 * c + m
            here = (t == g) & (c == e)

            @pl.when(jnp.logical_not(here))
            def _():
                remote(docs_in, D.at[g], ds_.at[2 * m + e], dr.at[0], (t, 2 * z + e)).start()

            @pl.when(here)
            def _():
                pltpu.make_async_copy(docs_in, D.at[g], dr.at[0]).start()

    def pass_on(k, slot, part, device):
        remote(part, part, ags.at[k], agr.at[k, slot], device).start()

    def landed(k, slot, count):
        rows = 32 * count
        size = W.at[0:3, 0:rows, :] if k == 0 else W.at[0:1, 0:rows, :] if k == 1 else W.at[0:2, 0:rows, :]
        remote(size, size, ags.at[k], agr.at[k, slot], (g, rp)).wait_recv()

    def own_send(k):
        part = piece_of(W, k, g, c, zp, 2)
        pass_on(k, 0, part, (gx, r))
        pass_on(k, 0, part, (gy, r))

    def relay(k):
        landed(k, 0, 4)
        pass_on(k, 1, piece_of(W, k, gx, c, zp, 1), (gy, r))
        pass_on(k, 1, piece_of(W, k, gy, c, zp + 1, 1), (gx, r))
        pass_on(k, 2, piece_of(W, k, gx, c, 2 * zp, 1), (g, rz))
        pass_on(k, 2, piece_of(W, k, gy, c, 2 * zp, 1), (g, rz))

    def diagonal(k):
        landed(k, 1, 2)
        pass_on(k, 3, piece_of(W, k, gd, c, 2 * zp, 1), (g, rz))

    def join_near(k):
        landed(k, 2, 2)
        for chip in (gx, gy):
            pass_on(k, 4, piece_of(W, k, chip, c), (g, rp))

    def join_far(k):
        landed(k, 3, 1)
        pass_on(k, 5, piece_of(W, k, gd, c), (g, rp))

    def complete_near(k):
        landed(k, 4, 6)

    def complete_far(k):
        landed(k, 5, 3)

    def complete(k):
        complete_near(k)
        complete_far(k)

    def gather_serve(*slot):
        for name, k in GATHER.get(slot, ()):
            gather_services[name](k)

    gather_services = {
        "own": own_send, "relay": relay, "diagonal": diagonal, "jn": join_near, "jf": join_far,
        "x1": lambda k: reshard(tok, x_rows, xs, xr, (1,)), "g": lambda k: reshard(og, g_rows, gs, gr),
    }

    def gather_drain(k):
        rows = 32 * 18
        size = W.at[0:3, 0:rows, :] if k == 0 else W.at[0:1, 0:rows, :] if k == 1 else W.at[0:2, 0:rows, :]
        remote(size, size, ags.at[k], agr.at[k, 0], (g, rp)).wait_send()

    for slot, chip in enumerate((gx, gy, gd)):
        remote(PK.at[g], PK.at[g], ps.at[0], pr.at[0], (chip, r)).start()
    for i in range(3):
        local[i].wait()
    own_send(0)
    reshard(tok, x_rows, xs, xr, (0,))
    for i in range(3, 9):
        local[i].wait()

    remote(PK.at[0:3], PK.at[0:3], ps.at[0], pr.at[0], (gx, r)).wait_recv()
    PF[...] = PK[0].astype(F32) + PK[1].astype(F32) + PK[2].astype(F32) + PK[3].astype(F32)
    remote(D, D, ds_.at[0], dr.at[0], (g, r)).wait_recv()
    for b in range(2):
        row = jnp.broadcast_to(D[2 * c + b, pl.ds(g % 2, 1), :].astype(F32), (128, 256))
        DC[256 * b : 256 * b + 256, :] = row.T
    for i in range(4):
        DR[:, 256 * i : 256 * i + 256] = jnp.broadcast_to(D[i, pl.ds(g % 2, 1), :].astype(F32), (8, 256))
    for i in range(4):
        keys = jnp.broadcast_to(D[i, pl.ds(g % 2, 1), :].astype(F32), (8, 256)).T[:, 0:1]
        for b in range(2):
            rows = D[2 * c + b, pl.ds(g % 2, 1), :].astype(F32)
            MASK[256 * i : 256 * i + 256, 256 * b : 256 * b + 256] = jnp.where(keys == rows, 0.0, NEGATIVE)
    gather_serve("pre")
    for b in range(2):
        reshard_wait(tok, x_rows, xs, xr, b)
    remote(X, Xo, lls.at[0], llr.at[0], (g, rp)).start()
    complete(0)
    own_rows = pl.ds(pl.multiple_of(512 * c, 512), 512)
    their_rows = pl.ds(pl.multiple_of(512 * (1 - c), 512), 512)

    def project(w, t, dst):
        cols = pl.ds(pl.multiple_of(256 * t, 256), 256)
        out = dot(X[...], W[w, :, cols]) + PF[pl.ds(w, 1), cols]
        return cols, out.astype(BF16)

    @pl.loop(0, 6)
    def _(i):
        w = i // 3
        cols, out = project(1 + w, i % 3, None)
        KV[w, own_rows, cols] = out

    for w in range(2):
        piece = KV.at[w, own_rows, :]
        remote(piece, piece, kvs.at[0], kvr.at[0], (g, rp)).start()
    gather_serve("kv")

    @pl.loop(0, 3)
    def _(i):
        cols, out = project(0, i, None)
        Q[:, cols] = out

    gather_serve("q")
    part = KV.at[:, their_rows, :]
    remote(part, part, kvs.at[0], kvr.at[0], (g, rp)).wait_recv()

    def at_step(i):
        pair, b = i // 2, i % 2
        return pair, pl.ds(pl.multiple_of(128 * pair, 128), 128), pl.ds(pl.multiple_of(256 * b, 256), 256)

    left_lanes = lax.broadcasted_iota(jnp.int32, (256, 128), 1) < 64

    def score(i, hh, S, peaks):
        pair, lanes, rows = at_step(i)
        q = Q[rows, lanes].astype(F32) * (HEAD_DIM ** -0.5)
        qh = jnp.where(left_lanes if hh == 0 else jnp.logical_not(left_lanes), q, 0.0).astype(BF16)
        s = dot_nt(qh, KV[0, :, lanes])
        s = jnp.where(DC[rows, 0:1] == DR[0:1, :], s, NEGATIVE)
        S[...] = s
        peaks[...] = jnp.broadcast_to(jnp.max(s, axis=1, keepdims=True), (256, 128))

    def soften(i, hh, S, peaks, vp):
        pair, lanes, rows = at_step(i)
        peak = peaks[...]
        e = jnp.exp(S[...] - peak[:, 0:1])
        total = jnp.sum(e, axis=1, keepdims=True)
        lane = lax.broadcasted_iota(jnp.int32, (256, 128), 1)
        LC[rows, :] = jnp.where(lane == 2 * pair + hh, peak + jnp.log(total), LC[rows, :])
        return dot(e.astype(BF16), vp) / total

    LC[...] = jnp.zeros_like(LC)
    score(0, 0, SA, PA)

    @pl.loop(0, 12)
    def _(i):
        pair, lanes, rows = at_step(i)
        vp = KV[1, :, lanes]
        score(i, 1, SB, PB)
        out0 = soften(i, 0, SA, PA, vp)
        score((i + 1) % 12, 0, SA, PA)
        out1 = soften(i, 1, SB, PB, vp)
        AT[rows, lanes] = jnp.where(left_lanes, out0, out1).astype(BF16)

        for k in range(12):
            if ("a", k) in GATHER:
                @pl.when(i == k)
                def _():
                    gather_serve("a", k)

    LSE[...] = LC[...].T[0:16, :]
    remote(AT, ATo, lls.at[1], llr.at[1], (g, rp)).start()
    gather_serve("out")
    complete(1)

    @pl.loop(0, 2)
    def _(i):
        rows = pl.ds(pl.multiple_of(256 * i, 256), 256)
        first = X[rows, :].astype(F32) + dot(AT[rows, :], W[3]) + PF[3:4, :]
        R1[rows, :] = first
        shape, _ = norm_parts(first)
        normed = shape * PF[4:5, :] + PF[5:6, :]
        R2[rows, :] = normed + PF[6:7, :]
        NL[rows, :] = normed.astype(BF16)

    remote(NL, NLo, lls.at[2], llr.at[2], (g, rp)).start()
    gather_serve("up")
    complete(2)
    complete(3)

    def up(t):
        u, tt = t // 3, t % 3
        cols = pl.ds(pl.multiple_of(256 * tt, 256), 256)
        wide = pl.ds(pl.multiple_of(256 * t, 256), 256)
        h = dot(NL[...], W[4 + u, :, cols]) + PF[pl.ds(12 + u, 1), cols]
        cdf = 0.5 * (1.0 + lax.erf(h * (0.5 ** 0.5)))
        ACT[c, :, wide] = (h * cdf).astype(BF16)
        GP[:, wide] = (cdf + h * jnp.exp(-0.5 * h * h) * 0.3989422804014327).astype(BF16)

    @pl.loop(0, 12)
    def _(t):
        up(t)

        for k in range(12):
            if ("u", k) in GATHER:
                @pl.when(t == k)
                def _():
                    gather_serve("u", k)

    remote(ACT.at[c], ACT.at[c], lls.at[3], llr.at[3], (g, rp)).start()

    def down(k):
        deep = pl.ds(pl.multiple_of(768 * k, 256), 768)

        @pl.loop(0, 3)
        def _(tt):
            cols = pl.ds(pl.multiple_of(256 * tt, 256), 256)
            R2[:, cols] += dot(ACT[c, :, deep], W[8 + k, :, cols])

    down(g)
    gather_serve("dn")
    complete_near(4)
    complete_near(5)
    down(gx)
    down(gy)
    gather_serve("df")
    complete_far(4)
    complete_far(5)
    down(gd)
    gather_serve("G")

    def forward_drain():
        reshard_drain(tok, x_rows, xs, xr)
        reshard_drain(og, g_rows, gs, gr)
        for m in range(2):
            for e in range(2):
                t = 2 * c + m
                here = (t == g) & (c == e)

                @pl.when(jnp.logical_not(here))
                def _():
                    remote(docs_in, D.at[g], ds_.at[2 * m + e], dr.at[0], (t, 2 * z + e)).wait_send()
        remote(PK.at[0:3], PK.at[0:3], ps.at[0], pr.at[0], (gx, r)).wait_send()
        part = KV.at[:, own_rows, :]
        remote(part, part, kvs.at[0], kvr.at[0], (g, rp)).wait_send()
        for i, (src, dst) in enumerate(((X, Xo), (AT, ATo), (NL, NLo), (ACT.at[c], ACT.at[c]))):
            remote(src, dst, lls.at[i], llr.at[i], (g, rp)).wait_send()

    loads = {}

    def load(name, slot, dst):
        src = {"x": Xo, "att": ATo, "nl": NLo}[name]
        remote(src, src, lls.at[slot], llr.at[slot], (g, rp)).wait_recv()
        copy = pltpu.make_async_copy(src, dst, lsem.at[9 + slot])
        copy.start()
        loads[name] = copy

    def grad(j, q, part=None):
        start, size = 0, 192
        if part is not None:
            start, size = 96 * part, 96
        if j < 4:
            return W.at[8 + q // 2, pl.ds(192 * j + start, size), pl.ds(pl.multiple_of(384 * (q % 2), 128), 384)]
        rows = pl.ds(pl.multiple_of(192 * q + start, 16), size)
        if j < 8:
            return W.at[10 + (j - 4) // 2, rows, 384 * (j % 2) : 384 * (j % 2) + 384]
        return W.at[4 + (j - 8) // 2, rows, 384 * (j % 2) : 384 * (j % 2) + 384]

    def parts_of(j):
        if j in SHARED:
            return ((64 * zp, 64), (64 * zp + 64, 64))
        return ((0, 96), (96, 96))

    def rows_of(ref, start, size):
        return ref.at[pl.ds(pl.multiple_of(start, 16), size)]

    def grad(j, q, start=0, size=192):
        if j < 4:
            return W.at[
                8 + q // 2, pl.ds(pl.multiple_of(192 * j + start, 16), size), pl.ds(pl.multiple_of(384 * (q % 2), 128), 384)
            ]
        rows = pl.ds(pl.multiple_of(192 * q + start, 16), size)
        if j < 8:
            return W.at[10 + (j - 4) // 2, rows, 384 * (j % 2) : 384 * (j % 2) + 384]
        return W.at[4 + (j - 8) // 2, rows, 384 * (j % 2) : 384 * (j % 2) + 384]

    def share(j):
        for slot, q in enumerate((gx, gy, gd)):
            remote(
                grad(j, q, 128 - 128 * zp, 64), ZF.at[SHARED.index(j), slot], hops.at[j], zfr.at[SHARED.index(j)], (g, rz)
            ).start()

    def shared(j):
        k = SHARED.index(j)
        remote(ZF.at[k], ZF.at[k], hops.at[j], zfr.at[k], (g, rz)).wait_recv()
        for slot, q in enumerate((gx, gy, gd)):
            mine = grad(j, q, 128 * zp, 64)
            mine[...] = (mine[...].astype(F32) + ZF[k, slot].astype(F32)).astype(BF16)

    def first(j):
        for side, (chip, (start, size)) in enumerate(zip((gy, gx), parts_of(j))):
            remote(grad(j, gd, start, size), P1.at[j, side, 0:size], hops.at[j], p1r.at[j], (chip, r)).start()

    def plain(j):
        (first_a, size), (first_b, _) = parts_of(j)
        remote(grad(j, gx, first_b, size), rows_of(P2.at[j, 0], first_b, size), hops.at[j], p2r.at[j], (gx, r)).start()
        remote(grad(j, gy, first_a, size), rows_of(P2.at[j, 1], first_a, size), hops.at[j], p2r.at[j], (gy, r)).start()

    def passed(j):
        size = parts_of(j)[0][1]
        both = P1.at[j, :, 0:size]
        remote(both, both, hops.at[j], p1r.at[j], (gx, r)).wait_recv()
        for side, chip in enumerate((gx, gy)):
            start = parts_of(j)[side][0]
            mine = grad(j, chip, start, size)
            mine[...] = (mine[...].astype(F32) + P1[j, side, 0:size].astype(F32)).astype(BF16)
            remote(mine, rows_of(P2.at[j, side], start, size), hops.at[j], p2r.at[j], (chip, r)).start()

    def own(j):
        start, size = parts_of(j)[0][0], 2 * parts_of(j)[0][1]
        both = P2.at[j, :, 0:size]
        remote(both, both, hops.at[j], p2r.at[j], (gx, r)).wait_recv()
        moved = pl.ds(pl.multiple_of(start, 16), size)
        arrived = P2[j, 0, moved].astype(F32) + P2[j, 1, moved].astype(F32)
        P2[j, 0, moved] = (grad(j, g, start, size)[...].astype(F32) + arrived).astype(BF16)
        if j in SHARED:
            P2[j, 0, pl.ds(pl.multiple_of(128 - 128 * zp, 16), 64)] = grad(j, g, 128 - 128 * zp, 64)[...]

        @pl.when(outer)
        def _():
            remote(P2.at[j, 0], ZR.at[j, 0], zs.at[j], zr.at[j, 0], zdev(zin)).start()

    def chain(j):
        @pl.when(inner)
        def _():
            remote(P2.at[j, 0], ZR.at[j, 0], zs.at[j], zr.at[j, 0], zdev(zother)).wait_recv()
            P2[j, 0] = (P2[j, 0].astype(F32) + ZR[j, 0].astype(F32)).astype(BF16)
            remote(P2.at[j, 0], ZR.at[j, 1], zs.at[j], zr.at[j, 1], zdev(zother)).start()

    def hand_over(j):
        remote(P2.at[j, 1], To.at[c, j], ts.at[0], tr.at[0], (g, rp)).start()
        pltpu.make_async_copy(P2.at[j, 1], To.at[c, j], osem.at[0]).start()

    def fin_in(j):
        @pl.when(inner)
        def _():
            remote(P2.at[j, 0], ZR.at[j, 1], zs.at[j], zr.at[j, 1], zdev(zother)).wait_recv()
            P2[j, 1] = (P2[j, 0].astype(F32) + ZR[j, 1].astype(F32)).astype(BF16)
            remote(P2.at[j, 1], ZR.at[j, 0], zs.at[j], zr.at[j, 0], zdev(zout)).start()
            hand_over(j)

    def fin_out(j):
        @pl.when(outer)
        def _():
            remote(P2.at[j, 1], ZR.at[j, 0], zs.at[j], zr.at[j, 0], zdev(zin)).wait_recv()
            P2[j, 1] = ZR[j, 0]
            hand_over(j)

    def drain(j):
        total = W.at[0, 0:576, 0:384]
        remote(total, total, hops.at[j], p1r.at[j], (gx, r)).wait_send()

        @pl.when(inner)
        def _():
            remote(ZR.at[j], ZR.at[j], zs.at[j], zr.at[j, 0], zdev(zother)).wait_send()

        @pl.when(outer)
        def _():
            remote(ZR.at[j, 0], ZR.at[j, 0], zs.at[j], zr.at[j, 0], zdev(zother)).wait_send()

    def serve(*slot):
        for name, j in SCHEDULE.get(slot, ()):
            services[name](j)

    def give_back(src, out, ssem, rsem):
        for b in range(2):
            t, e = 2 * c + b, g // 2
            here = (t == g) & (e == c)
            src_b = src.at[256 * b : 256 * b + 256, :]
            dst = out.at[g % 2]

            @pl.when(jnp.logical_not(here))
            def _():
                remote(src_b, dst, ssem.at[b], rsem.at[g % 2], (t, 2 * z + e)).start()

            @pl.when(here)
            def _():
                pltpu.make_async_copy(src_b, dst, rsem.at[g % 2]).start()

    def give_back_drain(src, out, ssem, rsem):
        for b in range(2):
            t, e = 2 * c + b, g // 2
            here = (t == g) & (e == c)
            src_b = src.at[256 * b : 256 * b + 256, :]

            @pl.when(jnp.logical_not(here))
            def _():
                remote(src_b, out.at[0], ssem.at[b], rsem.at[0], (t, 2 * z + e)).wait_send()

            remote(src_b, out.at[b], ssem.at[b], rsem.at[b], (g, rp)).wait_recv()

    services = {
        "passed": passed, "own": own, "chain": chain, "fin_in": fin_in, "fin_out": fin_out,
        "share": share, "shared": shared, "first": first, "plain": plain,
        "gi": lambda j: give_back(LO2, GIo, gis, gir),
    }

    def exchange(slot, src, dst):
        remote(src, dst, xs_.at[slot], xr_.at[slot], (g, rp)).start()

    def exchanged(slot, dst):
        remote(dst, dst, xs_.at[slot], xr_.at[slot], (g, rp)).wait_recv()

    def exchange_drain(slot, dst):
        remote(dst, dst, xs_.at[slot], xr_.at[slot], (g, rp)).wait_send()

    mine384 = pl.ds(pl.multiple_of(384 * c, 128), 384)
    theirs384 = pl.ds(pl.multiple_of(384 * (1 - c), 128), 384)

    def norm_back(values, gain, grad_out):
        shape, inverse = norm_parts(values)
        pulled = grad_out * gain
        d = inverse * (
            pulled
            - jnp.mean(pulled, axis=-1, keepdims=True)
            - shape * jnp.mean(pulled * shape, axis=-1, keepdims=True)
        )
        return shape, d

    for b in range(2):
        reshard_wait(og, g_rows, gs, gr, b)

    @pl.loop(0, 4)
    def _(i):
        rows = pl.ds(pl.multiple_of(128 * i, 128), 128)
        up = G[rows, :].astype(F32)
        shape, d = norm_back(R2[rows, :], PF[7:8, :], up)
        LO[rows, :] = (shape * PF[7:8, :] + PF[8:9, :]).astype(BF16)
        R2[rows, :] = d
        low = d.astype(BF16)
        DF[rows, :] = low
        BG[7:8, :] += columns(up * shape)
        BG[8:9, :] += columns(up)
        BG[6:7, :] += columns(low.astype(F32))

    exchange(0, DF.at[:, theirs384], DFP)
    give_back(LO, LOo, los, lor)

    def d_hidden(i):
        t = (i + 6 * (1 - c)) % 12
        tt = t % 3
        wide = pl.ds(pl.multiple_of(256 * t, 256), 256)
        back = dot_nt(DF[...], W[8 + t // 3, pl.ds(pl.multiple_of(256 * tt, 256), 256), :])
        low = (back * GP[:, wide].astype(F32)).astype(BF16)
        GP[:, wide] = low
        BG[pl.ds(12 + t // 3, 1), pl.ds(pl.multiple_of(256 * tt, 256), 256)] = columns(low.astype(F32))

    @pl.loop(0, 6)
    def _(i):
        d_hidden(i)

    exchange(1, GP.at[:, pl.ds(pl.multiple_of(1536 * (1 - c), 128), 1536)], DHP)

    @pl.loop(6, 12)
    def _(i):
        d_hidden(i)

    remote(ACT.at[1 - c], ACT.at[1 - c], lls.at[3], llr.at[3], (g, rp)).wait_recv()
    forward_drain()
    for k in range(GROUPS):
        gather_drain(k)
    exchanged(0, DFP)

    def pair_tn(own_left, their_left, own_right, their_right):
        return dot_tn(own_left, own_right) + dot_tn(their_left, their_right)

    def down_quarter(q):
        @pl.loop(0, 3)
        def _(i):
            lanes = pl.ds(pl.multiple_of(768 * q + 256 * i, 256), 256)
            out = pair_tn(ACT[c, :, lanes], ACT[1 - c, :, lanes], DF[:, mine384], DFP[...])
            W[8 + q // 2, pl.ds(pl.multiple_of(256 * i, 256), 256), pl.ds(pl.multiple_of(384 * (q % 2), 128), 384)] = (
                out.astype(BF16)
            )

    down_quarter(gd)
    serve("down", 0)
    down_quarter(gx)
    down_quarter(gy)
    serve("down", 1)
    down_quarter(g)
    serve("down", 2)
    load("nl", 2, ACT.at[0, :, 0:768])
    load("att", 1, ACT.at[0, :, 768:1536])
    load("x", 0, ACT.at[0, :, 1536:2304])

    @pl.loop(0, 3)
    def _(i):
        cols = pl.ds(pl.multiple_of(256 * i, 256), 256)
        total = R2[:, cols]
        for u in range(4):
            total = total + dot_nt(GP[:, 768 * u : 768 * u + 768], W[4 + u, cols, :])
        R2[:, cols] = total

    serve("normed")

    @pl.loop(0, 4)
    def _(i):
        rows = pl.ds(pl.multiple_of(128 * i, 128), 128)
        up = R2[rows, :]
        shape, d = norm_back(R1[rows, :], PF[4:5, :], up)
        R2[rows, :] = d
        low = d.astype(BF16)
        DB[rows, :] = low
        BG[4:5, :] += columns(up * shape)
        BG[5:6, :] += columns(up)
        BG[3:4, :] += columns(low.astype(F32))

    exchange(2, DB.at[:, theirs384], DBP)
    serve("ln1")
    exchanged(1, DHP)
    loads["nl"].wait()

    for j in range(4, 8):
        jj = j - 4
        own_cols = pl.ds(pl.multiple_of(1536 * c + 384 * jj, 128), 384)

        @pl.loop(0, 3)
        def _(i):
            lanes = pl.ds(pl.multiple_of(256 * i, 256), 256)
            out = pair_tn(NL[:, lanes], ACT[0, :, lanes], GP[:, own_cols], DHP[:, 384 * jj : 384 * jj + 384])
            W[10 + jj // 2, lanes, 384 * (jj % 2) : 384 * (jj % 2) + 384] = out.astype(BF16)

        serve("up", j)

    @pl.loop(0, 3)
    def _(i):
        cols = pl.ds(pl.multiple_of(256 * i, 256), 256)
        DATT[:, cols] = dot_nt(DB[...], W[3, cols, :]).astype(BF16)

    serve("datt")
    exchanged(2, DBP)
    loads["att"].wait()

    def square_grad(j, offset, own_left, own_right, their_right):
        @pl.loop(0, 3)
        def _(i):
            lanes = pl.ds(pl.multiple_of(offset + 256 * i, 256), 256)
            cols = pl.ds(pl.multiple_of(256 * i, 256), 256)
            out = pair_tn(own_left[:, cols], ACT[0, :, lanes], own_right[...], their_right[...])
            W[4 + (j - 8) // 2, cols, 384 * (j % 2) : 384 * (j % 2) + 384] = (
                out.astype(BF16)
            )

    square_grad(8, 768, AT, DB.at[:, mine384], DBP)
    serve("sq", 8)

    loads["x"].wait()

    @pl.loop(0, 12)
    def _(i):
        turn, ours, b = i // 4, (i // 2) % 2, i % 2
        pair = turn + 3 * (c * ours + (1 - c) * (1 - ours))
        lanes = pl.ds(pl.multiple_of(128 * pair, 128), 128)
        half_lanes = pl.ds(pl.multiple_of(128 * turn, 128), 128)
        cols = pl.ds(pl.multiple_of(256 * b, 256), 256)
        qs = Q[cols, lanes].astype(F32) * (HEAD_DIM ** -0.5)
        do = DATT[cols, lanes].astype(F32)
        qt, dot_t = qs.T, do.T
        kp = KV[0, :, lanes]
        vp = KV[1, :, lanes]
        kt = kp.astype(F32).T.astype(BF16)
        weigh = (do * AT[cols, lanes].astype(F32)).T
        top = lax.broadcasted_iota(jnp.int32, (128, 256), 0) < 64
        left = lax.broadcasted_iota(jnp.int32, (256, 128), 1) < 64
        dk = dv = None
        pieces = []
        for hh in range(2):
            rows_in = top if hh == 0 else jnp.logical_not(top)
            lanes_in = left if hh == 0 else jnp.logical_not(left)
            s = dot(kp, jnp.where(rows_in, qt, 0.0).astype(BF16)) + MASK[:, cols]
            p = jnp.exp(s - LSE[pl.ds(2 * pair + hh, 1), cols])
            dp = dot(vp, jnp.where(rows_in, dot_t, 0.0).astype(BF16))
            ds = (p * (dp - columns(weigh[64 * hh : 64 * hh + 64, :]))).astype(BF16)
            dv_h = dot(p.astype(BF16), jnp.where(lanes_in, do, 0.0).astype(BF16))
            dk_h = dot(ds, jnp.where(lanes_in, qs, 0.0).astype(BF16))
            dv = dv_h if dv is None else dv + dv_h
            dk = dk_h if dk is None else dk + dk_h
            pieces.append(dot(kt[64 * hh : 64 * hh + 64, :], ds))
        DQ[cols, lanes] = (jnp.concatenate(pieces, axis=0).T * (HEAD_DIM ** -0.5)).astype(BF16)

        @pl.when(b == 0)
        def _():
            ACC[0] = dk
            ACC[1] = dv

        @pl.when((b == 1) & (ours == 0))
        def _():
            DKS[0, :, half_lanes] = (ACC[0] + dk).astype(BF16)
            DKS[1, :, half_lanes] = (ACC[1] + dv).astype(BF16)
            exchange(3 + turn, DKS.at[:, :, half_lanes], DKR.at[:, :, half_lanes])
            exchange(6 + turn, DQ.at[:, lanes], DQP.at[:, half_lanes])

        @pl.when((b == 1) & (ours == 1))
        def _():
            exchanged(3 + turn, DKR.at[:, :, half_lanes])
            DKF[0, :, half_lanes] = (ACC[0] + dk + DKR[0, :, half_lanes].astype(F32)).astype(BF16)
            DKF[1, :, half_lanes] = (ACC[1] + dv + DKR[1, :, half_lanes].astype(F32)).astype(BF16)
            exchange(9 + turn, DKF.at[:, their_rows, half_lanes], DKP.at[:, :, half_lanes])
            exchanged(6 + turn, DQP.at[:, half_lanes])
            RC[0, :, 0:128] = DQ[:, lanes]
            RC[1, :, 0:128] = DQP[:, half_lanes]
            for w in range(2):
                RC[0, :, 128 + 128 * w : 256 + 128 * w] = DKF[w, own_rows, half_lanes]
                RC[1, :, 128 + 128 * w : 256 + 128 * w] = DKF[w, their_rows, half_lanes]

            @pl.loop(0, 3)
            def _(t):
                tile = pl.ds(pl.multiple_of(256 * t, 256), 256)
                theirs = pl.ds(pl.multiple_of(1536 + 256 * t, 256), 256)
                out = pair_tn(X[:, tile], ACT[0, :, theirs], RC[0], RC[1])
                W[4 + (1 + turn) // 2, tile, pl.ds(pl.multiple_of(384 * ((1 + turn) % 2), 128), 384)] = out.astype(BF16)

        for k in range(12):
            if ("a", k) in SCHEDULE:
                @pl.when(i == k)
                def _():
                    serve("a", k)

    BG[0:1, :] = columns(DQ[...].astype(F32))
    BG[2:3, mine384] = columns(DKF[1].astype(F32))

    BS[...] = BG[...].astype(BF16)
    others = [(gg, rr, k) for k, (gg, rr) in enumerate(
        ((g, rp), (gx, r), (gx, rp), (gy, r), (gy, rp), (gd, r), (gd, rp)))]
    slot_of = 2 * g + c
    for gg, rr, k in others:
        remote(BS, BR.at[slot_of], b1s.at[0], b1r.at[0], (gg, rr)).start()
    BR[slot_of] = BS[...]

    serve("end")

    for k in range(3):
        exchanged(9 + k, DKP.at[:, :, 128 * k : 128 * k + 128])

    @pl.loop(0, 3)
    def _(i):
        cols = pl.ds(pl.multiple_of(256 * i, 256), 256)
        total = R2[:, cols] + dot_nt(DQ[...], W[0, cols, :])
        for w in range(2):
            total = total + dot_nt(DKF[w, own_rows, :], W[1 + w, cols, mine384])
            total = total + dot_nt(DKP[w], W[1 + w, cols, theirs384])
        LO2[:, cols] = total.astype(BF16)

    serve("inp")
    remote(BR.at[0:7], BR.at[0:7], b1s.at[0], b1r.at[0], (g, rp)).wait_recv()
    total = BR[0].astype(F32)
    for k in range(1, 8):
        total = total + BR[k].astype(F32)
    BZ[0] = total.astype(BF16)

    @pl.when(outer)
    def _():
        remote(BZ.at[0], BZ.at[1], b1s.at[1], b1r.at[1], zdev(zin)).start()

    def small_chain():
        @pl.when(inner)
        def _():
            remote(BZ.at[1], BZ.at[1], b1s.at[1], b1r.at[1], zdev(zother)).wait_recv()
            BZ[2] = (BZ[0].astype(F32) + BZ[1].astype(F32)).astype(BF16)
            remote(BZ.at[2], BZ.at[3], b1s.at[1], b1r.at[2], zdev(zother)).start()

    def small_in():
        @pl.when(inner)
        def _():
            remote(BZ.at[3], BZ.at[3], b1s.at[1], b1r.at[2], zdev(zother)).wait_recv()
            BZ[4] = (BZ[2].astype(F32) + BZ[3].astype(F32)).astype(BF16)
            remote(BZ.at[4], BZ.at[1], b1s.at[2], b1r.at[1], zdev(zout)).start()

    def small_out():
        @pl.when(outer)
        def _():
            remote(BZ.at[1], BZ.at[1], b1s.at[1], b1r.at[1], zdev(zin)).wait_recv()
            BZ[4] = BZ[1]

    services.update(
        small_chain=lambda j: small_chain(), small_in=lambda j: small_in(), small_out=lambda j: small_out()
    )
    serve("tail")
    BT[...] = BZ[4].astype(F32)
    bt_copy = pltpu.make_async_copy(BT, BTo, osem.at[1])
    bt_copy.start()

    for j in range(CHUNKS):
        drain(j)
    halves = remote(To.at[c], To.at[1 - c], ts.at[0], tr.at[0], (g, rp))
    halves.wait_send()
    halves.wait_recv()
    pltpu.make_async_copy(To.at[c], To.at[c], osem.at[0]).wait()
    for slot, dst in ((0, DFP), (1, DHP), (2, DBP)):
        exchange_drain(slot, dst)
    for k in range(3):
        part = slice(128 * k, 128 * k + 128)
        exchange_drain(3 + k, DKR.at[:, :, part])
        exchange_drain(6 + k, DQP.at[:, part])
        exchange_drain(9 + k, DKP.at[:, :, part])
    give_back_drain(LO, LOo, los, lor)
    give_back_drain(LO2, GIo, gis, gir)
    remote(BR.at[0:7], BR.at[0:7], b1s.at[0], b1r.at[0], (g, rp)).wait_send()
    remote(BZ.at[0], BZ.at[0], b1s.at[1], b1r.at[1], zdev(zother)).wait_send()

    @pl.when(inner)
    def _():
        remote(BZ.at[0], BZ.at[0], b1s.at[2], b1r.at[1], zdev(zother)).wait_send()

    bt_copy.wait()


def sds(shape, dtype=BF16):
    return jax.ShapeDtypeStruct(shape, dtype)


def layer(*args):
    out = [
        sds((2, 256, 768)), sds((2, 256, 768)), sds((2, CHUNKS, 192, 384)), sds((16, 768), F32),
        sds((512, 768)), sds((512, 768)), sds((512, 768)),
    ]
    dma = pltpu.SemaphoreType.DMA
    v = pltpu.VMEM
    return pl.pallas_call(
        layer_kernel,
        out_shape=out,
        in_specs=[ANY] * 18,
        out_specs=[ANY] * len(out),
        scratch_shapes=[
            v((12, 768, 768), BF16), v((CHUNKS, 2, 96, 384), BF16), v((CHUNKS, 2, 192, 384), BF16),
            v((CHUNKS, 2, 192, 384), BF16),
            v((2, 512, 3072), BF16), v((512, 3072), BF16), v((512, 1536), BF16), v((512, 768), BF16),
            v((2, 1024, 768), BF16), v((1024, 512), F32), v((16, 512), F32),
            v((512, 768), F32), v((512, 768), F32), v((512, 768), BF16), v((16, 768), F32),
            v((512, 768), BF16), v((512, 384), BF16), v((512, 768), BF16), v((512, 384), BF16),
            v((512, 768), BF16), v((512, 384), BF16), v((2, 1024, 384), BF16),
            v((2, 1024, 384), BF16), v((2, 1024, 384), BF16), v((2, 512, 384), BF16),
            v((512, 768), BF16), v((2, 1024, 128), F32), v((16, 768), F32), v((8, 16, 768), BF16),
            v((16, 768), BF16), v((5, 16, 768), BF16), v((16, 768), F32),
            v((512, 768), BF16), v((512, 768), BF16), v((512, 768), BF16), v((256, 1024), F32), v((256, 1024), F32),
            v((256, 128), F32), v((256, 128), F32), v((512, 128), F32), v((8, 1024), F32), v((512, 128), F32),
            v((4, 2, 256), jnp.int32), v((4, 16, 768), BF16), v((len(SHARED), 3, 64, 384), BF16), v((2, 512, 384), BF16),
            *[v((192,), BF16)] * 8, v((768,), BF16),
            dma((12,)), dma((9,)), dma((CHUNKS,)), dma((CHUNKS,)), dma((CHUNKS,)), dma((CHUNKS,)), dma((CHUNKS, 2)),
            dma((len(SHARED),)), dma((1,)), dma((1,)), dma((12,)), dma((12,)),
            dma((2,)), dma((2,)), dma((2,)), dma((2,)), dma((3,)), dma((3,)), dma((2,)),
            dma((GROUPS,)), dma((GROUPS, 6)), dma((2,)), dma((2,)), dma((4,)), dma((1,)),
            dma((1,)), dma((1,)), dma((2,)), dma((2,)), dma((1,)), dma((1,)), dma((4,)), dma((4,)),
        ],
        compiler_params=pltpu.CompilerParams(
            collective_id=0, has_side_effects=True, vmem_limit_bytes=67043328
        ),
    )(*args)


def spread_kernel(
    Ti, GIi, LOi, BTi,
    LOo, GIo, WQo, WKo, WVo, WOo, WUo, WDo, BQo, BVo, BOo, GAo, SAo, BUo, BDo, GFo, SFo,
    T, GI, LO, OUT, GIF, sem, osem,
):
    g = lax.axis_index("group")
    order = (0, 1, 2, 3, 4, 5, 6, 7, 8, 9, 10, 11)
    loads = []
    for j in order:
        loads.append(pltpu.make_async_copy(Ti.at[:, j], T.at[:, j], sem.at[j]))
    loads.append(pltpu.make_async_copy(GIi, GI, sem.at[12]))
    loads.append(pltpu.make_async_copy(LOi, LO, sem.at[13]))
    for copy in loads:
        copy.start()
    stores = []

    def store(src, dst):
        copy = pltpu.make_async_copy(src, dst, osem.at[len(stores)])
        copy.start()
        stores.append(copy)

    for j in range(9):
        loads[j].wait()
        for e in range(2):
            OUT[j, :, 384 * e : 384 * e + 384] = T[e, j].astype(F32)
        if j < 4:
            store(OUT.at[j], WDo.at[192 * j : 192 * j + 192, :])
        elif j < 8:
            for e in range(2):
                start = 1536 * e + 384 * (j - 4)
                store(OUT.at[j, :, 384 * e : 384 * e + 384], WUo.at[:, start : start + 384])
        else:
            store(OUT.at[j], WOo)
    for j in range(9, 12):
        loads[j].wait()
    for w, ref in enumerate((WQo, WKo, WVo)):
        for turn in range(3):
            for e in range(2):
                start = 384 * e + 128 * turn
                OUT[9 + w, :, start : start + 128] = T[e, 9 + turn, :, 128 * w : 128 * w + 128].astype(F32)
        store(OUT.at[9 + w], ref)
    loads[12].wait()
    GIF[...] = GI[...].astype(F32)
    store(GIF, GIo)
    loads[13].wait()
    store(LO, LOo)
    moved = pltpu.roll(BTi[...], (768 - 192 * g) % 768, 1)
    for row, ref in ((0, BQo), (2, BVo), (3, BOo), (4, GAo), (5, SAo), (6, BDo), (7, GFo), (8, SFo)):
        ref[...] = moved[row, 0:192]
    up = BTi[pl.ds(12 + g, 1), :]
    BUo[...] = up[0, :]
    for copy in stores:
        copy.wait()


def spread(totals, grad_input, layer_out, small):
    square = sds((192, 768), F32)
    short = sds((192,), F32)
    whole = pl.BlockSpec(memory_space=pltpu.VMEM)
    dma = pltpu.SemaphoreType.DMA
    return pl.pallas_call(
        spread_kernel,
        out_shape=[
            sds((2, 256, 768)), sds((2, 256, 768), F32), square, square, square, square,
            sds((192, 3072), F32), sds((768, 768), F32),
            short, short, short, short, short, sds((768,), F32), short, short, short,
        ],
        in_specs=[ANY, ANY, ANY, whole],
        out_specs=[ANY] * 8 + [whole] * 9,
        scratch_shapes=[
            pltpu.VMEM((2, CHUNKS, 192, 384), BF16), pltpu.VMEM((2, 256, 768), BF16), pltpu.VMEM((2, 256, 768), BF16),
            pltpu.VMEM((CHUNKS, 192, 768), F32), pltpu.VMEM((2, 256, 768), F32), dma((14,)), dma((20,)),
        ],
        compiler_params=pltpu.CompilerParams(vmem_limit_bytes=66000000),
    )(totals, grad_input, layer_out, small)


def fits(mesh):
    return dict(mesh.shape) == {"group": 4, "replica": 8}


def fast(
    tokens_in, doc_ids, out_grad, w_query, w_key, w_value, w_out, w_up, w_down, b_query, b_value, b_out,
    gain_attn, shift_attn, b_up, b_down, gain_ffn, shift_ffn,
):
    layer_out, grad_input, totals, small, *_ = layer(
        tokens_in, doc_ids, out_grad, w_query, w_key, w_value, w_out, w_up, w_down,
        b_query, b_value, b_out, gain_attn, shift_attn, b_down, gain_ffn, shift_ffn, b_up,
    )
    return tuple(spread(totals, grad_input, layer_out, small))


def layer_norm(values, gain, shift):
    centre = values - jnp.mean(values, axis=-1, keepdims=True)
    spread = jnp.mean(centre * centre, axis=-1, keepdims=True)
    return centre * lax.rsqrt(spread + EPSILON) * gain + shift


def norm_pull(values, gain, shift, grad):
    result, pullback = jax.vjp(
        layer_norm, values, gain.astype(jnp.float32), shift.astype(jnp.float32)
    )
    return (result, pullback(grad))


def exact_gelu(values):
    return jax.nn.gelu(values, approximate=False)


def project(inputs, weight, bias):
    return jnp.dot(inputs, weight, preferred_element_type=jnp.float32) + bias.astype(jnp.float32)


def contract_rows(left, right):
    return lax.dot_general(
        left, right, (((0,), (0,)), ((), ())), preferred_element_type=jnp.float32
    )


def against_rows(grad, weight):
    return lax.dot_general(
        grad, weight, (((1,), (1,)), ((), ())), preferred_element_type=jnp.float32
    )


def column_sum(values):
    return jnp.sum(values.astype(jnp.float32), axis=0)


def add_pair(first, second):
    return first + second


def scores_of(query, keys_all, allowed):
    rows = query.shape[0]
    length = keys_all.shape[0]
    scaling = HEAD_DIM ** (-0.5)
    scores = (
        jnp.einsum(
            "qhd,khd->hqk",
            query.reshape(rows, HEADS, HEAD_DIM),
            keys_all.reshape(length, HEADS, HEAD_DIM),
            preferred_element_type=jnp.float32,
        )
        * scaling
    )
    return jnp.where(allowed[None], scores, NEGATIVE)


def attention_forward(query, keys_all, values_all, allowed):
    rows = query.shape[0]
    length = keys_all.shape[0]
    scores = scores_of(query, keys_all, allowed)
    row_max = jnp.max(scores, axis=-1, keepdims=True)
    exponent = jnp.exp(scores - row_max)
    total = jnp.sum(exponent, axis=-1, keepdims=True)
    probs = (exponent / total).astype(jnp.bfloat16)
    log_total = row_max[..., 0] + jnp.log(total[..., 0])
    joined = jnp.einsum(
        "hqk,khd->qhd",
        probs,
        values_all.reshape(length, HEADS, HEAD_DIM),
        preferred_element_type=jnp.float32,
    )
    return (joined.reshape(rows, HEADS * HEAD_DIM), log_total)


def score_grads(query, keys_all, values_all, allowed, log_total, d_attended):
    rows = query.shape[0]
    length = keys_all.shape[0]
    scores = scores_of(query, keys_all, allowed)
    probs = jnp.exp(scores - log_total[..., None])
    d_heads = d_attended.reshape(rows, HEADS, HEAD_DIM)
    d_probs = jnp.einsum(
        "qhd,khd->hqk",
        d_heads,
        values_all.reshape(length, HEADS, HEAD_DIM),
        preferred_element_type=jnp.float32,
    )
    row_term = jnp.sum(probs * d_probs, axis=-1)
    d_scores = (probs * (d_probs - row_term[..., None])).astype(jnp.bfloat16)
    return (probs, d_scores, row_term)


def attention_backward(query, keys_all, values_all, allowed, log_total, d_attended):
    rows = query.shape[0]
    length = keys_all.shape[0]
    scaling = HEAD_DIM ** (-0.5)
    probs, d_scores, row_term = score_grads(
        query, keys_all, values_all, allowed, log_total, d_attended
    )
    d_heads = d_attended.reshape(rows, HEADS, HEAD_DIM)
    d_values_part = jnp.einsum(
        "hqk,qhd->khd", probs.astype(jnp.bfloat16), d_heads, preferred_element_type=jnp.float32
    ).reshape(length, HEADS * HEAD_DIM)
    d_query = (
        jnp.einsum(
            "hqk,khd->qhd",
            d_scores,
            keys_all.reshape(length, HEADS, HEAD_DIM),
            preferred_element_type=jnp.float32,
        ).reshape(rows, HEADS * HEAD_DIM)
        * scaling
    )
    d_keys_part = (
        jnp.einsum(
            "hqk,qhd->khd",
            d_scores,
            query.reshape(rows, HEADS, HEAD_DIM),
            preferred_element_type=jnp.float32,
        ).reshape(length, HEADS * HEAD_DIM)
        * scaling
    )
    return (d_query, d_keys_part, d_values_part, row_term)


def owner_sum(grads):
    return (
        lax.psum_scatter(
            grads[0].astype(jnp.bfloat16), "group", scatter_dimension=0, tiled=True
        ).astype(jnp.float32),
        lax.psum_scatter(
            grads[1].astype(jnp.bfloat16), "group", scatter_dimension=0, tiled=True
        ).astype(jnp.float32),
        lax.psum_scatter(
            grads[2].astype(jnp.bfloat16), "group", scatter_dimension=0, tiled=True
        ).astype(jnp.float32),
        lax.psum_scatter(
            grads[3].astype(jnp.bfloat16), "group", scatter_dimension=0, tiled=True
        ).astype(jnp.float32),
        lax.psum_scatter(
            grads[4].astype(jnp.bfloat16), "group", scatter_dimension=0, tiled=True
        ).astype(jnp.float32),
        lax.psum_scatter(
            grads[5].astype(jnp.bfloat16), "group", scatter_dimension=0, tiled=True
        ).astype(jnp.float32),
        lax.psum_scatter(
            grads[6].astype(jnp.bfloat16), "group", scatter_dimension=0, tiled=True
        ).astype(jnp.float32),
        lax.psum_scatter(
            grads[7].astype(jnp.bfloat16), "group", scatter_dimension=0, tiled=True
        ).astype(jnp.float32),
        lax.psum_scatter(
            grads[8].astype(jnp.bfloat16), "group", scatter_dimension=0, tiled=True
        ).astype(jnp.float32),
        lax.psum_scatter(
            grads[9].astype(jnp.bfloat16), "group", scatter_dimension=0, tiled=True
        ).astype(jnp.float32),
        lax.psum_scatter(
            grads[10].astype(jnp.bfloat16), "group", scatter_dimension=0, tiled=True
        ).astype(jnp.float32),
        lax.psum_scatter(
            grads[11].astype(jnp.bfloat16), "group", scatter_dimension=0, tiled=True
        ).astype(jnp.float32),
        lax.psum_scatter(
            grads[12].astype(jnp.bfloat16), "group", scatter_dimension=0, tiled=True
        ).astype(jnp.float32),
        lax.psum_scatter(
            grads[13].astype(jnp.bfloat16), "group", scatter_dimension=0, tiled=True
        ).astype(jnp.float32),
        lax.psum_scatter(
            grads[14].astype(jnp.bfloat16), "group", scatter_dimension=0, tiled=True
        ).astype(jnp.float32),
    )


def shards(
    tokens_in,
    doc_ids,
    out_grad,
    w_query,
    w_key,
    w_value,
    w_out,
    w_up,
    w_down,
    b_query,
    b_value,
    b_out,
    gain_attn,
    shift_attn,
    b_up,
    b_down,
    gain_ffn,
    shift_ffn,
):
    gathered = (
        lax.all_gather(w_query, "group", axis=0, tiled=True),
        lax.all_gather(w_key, "group", axis=0, tiled=True),
        lax.all_gather(w_value, "group", axis=0, tiled=True),
        lax.all_gather(w_out, "group", axis=0, tiled=True),
        lax.all_gather(w_up, "group", axis=0, tiled=True),
        lax.all_gather(w_down, "group", axis=0, tiled=True),
        lax.all_gather(b_query, "group", axis=0, tiled=True),
        lax.all_gather(b_value, "group", axis=0, tiled=True),
        lax.all_gather(b_out, "group", axis=0, tiled=True),
        lax.all_gather(gain_attn, "group", axis=0, tiled=True),
        lax.all_gather(shift_attn, "group", axis=0, tiled=True),
        lax.all_gather(b_up, "group", axis=0, tiled=True),
        lax.all_gather(b_down, "group", axis=0, tiled=True),
        lax.all_gather(gain_ffn, "group", axis=0, tiled=True),
        lax.all_gather(shift_ffn, "group", axis=0, tiled=True),
    )
    (
        query_weight,
        key_weight,
        value_weight,
        out_weight,
        up_weight,
        down_weight,
        query_bias,
        value_bias,
        out_bias,
        attn_gain,
        attn_shift,
        up_bias,
        down_bias,
        ffn_gain,
        ffn_shift,
    ) = gathered
    micros = tokens_in.shape[0]
    outputs = []
    stored = []
    for micro in range(micros):
        inputs = tokens_in[micro]
        segment = doc_ids[micro]
        query = project(inputs, query_weight, query_bias).astype(jnp.bfloat16)
        keys = jnp.dot(inputs, key_weight, preferred_element_type=jnp.float32).astype(jnp.bfloat16)
        values = project(inputs, value_weight, value_bias).astype(jnp.bfloat16)
        keys_all, values_all, seg_all = (
            lax.all_gather(keys, "group", axis=0, tiled=True),
            lax.all_gather(values, "group", axis=0, tiled=True),
            lax.all_gather(segment, "group", axis=0, tiled=True),
        )
        allowed = segment[:, None] == seg_all[None, :]
        attended, log_total = attention_forward(query, keys_all, values_all, allowed)
        attended = attended.astype(jnp.bfloat16)
        resid_one = inputs.astype(jnp.float32) + project(attended, out_weight, out_bias)
        normed = layer_norm(
            resid_one, attn_gain.astype(jnp.float32), attn_shift.astype(jnp.float32)
        )
        hidden = project(normed.astype(jnp.bfloat16), up_weight, up_bias)
        activated = exact_gelu(hidden).astype(jnp.bfloat16)
        resid_two = normed + project(activated, down_weight, down_bias)
        result = layer_norm(resid_two, ffn_gain.astype(jnp.float32), ffn_shift.astype(jnp.float32))
        outputs.append(result.astype(jnp.bfloat16))
        stored.append((query, keys, values, log_total, attended, resid_one, hidden, resid_two))
    gathered = (
        lax.all_gather(w_query, "group", axis=0, tiled=True),
        lax.all_gather(w_key, "group", axis=0, tiled=True),
        lax.all_gather(w_value, "group", axis=0, tiled=True),
        lax.all_gather(w_out, "group", axis=0, tiled=True),
        lax.all_gather(w_up, "group", axis=0, tiled=True),
        lax.all_gather(w_down, "group", axis=0, tiled=True),
        lax.all_gather(b_query, "group", axis=0, tiled=True),
        lax.all_gather(b_value, "group", axis=0, tiled=True),
        lax.all_gather(b_out, "group", axis=0, tiled=True),
        lax.all_gather(gain_attn, "group", axis=0, tiled=True),
        lax.all_gather(shift_attn, "group", axis=0, tiled=True),
        lax.all_gather(b_up, "group", axis=0, tiled=True),
        lax.all_gather(b_down, "group", axis=0, tiled=True),
        lax.all_gather(gain_ffn, "group", axis=0, tiled=True),
        lax.all_gather(shift_ffn, "group", axis=0, tiled=True),
    )
    (
        query_weight,
        key_weight,
        value_weight,
        out_weight,
        up_weight,
        down_weight,
        query_bias,
        value_bias,
        out_bias,
        attn_gain,
        attn_shift,
        up_bias,
        down_bias,
        ffn_gain,
        ffn_shift,
    ) = gathered
    totals = tuple((jnp.zeros(member.shape, jnp.float32) for member in gathered))
    input_grads = []
    for micro in range(micros):
        inputs = tokens_in[micro]
        segment = doc_ids[micro]
        query, keys, values, log_total, attended, resid_one, hidden, resid_two = stored[micro]
        upstream = out_grad[micro].astype(jnp.float32)
        unused_out, (d_resid_two, g_ffn_gain, g_ffn_shift) = norm_pull(
            resid_two, ffn_gain, ffn_shift, upstream
        )
        d_ffn = d_resid_two.astype(jnp.bfloat16)
        activated, gelu_pull = jax.vjp(exact_gelu, hidden)
        activated = activated.astype(jnp.bfloat16)
        g_down_w = contract_rows(activated, d_ffn)
        g_down_b = column_sum(d_ffn)
        d_activated = against_rows(d_ffn, down_weight)
        d_hidden = gelu_pull(d_activated)[0].astype(jnp.bfloat16)
        normed = layer_norm(
            resid_one, attn_gain.astype(jnp.float32), attn_shift.astype(jnp.float32)
        )
        normed_low = normed.astype(jnp.bfloat16)
        g_up_w = contract_rows(normed_low, d_hidden)
        g_up_b = column_sum(d_hidden)
        d_normed = against_rows(d_hidden, up_weight) + d_resid_two
        unused_norm, (d_resid_one, g_attn_gain, g_attn_shift) = norm_pull(
            resid_one, attn_gain, attn_shift, d_normed
        )
        d_branch = d_resid_one.astype(jnp.bfloat16)
        g_out_w = contract_rows(attended, d_branch)
        g_out_b = column_sum(d_branch)
        d_attended = against_rows(d_branch, out_weight).astype(jnp.bfloat16)
        keys_all, values_all, seg_all = (
            lax.all_gather(keys, "group", axis=0, tiled=True),
            lax.all_gather(values, "group", axis=0, tiled=True),
            lax.all_gather(segment, "group", axis=0, tiled=True),
        )
        allowed = segment[:, None] == seg_all[None, :]
        d_query, d_keys_part, d_values_part, row_term = attention_backward(
            query, keys_all, values_all, allowed, log_total, d_attended
        )
        d_keys, d_values = (
            lax.psum_scatter(
                d_keys_part.astype(jnp.bfloat16), "group", scatter_dimension=0, tiled=True
            ).astype(jnp.float32),
            lax.psum_scatter(
                d_values_part.astype(jnp.bfloat16), "group", scatter_dimension=0, tiled=True
            ).astype(jnp.float32),
        )
        d_query = d_query.astype(jnp.bfloat16)
        d_keys = d_keys.astype(jnp.bfloat16)
        d_values = d_values.astype(jnp.bfloat16)
        g_query_w = contract_rows(inputs, d_query)
        g_key_w = contract_rows(inputs, d_keys)
        g_value_w = contract_rows(inputs, d_values)
        g_query_b = column_sum(d_query)
        g_value_b = column_sum(d_values)
        input_grad = (
            d_resid_one
            + against_rows(d_query, query_weight)
            + against_rows(d_keys, key_weight)
            + against_rows(d_values, value_weight)
        )
        input_grads.append(input_grad)
        micro_grads = (
            g_query_w,
            g_key_w,
            g_value_w,
            g_out_w,
            g_up_w,
            g_down_w,
            g_query_b,
            g_value_b,
            g_out_b,
            g_attn_gain,
            g_attn_shift,
            g_up_b,
            g_down_b,
            g_ffn_gain,
            g_ffn_shift,
        )
        totals = jax.tree.map(add_pair, totals, micro_grads)
    totals = tuple(owner_sum(totals))
    summed = (
        lax.psum(totals[0].astype(jnp.bfloat16), "replica").astype(jnp.float32),
        lax.psum(totals[1].astype(jnp.bfloat16), "replica").astype(jnp.float32),
        lax.psum(totals[2].astype(jnp.bfloat16), "replica").astype(jnp.float32),
        lax.psum(totals[3].astype(jnp.bfloat16), "replica").astype(jnp.float32),
        lax.psum(totals[4].astype(jnp.bfloat16), "replica").astype(jnp.float32),
        lax.psum(totals[5].astype(jnp.bfloat16), "replica").astype(jnp.float32),
        lax.psum(totals[6].astype(jnp.bfloat16), "replica").astype(jnp.float32),
        lax.psum(totals[7].astype(jnp.bfloat16), "replica").astype(jnp.float32),
        lax.psum(totals[8].astype(jnp.bfloat16), "replica").astype(jnp.float32),
        lax.psum(totals[9].astype(jnp.bfloat16), "replica").astype(jnp.float32),
        lax.psum(totals[10].astype(jnp.bfloat16), "replica").astype(jnp.float32),
        lax.psum(totals[11].astype(jnp.bfloat16), "replica").astype(jnp.float32),
        lax.psum(totals[12].astype(jnp.bfloat16), "replica").astype(jnp.float32),
        lax.psum(totals[13].astype(jnp.bfloat16), "replica").astype(jnp.float32),
        lax.psum(totals[14].astype(jnp.bfloat16), "replica").astype(jnp.float32),
    )
    layer_out = jnp.stack(outputs)
    grad_input = jnp.stack(input_grads)
    return (
        layer_out,
        grad_input,
        summed[0],
        summed[1],
        summed[2],
        summed[3],
        summed[4],
        summed[5],
        summed[6],
        summed[7],
        summed[8],
        summed[9],
        summed[10],
        summed[11],
        summed[12],
        summed[13],
        summed[14],
    )


def solution(mesh):
    return jax.shard_map(
        shards if not fits(mesh) else fast,
        mesh=mesh,
        in_specs=(
            P("replica", "group", None),
            P("replica", "group"),
            P("replica", "group", None),
            P("group", None),
            P("group", None),
            P("group", None),
            P("group", None),
            P("group", None),
            P("group", None),
            P("group"),
            P("group"),
            P("group"),
            P("group"),
            P("group"),
            P("group"),
            P("group"),
            P("group"),
            P("group"),
        ),
        out_specs=(
            P("replica", "group", None),
            P("replica", "group", None),
            P("group", None),
            P("group", None),
            P("group", None),
            P("group", None),
            P("group", None),
            P("group", None),
            P("group"),
            P("group"),
            P("group"),
            P("group"),
            P("group"),
            P("group"),
            P("group"),
            P("group"),
            P("group"),
        ),
        check_vma=False,
    )
```

```python
import functools

import jax
import jax.numpy as jnp
from jax import lax
from jax.experimental import pallas as pl
from jax.experimental.pallas import tpu as pltpu
from jax.sharding import PartitionSpec as P

HEADS = 12
HEAD_DIM = 64
EPSILON = 1e-05
NEGATIVE = -1e30
F32 = jnp.float32
BF16 = jnp.bfloat16
MESH = pl.DeviceIdType.MESH
ANY = pl.BlockSpec(memory_space=pl.ANY)


class Place:
    def __init__(self):
        self.g = lax.axis_index("group")
        self.r = lax.axis_index("replica")
        self.c = self.r % 2
        self.z = self.r // 2
        self.gx = self.g + 1 - 2 * (self.g % 2)
        self.gy = self.g + 2 - 4 * (self.g // 2)
        self.gd = 3 - self.g
        self.rp = self.r + 1 - 2 * self.c


def remote(src, dst, send, recv, device):
    return pltpu.make_async_remote_copy(
        src_ref=src, dst_ref=dst, send_sem=send, recv_sem=recv, device_id=device, device_id_type=MESH
    )


def plane_barrier(place, extra=()):
    barrier = pltpu.get_barrier_semaphore()
    for g in (place.g, place.gx, place.gy, place.gd):
        for r in (place.r, place.rp):
            if g is place.g and r is place.r:
                continue
            pl.semaphore_signal(barrier, inc=1, device_id=(g, r), device_id_type=MESH)
    return barrier


def dot(a, b):
    return jnp.dot(a, b, preferred_element_type=F32)


def norm_parts(values):
    centre = values - jnp.mean(values, axis=-1, keepdims=True)
    spread = jnp.mean(centre * centre, axis=-1, keepdims=True)
    inverse = lax.rsqrt(spread + EPSILON)
    return centre * inverse, inverse


def dot_nt(a, b):
    return lax.dot_general(a, b, (((1,), (1,)), ((), ())), preferred_element_type=F32)


def dot_tn(a, b):
    return lax.dot_general(a, b, (((0,), (0,)), ((), ())), preferred_element_type=F32)


def columns(values):
    return jnp.sum(values, axis=0, keepdims=True)


CHUNKS = 12


SHARED = (2, 3, 5, 7,)
SCHEDULE = {
    ("down", 0): (
        ("first", 0), ("first", 1),
    ),
    ("down", 1): (
        ("plain", 0), ("plain", 1), ("share", 2), ("share", 3),
    ),
    ("down", 2): (
        ("passed", 0),
    ),
    ("normed",): (
        ("passed", 1), ("shared", 2), ("first", 2), ("plain", 2),
    ),
    ("up", 4): (
        ("first", 4), ("plain", 4), ("own", 0), ("shared", 3),
        ("first", 3), ("plain", 3),
    ),
    ("up", 5): (
        ("share", 5), ("own", 1), ("passed", 2),
    ),
    ("up", 6): (
        ("first", 6), ("plain", 6),
    ),
    ("up", 7): (
        ("share", 7), ("passed", 4),
    ),
    ("datt",): (
        ("chain", 0),
    ),
    ("sq", 8): (
        ("first", 8), ("plain", 8), ("passed", 3), ("shared", 5),
        ("first", 5), ("plain", 5),
    ),
    ("a", 0): (
        ("own", 2),
    ),
    ("a", 1): (
        ("chain", 1), ("fin_in", 0), ("passed", 6),
    ),
    ("a", 2): (
        ("own", 4), ("shared", 7), ("first", 7), ("plain", 7),
    ),
    ("a", 3): (
        ("first", 9), ("plain", 9), ("own", 3), ("chain", 2),
        ("fin_in", 1),
    ),
    ("a", 4): (
        ("chain", 4), ("fin_out", 0), ("passed", 5),
    ),
    ("a", 5): (
        ("own", 6), ("passed", 7), ("passed", 8),
    ),
    ("a", 6): (
        ("chain", 3), ("fin_in", 2), ("fin_out", 1),
    ),
    ("a", 7): (
        ("first", 10), ("plain", 10), ("own", 5), ("own", 7),
        ("chain", 6),
    ),
    ("a", 8): (
        ("own", 8), ("fin_in", 3), ("fin_in", 4),
    ),
    ("a", 9): (
        ("chain", 5), ("fin_out", 2), ("passed", 9),
    ),
    ("a", 10): (
        ("fin_in", 6), ("passed", 10), ("chain", 7),
    ),
    ("a", 11): (
        ("first", 11), ("plain", 11), ("own", 9), ("own", 10),
        ("chain", 8),
    ),
    ("end",): (
        ("fin_in", 5), ("fin_out", 3), ("fin_out", 4),
    ),
    ("inp", 2): (
        ("chain", 9), ("fin_in", 7), ("fin_out", 6), ("passed", 11),
    ),
    ("tail",): (
        ("fin_in", 8), ("gi", 0), ("small_chain", 0), ("chain", 10),
        ("fin_out", 5), ("own", 11), ("small_in", 0), ("fin_in", 9),
        ("fin_out", 7), ("chain", 11), ("fin_in", 10), ("fin_out", 8),
        ("fin_out", 9), ("fin_in", 11), ("fin_out", 10), ("fin_out", 11),
        ("small_out", 0),
    ),
}

GATHER = {
    ("pre",): (
        ("relay", 0), ("x1", 0), ("diagonal", 0), ("own", 1),
        ("jn", 0), ("jf", 0), ("own", 2), ("relay", 1),
    ),
    ("kv",): (
        ("own", 3),
    ),
    ("q",): (
        ("jn", 1), ("relay", 2),
    ),
    ("a", 0): (
        ("diagonal", 1),
    ),
    ("a", 1): (
        ("own", 4),
    ),
    ("a", 4): (
        ("relay", 3), ("jn", 2),
    ),
    ("a", 5): (
        ("jf", 1),
    ),
    ("a", 6): (
        ("diagonal", 2),
    ),
    ("a", 8): (
        ("own", 5),
    ),
    ("a", 10): (
        ("relay", 4), ("jn", 3),
    ),
    ("up",): (
        ("diagonal", 3), ("jf", 2), ("relay", 5), ("g", 0),
        ("jn", 4), ("diagonal", 4), ("jf", 3),
    ),
    ("u", 1): (
        ("diagonal", 5),
    ),
    ("u", 7): (
        ("jn", 5),
    ),
    ("df",): (
        ("jf", 4), ("jf", 5),
    ),
}


GROUPS = 6


def piece_of(W, k, chip, core, first=0, count=3):
    if k < 4:
        lo, hi = ((0, 3), (3, 4), (4, 6), (6, 8))[k]
        return W.at[lo:hi, pl.ds(pl.multiple_of(192 * chip + 96 * core + 32 * first, 16), 32 * count), :]
    start = 384 * (k - 4) + 192 * core + 64 * first
    return W.at[8 + chip, pl.ds(pl.multiple_of(start, 16), 64 * count), :]


def layer_kernel(
    tok, docs_in, og, wq, wk, wv, wo, wup, wdn,
    bq_in, bv_in, bo_in, ga_in, sa_in, bd_in, gf_in, sf_in, bu_in,
    LOo, GIo, To, BTo, Xo, ATo, NLo,
    W, P1, P2, ZR, ACT, GP, DHP, Q, KV, MASK, LSE, R1, R2, G, PF,
    DF, DFP, DB, DBP, DQ, DQP, DKS, DKR, DKF, DKP, LO, ACC, BG, BR, BS, BZ, BT,
    X, AT, NL, SA, SB, PA, PB, DC, DR, LC, D, PK, ZF, RC, bq, bv, bo, ga, sa, bd, gf, sf, bu,
    lsem, vsem, hops, p1r, p2r, zs, zr, zl, zfr, ts, tr, xs_, xr_, los, lor, gis, gir, b1s, b1r, osem,
    ags, agr, xs, xr, ds_, dr, ps, pr, gs, gr, kvs, kvr, lls, llr,
):
    DATT, LO2 = G, NL
    me = Place()
    g, r, c, z = me.g, me.r, me.c, me.z
    gx, gy, gd, rp = me.gx, me.gy, me.gd, me.rp
    outer = (z == 0) | (z == 3)
    inner = jnp.logical_not(outer)
    zin, zout, zother = 1 + z // 3, 3 * (z - 1), 3 - z
    zp = z % 2
    rz = r + 2 - 4 * zp

    def zdev(zz):
        return (g, 2 * zz + c)

    barrier = plane_barrier(me)
    pl.semaphore_signal(barrier, inc=1, device_id=(g, rz), device_id_type=MESH)

    @pl.when(inner)
    def _():
        pl.semaphore_signal(barrier, inc=1, device_id=zdev(zother), device_id_type=MESH)

    vectors = []
    for i, (src, dst) in enumerate((
        (bq_in, bq), (bv_in, bv), (bo_in, bo), (ga_in, ga), (sa_in, sa), (bd_in, bd), (gf_in, gf), (sf_in, sf), (bu_in, bu),
    )):
        vectors.append(pltpu.make_async_copy(src, dst, vsem.at[i]))
        vectors[-1].start()

    local = []
    for w, ref in enumerate((wq, wk, wv, wo)):
        local.append((ref, W.at[w, pl.ds(pl.multiple_of(192 * g, 16), 192), :]))
    for u in range(4):
        local.append((wup.at[:, 768 * u : 768 * u + 768], W.at[4 + u, pl.ds(pl.multiple_of(192 * g, 16), 192), :]))
    local.append((wdn, W.at[8 + g]))
    local = [pltpu.make_async_copy(a, b, lsem.at[i]) for i, (a, b) in enumerate(local)]
    for copy in local:
        copy.start()

    own_lane = lax.broadcasted_iota(jnp.int32, (1, 768), 1) // 192 == g
    for copy in vectors:
        copy.wait()
    for row, ref in ((0, bq), (2, bv), (3, bo), (4, ga), (5, sa), (6, bd), (7, gf), (8, sf)):
        piece = ref[...].astype(F32).reshape(1, 192)
        PF[row : row + 1, :] = jnp.where(own_lane, jnp.concatenate([piece] * 4, axis=1), 0.0)
    for row in (1, 9, 10, 11):
        PF[row : row + 1, :] = jnp.zeros((1, 768), F32)
    tall = lax.broadcasted_iota(jnp.int32, (4, 768), 0) == g
    PF[12:16, :] = jnp.where(tall, bu[...].astype(F32).reshape(1, 768), 0.0)
    PK[g] = PF[...].astype(BF16)

    BG[...] = jnp.zeros_like(BG)
    pl.semaphore_wait(barrier, 9 - z // 3 - (3 - z) // 3)

    def reshard(src, dst_of, ssem, rsem, blocks=(0, 1)):
        for m in blocks:
            t, e = 2 * c + m, g // 2
            b = g % 2
            here = (t == g) & (e == c)
            src_m = src.at[m]
            dst_b = dst_of(b)

            @pl.when(jnp.logical_not(here))
            def _():
                remote(src_m, dst_b, ssem.at[m], rsem.at[b], (t, 2 * z + e)).start()

            @pl.when(here)
            def _():
                pltpu.make_async_copy(src_m, dst_b, rsem.at[b]).start()

    def reshard_wait(src, dst_of, ssem, rsem, b):
        remote(src.at[0], dst_of(b), ssem.at[0], rsem.at[b], (g, r)).wait_recv()

    def reshard_drain(src, dst_of, ssem, rsem):
        for m in range(2):
            t, e = 2 * c + m, g // 2
            here = (t == g) & (e == c)

            @pl.when(jnp.logical_not(here))
            def _():
                remote(src.at[m], dst_of(0), ssem.at[m], rsem.at[0], (t, 2 * z + e)).wait_send()

    def x_rows(b):
        if isinstance(b, int):
            return X.at[256 * b : 256 * b + 256, :]
        return X.at[pl.ds(pl.multiple_of(256 * b, 256), 256), :]

    def g_rows(b):
        if isinstance(b, int):
            return G.at[256 * b : 256 * b + 256, :]
        return G.at[pl.ds(pl.multiple_of(256 * b, 256), 256), :]

    for m in range(2):
        for e in range(2):
            t = 2 * c + m
            here = (t == g) & (c == e)

            @pl.when(jnp.logical_not(here))
            def _():
                remote(docs_in, D.at[g], ds_.at[2 * m + e], dr.at[0], (t, 2 * z + e)).start()

            @pl.when(here)
            def _():
                pltpu.make_async_copy(docs_in, D.at[g], dr.at[0]).start()

    def pass_on(k, slot, part, device):
        remote(part, part, ags.at[k], agr.at[k, slot], device).start()

    def landed(k, slot, count):
        rows = 32 * count
        size = W.at[0:3, 0:rows, :] if k == 0 else W.at[0:1, 0:rows, :] if k == 1 else W.at[0:2, 0:rows, :]
        remote(size, size, ags.at[k], agr.at[k, slot], (g, rp)).wait_recv()

    def own_send(k):
        part = piece_of(W, k, g, c, zp, 2)
        pass_on(k, 0, part, (gx, r))
        pass_on(k, 0, part, (gy, r))

    def relay(k):
        landed(k, 0, 4)
        pass_on(k, 1, piece_of(W, k, gx, c, zp, 1), (gy, r))
        pass_on(k, 1, piece_of(W, k, gy, c, zp + 1, 1), (gx, r))
        pass_on(k, 2, piece_of(W, k, gx, c, 2 * zp, 1), (g, rz))
        pass_on(k, 2, piece_of(W, k, gy, c, 2 * zp, 1), (g, rz))

    def diagonal(k):
        landed(k, 1, 2)
        pass_on(k, 3, piece_of(W, k, gd, c, 2 * zp, 1), (g, rz))

    def join_near(k):
        landed(k, 2, 2)
        for chip in (gx, gy):
            pass_on(k, 4, piece_of(W, k, chip, c), (g, rp))

    def join_far(k):
        landed(k, 3, 1)
        pass_on(k, 5, piece_of(W, k, gd, c), (g, rp))

    def complete_near(k):
        landed(k, 4, 6)

    def complete_far(k):
        landed(k, 5, 3)

    def complete(k):
        complete_near(k)
        complete_far(k)

    def gather_serve(*slot):
        for name, k in GATHER.get(slot, ()):
            gather_services[name](k)

    gather_services = {
        "own": own_send, "relay": relay, "diagonal": diagonal, "jn": join_near, "jf": join_far,
        "x1": lambda k: reshard(tok, x_rows, xs, xr, (1,)), "g": lambda k: reshard(og, g_rows, gs, gr),
    }

    def gather_drain(k):
        rows = 32 * 18
        size = W.at[0:3, 0:rows, :] if k == 0 else W.at[0:1, 0:rows, :] if k == 1 else W.at[0:2, 0:rows, :]
        remote(size, size, ags.at[k], agr.at[k, 0], (g, rp)).wait_send()

    for slot, chip in enumerate((gx, gy, gd)):
        remote(PK.at[g], PK.at[g], ps.at[0], pr.at[0], (chip, r)).start()
    for i in range(3):
        local[i].wait()
    own_send(0)
    reshard(tok, x_rows, xs, xr, (0,))
    for i in range(3, 9):
        local[i].wait()

    remote(PK.at[0:3], PK.at[0:3], ps.at[0], pr.at[0], (gx, r)).wait_recv()
    PF[...] = PK[0].astype(F32) + PK[1].astype(F32) + PK[2].astype(F32) + PK[3].astype(F32)
    remote(D, D, ds_.at[0], dr.at[0], (g, r)).wait_recv()
    for b in range(2):
        row = jnp.broadcast_to(D[2 * c + b, pl.ds(g % 2, 1), :].astype(F32), (128, 256))
        DC[256 * b : 256 * b + 256, :] = row.T
    for i in range(4):
        DR[:, 256 * i : 256 * i + 256] = jnp.broadcast_to(D[i, pl.ds(g % 2, 1), :].astype(F32), (8, 256))
    for i in range(4):
        keys = jnp.broadcast_to(D[i, pl.ds(g % 2, 1), :].astype(F32), (8, 256)).T[:, 0:1]
        for b in range(2):
            rows = D[2 * c + b, pl.ds(g % 2, 1), :].astype(F32)
            MASK[256 * i : 256 * i + 256, 256 * b : 256 * b + 256] = jnp.where(keys == rows, 0.0, NEGATIVE)
    gather_serve("pre")
    for b in range(2):
        reshard_wait(tok, x_rows, xs, xr, b)
    remote(X, Xo, lls.at[0], llr.at[0], (g, rp)).start()
    complete(0)
    own_rows = pl.ds(pl.multiple_of(512 * c, 512), 512)
    their_rows = pl.ds(pl.multiple_of(512 * (1 - c), 512), 512)

    def project(w, t, dst):
        cols = pl.ds(pl.multiple_of(256 * t, 256), 256)
        out = dot(X[...], W[w, :, cols]) + PF[pl.ds(w, 1), cols]
        return cols, out.astype(BF16)

    @pl.loop(0, 6, unroll=3)
    def _(i):
        w = i // 3
        cols, out = project(1 + w, i % 3, None)
        KV[w, own_rows, cols] = out

    for w in range(2):
        piece = KV.at[w, own_rows, :]
        remote(piece, piece, kvs.at[0], kvr.at[0], (g, rp)).start()
    gather_serve("kv")

    @pl.loop(0, 3, unroll=3)
    def _(i):
        cols, out = project(0, i, None)
        Q[:, cols] = out

    gather_serve("q")
    part = KV.at[:, their_rows, :]
    remote(part, part, kvs.at[0], kvr.at[0], (g, rp)).wait_recv()

    def at_step(i):
        pair, b = i // 2, i % 2
        return pair, pl.ds(pl.multiple_of(128 * pair, 128), 128), pl.ds(pl.multiple_of(256 * b, 256), 256)

    left_lanes = lax.broadcasted_iota(jnp.int32, (256, 128), 1) < 64

    def score(i, hh, S, peaks):
        pair, lanes, rows = at_step(i)
        q = Q[rows, lanes].astype(F32) * (HEAD_DIM ** -0.5)
        qh = jnp.where(left_lanes if hh == 0 else jnp.logical_not(left_lanes), q, 0.0).astype(BF16)
        s = dot_nt(qh, KV[0, :, lanes])
        s = jnp.where(DC[rows, 0:1] == DR[0:1, :], s, NEGATIVE)
        S[...] = s
        peaks[...] = jnp.broadcast_to(jnp.max(s, axis=1, keepdims=True), (256, 128))

    def soften(i, hh, S, peaks, vp):
        pair, lanes, rows = at_step(i)
        peak = peaks[...]
        e = jnp.exp(S[...] - peak[:, 0:1])
        total = jnp.sum(e, axis=1, keepdims=True)
        lane = lax.broadcasted_iota(jnp.int32, (256, 128), 1)
        LC[rows, :] = jnp.where(lane == 2 * pair + hh, peak + jnp.log(total), LC[rows, :])
        return dot(e.astype(BF16), vp) / total

    LC[...] = jnp.zeros_like(LC)
    score(0, 0, SA, PA)

    @pl.loop(0, 12)
    def _(i):
        pair, lanes, rows = at_step(i)
        vp = KV[1, :, lanes]
        score(i, 1, SB, PB)
        out0 = soften(i, 0, SA, PA, vp)
        score((i + 1) % 12, 0, SA, PA)
        out1 = soften(i, 1, SB, PB, vp)
        AT[rows, lanes] = jnp.where(left_lanes, out0, out1).astype(BF16)

        for k in range(12):
            if ("a", k) in GATHER:
                @pl.when(i == k)
                def _():
                    gather_serve("a", k)

    LSE[...] = LC[...].T[0:16, :]
    remote(AT, ATo, lls.at[1], llr.at[1], (g, rp)).start()
    gather_serve("out")
    complete(1)

    @pl.loop(0, 2)
    def _(i):
        rows = pl.ds(pl.multiple_of(256 * i, 256), 256)
        first = X[rows, :].astype(F32) + dot(AT[rows, :], W[3]) + PF[3:4, :]
        R1[rows, :] = first
        shape, _ = norm_parts(first)
        normed = shape * PF[4:5, :] + PF[5:6, :]
        R2[rows, :] = normed + PF[6:7, :]
        NL[rows, :] = normed.astype(BF16)

    remote(NL, NLo, lls.at[2], llr.at[2], (g, rp)).start()
    gather_serve("up")
    complete(2)
    complete(3)

    def up(t):
        u, tt = t // 3, t % 3
        cols = pl.ds(pl.multiple_of(256 * tt, 256), 256)
        wide = pl.ds(pl.multiple_of(256 * t, 256), 256)
        h = dot(NL[...], W[4 + u, :, cols]) + PF[pl.ds(12 + u, 1), cols]
        cdf = 0.5 * (1.0 + lax.erf(h * (0.5 ** 0.5)))
        ACT[c, :, wide] = (h * cdf).astype(BF16)
        GP[:, wide] = (cdf + h * jnp.exp(-0.5 * h * h) * 0.3989422804014327).astype(BF16)

    @pl.loop(0, 12)
    def _(t):
        up(t)

        for k in range(12):
            if ("u", k) in GATHER:
                @pl.when(t == k)
                def _():
                    gather_serve("u", k)

    remote(ACT.at[c], ACT.at[c], lls.at[3], llr.at[3], (g, rp)).start()

    def down(k):
        deep = pl.ds(pl.multiple_of(768 * k, 256), 768)

        @pl.loop(0, 3, unroll=3)
        def _(tt):
            cols = pl.ds(pl.multiple_of(256 * tt, 256), 256)
            R2[:, cols] += dot(ACT[c, :, deep], W[8 + k, :, cols])

    down(g)
    gather_serve("dn")
    complete_near(4)
    complete_near(5)
    down(gx)
    down(gy)
    gather_serve("df")
    complete_far(4)
    complete_far(5)
    down(gd)
    gather_serve("G")

    def forward_drain():
        reshard_drain(tok, x_rows, xs, xr)
        reshard_drain(og, g_rows, gs, gr)
        for m in range(2):
            for e in range(2):
                t = 2 * c + m
                here = (t == g) & (c == e)

                @pl.when(jnp.logical_not(here))
                def _():
                    remote(docs_in, D.at[g], ds_.at[2 * m + e], dr.at[0], (t, 2 * z + e)).wait_send()
        remote(PK.at[0:3], PK.at[0:3], ps.at[0], pr.at[0], (gx, r)).wait_send()
        part = KV.at[:, own_rows, :]
        remote(part, part, kvs.at[0], kvr.at[0], (g, rp)).wait_send()
        for i, (src, dst) in enumerate(((X, Xo), (AT, ATo), (NL, NLo), (ACT.at[c], ACT.at[c]))):
            remote(src, dst, lls.at[i], llr.at[i], (g, rp)).wait_send()

    loads = {}

    def load(name, slot, dst):
        src = {"x": Xo, "att": ATo, "nl": NLo}[name]
        remote(src, src, lls.at[slot], llr.at[slot], (g, rp)).wait_recv()
        copy = pltpu.make_async_copy(src, dst, lsem.at[9 + slot])
        copy.start()
        loads[name] = copy

    def grad(j, q, part=None):
        start, size = 0, 192
        if part is not None:
            start, size = 96 * part, 96
        if j < 4:
            return W.at[8 + q // 2, pl.ds(192 * j + start, size), pl.ds(pl.multiple_of(384 * (q % 2), 128), 384)]
        rows = pl.ds(pl.multiple_of(192 * q + start, 16), size)
        if j < 8:
            return W.at[10 + (j - 4) // 2, rows, 384 * (j % 2) : 384 * (j % 2) + 384]
        return W.at[4 + (j - 8) // 2, rows, 384 * (j % 2) : 384 * (j % 2) + 384]

    def parts_of(j):
        if j in SHARED:
            return ((64 * zp, 64), (64 * zp + 64, 64))
        return ((0, 96), (96, 96))

    def rows_of(ref, start, size):
        return ref.at[pl.ds(pl.multiple_of(start, 16), size)]

    def grad(j, q, start=0, size=192):
        if j < 4:
            return W.at[
                8 + q // 2, pl.ds(pl.multiple_of(192 * j + start, 16), size), pl.ds(pl.multiple_of(384 * (q % 2), 128), 384)
            ]
        rows = pl.ds(pl.multiple_of(192 * q + start, 16), size)
        if j < 8:
            return W.at[10 + (j - 4) // 2, rows, 384 * (j % 2) : 384 * (j % 2) + 384]
        return W.at[4 + (j - 8) // 2, rows, 384 * (j % 2) : 384 * (j % 2) + 384]

    def share(j):
        for slot, q in enumerate((gx, gy, gd)):
            remote(
                grad(j, q, 128 - 128 * zp, 64), ZF.at[SHARED.index(j), slot], hops.at[j], zfr.at[SHARED.index(j)], (g, rz)
            ).start()

    def shared(j):
        k = SHARED.index(j)
        remote(ZF.at[k], ZF.at[k], hops.at[j], zfr.at[k], (g, rz)).wait_recv()
        for slot, q in enumerate((gx, gy, gd)):
            mine = grad(j, q, 128 * zp, 64)
            mine[...] = (mine[...].astype(F32) + ZF[k, slot].astype(F32)).astype(BF16)

    def first(j):
        for side, (chip, (start, size)) in enumerate(zip((gy, gx), parts_of(j))):
            remote(grad(j, gd, start, size), P1.at[j, side, 0:size], hops.at[j], p1r.at[j], (chip, r)).start()

    def plain(j):
        (first_a, size), (first_b, _) = parts_of(j)
        remote(grad(j, gx, first_b, size), rows_of(P2.at[j, 0], first_b, size), hops.at[j], p2r.at[j], (gx, r)).start()
        remote(grad(j, gy, first_a, size), rows_of(P2.at[j, 1], first_a, size), hops.at[j], p2r.at[j], (gy, r)).start()

    def passed(j):
        size = parts_of(j)[0][1]
        both = P1.at[j, :, 0:size]
        remote(both, both, hops.at[j], p1r.at[j], (gx, r)).wait_recv()
        for side, chip in enumerate((gx, gy)):
            start = parts_of(j)[side][0]
            mine = grad(j, chip, start, size)
            mine[...] = (mine[...].astype(F32) + P1[j, side, 0:size].astype(F32)).astype(BF16)
            remote(mine, rows_of(P2.at[j, side], start, size), hops.at[j], p2r.at[j], (chip, r)).start()

    def own(j):
        start, size = parts_of(j)[0][0], 2 * parts_of(j)[0][1]
        both = P2.at[j, :, 0:size]
        remote(both, both, hops.at[j], p2r.at[j], (gx, r)).wait_recv()
        moved = pl.ds(pl.multiple_of(start, 16), size)
        arrived = P2[j, 0, moved].astype(F32) + P2[j, 1, moved].astype(F32)
        P2[j, 0, moved] = (grad(j, g, start, size)[...].astype(F32) + arrived).astype(BF16)
        if j in SHARED:
            P2[j, 0, pl.ds(pl.multiple_of(128 - 128 * zp, 16), 64)] = grad(j, g, 128 - 128 * zp, 64)[...]

        @pl.when(outer)
        def _():
            for rows, p in along_z(j):
                z_copy(j, 0, rows, 0, p, zin).start()

    def along_z(j):
        return [(slice(64 * p, 64 * p + 64), p) for p in range(3)] if j == CHUNKS - 1 else [(slice(0, 192), None)]

    def z_copy(j, slot, rows, side, p, to):
        arrived = zr.at[j, side] if p is None else zl.at[side, p]
        return remote(P2.at[j, slot, rows], ZR.at[j, side, rows], zs.at[j], arrived, zdev(to))

    def chain(j):
        @pl.when(inner)
        def _():
            for rows, p in along_z(j):
                z_copy(j, 0, rows, 0, p, zother).wait_recv()
                P2[j, 0, rows] = (P2[j, 0, rows].astype(F32) + ZR[j, 0, rows].astype(F32)).astype(BF16)
                z_copy(j, 0, rows, 1, p, zother).start()

    def hand_over(j):
        remote(P2.at[j, 1], To.at[c, j], ts.at[0], tr.at[0], (g, rp)).start()
        pltpu.make_async_copy(P2.at[j, 1], To.at[c, j], osem.at[0]).start()

    def fin_in(j):
        @pl.when(inner)
        def _():
            for rows, p in along_z(j):
                z_copy(j, 0, rows, 1, p, zother).wait_recv()
                P2[j, 1, rows] = (P2[j, 0, rows].astype(F32) + ZR[j, 1, rows].astype(F32)).astype(BF16)
                z_copy(j, 1, rows, 0, p, zout).start()
            hand_over(j)

    def fin_out(j):
        @pl.when(outer)
        def _():
            for rows, p in along_z(j):
                z_copy(j, 1, rows, 0, p, zin).wait_recv()
                P2[j, 1, rows] = ZR[j, 0, rows]
            hand_over(j)

    def drain(j):
        total = W.at[0, 0:576, 0:384]
        remote(total, total, hops.at[j], p1r.at[j], (gx, r)).wait_send()

        @pl.when(inner)
        def _():
            remote(ZR.at[j], ZR.at[j], zs.at[j], zr.at[j, 0], zdev(zother)).wait_send()

        @pl.when(outer)
        def _():
            remote(ZR.at[j, 0], ZR.at[j, 0], zs.at[j], zr.at[j, 0], zdev(zother)).wait_send()

    def serve(*slot):
        for name, j in SCHEDULE.get(slot, ()):
            services[name](j)

    def give_back(src, out, ssem, rsem):
        for b in range(2):
            t, e = 2 * c + b, g // 2
            here = (t == g) & (e == c)
            src_b = src.at[256 * b : 256 * b + 256, :]
            dst = out.at[g % 2]

            @pl.when(jnp.logical_not(here))
            def _():
                remote(src_b, dst, ssem.at[b], rsem.at[g % 2], (t, 2 * z + e)).start()

            @pl.when(here)
            def _():
                pltpu.make_async_copy(src_b, dst, rsem.at[g % 2]).start()

    def give_back_drain(src, out, ssem, rsem):
        for b in range(2):
            t, e = 2 * c + b, g // 2
            here = (t == g) & (e == c)
            src_b = src.at[256 * b : 256 * b + 256, :]

            @pl.when(jnp.logical_not(here))
            def _():
                remote(src_b, out.at[0], ssem.at[b], rsem.at[0], (t, 2 * z + e)).wait_send()

            remote(src_b, out.at[b], ssem.at[b], rsem.at[b], (g, rp)).wait_recv()

    services = {
        "passed": passed, "own": own, "chain": chain, "fin_in": fin_in, "fin_out": fin_out,
        "share": share, "shared": shared, "first": first, "plain": plain,
        "gi": lambda j: give_back(LO2, GIo, gis, gir),
    }

    def exchange(slot, src, dst):
        remote(src, dst, xs_.at[slot], xr_.at[slot], (g, rp)).start()

    def exchanged(slot, dst):
        remote(dst, dst, xs_.at[slot], xr_.at[slot], (g, rp)).wait_recv()

    def exchange_drain(slot, dst):
        remote(dst, dst, xs_.at[slot], xr_.at[slot], (g, rp)).wait_send()

    mine384 = pl.ds(pl.multiple_of(384 * c, 128), 384)
    theirs384 = pl.ds(pl.multiple_of(384 * (1 - c), 128), 384)

    def norm_back(values, gain, grad_out):
        shape, inverse = norm_parts(values)
        pulled = grad_out * gain
        d = inverse * (
            pulled
            - jnp.mean(pulled, axis=-1, keepdims=True)
            - shape * jnp.mean(pulled * shape, axis=-1, keepdims=True)
        )
        return shape, d

    for b in range(2):
        reshard_wait(og, g_rows, gs, gr, b)

    @pl.loop(0, 4)
    def _(i):
        rows = pl.ds(pl.multiple_of(128 * i, 128), 128)
        up = G[rows, :].astype(F32)
        shape, d = norm_back(R2[rows, :], PF[7:8, :], up)
        LO[rows, :] = (shape * PF[7:8, :] + PF[8:9, :]).astype(BF16)
        R2[rows, :] = d
        low = d.astype(BF16)
        DF[rows, :] = low
        BG[7:8, :] += columns(up * shape)
        BG[8:9, :] += columns(up)
        BG[6:7, :] += columns(low.astype(F32))

    exchange(0, DF.at[:, theirs384], DFP)
    give_back(LO, LOo, los, lor)

    def d_hidden(i):
        t = (i + 6 * (1 - c)) % 12
        tt = t % 3
        wide = pl.ds(pl.multiple_of(256 * t, 256), 256)
        back = dot_nt(DF[...], W[8 + t // 3, pl.ds(pl.multiple_of(256 * tt, 256), 256), :])
        low = (back * GP[:, wide].astype(F32)).astype(BF16)
        GP[:, wide] = low
        BG[pl.ds(12 + t // 3, 1), pl.ds(pl.multiple_of(256 * tt, 256), 256)] = columns(low.astype(F32))

    @pl.loop(0, 6, unroll=3)
    def _(i):
        d_hidden(i)

    exchange(1, GP.at[:, pl.ds(pl.multiple_of(1536 * (1 - c), 128), 1536)], DHP)

    @pl.loop(6, 12, unroll=3)
    def _(i):
        d_hidden(i)

    remote(ACT.at[1 - c], ACT.at[1 - c], lls.at[3], llr.at[3], (g, rp)).wait_recv()
    forward_drain()
    for k in range(GROUPS):
        gather_drain(k)
    exchanged(0, DFP)

    def pair_tn(own_left, their_left, own_right, their_right):
        return dot_tn(own_left, own_right) + dot_tn(their_left, their_right)

    def down_quarter(q):
        @pl.loop(0, 3, unroll=3)
        def _(i):
            lanes = pl.ds(pl.multiple_of(768 * q + 256 * i, 256), 256)
            out = pair_tn(ACT[c, :, lanes], ACT[1 - c, :, lanes], DF[:, mine384], DFP[...])
            W[8 + q // 2, pl.ds(pl.multiple_of(256 * i, 256), 256), pl.ds(pl.multiple_of(384 * (q % 2), 128), 384)] = (
                out.astype(BF16)
            )

    down_quarter(gd)
    serve("down", 0)
    down_quarter(gx)
    down_quarter(gy)
    serve("down", 1)
    down_quarter(g)
    serve("down", 2)
    load("nl", 2, ACT.at[0, :, 0:768])
    load("att", 1, ACT.at[0, :, 768:1536])
    load("x", 0, ACT.at[0, :, 1536:2304])

    @pl.loop(0, 3, unroll=3)
    def _(i):
        cols = pl.ds(pl.multiple_of(256 * i, 256), 256)
        total = R2[:, cols]
        for u in range(4):
            total = total + dot_nt(GP[:, 768 * u : 768 * u + 768], W[4 + u, cols, :])
        R2[:, cols] = total

    serve("normed")

    @pl.loop(0, 4)
    def _(i):
        rows = pl.ds(pl.multiple_of(128 * i, 128), 128)
        up = R2[rows, :]
        shape, d = norm_back(R1[rows, :], PF[4:5, :], up)
        R2[rows, :] = d
        low = d.astype(BF16)
        DB[rows, :] = low
        BG[4:5, :] += columns(up * shape)
        BG[5:6, :] += columns(up)
        BG[3:4, :] += columns(low.astype(F32))

    exchange(2, DB.at[:, theirs384], DBP)
    serve("ln1")
    exchanged(1, DHP)
    loads["nl"].wait()

    for j in range(4, 8):
        jj = j - 4
        own_cols = pl.ds(pl.multiple_of(1536 * c + 384 * jj, 128), 384)

        @pl.loop(0, 3, unroll=3)
        def _(i):
            lanes = pl.ds(pl.multiple_of(256 * i, 256), 256)
            out = pair_tn(NL[:, lanes], ACT[0, :, lanes], GP[:, own_cols], DHP[:, 384 * jj : 384 * jj + 384])
            W[10 + jj // 2, lanes, 384 * (jj % 2) : 384 * (jj % 2) + 384] = out.astype(BF16)

        serve("up", j)

    @pl.loop(0, 3, unroll=3)
    def _(i):
        cols = pl.ds(pl.multiple_of(256 * i, 256), 256)
        DATT[:, cols] = dot_nt(DB[...], W[3, cols, :]).astype(BF16)

    serve("datt")
    exchanged(2, DBP)
    loads["att"].wait()

    def square_grad(j, offset, own_left, own_right, their_right):
        @pl.loop(0, 3, unroll=3)
        def _(i):
            lanes = pl.ds(pl.multiple_of(offset + 256 * i, 256), 256)
            cols = pl.ds(pl.multiple_of(256 * i, 256), 256)
            out = pair_tn(own_left[:, cols], ACT[0, :, lanes], own_right[...], their_right[...])
            W[4 + (j - 8) // 2, cols, 384 * (j % 2) : 384 * (j % 2) + 384] = (
                out.astype(BF16)
            )

    square_grad(8, 768, AT, DB.at[:, mine384], DBP)
    serve("sq", 8)

    loads["x"].wait()

    @pl.loop(0, 12)
    def _(i):
        turn, ours, b = i // 4, (i // 2) % 2, i % 2
        pair = turn + 3 * (c * ours + (1 - c) * (1 - ours))
        lanes = pl.ds(pl.multiple_of(128 * pair, 128), 128)
        half_lanes = pl.ds(pl.multiple_of(128 * turn, 128), 128)
        cols = pl.ds(pl.multiple_of(256 * b, 256), 256)
        @pl.when(b == 0)
        def _():
            ACC[...] = jnp.zeros_like(ACC)

        def block(keys):
            qs = Q[cols, lanes].astype(F32) * (HEAD_DIM ** -0.5)
            do = DATT[cols, lanes].astype(F32)
            qt, dot_t = qs.T, do.T
            kp = KV[0, keys, lanes]
            vp = KV[1, keys, lanes]
            kt = kp.astype(F32).T.astype(BF16)
            weigh = (do * AT[cols, lanes].astype(F32)).T
            top = lax.broadcasted_iota(jnp.int32, (128, 256), 0) < 64
            left = lax.broadcasted_iota(jnp.int32, (256, 128), 1) < 64
            dk = dv = None
            pieces = []
            for hh in range(2):
                rows_in = top if hh == 0 else jnp.logical_not(top)
                lanes_in = left if hh == 0 else jnp.logical_not(left)
                s = dot(kp, jnp.where(rows_in, qt, 0.0).astype(BF16)) + MASK[keys, cols]
                p = jnp.exp(s - LSE[pl.ds(2 * pair + hh, 1), cols])
                dp = dot(vp, jnp.where(rows_in, dot_t, 0.0).astype(BF16))
                ds = (p * (dp - columns(weigh[64 * hh : 64 * hh + 64, :]))).astype(BF16)
                dv_h = dot(p.astype(BF16), jnp.where(lanes_in, do, 0.0).astype(BF16))
                dk_h = dot(ds, jnp.where(lanes_in, qs, 0.0).astype(BF16))
                dv = dv_h if dv is None else dv + dv_h
                dk = dk_h if dk is None else dk + dk_h
                pieces.append(dot(kt[64 * hh : 64 * hh + 64, :], ds))
            DQ[cols, lanes] = (jnp.concatenate(pieces, axis=0).T * (HEAD_DIM ** -0.5)).astype(BF16)
            ACC[0, keys, :] += dk
            ACC[1, keys, :] += dv

        @pl.when(b == c)
        def _():
            block(pl.ds(pl.multiple_of(256 * c, 256), 768))

        @pl.when(b != c)
        def _():
            block(slice(0, 1024))

        @pl.when((b == 1) & (ours == 0))
        def _():
            DKS[0, :, half_lanes] = ACC[0].astype(BF16)
            DKS[1, :, half_lanes] = ACC[1].astype(BF16)
            exchange(3 + turn, DKS.at[:, :, half_lanes], DKR.at[:, :, half_lanes])
            exchange(6 + turn, DQ.at[:, lanes], DQP.at[:, half_lanes])

        @pl.when((b == 1) & (ours == 1))
        def _():
            exchanged(3 + turn, DKR.at[:, :, half_lanes])
            DKF[0, :, half_lanes] = (ACC[0] + DKR[0, :, half_lanes].astype(F32)).astype(BF16)
            DKF[1, :, half_lanes] = (ACC[1] + DKR[1, :, half_lanes].astype(F32)).astype(BF16)
            exchange(9 + turn, DKF.at[:, their_rows, half_lanes], DKP.at[:, :, half_lanes])
            exchanged(6 + turn, DQP.at[:, half_lanes])
            RC[0, :, 0:128] = DQ[:, lanes]
            RC[1, :, 0:128] = DQP[:, half_lanes]
            for w in range(2):
                RC[0, :, 128 + 128 * w : 256 + 128 * w] = DKF[w, own_rows, half_lanes]
                RC[1, :, 128 + 128 * w : 256 + 128 * w] = DKF[w, their_rows, half_lanes]

            @pl.loop(0, 3, unroll=3)
            def _(t):
                tile = pl.ds(pl.multiple_of(256 * t, 256), 256)
                theirs = pl.ds(pl.multiple_of(1536 + 256 * t, 256), 256)
                out = pair_tn(X[:, tile], ACT[0, :, theirs], RC[0], RC[1])
                W[4 + (1 + turn) // 2, tile, pl.ds(pl.multiple_of(384 * ((1 + turn) % 2), 128), 384)] = out.astype(BF16)

        for k in range(12):
            if ("a", k) in SCHEDULE:
                @pl.when(i == k)
                def _():
                    serve("a", k)

    BG[0:1, :] = columns(DQ[...].astype(F32))
    BG[2:3, mine384] = columns(DKF[1].astype(F32))

    BS[...] = BG[...].astype(BF16)
    others = [(gg, rr, k) for k, (gg, rr) in enumerate(
        ((g, rp), (gx, r), (gx, rp), (gy, r), (gy, rp), (gd, r), (gd, rp)))]
    slot_of = 2 * g + c
    for gg, rr, k in others:
        remote(BS, BR.at[slot_of], b1s.at[0], b1r.at[0], (gg, rr)).start()
    BR[slot_of] = BS[...]

    serve("end")

    for k in range(3):
        exchanged(9 + k, DKP.at[:, :, 128 * k : 128 * k + 128])

    for i in range(3):
        cols = slice(256 * i, 256 * i + 256)
        total = R2[:, cols] + dot_nt(DQ[...], W[0, cols, :])
        for w in range(2):
            total = total + dot_nt(DKF[w, own_rows, :], W[1 + w, cols, mine384])
            total = total + dot_nt(DKP[w], W[1 + w, cols, theirs384])
        LO2[:, cols] = total.astype(BF16)
        serve("inp", i)

    remote(BR.at[0:7], BR.at[0:7], b1s.at[0], b1r.at[0], (g, rp)).wait_recv()
    total = BR[0].astype(F32)
    for k in range(1, 8):
        total = total + BR[k].astype(F32)
    BZ[0] = total.astype(BF16)

    @pl.when(outer)
    def _():
        remote(BZ.at[0], BZ.at[1], b1s.at[1], b1r.at[1], zdev(zin)).start()

    def small_chain():
        @pl.when(inner)
        def _():
            remote(BZ.at[1], BZ.at[1], b1s.at[1], b1r.at[1], zdev(zother)).wait_recv()
            BZ[2] = (BZ[0].astype(F32) + BZ[1].astype(F32)).astype(BF16)
            remote(BZ.at[2], BZ.at[3], b1s.at[1], b1r.at[2], zdev(zother)).start()

    def small_in():
        @pl.when(inner)
        def _():
            remote(BZ.at[3], BZ.at[3], b1s.at[1], b1r.at[2], zdev(zother)).wait_recv()
            BZ[4] = (BZ[2].astype(F32) + BZ[3].astype(F32)).astype(BF16)
            remote(BZ.at[4], BZ.at[1], b1s.at[2], b1r.at[1], zdev(zout)).start()

    def small_out():
        @pl.when(outer)
        def _():
            remote(BZ.at[1], BZ.at[1], b1s.at[1], b1r.at[1], zdev(zin)).wait_recv()
            BZ[4] = BZ[1]

    services.update(
        small_chain=lambda j: small_chain(), small_in=lambda j: small_in(), small_out=lambda j: small_out()
    )
    serve("tail")
    BT[...] = BZ[4].astype(F32)
    bt_copy = pltpu.make_async_copy(BT, BTo, osem.at[1])
    bt_copy.start()

    for j in range(CHUNKS):
        drain(j)
    halves = remote(To.at[c], To.at[1 - c], ts.at[0], tr.at[0], (g, rp))
    halves.wait_send()
    halves.wait_recv()
    pltpu.make_async_copy(To.at[c], To.at[c], osem.at[0]).wait()
    for slot, dst in ((0, DFP), (1, DHP), (2, DBP)):
        exchange_drain(slot, dst)
    for k in range(3):
        part = slice(128 * k, 128 * k + 128)
        exchange_drain(3 + k, DKR.at[:, :, part])
        exchange_drain(6 + k, DQP.at[:, part])
        exchange_drain(9 + k, DKP.at[:, :, part])
    give_back_drain(LO, LOo, los, lor)
    give_back_drain(LO2, GIo, gis, gir)
    remote(BR.at[0:7], BR.at[0:7], b1s.at[0], b1r.at[0], (g, rp)).wait_send()
    remote(BZ.at[0], BZ.at[0], b1s.at[1], b1r.at[1], zdev(zother)).wait_send()

    @pl.when(inner)
    def _():
        remote(BZ.at[0], BZ.at[0], b1s.at[2], b1r.at[1], zdev(zother)).wait_send()

    bt_copy.wait()


def sds(shape, dtype=BF16):
    return jax.ShapeDtypeStruct(shape, dtype)


def layer(*args):
    out = [
        sds((2, 256, 768)), sds((2, 256, 768)), sds((2, CHUNKS, 192, 384)), sds((16, 768), F32),
        sds((512, 768)), sds((512, 768)), sds((512, 768)),
    ]
    dma = pltpu.SemaphoreType.DMA
    v = pltpu.VMEM
    return pl.pallas_call(
        layer_kernel,
        out_shape=out,
        in_specs=[ANY] * 18,
        out_specs=[ANY] * len(out),
        scratch_shapes=[
            v((12, 768, 768), BF16), v((CHUNKS, 2, 96, 384), BF16), v((CHUNKS, 2, 192, 384), BF16),
            v((CHUNKS, 2, 192, 384), BF16),
            v((2, 512, 3072), BF16), v((512, 3072), BF16), v((512, 1536), BF16), v((512, 768), BF16),
            v((2, 1024, 768), BF16), v((1024, 512), F32), v((16, 512), F32),
            v((512, 768), F32), v((512, 768), F32), v((512, 768), BF16), v((16, 768), F32),
            v((512, 768), BF16), v((512, 384), BF16), v((512, 768), BF16), v((512, 384), BF16),
            v((512, 768), BF16), v((512, 384), BF16), v((2, 1024, 384), BF16),
            v((2, 1024, 384), BF16), v((2, 1024, 384), BF16), v((2, 512, 384), BF16),
            v((512, 768), BF16), v((2, 1024, 128), F32), v((16, 768), F32), v((8, 16, 768), BF16),
            v((16, 768), BF16), v((5, 16, 768), BF16), v((16, 768), F32),
            v((512, 768), BF16), v((512, 768), BF16), v((512, 768), BF16), v((256, 1024), F32), v((256, 1024), F32),
            v((256, 128), F32), v((256, 128), F32), v((512, 128), F32), v((8, 1024), F32), v((512, 128), F32),
            v((4, 2, 256), jnp.int32), v((4, 16, 768), BF16), v((len(SHARED), 3, 64, 384), BF16), v((2, 512, 384), BF16),
            *[v((192,), BF16)] * 8, v((768,), BF16),
            dma((12,)), dma((9,)), dma((CHUNKS,)), dma((CHUNKS,)), dma((CHUNKS,)), dma((CHUNKS,)), dma((CHUNKS, 2)),
            dma((2, 3)), dma((len(SHARED),)), dma((1,)), dma((1,)), dma((12,)), dma((12,)),
            dma((2,)), dma((2,)), dma((2,)), dma((2,)), dma((3,)), dma((3,)), dma((2,)),
            dma((GROUPS,)), dma((GROUPS, 6)), dma((2,)), dma((2,)), dma((4,)), dma((1,)),
            dma((1,)), dma((1,)), dma((2,)), dma((2,)), dma((1,)), dma((1,)), dma((4,)), dma((4,)),
        ],
        compiler_params=pltpu.CompilerParams(
            collective_id=0, has_side_effects=True, vmem_limit_bytes=67043328
        ),
    )(*args)


def spread_kernel(
    Ti, GIi, LOi, BTi,
    LOo, GIo, WQo, WKo, WVo, WOo, WUo, WDo, BQo, BVo, BOo, GAo, SAo, BUo, BDo, GFo, SFo,
    T, GI, LO, OUT, GIF, sem, osem,
):
    g = lax.axis_index("group")
    order = (0, 1, 2, 3, 4, 5, 6, 7, 8, 9, 10, 11)
    loads = []
    for j in order:
        loads.append(pltpu.make_async_copy(Ti.at[:, j], T.at[:, j], sem.at[j]))
    loads.append(pltpu.make_async_copy(GIi, GI, sem.at[12]))
    loads.append(pltpu.make_async_copy(LOi, LO, sem.at[13]))
    for copy in loads:
        copy.start()
    stores = []

    def store(src, dst):
        copy = pltpu.make_async_copy(src, dst, osem.at[len(stores)])
        copy.start()
        stores.append(copy)

    for j in range(9):
        loads[j].wait()
        for e in range(2):
            OUT[j, :, 384 * e : 384 * e + 384] = T[e, j].astype(F32)
        if j < 4:
            store(OUT.at[j], WDo.at[192 * j : 192 * j + 192, :])
        elif j < 8:
            for e in range(2):
                start = 1536 * e + 384 * (j - 4)
                store(OUT.at[j, :, 384 * e : 384 * e + 384], WUo.at[:, start : start + 384])
        else:
            store(OUT.at[j], WOo)
    for j in range(9, 12):
        loads[j].wait()
    for w, ref in enumerate((WQo, WKo, WVo)):
        for turn in range(3):
            for e in range(2):
                start = 384 * e + 128 * turn
                OUT[9 + w, :, start : start + 128] = T[e, 9 + turn, :, 128 * w : 128 * w + 128].astype(F32)
        store(OUT.at[9 + w], ref)
    loads[12].wait()
    GIF[...] = GI[...].astype(F32)
    store(GIF, GIo)
    loads[13].wait()
    store(LO, LOo)
    moved = pltpu.roll(BTi[...], (768 - 192 * g) % 768, 1)
    for row, ref in ((0, BQo), (2, BVo), (3, BOo), (4, GAo), (5, SAo), (6, BDo), (7, GFo), (8, SFo)):
        ref[...] = moved[row, 0:192]
    up = BTi[pl.ds(12 + g, 1), :]
    BUo[...] = up[0, :]
    for copy in stores:
        copy.wait()


def spread(totals, grad_input, layer_out, small):
    square = sds((192, 768), F32)
    short = sds((192,), F32)
    whole = pl.BlockSpec(memory_space=pltpu.VMEM)
    dma = pltpu.SemaphoreType.DMA
    return pl.pallas_call(
        spread_kernel,
        out_shape=[
            sds((2, 256, 768)), sds((2, 256, 768), F32), square, square, square, square,
            sds((192, 3072), F32), sds((768, 768), F32),
            short, short, short, short, short, sds((768,), F32), short, short, short,
        ],
        in_specs=[ANY, ANY, ANY, whole],
        out_specs=[ANY] * 8 + [whole] * 9,
        scratch_shapes=[
            pltpu.VMEM((2, CHUNKS, 192, 384), BF16), pltpu.VMEM((2, 256, 768), BF16), pltpu.VMEM((2, 256, 768), BF16),
            pltpu.VMEM((CHUNKS, 192, 768), F32), pltpu.VMEM((2, 256, 768), F32), dma((14,)), dma((20,)),
        ],
        compiler_params=pltpu.CompilerParams(vmem_limit_bytes=66000000),
    )(totals, grad_input, layer_out, small)


def fits(mesh):
    return dict(mesh.shape) == {"group": 4, "replica": 8}


def fast(
    tokens_in, doc_ids, out_grad, w_query, w_key, w_value, w_out, w_up, w_down, b_query, b_value, b_out,
    gain_attn, shift_attn, b_up, b_down, gain_ffn, shift_ffn,
):
    layer_out, grad_input, totals, small, *_ = layer(
        tokens_in, doc_ids, out_grad, w_query, w_key, w_value, w_out, w_up, w_down,
        b_query, b_value, b_out, gain_attn, shift_attn, b_down, gain_ffn, shift_ffn, b_up,
    )
    return tuple(spread(totals, grad_input, layer_out, small))


def layer_norm(values, gain, shift):
    centre = values - jnp.mean(values, axis=-1, keepdims=True)
    spread = jnp.mean(centre * centre, axis=-1, keepdims=True)
    return centre * lax.rsqrt(spread + EPSILON) * gain + shift


def norm_pull(values, gain, shift, grad):
    result, pullback = jax.vjp(
        layer_norm, values, gain.astype(jnp.float32), shift.astype(jnp.float32)
    )
    return (result, pullback(grad))


def exact_gelu(values):
    return jax.nn.gelu(values, approximate=False)


def project(inputs, weight, bias):
    return jnp.dot(inputs, weight, preferred_element_type=jnp.float32) + bias.astype(jnp.float32)


def contract_rows(left, right):
    return lax.dot_general(
        left, right, (((0,), (0,)), ((), ())), preferred_element_type=jnp.float32
    )


def against_rows(grad, weight):
    return lax.dot_general(
        grad, weight, (((1,), (1,)), ((), ())), preferred_element_type=jnp.float32
    )


def column_sum(values):
    return jnp.sum(values.astype(jnp.float32), axis=0)


def add_pair(first, second):
    return first + second


def scores_of(query, keys_all, allowed):
    rows = query.shape[0]
    length = keys_all.shape[0]
    scaling = HEAD_DIM ** (-0.5)
    scores = (
        jnp.einsum(
            "qhd,khd->hqk",
            query.reshape(rows, HEADS, HEAD_DIM),
            keys_all.reshape(length, HEADS, HEAD_DIM),
            preferred_element_type=jnp.float32,
        )
        * scaling
    )
    return jnp.where(allowed[None], scores, NEGATIVE)


def attention_forward(query, keys_all, values_all, allowed):
    rows = query.shape[0]
    length = keys_all.shape[0]
    scores = scores_of(query, keys_all, allowed)
    row_max = jnp.max(scores, axis=-1, keepdims=True)
    exponent = jnp.exp(scores - row_max)
    total = jnp.sum(exponent, axis=-1, keepdims=True)
    probs = (exponent / total).astype(jnp.bfloat16)
    log_total = row_max[..., 0] + jnp.log(total[..., 0])
    joined = jnp.einsum(
        "hqk,khd->qhd",
        probs,
        values_all.reshape(length, HEADS, HEAD_DIM),
        preferred_element_type=jnp.float32,
    )
    return (joined.reshape(rows, HEADS * HEAD_DIM), log_total)


def score_grads(query, keys_all, values_all, allowed, log_total, d_attended):
    rows = query.shape[0]
    length = keys_all.shape[0]
    scores = scores_of(query, keys_all, allowed)
    probs = jnp.exp(scores - log_total[..., None])
    d_heads = d_attended.reshape(rows, HEADS, HEAD_DIM)
    d_probs = jnp.einsum(
        "qhd,khd->hqk",
        d_heads,
        values_all.reshape(length, HEADS, HEAD_DIM),
        preferred_element_type=jnp.float32,
    )
    row_term = jnp.sum(probs * d_probs, axis=-1)
    d_scores = (probs * (d_probs - row_term[..., None])).astype(jnp.bfloat16)
    return (probs, d_scores, row_term)


def attention_backward(query, keys_all, values_all, allowed, log_total, d_attended):
    rows = query.shape[0]
    length = keys_all.shape[0]
    scaling = HEAD_DIM ** (-0.5)
    probs, d_scores, row_term = score_grads(
        query, keys_all, values_all, allowed, log_total, d_attended
    )
    d_heads = d_attended.reshape(rows, HEADS, HEAD_DIM)
    d_values_part = jnp.einsum(
        "hqk,qhd->khd", probs.astype(jnp.bfloat16), d_heads, preferred_element_type=jnp.float32
    ).reshape(length, HEADS * HEAD_DIM)
    d_query = (
        jnp.einsum(
            "hqk,khd->qhd",
            d_scores,
            keys_all.reshape(length, HEADS, HEAD_DIM),
            preferred_element_type=jnp.float32,
        ).reshape(rows, HEADS * HEAD_DIM)
        * scaling
    )
    d_keys_part = (
        jnp.einsum(
            "hqk,qhd->khd",
            d_scores,
            query.reshape(rows, HEADS, HEAD_DIM),
            preferred_element_type=jnp.float32,
        ).reshape(length, HEADS * HEAD_DIM)
        * scaling
    )
    return (d_query, d_keys_part, d_values_part, row_term)


def owner_sum(grads):
    return (
        lax.psum_scatter(
            grads[0].astype(jnp.bfloat16), "group", scatter_dimension=0, tiled=True
        ).astype(jnp.float32),
        lax.psum_scatter(
            grads[1].astype(jnp.bfloat16), "group", scatter_dimension=0, tiled=True
        ).astype(jnp.float32),
        lax.psum_scatter(
            grads[2].astype(jnp.bfloat16), "group", scatter_dimension=0, tiled=True
        ).astype(jnp.float32),
        lax.psum_scatter(
            grads[3].astype(jnp.bfloat16), "group", scatter_dimension=0, tiled=True
        ).astype(jnp.float32),
        lax.psum_scatter(
            grads[4].astype(jnp.bfloat16), "group", scatter_dimension=0, tiled=True
        ).astype(jnp.float32),
        lax.psum_scatter(
            grads[5].astype(jnp.bfloat16), "group", scatter_dimension=0, tiled=True
        ).astype(jnp.float32),
        lax.psum_scatter(
            grads[6].astype(jnp.bfloat16), "group", scatter_dimension=0, tiled=True
        ).astype(jnp.float32),
        lax.psum_scatter(
            grads[7].astype(jnp.bfloat16), "group", scatter_dimension=0, tiled=True
        ).astype(jnp.float32),
        lax.psum_scatter(
            grads[8].astype(jnp.bfloat16), "group", scatter_dimension=0, tiled=True
        ).astype(jnp.float32),
        lax.psum_scatter(
            grads[9].astype(jnp.bfloat16), "group", scatter_dimension=0, tiled=True
        ).astype(jnp.float32),
        lax.psum_scatter(
            grads[10].astype(jnp.bfloat16), "group", scatter_dimension=0, tiled=True
        ).astype(jnp.float32),
        lax.psum_scatter(
            grads[11].astype(jnp.bfloat16), "group", scatter_dimension=0, tiled=True
        ).astype(jnp.float32),
        lax.psum_scatter(
            grads[12].astype(jnp.bfloat16), "group", scatter_dimension=0, tiled=True
        ).astype(jnp.float32),
        lax.psum_scatter(
            grads[13].astype(jnp.bfloat16), "group", scatter_dimension=0, tiled=True
        ).astype(jnp.float32),
        lax.psum_scatter(
            grads[14].astype(jnp.bfloat16), "group", scatter_dimension=0, tiled=True
        ).astype(jnp.float32),
    )


def shards(
    tokens_in,
    doc_ids,
    out_grad,
    w_query,
    w_key,
    w_value,
    w_out,
    w_up,
    w_down,
    b_query,
    b_value,
    b_out,
    gain_attn,
    shift_attn,
    b_up,
    b_down,
    gain_ffn,
    shift_ffn,
):
    gathered = (
        lax.all_gather(w_query, "group", axis=0, tiled=True),
        lax.all_gather(w_key, "group", axis=0, tiled=True),
        lax.all_gather(w_value, "group", axis=0, tiled=True),
        lax.all_gather(w_out, "group", axis=0, tiled=True),
        lax.all_gather(w_up, "group", axis=0, tiled=True),
        lax.all_gather(w_down, "group", axis=0, tiled=True),
        lax.all_gather(b_query, "group", axis=0, tiled=True),
        lax.all_gather(b_value, "group", axis=0, tiled=True),
        lax.all_gather(b_out, "group", axis=0, tiled=True),
        lax.all_gather(gain_attn, "group", axis=0, tiled=True),
        lax.all_gather(shift_attn, "group", axis=0, tiled=True),
        lax.all_gather(b_up, "group", axis=0, tiled=True),
        lax.all_gather(b_down, "group", axis=0, tiled=True),
        lax.all_gather(gain_ffn, "group", axis=0, tiled=True),
        lax.all_gather(shift_ffn, "group", axis=0, tiled=True),
    )
    (
        query_weight,
        key_weight,
        value_weight,
        out_weight,
        up_weight,
        down_weight,
        query_bias,
        value_bias,
        out_bias,
        attn_gain,
        attn_shift,
        up_bias,
        down_bias,
        ffn_gain,
        ffn_shift,
    ) = gathered
    micros = tokens_in.shape[0]
    outputs = []
    stored = []
    for micro in range(micros):
        inputs = tokens_in[micro]
        segment = doc_ids[micro]
        query = project(inputs, query_weight, query_bias).astype(jnp.bfloat16)
        keys = jnp.dot(inputs, key_weight, preferred_element_type=jnp.float32).astype(jnp.bfloat16)
        values = project(inputs, value_weight, value_bias).astype(jnp.bfloat16)
        keys_all, values_all, seg_all = (
            lax.all_gather(keys, "group", axis=0, tiled=True),
            lax.all_gather(values, "group", axis=0, tiled=True),
            lax.all_gather(segment, "group", axis=0, tiled=True),
        )
        allowed = segment[:, None] == seg_all[None, :]
        attended, log_total = attention_forward(query, keys_all, values_all, allowed)
        attended = attended.astype(jnp.bfloat16)
        resid_one = inputs.astype(jnp.float32) + project(attended, out_weight, out_bias)
        normed = layer_norm(
            resid_one, attn_gain.astype(jnp.float32), attn_shift.astype(jnp.float32)
        )
        hidden = project(normed.astype(jnp.bfloat16), up_weight, up_bias)
        activated = exact_gelu(hidden).astype(jnp.bfloat16)
        resid_two = normed + project(activated, down_weight, down_bias)
        result = layer_norm(resid_two, ffn_gain.astype(jnp.float32), ffn_shift.astype(jnp.float32))
        outputs.append(result.astype(jnp.bfloat16))
        stored.append((query, keys, values, log_total, attended, resid_one, hidden, resid_two))
    gathered = (
        lax.all_gather(w_query, "group", axis=0, tiled=True),
        lax.all_gather(w_key, "group", axis=0, tiled=True),
        lax.all_gather(w_value, "group", axis=0, tiled=True),
        lax.all_gather(w_out, "group", axis=0, tiled=True),
        lax.all_gather(w_up, "group", axis=0, tiled=True),
        lax.all_gather(w_down, "group", axis=0, tiled=True),
        lax.all_gather(b_query, "group", axis=0, tiled=True),
        lax.all_gather(b_value, "group", axis=0, tiled=True),
        lax.all_gather(b_out, "group", axis=0, tiled=True),
        lax.all_gather(gain_attn, "group", axis=0, tiled=True),
        lax.all_gather(shift_attn, "group", axis=0, tiled=True),
        lax.all_gather(b_up, "group", axis=0, tiled=True),
        lax.all_gather(b_down, "group", axis=0, tiled=True),
        lax.all_gather(gain_ffn, "group", axis=0, tiled=True),
        lax.all_gather(shift_ffn, "group", axis=0, tiled=True),
    )
    (
        query_weight,
        key_weight,
        value_weight,
        out_weight,
        up_weight,
        down_weight,
        query_bias,
        value_bias,
        out_bias,
        attn_gain,
        attn_shift,
        up_bias,
        down_bias,
        ffn_gain,
        ffn_shift,
    ) = gathered
    totals = tuple((jnp.zeros(member.shape, jnp.float32) for member in gathered))
    input_grads = []
    for micro in range(micros):
        inputs = tokens_in[micro]
        segment = doc_ids[micro]
        query, keys, values, log_total, attended, resid_one, hidden, resid_two = stored[micro]
        upstream = out_grad[micro].astype(jnp.float32)
        unused_out, (d_resid_two, g_ffn_gain, g_ffn_shift) = norm_pull(
            resid_two, ffn_gain, ffn_shift, upstream
        )
        d_ffn = d_resid_two.astype(jnp.bfloat16)
        activated, gelu_pull = jax.vjp(exact_gelu, hidden)
        activated = activated.astype(jnp.bfloat16)
        g_down_w = contract_rows(activated, d_ffn)
        g_down_b = column_sum(d_ffn)
        d_activated = against_rows(d_ffn, down_weight)
        d_hidden = gelu_pull(d_activated)[0].astype(jnp.bfloat16)
        normed = layer_norm(
            resid_one, attn_gain.astype(jnp.float32), attn_shift.astype(jnp.float32)
        )
        normed_low = normed.astype(jnp.bfloat16)
        g_up_w = contract_rows(normed_low, d_hidden)
        g_up_b = column_sum(d_hidden)
        d_normed = against_rows(d_hidden, up_weight) + d_resid_two
        unused_norm, (d_resid_one, g_attn_gain, g_attn_shift) = norm_pull(
            resid_one, attn_gain, attn_shift, d_normed
        )
        d_branch = d_resid_one.astype(jnp.bfloat16)
        g_out_w = contract_rows(attended, d_branch)
        g_out_b = column_sum(d_branch)
        d_attended = against_rows(d_branch, out_weight).astype(jnp.bfloat16)
        keys_all, values_all, seg_all = (
            lax.all_gather(keys, "group", axis=0, tiled=True),
            lax.all_gather(values, "group", axis=0, tiled=True),
            lax.all_gather(segment, "group", axis=0, tiled=True),
        )
        allowed = segment[:, None] == seg_all[None, :]
        d_query, d_keys_part, d_values_part, row_term = attention_backward(
            query, keys_all, values_all, allowed, log_total, d_attended
        )
        d_keys, d_values = (
            lax.psum_scatter(
                d_keys_part.astype(jnp.bfloat16), "group", scatter_dimension=0, tiled=True
            ).astype(jnp.float32),
            lax.psum_scatter(
                d_values_part.astype(jnp.bfloat16), "group", scatter_dimension=0, tiled=True
            ).astype(jnp.float32),
        )
        d_query = d_query.astype(jnp.bfloat16)
        d_keys = d_keys.astype(jnp.bfloat16)
        d_values = d_values.astype(jnp.bfloat16)
        g_query_w = contract_rows(inputs, d_query)
        g_key_w = contract_rows(inputs, d_keys)
        g_value_w = contract_rows(inputs, d_values)
        g_query_b = column_sum(d_query)
        g_value_b = column_sum(d_values)
        input_grad = (
            d_resid_one
            + against_rows(d_query, query_weight)
            + against_rows(d_keys, key_weight)
            + against_rows(d_values, value_weight)
        )
        input_grads.append(input_grad)
        micro_grads = (
            g_query_w,
            g_key_w,
            g_value_w,
            g_out_w,
            g_up_w,
            g_down_w,
            g_query_b,
            g_value_b,
            g_out_b,
            g_attn_gain,
            g_attn_shift,
            g_up_b,
            g_down_b,
            g_ffn_gain,
            g_ffn_shift,
        )
        totals = jax.tree.map(add_pair, totals, micro_grads)
    totals = tuple(owner_sum(totals))
    summed = (
        lax.psum(totals[0].astype(jnp.bfloat16), "replica").astype(jnp.float32),
        lax.psum(totals[1].astype(jnp.bfloat16), "replica").astype(jnp.float32),
        lax.psum(totals[2].astype(jnp.bfloat16), "replica").astype(jnp.float32),
        lax.psum(totals[3].astype(jnp.bfloat16), "replica").astype(jnp.float32),
        lax.psum(totals[4].astype(jnp.bfloat16), "replica").astype(jnp.float32),
        lax.psum(totals[5].astype(jnp.bfloat16), "replica").astype(jnp.float32),
        lax.psum(totals[6].astype(jnp.bfloat16), "replica").astype(jnp.float32),
        lax.psum(totals[7].astype(jnp.bfloat16), "replica").astype(jnp.float32),
        lax.psum(totals[8].astype(jnp.bfloat16), "replica").astype(jnp.float32),
        lax.psum(totals[9].astype(jnp.bfloat16), "replica").astype(jnp.float32),
        lax.psum(totals[10].astype(jnp.bfloat16), "replica").astype(jnp.float32),
        lax.psum(totals[11].astype(jnp.bfloat16), "replica").astype(jnp.float32),
        lax.psum(totals[12].astype(jnp.bfloat16), "replica").astype(jnp.float32),
        lax.psum(totals[13].astype(jnp.bfloat16), "replica").astype(jnp.float32),
        lax.psum(totals[14].astype(jnp.bfloat16), "replica").astype(jnp.float32),
    )
    layer_out = jnp.stack(outputs)
    grad_input = jnp.stack(input_grads)
    return (
        layer_out,
        grad_input,
        summed[0],
        summed[1],
        summed[2],
        summed[3],
        summed[4],
        summed[5],
        summed[6],
        summed[7],
        summed[8],
        summed[9],
        summed[10],
        summed[11],
        summed[12],
        summed[13],
        summed[14],
    )


def solution(mesh):
    return jax.shard_map(
        shards if not fits(mesh) else fast,
        mesh=mesh,
        in_specs=(
            P("replica", "group", None),
            P("replica", "group"),
            P("replica", "group", None),
            P("group", None),
            P("group", None),
            P("group", None),
            P("group", None),
            P("group", None),
            P("group", None),
            P("group"),
            P("group"),
            P("group"),
            P("group"),
            P("group"),
            P("group"),
            P("group"),
            P("group"),
            P("group"),
        ),
        out_specs=(
            P("replica", "group", None),
            P("replica", "group", None),
            P("group", None),
            P("group", None),
            P("group", None),
            P("group", None),
            P("group", None),
            P("group", None),
            P("group"),
            P("group"),
            P("group"),
            P("group"),
            P("group"),
            P("group"),
            P("group"),
            P("group"),
            P("group"),
        ),
        check_vma=False,
    )
```

```python
import functools

import jax
import jax.numpy as jnp
from jax import lax
from jax.experimental import pallas as pl
from jax.experimental.pallas import tpu as pltpu
from jax.sharding import PartitionSpec as P

HEADS = 12
HEAD_DIM = 64
EPSILON = 1e-05
NEGATIVE = -1e30
F32 = jnp.float32
BF16 = jnp.bfloat16
MESH = pl.DeviceIdType.MESH
ANY = pl.BlockSpec(memory_space=pl.ANY)


class Place:
    def __init__(self):
        self.g = lax.axis_index("group")
        self.r = lax.axis_index("replica")
        self.c = self.r % 2
        self.z = self.r // 2
        self.gx = self.g + 1 - 2 * (self.g % 2)
        self.gy = self.g + 2 - 4 * (self.g // 2)
        self.gd = 3 - self.g
        self.rp = self.r + 1 - 2 * self.c


def remote(src, dst, send, recv, device):
    return pltpu.make_async_remote_copy(
        src_ref=src, dst_ref=dst, send_sem=send, recv_sem=recv, device_id=device, device_id_type=MESH
    )


def plane_barrier(place, extra=()):
    barrier = pltpu.get_barrier_semaphore()
    for g in (place.g, place.gx, place.gy, place.gd):
        for r in (place.r, place.rp):
            if g is place.g and r is place.r:
                continue
            pl.semaphore_signal(barrier, inc=1, device_id=(g, r), device_id_type=MESH)
    return barrier


def dot(a, b):
    return jnp.dot(a, b, preferred_element_type=F32)


def norm_parts(values):
    centre = values - jnp.mean(values, axis=-1, keepdims=True)
    spread = jnp.mean(centre * centre, axis=-1, keepdims=True)
    inverse = lax.rsqrt(spread + EPSILON)
    return centre * inverse, inverse


def dot_nt(a, b):
    return lax.dot_general(a, b, (((1,), (1,)), ((), ())), preferred_element_type=F32)


def dot_tn(a, b):
    return lax.dot_general(a, b, (((0,), (0,)), ((), ())), preferred_element_type=F32)


def columns(values):
    return jnp.sum(values, axis=0, keepdims=True)


CHUNKS = 12


SHARED = (2, 3, 5, 7,)
SCHEDULE = {
    ("down", 0): (
        ("first", 0), ("first", 1),
    ),
    ("down", 1): (
        ("plain", 0), ("plain", 1), ("share", 2), ("share", 3),
    ),
    ("down", 2): (
        ("passed", 0),
    ),
    ("normed",): (
        ("passed", 1), ("shared", 2), ("first", 2), ("plain", 2),
    ),
    ("up", 4): (
        ("first", 4), ("plain", 4), ("own", 0), ("shared", 3),
        ("first", 3), ("plain", 3),
    ),
    ("up", 5): (
        ("share", 5), ("own", 1), ("passed", 2),
    ),
    ("up", 6): (
        ("first", 6), ("plain", 6),
    ),
    ("up", 7): (
        ("share", 7), ("passed", 4),
    ),
    ("datt",): (
        ("chain", 0),
    ),
    ("sq", 8): (
        ("first", 8), ("plain", 8), ("passed", 3), ("shared", 5),
        ("first", 5), ("plain", 5),
    ),
    ("a", 0): (
        ("own", 2),
    ),
    ("a", 1): (
        ("chain", 1), ("fin_in", 0), ("passed", 6),
    ),
    ("a", 2): (
        ("own", 4), ("shared", 7), ("first", 7), ("plain", 7),
    ),
    ("a", 3): (
        ("first", 9), ("plain", 9), ("own", 3), ("chain", 2),
        ("fin_in", 1),
    ),
    ("a", 4): (
        ("chain", 4), ("fin_out", 0), ("passed", 5),
    ),
    ("a", 5): (
        ("own", 6), ("passed", 7), ("passed", 8),
    ),
    ("a", 6): (
        ("chain", 3), ("fin_in", 2), ("fin_out", 1),
    ),
    ("a", 7): (
        ("first", 10), ("plain", 10), ("own", 5), ("own", 7),
        ("chain", 6),
    ),
    ("a", 8): (
        ("own", 8), ("fin_in", 3), ("fin_in", 4),
    ),
    ("a", 9): (
        ("chain", 5), ("fin_out", 2), ("passed", 9),
    ),
    ("a", 10): (
        ("fin_in", 6), ("passed", 10), ("chain", 7),
    ),
    ("a", 11): (
        ("first", 11), ("plain", 11), ("own", 9), ("own", 10),
        ("chain", 8),
    ),
    ("end",): (
        ("fin_in", 5), ("fin_out", 3), ("fin_out", 4),
    ),
    ("inp", 2): (
        ("chain", 9), ("fin_in", 7), ("fin_out", 6), ("passed", 11),
    ),
    ("tail",): (
        ("fin_in", 8), ("gi", 0), ("small_chain", 0), ("chain", 10),
        ("fin_out", 5), ("own", 11), ("small_in", 0), ("fin_in", 9),
        ("fin_out", 7), ("chain", 11), ("fin_in", 10), ("fin_out", 8),
        ("fin_out", 9), ("fin_in", 11), ("fin_out", 10), ("fin_out", 11),
        ("small_out", 0),
    ),
}

GATHER = {
    ("pre",): (
        ("relay", 0), ("x1", 0), ("diagonal", 0), ("own", 1),
        ("jn", 0), ("jf", 0), ("own", 2), ("relay", 1),
    ),
    ("kv",): (
        ("own", 3),
    ),
    ("q",): (
        ("jn", 1), ("relay", 2),
    ),
    ("a", 0): (
        ("diagonal", 1),
    ),
    ("a", 1): (
        ("own", 4),
    ),
    ("a", 4): (
        ("relay", 3), ("jn", 2),
    ),
    ("a", 5): (
        ("jf", 1),
    ),
    ("a", 6): (
        ("diagonal", 2),
    ),
    ("a", 8): (
        ("own", 5),
    ),
    ("a", 10): (
        ("relay", 4), ("jn", 3),
    ),
    ("up",): (
        ("diagonal", 3), ("jf", 2), ("relay", 5), ("g", 0),
        ("jn", 4), ("diagonal", 4), ("jf", 3),
    ),
    ("u", 1): (
        ("diagonal", 5),
    ),
    ("u", 7): (
        ("jn", 5),
    ),
    ("df",): (
        ("jf", 4), ("jf", 5),
    ),
}


GROUPS = 6


def piece_of(W, k, chip, core, first=0, count=3):
    if k < 4:
        lo, hi = ((0, 3), (3, 4), (4, 6), (6, 8))[k]
        return W.at[lo:hi, pl.ds(pl.multiple_of(192 * chip + 96 * core + 32 * first, 16), 32 * count), :]
    start = 384 * (k - 4) + 192 * core + 64 * first
    return W.at[8 + chip, pl.ds(pl.multiple_of(start, 16), 64 * count), :]


def layer_kernel(
    tok, docs_in, og, wq, wk, wv, wo, wup, wdn,
    bq_in, bv_in, bo_in, ga_in, sa_in, bd_in, gf_in, sf_in, bu_in,
    LOo, GIo, To, BTo, Xo, ATo, NLo,
    W, P1, P2, ZR, ACT, GP, DHP, Q, KV, MASK, LSE, R1, R2, G, PF,
    DF, DFP, DB, DBP, DQ, DQP, DKS, DKR, DKF, DKP, LO, ACC, BG, BR, BS, BZ, BT,
    X, AT, NL, SA, SB, PA, PB, DC, DR, LC, D, PK, ZF, RC, bq, bv, bo, ga, sa, bd, gf, sf, bu,
    lsem, vsem, hops, p1r, p2r, zs, zr, zl, zfr, ts, tr, xs_, xr_, los, lor, gis, gir, b1s, b1r, osem,
    ags, agr, xs, xr, ds_, dr, ps, pr, gs, gr, kvs, kvr, lls, llr,
):
    DATT, LO2 = G, NL
    me = Place()
    g, r, c, z = me.g, me.r, me.c, me.z
    gx, gy, gd, rp = me.gx, me.gy, me.gd, me.rp
    outer = (z == 0) | (z == 3)
    inner = jnp.logical_not(outer)
    zin, zout, zother = 1 + z // 3, 3 * (z - 1), 3 - z
    zp = z % 2
    rz = r + 2 - 4 * zp

    def zdev(zz):
        return (g, 2 * zz + c)

    barrier = plane_barrier(me)
    pl.semaphore_signal(barrier, inc=1, device_id=(g, rz), device_id_type=MESH)

    @pl.when(inner)
    def _():
        pl.semaphore_signal(barrier, inc=1, device_id=zdev(zother), device_id_type=MESH)

    vectors = []
    for i, (src, dst) in enumerate((
        (bq_in, bq), (bv_in, bv), (bo_in, bo), (ga_in, ga), (sa_in, sa), (bd_in, bd), (gf_in, gf), (sf_in, sf), (bu_in, bu),
    )):
        vectors.append(pltpu.make_async_copy(src, dst, vsem.at[i]))
        vectors[-1].start()

    local = []
    for w, ref in enumerate((wq, wk, wv, wo)):
        local.append((ref, W.at[w, pl.ds(pl.multiple_of(192 * g, 16), 192), :]))
    for u in range(4):
        local.append((wup.at[:, 768 * u : 768 * u + 768], W.at[4 + u, pl.ds(pl.multiple_of(192 * g, 16), 192), :]))
    local.append((wdn, W.at[8 + g]))
    local = [pltpu.make_async_copy(a, b, lsem.at[i]) for i, (a, b) in enumerate(local)]
    for copy in local:
        copy.start()

    own_lane = lax.broadcasted_iota(jnp.int32, (1, 768), 1) // 192 == g
    for copy in vectors:
        copy.wait()
    for row, ref in ((0, bq), (2, bv), (3, bo), (4, ga), (5, sa), (6, bd), (7, gf), (8, sf)):
        piece = ref[...].astype(F32).reshape(1, 192)
        PF[row : row + 1, :] = jnp.where(own_lane, jnp.concatenate([piece] * 4, axis=1), 0.0)
    for row in (1, 9, 10, 11):
        PF[row : row + 1, :] = jnp.zeros((1, 768), F32)
    tall = lax.broadcasted_iota(jnp.int32, (4, 768), 0) == g
    PF[12:16, :] = jnp.where(tall, bu[...].astype(F32).reshape(1, 768), 0.0)
    PK[g] = PF[...].astype(BF16)

    BG[...] = jnp.zeros_like(BG)
    pl.semaphore_wait(barrier, 9 - z // 3 - (3 - z) // 3)

    def reshard(src, dst_of, ssem, rsem, blocks=(0, 1)):
        for m in blocks:
            t, e = 2 * c + m, g // 2
            b = g % 2
            here = (t == g) & (e == c)
            src_m = src.at[m]
            dst_b = dst_of(b)

            @pl.when(jnp.logical_not(here))
            def _():
                remote(src_m, dst_b, ssem.at[m], rsem.at[b], (t, 2 * z + e)).start()

            @pl.when(here)
            def _():
                pltpu.make_async_copy(src_m, dst_b, rsem.at[b]).start()

    def reshard_wait(src, dst_of, ssem, rsem, b):
        remote(src.at[0], dst_of(b), ssem.at[0], rsem.at[b], (g, r)).wait_recv()

    def reshard_drain(src, dst_of, ssem, rsem):
        for m in range(2):
            t, e = 2 * c + m, g // 2
            here = (t == g) & (e == c)

            @pl.when(jnp.logical_not(here))
            def _():
                remote(src.at[m], dst_of(0), ssem.at[m], rsem.at[0], (t, 2 * z + e)).wait_send()

    def x_rows(b):
        if isinstance(b, int):
            return X.at[256 * b : 256 * b + 256, :]
        return X.at[pl.ds(pl.multiple_of(256 * b, 256), 256), :]

    def g_rows(b):
        if isinstance(b, int):
            return G.at[256 * b : 256 * b + 256, :]
        return G.at[pl.ds(pl.multiple_of(256 * b, 256), 256), :]

    for m in range(2):
        for e in range(2):
            t = 2 * c + m
            here = (t == g) & (c == e)

            @pl.when(jnp.logical_not(here))
            def _():
                remote(docs_in, D.at[g], ds_.at[2 * m + e], dr.at[0], (t, 2 * z + e)).start()

            @pl.when(here)
            def _():
                pltpu.make_async_copy(docs_in, D.at[g], dr.at[0]).start()

    def pass_on(k, slot, part, device):
        remote(part, part, ags.at[k], agr.at[k, slot], device).start()

    def landed(k, slot, count):
        rows = 32 * count
        size = W.at[0:3, 0:rows, :] if k == 0 else W.at[0:1, 0:rows, :] if k == 1 else W.at[0:2, 0:rows, :]
        remote(size, size, ags.at[k], agr.at[k, slot], (g, rp)).wait_recv()

    def own_send(k):
        part = piece_of(W, k, g, c, zp, 2)
        pass_on(k, 0, part, (gx, r))
        pass_on(k, 0, part, (gy, r))

    def relay(k):
        landed(k, 0, 4)
        pass_on(k, 1, piece_of(W, k, gx, c, zp, 1), (gy, r))
        pass_on(k, 1, piece_of(W, k, gy, c, zp + 1, 1), (gx, r))
        pass_on(k, 2, piece_of(W, k, gx, c, 2 * zp, 1), (g, rz))
        pass_on(k, 2, piece_of(W, k, gy, c, 2 * zp, 1), (g, rz))

    def diagonal(k):
        landed(k, 1, 2)
        pass_on(k, 3, piece_of(W, k, gd, c, 2 * zp, 1), (g, rz))

    def join_near(k):
        landed(k, 2, 2)
        for chip in (gx, gy):
            pass_on(k, 4, piece_of(W, k, chip, c), (g, rp))

    def join_far(k):
        landed(k, 3, 1)
        pass_on(k, 5, piece_of(W, k, gd, c), (g, rp))

    def complete_near(k):
        landed(k, 4, 6)

    def complete_far(k):
        landed(k, 5, 3)

    def complete(k):
        complete_near(k)
        complete_far(k)

    def gather_serve(*slot):
        for name, k in GATHER.get(slot, ()):
            gather_services[name](k)

    gather_services = {
        "own": own_send, "relay": relay, "diagonal": diagonal, "jn": join_near, "jf": join_far,
        "x1": lambda k: reshard(tok, x_rows, xs, xr, (1,)), "g": lambda k: reshard(og, g_rows, gs, gr),
    }

    def gather_drain(k):
        rows = 32 * 18
        size = W.at[0:3, 0:rows, :] if k == 0 else W.at[0:1, 0:rows, :] if k == 1 else W.at[0:2, 0:rows, :]
        remote(size, size, ags.at[k], agr.at[k, 0], (g, rp)).wait_send()

    for slot, chip in enumerate((gx, gy, gd)):
        remote(PK.at[g], PK.at[g], ps.at[0], pr.at[0], (chip, r)).start()
    for i in range(3):
        local[i].wait()
    own_send(0)
    reshard(tok, x_rows, xs, xr, (0,))
    for i in range(3, 9):
        local[i].wait()

    remote(PK.at[0:3], PK.at[0:3], ps.at[0], pr.at[0], (gx, r)).wait_recv()
    PF[...] = PK[0].astype(F32) + PK[1].astype(F32) + PK[2].astype(F32) + PK[3].astype(F32)
    remote(D, D, ds_.at[0], dr.at[0], (g, r)).wait_recv()
    for b in range(2):
        row = jnp.broadcast_to(D[2 * c + b, pl.ds(g % 2, 1), :].astype(F32), (128, 256))
        DC[256 * b : 256 * b + 256, :] = row.T
    for i in range(4):
        DR[:, 256 * i : 256 * i + 256] = jnp.broadcast_to(D[i, pl.ds(g % 2, 1), :].astype(F32), (8, 256))
    for i in range(4):
        keys = jnp.broadcast_to(D[i, pl.ds(g % 2, 1), :].astype(F32), (8, 256)).T[:, 0:1]
        for b in range(2):
            rows = D[2 * c + b, pl.ds(g % 2, 1), :].astype(F32)
            MASK[256 * i : 256 * i + 256, 256 * b : 256 * b + 256] = jnp.where(keys == rows, 0.0, NEGATIVE)
    gather_serve("pre")
    for b in range(2):
        reshard_wait(tok, x_rows, xs, xr, b)
    remote(X, Xo, lls.at[0], llr.at[0], (g, rp)).start()
    complete(0)
    own_rows = pl.ds(pl.multiple_of(512 * c, 512), 512)
    their_rows = pl.ds(pl.multiple_of(512 * (1 - c), 512), 512)

    def project(w, t, dst):
        cols = pl.ds(pl.multiple_of(256 * t, 256), 256)
        out = dot(X[...], W[w, :, cols]) + PF[pl.ds(w, 1), cols]
        return cols, out.astype(BF16)

    @pl.loop(0, 6, unroll=3)
    def _(i):
        w = i // 3
        cols, out = project(1 + w, i % 3, None)
        KV[w, own_rows, cols] = out

    for w in range(2):
        piece = KV.at[w, own_rows, :]
        remote(piece, piece, kvs.at[0], kvr.at[0], (g, rp)).start()
    gather_serve("kv")

    @pl.loop(0, 3, unroll=3)
    def _(i):
        cols, out = project(0, i, None)
        Q[:, cols] = out

    gather_serve("q")
    part = KV.at[:, their_rows, :]
    remote(part, part, kvs.at[0], kvr.at[0], (g, rp)).wait_recv()

    def at_step(i):
        pair, b = i // 2, i % 2
        return pair, pl.ds(pl.multiple_of(128 * pair, 128), 128), pl.ds(pl.multiple_of(256 * b, 256), 256)

    left_lanes = lax.broadcasted_iota(jnp.int32, (256, 128), 1) < 64

    def score(i, hh, S, peaks):
        pair, lanes, rows = at_step(i)
        q = Q[rows, lanes].astype(F32) * (HEAD_DIM ** -0.5)
        qh = jnp.where(left_lanes if hh == 0 else jnp.logical_not(left_lanes), q, 0.0).astype(BF16)
        s = dot_nt(qh, KV[0, :, lanes])
        s = jnp.where(DC[rows, 0:1] == DR[0:1, :], s, NEGATIVE)
        S[...] = s
        peaks[...] = jnp.broadcast_to(jnp.max(s, axis=1, keepdims=True), (256, 128))

    def soften(i, hh, S, peaks, vp):
        pair, lanes, rows = at_step(i)
        peak = peaks[...]
        e = jnp.exp(S[...] - peak[:, 0:1])
        total = jnp.sum(e, axis=1, keepdims=True)
        lane = lax.broadcasted_iota(jnp.int32, (256, 128), 1)
        LC[rows, :] = jnp.where(lane == 2 * pair + hh, peak + jnp.log(total), LC[rows, :])
        return dot(e.astype(BF16), vp) / total

    LC[...] = jnp.zeros_like(LC)
    score(0, 0, SA, PA)

    @pl.loop(0, 12)
    def _(i):
        pair, lanes, rows = at_step(i)
        vp = KV[1, :, lanes]
        score(i, 1, SB, PB)
        out0 = soften(i, 0, SA, PA, vp)
        score((i + 1) % 12, 0, SA, PA)
        out1 = soften(i, 1, SB, PB, vp)
        AT[rows, lanes] = jnp.where(left_lanes, out0, out1).astype(BF16)

        for k in range(12):
            if ("a", k) in GATHER:
                @pl.when(i == k)
                def _():
                    gather_serve("a", k)

    LSE[...] = LC[...].T[0:16, :]
    remote(AT, ATo, lls.at[1], llr.at[1], (g, rp)).start()
    gather_serve("out")
    complete(1)

    @pl.loop(0, 2)
    def _(i):
        rows = pl.ds(pl.multiple_of(256 * i, 256), 256)
        first = X[rows, :].astype(F32) + dot(AT[rows, :], W[3]) + PF[3:4, :]
        R1[rows, :] = first
        shape, _ = norm_parts(first)
        normed = shape * PF[4:5, :] + PF[5:6, :]
        R2[rows, :] = normed + PF[6:7, :]
        NL[rows, :] = normed.astype(BF16)

    remote(NL, NLo, lls.at[2], llr.at[2], (g, rp)).start()
    gather_serve("up")
    complete(2)
    complete(3)

    def up(t):
        u, tt = t // 3, t % 3
        cols = pl.ds(pl.multiple_of(256 * tt, 256), 256)
        wide = pl.ds(pl.multiple_of(256 * t, 256), 256)
        h = dot(NL[...], W[4 + u, :, cols]) + PF[pl.ds(12 + u, 1), cols]
        cdf = 0.5 * (1.0 + lax.erf(h * (0.5 ** 0.5)))
        ACT[c, :, wide] = (h * cdf).astype(BF16)
        GP[:, wide] = (cdf + h * jnp.exp(-0.5 * h * h) * 0.3989422804014327).astype(BF16)

    @pl.loop(0, 12)
    def _(t):
        up(t)

        for k in range(12):
            if ("u", k) in GATHER:
                @pl.when(t == k)
                def _():
                    gather_serve("u", k)

    remote(ACT.at[c], ACT.at[c], lls.at[3], llr.at[3], (g, rp)).start()

    def down(k):
        deep = pl.ds(pl.multiple_of(768 * k, 256), 768)

        @pl.loop(0, 3, unroll=3)
        def _(tt):
            cols = pl.ds(pl.multiple_of(256 * tt, 256), 256)
            R2[:, cols] += dot(ACT[c, :, deep], W[8 + k, :, cols])

    down(g)
    gather_serve("dn")
    complete_near(4)
    complete_near(5)
    down(gx)
    down(gy)
    gather_serve("df")
    complete_far(4)
    complete_far(5)
    down(gd)
    gather_serve("G")

    def forward_drain():
        reshard_drain(tok, x_rows, xs, xr)
        reshard_drain(og, g_rows, gs, gr)
        for m in range(2):
            for e in range(2):
                t = 2 * c + m
                here = (t == g) & (c == e)

                @pl.when(jnp.logical_not(here))
                def _():
                    remote(docs_in, D.at[g], ds_.at[2 * m + e], dr.at[0], (t, 2 * z + e)).wait_send()
        remote(PK.at[0:3], PK.at[0:3], ps.at[0], pr.at[0], (gx, r)).wait_send()
        part = KV.at[:, own_rows, :]
        remote(part, part, kvs.at[0], kvr.at[0], (g, rp)).wait_send()
        for i, (src, dst) in enumerate(((X, Xo), (AT, ATo), (NL, NLo), (ACT.at[c], ACT.at[c]))):
            remote(src, dst, lls.at[i], llr.at[i], (g, rp)).wait_send()

    loads = {}

    def load(name, slot, dst):
        src = {"x": Xo, "att": ATo, "nl": NLo}[name]
        remote(src, src, lls.at[slot], llr.at[slot], (g, rp)).wait_recv()
        copy = pltpu.make_async_copy(src, dst, lsem.at[9 + slot])
        copy.start()
        loads[name] = copy

    def grad(j, q, part=None):
        start, size = 0, 192
        if part is not None:
            start, size = 96 * part, 96
        if j < 4:
            return W.at[8 + q // 2, pl.ds(192 * j + start, size), pl.ds(pl.multiple_of(384 * (q % 2), 128), 384)]
        rows = pl.ds(pl.multiple_of(192 * q + start, 16), size)
        if j < 8:
            return W.at[10 + (j - 4) // 2, rows, 384 * (j % 2) : 384 * (j % 2) + 384]
        return W.at[4 + (j - 8) // 2, rows, 384 * (j % 2) : 384 * (j % 2) + 384]

    def parts_of(j):
        if j in SHARED:
            return ((64 * zp, 64), (64 * zp + 64, 64))
        return ((0, 96), (96, 96))

    def rows_of(ref, start, size):
        return ref.at[pl.ds(pl.multiple_of(start, 16), size)]

    def grad(j, q, start=0, size=192):
        if j < 4:
            return W.at[
                8 + q // 2, pl.ds(pl.multiple_of(192 * j + start, 16), size), pl.ds(pl.multiple_of(384 * (q % 2), 128), 384)
            ]
        rows = pl.ds(pl.multiple_of(192 * q + start, 16), size)
        if j < 8:
            return W.at[10 + (j - 4) // 2, rows, 384 * (j % 2) : 384 * (j % 2) + 384]
        return W.at[4 + (j - 8) // 2, rows, 384 * (j % 2) : 384 * (j % 2) + 384]

    def share(j):
        for slot, q in enumerate((gx, gy, gd)):
            remote(
                grad(j, q, 128 - 128 * zp, 64), ZF.at[SHARED.index(j), slot], hops.at[j], zfr.at[SHARED.index(j)], (g, rz)
            ).start()

    def shared(j):
        k = SHARED.index(j)
        remote(ZF.at[k], ZF.at[k], hops.at[j], zfr.at[k], (g, rz)).wait_recv()
        for slot, q in enumerate((gx, gy, gd)):
            mine = grad(j, q, 128 * zp, 64)
            mine[...] = (mine[...].astype(F32) + ZF[k, slot].astype(F32)).astype(BF16)

    def first(j):
        for side, (chip, (start, size)) in enumerate(zip((gy, gx), parts_of(j))):
            remote(grad(j, gd, start, size), P1.at[j, side, 0:size], hops.at[j], p1r.at[j], (chip, r)).start()

    def plain(j):
        (first_a, size), (first_b, _) = parts_of(j)
        remote(grad(j, gx, first_b, size), rows_of(P2.at[j, 0], first_b, size), hops.at[j], p2r.at[j], (gx, r)).start()
        remote(grad(j, gy, first_a, size), rows_of(P2.at[j, 1], first_a, size), hops.at[j], p2r.at[j], (gy, r)).start()

    def passed(j):
        size = parts_of(j)[0][1]
        both = P1.at[j, :, 0:size]
        remote(both, both, hops.at[j], p1r.at[j], (gx, r)).wait_recv()
        for side, chip in enumerate((gx, gy)):
            start = parts_of(j)[side][0]
            mine = grad(j, chip, start, size)
            mine[...] = (mine[...].astype(F32) + P1[j, side, 0:size].astype(F32)).astype(BF16)
            remote(mine, rows_of(P2.at[j, side], start, size), hops.at[j], p2r.at[j], (chip, r)).start()

    def own(j):
        start, size = parts_of(j)[0][0], 2 * parts_of(j)[0][1]
        both = P2.at[j, :, 0:size]
        remote(both, both, hops.at[j], p2r.at[j], (gx, r)).wait_recv()
        moved = pl.ds(pl.multiple_of(start, 16), size)
        arrived = P2[j, 0, moved].astype(F32) + P2[j, 1, moved].astype(F32)
        P2[j, 0, moved] = (grad(j, g, start, size)[...].astype(F32) + arrived).astype(BF16)
        if j in SHARED:
            P2[j, 0, pl.ds(pl.multiple_of(128 - 128 * zp, 16), 64)] = grad(j, g, 128 - 128 * zp, 64)[...]

        @pl.when(outer)
        def _():
            for rows, p in along_z(j):
                z_copy(j, 0, rows, 0, p, zin).start()

    def along_z(j):
        return [(slice(64 * p, 64 * p + 64), p) for p in range(3)] if j == CHUNKS - 1 else [(slice(0, 192), None)]

    def z_copy(j, slot, rows, side, p, to):
        arrived = zr.at[j, side] if p is None else zl.at[side, p]
        return remote(P2.at[j, slot, rows], ZR.at[j, side, rows], zs.at[j], arrived, zdev(to))

    def chain(j):
        @pl.when(inner)
        def _():
            for rows, p in along_z(j):
                z_copy(j, 0, rows, 0, p, zother).wait_recv()
                P2[j, 0, rows] = (P2[j, 0, rows].astype(F32) + ZR[j, 0, rows].astype(F32)).astype(BF16)
                z_copy(j, 0, rows, 1, p, zother).start()

    def hand_over(j):
        remote(P2.at[j, 1], To.at[c, j], ts.at[0], tr.at[0], (g, rp)).start()
        pltpu.make_async_copy(P2.at[j, 1], To.at[c, j], osem.at[0]).start()

    def fin_in(j):
        @pl.when(inner)
        def _():
            for rows, p in along_z(j):
                z_copy(j, 0, rows, 1, p, zother).wait_recv()
                P2[j, 1, rows] = (P2[j, 0, rows].astype(F32) + ZR[j, 1, rows].astype(F32)).astype(BF16)
                z_copy(j, 1, rows, 0, p, zout).start()
            hand_over(j)

    def fin_out(j):
        @pl.when(outer)
        def _():
            for rows, p in along_z(j):
                z_copy(j, 1, rows, 0, p, zin).wait_recv()
                P2[j, 1, rows] = ZR[j, 0, rows]
            hand_over(j)

    def drain(j):
        total = W.at[0, 0:576, 0:384]
        remote(total, total, hops.at[j], p1r.at[j], (gx, r)).wait_send()

        @pl.when(inner)
        def _():
            remote(ZR.at[j], ZR.at[j], zs.at[j], zr.at[j, 0], zdev(zother)).wait_send()

        @pl.when(outer)
        def _():
            remote(ZR.at[j, 0], ZR.at[j, 0], zs.at[j], zr.at[j, 0], zdev(zother)).wait_send()

    def serve(*slot):
        for name, j in SCHEDULE.get(slot, ()):
            services[name](j)

    def give_back(src, out, ssem, rsem):
        for b in range(2):
            t, e = 2 * c + b, g // 2
            here = (t == g) & (e == c)
            src_b = src.at[256 * b : 256 * b + 256, :]
            dst = out.at[g % 2]

            @pl.when(jnp.logical_not(here))
            def _():
                remote(src_b, dst, ssem.at[b], rsem.at[g % 2], (t, 2 * z + e)).start()

            @pl.when(here)
            def _():
                pltpu.make_async_copy(src_b, dst, rsem.at[g % 2]).start()

    def give_back_drain(src, out, ssem, rsem):
        for b in range(2):
            t, e = 2 * c + b, g // 2
            here = (t == g) & (e == c)
            src_b = src.at[256 * b : 256 * b + 256, :]

            @pl.when(jnp.logical_not(here))
            def _():
                remote(src_b, out.at[0], ssem.at[b], rsem.at[0], (t, 2 * z + e)).wait_send()

            remote(src_b, out.at[b], ssem.at[b], rsem.at[b], (g, rp)).wait_recv()

    services = {
        "passed": passed, "own": own, "chain": chain, "fin_in": fin_in, "fin_out": fin_out,
        "share": share, "shared": shared, "first": first, "plain": plain,
        "gi": lambda j: give_back(LO2, GIo, gis, gir),
    }

    def exchange(slot, src, dst):
        remote(src, dst, xs_.at[slot], xr_.at[slot], (g, rp)).start()

    def exchanged(slot, dst):
        remote(dst, dst, xs_.at[slot], xr_.at[slot], (g, rp)).wait_recv()

    def exchange_drain(slot, dst):
        remote(dst, dst, xs_.at[slot], xr_.at[slot], (g, rp)).wait_send()

    mine384 = pl.ds(pl.multiple_of(384 * c, 128), 384)
    theirs384 = pl.ds(pl.multiple_of(384 * (1 - c), 128), 384)

    def norm_back(values, gain, grad_out):
        shape, inverse = norm_parts(values)
        pulled = grad_out * gain
        d = inverse * (
            pulled
            - jnp.mean(pulled, axis=-1, keepdims=True)
            - shape * jnp.mean(pulled * shape, axis=-1, keepdims=True)
        )
        return shape, d

    for b in range(2):
        reshard_wait(og, g_rows, gs, gr, b)

    @pl.loop(0, 4)
    def _(i):
        rows = pl.ds(pl.multiple_of(128 * i, 128), 128)
        up = G[rows, :].astype(F32)
        shape, d = norm_back(R2[rows, :], PF[7:8, :], up)
        LO[rows, :] = (shape * PF[7:8, :] + PF[8:9, :]).astype(BF16)
        R2[rows, :] = d
        low = d.astype(BF16)
        DF[rows, :] = low
        BG[7:8, :] += columns(up * shape)
        BG[8:9, :] += columns(up)
        BG[6:7, :] += columns(low.astype(F32))

    exchange(0, DF.at[:, theirs384], DFP)
    give_back(LO, LOo, los, lor)

    def d_hidden(i):
        t = (i + 6 * (1 - c)) % 12
        tt = t % 3
        wide = pl.ds(pl.multiple_of(256 * t, 256), 256)
        back = dot_nt(DF[...], W[8 + t // 3, pl.ds(pl.multiple_of(256 * tt, 256), 256), :])
        low = (back * GP[:, wide].astype(F32)).astype(BF16)
        GP[:, wide] = low
        BG[pl.ds(12 + t // 3, 1), pl.ds(pl.multiple_of(256 * tt, 256), 256)] = columns(low.astype(F32))

    @pl.loop(0, 6, unroll=3)
    def _(i):
        d_hidden(i)

    exchange(1, GP.at[:, pl.ds(pl.multiple_of(1536 * (1 - c), 128), 1536)], DHP)

    @pl.loop(6, 12, unroll=3)
    def _(i):
        d_hidden(i)

    remote(ACT.at[1 - c], ACT.at[1 - c], lls.at[3], llr.at[3], (g, rp)).wait_recv()
    forward_drain()
    for k in range(GROUPS):
        gather_drain(k)
    exchanged(0, DFP)

    def pair_tn(own_left, their_left, own_right, their_right):
        return dot_tn(own_left, own_right) + dot_tn(their_left, their_right)

    def down_quarter(q):
        @pl.loop(0, 3, unroll=3)
        def _(i):
            lanes = pl.ds(pl.multiple_of(768 * q + 256 * i, 256), 256)
            out = pair_tn(ACT[c, :, lanes], ACT[1 - c, :, lanes], DF[:, mine384], DFP[...])
            W[8 + q // 2, pl.ds(pl.multiple_of(256 * i, 256), 256), pl.ds(pl.multiple_of(384 * (q % 2), 128), 384)] = (
                out.astype(BF16)
            )

    down_quarter(gd)
    serve("down", 0)
    down_quarter(gx)
    down_quarter(gy)
    serve("down", 1)
    down_quarter(g)
    serve("down", 2)
    load("nl", 2, ACT.at[0, :, 0:768])
    load("att", 1, ACT.at[0, :, 768:1536])
    load("x", 0, ACT.at[0, :, 1536:2304])

    @pl.loop(0, 3, unroll=3)
    def _(i):
        cols = pl.ds(pl.multiple_of(256 * i, 256), 256)
        total = R2[:, cols]
        for u in range(4):
            total = total + dot_nt(GP[:, 768 * u : 768 * u + 768], W[4 + u, cols, :])
        R2[:, cols] = total

    serve("normed")

    @pl.loop(0, 4)
    def _(i):
        rows = pl.ds(pl.multiple_of(128 * i, 128), 128)
        up = R2[rows, :]
        shape, d = norm_back(R1[rows, :], PF[4:5, :], up)
        R2[rows, :] = d
        low = d.astype(BF16)
        DB[rows, :] = low
        BG[4:5, :] += columns(up * shape)
        BG[5:6, :] += columns(up)
        BG[3:4, :] += columns(low.astype(F32))

    exchange(2, DB.at[:, theirs384], DBP)
    serve("ln1")
    exchanged(1, DHP)
    loads["nl"].wait()

    for j in range(4, 8):
        jj = j - 4
        own_cols = pl.ds(pl.multiple_of(1536 * c + 384 * jj, 128), 384)

        @pl.loop(0, 3, unroll=3)
        def _(i):
            lanes = pl.ds(pl.multiple_of(256 * i, 256), 256)
            out = pair_tn(NL[:, lanes], ACT[0, :, lanes], GP[:, own_cols], DHP[:, 384 * jj : 384 * jj + 384])
            W[10 + jj // 2, lanes, 384 * (jj % 2) : 384 * (jj % 2) + 384] = out.astype(BF16)

        serve("up", j)

    @pl.loop(0, 3, unroll=3)
    def _(i):
        cols = pl.ds(pl.multiple_of(256 * i, 256), 256)
        DATT[:, cols] = dot_nt(DB[...], W[3, cols, :]).astype(BF16)

    serve("datt")
    exchanged(2, DBP)
    loads["att"].wait()

    def square_grad(j, offset, own_left, own_right, their_right):
        @pl.loop(0, 3, unroll=3)
        def _(i):
            lanes = pl.ds(pl.multiple_of(offset + 256 * i, 256), 256)
            cols = pl.ds(pl.multiple_of(256 * i, 256), 256)
            out = pair_tn(own_left[:, cols], ACT[0, :, lanes], own_right[...], their_right[...])
            W[4 + (j - 8) // 2, cols, 384 * (j % 2) : 384 * (j % 2) + 384] = (
                out.astype(BF16)
            )

    square_grad(8, 768, AT, DB.at[:, mine384], DBP)
    serve("sq", 8)

    loads["x"].wait()

    @pl.loop(0, 12)
    def _(i):
        turn, ours, b = i // 4, (i // 2) % 2, i % 2
        pair = turn + 3 * (c * ours + (1 - c) * (1 - ours))
        lanes = pl.ds(pl.multiple_of(128 * pair, 128), 128)
        half_lanes = pl.ds(pl.multiple_of(128 * turn, 128), 128)
        cols = pl.ds(pl.multiple_of(256 * b, 256), 256)
        @pl.when(b == 0)
        def _():
            ACC[...] = jnp.zeros_like(ACC)

        def block(keys):
            qs = Q[cols, lanes].astype(F32) * (HEAD_DIM ** -0.5)
            do = DATT[cols, lanes].astype(F32)
            qt, dot_t = qs.T, do.T
            kp = KV[0, keys, lanes]
            vp = KV[1, keys, lanes]
            kt = kp.astype(F32).T.astype(BF16)
            weigh = (do * AT[cols, lanes].astype(F32)).T
            top = lax.broadcasted_iota(jnp.int32, (128, 256), 0) < 64
            left = lax.broadcasted_iota(jnp.int32, (256, 128), 1) < 64
            dk = dv = None
            pieces = []
            for hh in range(2):
                rows_in = top if hh == 0 else jnp.logical_not(top)
                lanes_in = left if hh == 0 else jnp.logical_not(left)
                s = dot(kp, jnp.where(rows_in, qt, 0.0).astype(BF16)) + MASK[keys, cols]
                p = jnp.exp(s - LSE[pl.ds(2 * pair + hh, 1), cols])
                dp = dot(vp, jnp.where(rows_in, dot_t, 0.0).astype(BF16))
                ds = (p * (dp - columns(weigh[64 * hh : 64 * hh + 64, :]))).astype(BF16)
                dv_h = dot(p.astype(BF16), jnp.where(lanes_in, do, 0.0).astype(BF16))
                dk_h = dot(ds, jnp.where(lanes_in, qs, 0.0).astype(BF16))
                dv = dv_h if dv is None else dv + dv_h
                dk = dk_h if dk is None else dk + dk_h
                pieces.append(dot(kt[64 * hh : 64 * hh + 64, :], ds))
            DQ[cols, lanes] = (jnp.concatenate(pieces, axis=0).T * (HEAD_DIM ** -0.5)).astype(BF16)
            ACC[0, keys, :] += dk
            ACC[1, keys, :] += dv

        @pl.when(b == c)
        def _():
            block(pl.ds(pl.multiple_of(256 * c, 256), 768))

        @pl.when(b != c)
        def _():
            block(slice(0, 1024))

        @pl.when((b == 1) & (ours == 0))
        def _():
            DKS[0, :, half_lanes] = ACC[0].astype(BF16)
            DKS[1, :, half_lanes] = ACC[1].astype(BF16)
            exchange(3 + turn, DKS.at[:, :, half_lanes], DKR.at[:, :, half_lanes])
            exchange(6 + turn, DQ.at[:, lanes], DQP.at[:, half_lanes])

        @pl.when((b == 1) & (ours == 1))
        def _():
            exchanged(3 + turn, DKR.at[:, :, half_lanes])
            DKF[0, :, half_lanes] = (ACC[0] + DKR[0, :, half_lanes].astype(F32)).astype(BF16)
            DKF[1, :, half_lanes] = (ACC[1] + DKR[1, :, half_lanes].astype(F32)).astype(BF16)
            exchange(9 + turn, DKF.at[:, their_rows, half_lanes], DKP.at[:, :, half_lanes])
            exchanged(6 + turn, DQP.at[:, half_lanes])
            RC[0, :, 0:128] = DQ[:, lanes]
            RC[1, :, 0:128] = DQP[:, half_lanes]
            for w in range(2):
                RC[0, :, 128 + 128 * w : 256 + 128 * w] = DKF[w, own_rows, half_lanes]
                RC[1, :, 128 + 128 * w : 256 + 128 * w] = DKF[w, their_rows, half_lanes]

            @pl.loop(0, 3, unroll=3)
            def _(t):
                tile = pl.ds(pl.multiple_of(256 * t, 256), 256)
                theirs = pl.ds(pl.multiple_of(1536 + 256 * t, 256), 256)
                out = pair_tn(X[:, tile], ACT[0, :, theirs], RC[0], RC[1])
                W[4 + (1 + turn) // 2, tile, pl.ds(pl.multiple_of(384 * ((1 + turn) % 2), 128), 384)] = out.astype(BF16)

        for k in range(12):
            if ("a", k) in SCHEDULE:
                @pl.when(i == k)
                def _():
                    serve("a", k)

    BG[0:1, :] = columns(DQ[...].astype(F32))
    BG[2:3, mine384] = columns(DKF[1].astype(F32))

    BS[...] = BG[...].astype(BF16)
    others = [(gg, rr, k) for k, (gg, rr) in enumerate(
        ((g, rp), (gx, r), (gx, rp), (gy, r), (gy, rp), (gd, r), (gd, rp)))]
    slot_of = 2 * g + c
    for gg, rr, k in others:
        remote(BS, BR.at[slot_of], b1s.at[0], b1r.at[0], (gg, rr)).start()
    BR[slot_of] = BS[...]

    serve("end")

    for k in range(3):
        exchanged(9 + k, DKP.at[:, :, 128 * k : 128 * k + 128])

    for i in range(3):
        cols = slice(256 * i, 256 * i + 256)
        total = R2[:, cols] + dot_nt(DQ[...], W[0, cols, :])
        for w in range(2):
            total = total + dot_nt(DKF[w, own_rows, :], W[1 + w, cols, mine384])
            total = total + dot_nt(DKP[w], W[1 + w, cols, theirs384])
        LO2[:, cols] = total.astype(BF16)
        serve("inp", i)

    remote(BR.at[0:7], BR.at[0:7], b1s.at[0], b1r.at[0], (g, rp)).wait_recv()
    total = BR[0].astype(F32)
    for k in range(1, 8):
        total = total + BR[k].astype(F32)
    BZ[0] = total.astype(BF16)

    @pl.when(outer)
    def _():
        remote(BZ.at[0], BZ.at[1], b1s.at[1], b1r.at[1], zdev(zin)).start()

    def small_chain():
        @pl.when(inner)
        def _():
            remote(BZ.at[1], BZ.at[1], b1s.at[1], b1r.at[1], zdev(zother)).wait_recv()
            BZ[2] = (BZ[0].astype(F32) + BZ[1].astype(F32)).astype(BF16)
            remote(BZ.at[2], BZ.at[3], b1s.at[1], b1r.at[2], zdev(zother)).start()

    def small_in():
        @pl.when(inner)
        def _():
            remote(BZ.at[3], BZ.at[3], b1s.at[1], b1r.at[2], zdev(zother)).wait_recv()
            BZ[4] = (BZ[2].astype(F32) + BZ[3].astype(F32)).astype(BF16)
            remote(BZ.at[4], BZ.at[1], b1s.at[2], b1r.at[1], zdev(zout)).start()

    def small_out():
        @pl.when(outer)
        def _():
            remote(BZ.at[1], BZ.at[1], b1s.at[1], b1r.at[1], zdev(zin)).wait_recv()
            BZ[4] = BZ[1]

    services.update(
        small_chain=lambda j: small_chain(), small_in=lambda j: small_in(), small_out=lambda j: small_out()
    )
    serve("tail")
    BT[...] = BZ[4].astype(F32)
    bt_copy = pltpu.make_async_copy(BT, BTo, osem.at[1])
    bt_copy.start()

    for j in range(CHUNKS):
        drain(j)
    halves = remote(To.at[c], To.at[1 - c], ts.at[0], tr.at[0], (g, rp))
    halves.wait_send()
    halves.wait_recv()
    pltpu.make_async_copy(To.at[c], To.at[c], osem.at[0]).wait()
    for slot, dst in ((0, DFP), (1, DHP), (2, DBP)):
        exchange_drain(slot, dst)
    for k in range(3):
        part = slice(128 * k, 128 * k + 128)
        exchange_drain(3 + k, DKR.at[:, :, part])
        exchange_drain(6 + k, DQP.at[:, part])
        exchange_drain(9 + k, DKP.at[:, :, part])
    give_back_drain(LO, LOo, los, lor)
    give_back_drain(LO2, GIo, gis, gir)
    remote(BR.at[0:7], BR.at[0:7], b1s.at[0], b1r.at[0], (g, rp)).wait_send()
    remote(BZ.at[0], BZ.at[0], b1s.at[1], b1r.at[1], zdev(zother)).wait_send()

    @pl.when(inner)
    def _():
        remote(BZ.at[0], BZ.at[0], b1s.at[2], b1r.at[1], zdev(zother)).wait_send()

    bt_copy.wait()


def sds(shape, dtype=BF16):
    return jax.ShapeDtypeStruct(shape, dtype)


def layer(*args):
    out = [
        sds((2, 256, 768)), sds((2, 256, 768)), sds((2, CHUNKS, 192, 384)), sds((16, 768), F32),
        sds((512, 768)), sds((512, 768)), sds((512, 768)),
    ]
    dma = pltpu.SemaphoreType.DMA
    v = pltpu.VMEM
    return pl.pallas_call(
        layer_kernel,
        out_shape=out,
        in_specs=[ANY] * 18,
        out_specs=[ANY] * len(out),
        scratch_shapes=[
            v((12, 768, 768), BF16), v((CHUNKS, 2, 96, 384), BF16), v((CHUNKS, 2, 192, 384), BF16),
            v((CHUNKS, 2, 192, 384), BF16),
            v((2, 512, 3072), BF16), v((512, 3072), BF16), v((512, 1536), BF16), v((512, 768), BF16),
            v((2, 1024, 768), BF16), v((1024, 512), F32), v((16, 512), F32),
            v((512, 768), F32), v((512, 768), F32), v((512, 768), BF16), v((16, 768), F32),
            v((512, 768), BF16), v((512, 384), BF16), v((512, 768), BF16), v((512, 384), BF16),
            v((512, 768), BF16), v((512, 384), BF16), v((2, 1024, 384), BF16),
            v((2, 1024, 384), BF16), v((2, 1024, 384), BF16), v((2, 512, 384), BF16),
            v((512, 768), BF16), v((2, 1024, 128), F32), v((16, 768), F32), v((8, 16, 768), BF16),
            v((16, 768), BF16), v((5, 16, 768), BF16), v((16, 768), F32),
            v((512, 768), BF16), v((512, 768), BF16), v((512, 768), BF16), v((256, 1024), F32), v((256, 1024), F32),
            v((256, 128), F32), v((256, 128), F32), v((512, 128), F32), v((8, 1024), F32), v((512, 128), F32),
            v((4, 2, 256), jnp.int32), v((4, 16, 768), BF16), v((len(SHARED), 3, 64, 384), BF16), v((2, 512, 384), BF16),
            *[v((192,), BF16)] * 8, v((768,), BF16),
            dma((12,)), dma((9,)), dma((CHUNKS,)), dma((CHUNKS,)), dma((CHUNKS,)), dma((CHUNKS,)), dma((CHUNKS, 2)),
            dma((2, 3)), dma((len(SHARED),)), dma((1,)), dma((1,)), dma((12,)), dma((12,)),
            dma((2,)), dma((2,)), dma((2,)), dma((2,)), dma((3,)), dma((3,)), dma((2,)),
            dma((GROUPS,)), dma((GROUPS, 6)), dma((2,)), dma((2,)), dma((4,)), dma((1,)),
            dma((1,)), dma((1,)), dma((2,)), dma((2,)), dma((1,)), dma((1,)), dma((4,)), dma((4,)),
        ],
        compiler_params=pltpu.CompilerParams(
            collective_id=0, has_side_effects=True, vmem_limit_bytes=67043328
        ),
    )(*args)


def spread_kernel(
    Ti, GIi, LOi, BTi,
    LOo, GIo, WQo, WKo, WVo, WOo, WUo, WDo, BQo, BVo, BOo, GAo, SAo, BUo, BDo, GFo, SFo,
    T, GI, LO, OUT, GIF, sem, osem,
):
    g = lax.axis_index("group")
    order = (0, 1, 2, 3, 4, 5, 6, 7, 8, 9, 10, 11)
    loads = []
    for j in order:
        loads.append(pltpu.make_async_copy(Ti.at[:, j], T.at[:, j], sem.at[j]))
    loads.append(pltpu.make_async_copy(GIi, GI, sem.at[12]))
    loads.append(pltpu.make_async_copy(LOi, LO, sem.at[13]))
    for copy in loads[12:] + loads[:12]:
        copy.start()
    stores = []

    def store(src, dst):
        copy = pltpu.make_async_copy(src, dst, osem.at[len(stores)])
        copy.start()
        stores.append(copy)

    loads[13].wait()
    store(LO, LOo)
    loads[12].wait()
    GIF[...] = GI[...].astype(F32)
    store(GIF, GIo)
    for j in range(9):
        loads[j].wait()
        for e in range(2):
            OUT[j, :, 384 * e : 384 * e + 384] = T[e, j].astype(F32)
        if j < 4:
            store(OUT.at[j], WDo.at[192 * j : 192 * j + 192, :])
        elif j < 8:
            for e in range(2):
                start = 1536 * e + 384 * (j - 4)
                store(OUT.at[j, :, 384 * e : 384 * e + 384], WUo.at[:, start : start + 384])
        else:
            store(OUT.at[j], WOo)
    for j in range(9, 12):
        loads[j].wait()
    for w, ref in enumerate((WQo, WKo, WVo)):
        for turn in range(3):
            for e in range(2):
                start = 384 * e + 128 * turn
                OUT[9 + w, :, start : start + 128] = T[e, 9 + turn, :, 128 * w : 128 * w + 128].astype(F32)
        store(OUT.at[9 + w], ref)
    moved = pltpu.roll(BTi[...], (768 - 192 * g) % 768, 1)
    for row, ref in ((0, BQo), (2, BVo), (3, BOo), (4, GAo), (5, SAo), (6, BDo), (7, GFo), (8, SFo)):
        ref[...] = moved[row, 0:192]
    up = BTi[pl.ds(12 + g, 1), :]
    BUo[...] = up[0, :]
    for copy in stores:
        copy.wait()


def spread(totals, grad_input, layer_out, small):
    square = sds((192, 768), F32)
    short = sds((192,), F32)
    whole = pl.BlockSpec(memory_space=pltpu.VMEM)
    dma = pltpu.SemaphoreType.DMA
    return pl.pallas_call(
        spread_kernel,
        out_shape=[
            sds((2, 256, 768)), sds((2, 256, 768), F32), square, square, square, square,
            sds((192, 3072), F32), sds((768, 768), F32),
            short, short, short, short, short, sds((768,), F32), short, short, short,
        ],
        in_specs=[ANY, ANY, ANY, whole],
        out_specs=[ANY] * 8 + [whole] * 9,
        scratch_shapes=[
            pltpu.VMEM((2, CHUNKS, 192, 384), BF16), pltpu.VMEM((2, 256, 768), BF16), pltpu.VMEM((2, 256, 768), BF16),
            pltpu.VMEM((CHUNKS, 192, 768), F32), pltpu.VMEM((2, 256, 768), F32), dma((14,)), dma((20,)),
        ],
        compiler_params=pltpu.CompilerParams(vmem_limit_bytes=66000000),
    )(totals, grad_input, layer_out, small)


def fits(mesh):
    return dict(mesh.shape) == {"group": 4, "replica": 8}


def fast(
    tokens_in, doc_ids, out_grad, w_query, w_key, w_value, w_out, w_up, w_down, b_query, b_value, b_out,
    gain_attn, shift_attn, b_up, b_down, gain_ffn, shift_ffn,
):
    layer_out, grad_input, totals, small, *_ = layer(
        tokens_in, doc_ids, out_grad, w_query, w_key, w_value, w_out, w_up, w_down,
        b_query, b_value, b_out, gain_attn, shift_attn, b_down, gain_ffn, shift_ffn, b_up,
    )
    return tuple(spread(totals, grad_input, layer_out, small))


def layer_norm(values, gain, shift):
    centre = values - jnp.mean(values, axis=-1, keepdims=True)
    spread = jnp.mean(centre * centre, axis=-1, keepdims=True)
    return centre * lax.rsqrt(spread + EPSILON) * gain + shift


def norm_pull(values, gain, shift, grad):
    result, pullback = jax.vjp(
        layer_norm, values, gain.astype(jnp.float32), shift.astype(jnp.float32)
    )
    return (result, pullback(grad))


def exact_gelu(values):
    return jax.nn.gelu(values, approximate=False)


def project(inputs, weight, bias):
    return jnp.dot(inputs, weight, preferred_element_type=jnp.float32) + bias.astype(jnp.float32)


def contract_rows(left, right):
    return lax.dot_general(
        left, right, (((0,), (0,)), ((), ())), preferred_element_type=jnp.float32
    )


def against_rows(grad, weight):
    return lax.dot_general(
        grad, weight, (((1,), (1,)), ((), ())), preferred_element_type=jnp.float32
    )


def column_sum(values):
    return jnp.sum(values.astype(jnp.float32), axis=0)


def add_pair(first, second):
    return first + second


def scores_of(query, keys_all, allowed):
    rows = query.shape[0]
    length = keys_all.shape[0]
    scaling = HEAD_DIM ** (-0.5)
    scores = (
        jnp.einsum(
            "qhd,khd->hqk",
            query.reshape(rows, HEADS, HEAD_DIM),
            keys_all.reshape(length, HEADS, HEAD_DIM),
            preferred_element_type=jnp.float32,
        )
        * scaling
    )
    return jnp.where(allowed[None], scores, NEGATIVE)


def attention_forward(query, keys_all, values_all, allowed):
    rows = query.shape[0]
    length = keys_all.shape[0]
    scores = scores_of(query, keys_all, allowed)
    row_max = jnp.max(scores, axis=-1, keepdims=True)
    exponent = jnp.exp(scores - row_max)
    total = jnp.sum(exponent, axis=-1, keepdims=True)
    probs = (exponent / total).astype(jnp.bfloat16)
    log_total = row_max[..., 0] + jnp.log(total[..., 0])
    joined = jnp.einsum(
        "hqk,khd->qhd",
        probs,
        values_all.reshape(length, HEADS, HEAD_DIM),
        preferred_element_type=jnp.float32,
    )
    return (joined.reshape(rows, HEADS * HEAD_DIM), log_total)


def score_grads(query, keys_all, values_all, allowed, log_total, d_attended):
    rows = query.shape[0]
    length = keys_all.shape[0]
    scores = scores_of(query, keys_all, allowed)
    probs = jnp.exp(scores - log_total[..., None])
    d_heads = d_attended.reshape(rows, HEADS, HEAD_DIM)
    d_probs = jnp.einsum(
        "qhd,khd->hqk",
        d_heads,
        values_all.reshape(length, HEADS, HEAD_DIM),
        preferred_element_type=jnp.float32,
    )
    row_term = jnp.sum(probs * d_probs, axis=-1)
    d_scores = (probs * (d_probs - row_term[..., None])).astype(jnp.bfloat16)
    return (probs, d_scores, row_term)


def attention_backward(query, keys_all, values_all, allowed, log_total, d_attended):
    rows = query.shape[0]
    length = keys_all.shape[0]
    scaling = HEAD_DIM ** (-0.5)
    probs, d_scores, row_term = score_grads(
        query, keys_all, values_all, allowed, log_total, d_attended
    )
    d_heads = d_attended.reshape(rows, HEADS, HEAD_DIM)
    d_values_part = jnp.einsum(
        "hqk,qhd->khd", probs.astype(jnp.bfloat16), d_heads, preferred_element_type=jnp.float32
    ).reshape(length, HEADS * HEAD_DIM)
    d_query = (
        jnp.einsum(
            "hqk,khd->qhd",
            d_scores,
            keys_all.reshape(length, HEADS, HEAD_DIM),
            preferred_element_type=jnp.float32,
        ).reshape(rows, HEADS * HEAD_DIM)
        * scaling
    )
    d_keys_part = (
        jnp.einsum(
            "hqk,qhd->khd",
            d_scores,
            query.reshape(rows, HEADS, HEAD_DIM),
            preferred_element_type=jnp.float32,
        ).reshape(length, HEADS * HEAD_DIM)
        * scaling
    )
    return (d_query, d_keys_part, d_values_part, row_term)


def owner_sum(grads):
    return (
        lax.psum_scatter(
            grads[0].astype(jnp.bfloat16), "group", scatter_dimension=0, tiled=True
        ).astype(jnp.float32),
        lax.psum_scatter(
            grads[1].astype(jnp.bfloat16), "group", scatter_dimension=0, tiled=True
        ).astype(jnp.float32),
        lax.psum_scatter(
            grads[2].astype(jnp.bfloat16), "group", scatter_dimension=0, tiled=True
        ).astype(jnp.float32),
        lax.psum_scatter(
            grads[3].astype(jnp.bfloat16), "group", scatter_dimension=0, tiled=True
        ).astype(jnp.float32),
        lax.psum_scatter(
            grads[4].astype(jnp.bfloat16), "group", scatter_dimension=0, tiled=True
        ).astype(jnp.float32),
        lax.psum_scatter(
            grads[5].astype(jnp.bfloat16), "group", scatter_dimension=0, tiled=True
        ).astype(jnp.float32),
        lax.psum_scatter(
            grads[6].astype(jnp.bfloat16), "group", scatter_dimension=0, tiled=True
        ).astype(jnp.float32),
        lax.psum_scatter(
            grads[7].astype(jnp.bfloat16), "group", scatter_dimension=0, tiled=True
        ).astype(jnp.float32),
        lax.psum_scatter(
            grads[8].astype(jnp.bfloat16), "group", scatter_dimension=0, tiled=True
        ).astype(jnp.float32),
        lax.psum_scatter(
            grads[9].astype(jnp.bfloat16), "group", scatter_dimension=0, tiled=True
        ).astype(jnp.float32),
        lax.psum_scatter(
            grads[10].astype(jnp.bfloat16), "group", scatter_dimension=0, tiled=True
        ).astype(jnp.float32),
        lax.psum_scatter(
            grads[11].astype(jnp.bfloat16), "group", scatter_dimension=0, tiled=True
        ).astype(jnp.float32),
        lax.psum_scatter(
            grads[12].astype(jnp.bfloat16), "group", scatter_dimension=0, tiled=True
        ).astype(jnp.float32),
        lax.psum_scatter(
            grads[13].astype(jnp.bfloat16), "group", scatter_dimension=0, tiled=True
        ).astype(jnp.float32),
        lax.psum_scatter(
            grads[14].astype(jnp.bfloat16), "group", scatter_dimension=0, tiled=True
        ).astype(jnp.float32),
    )


def shards(
    tokens_in,
    doc_ids,
    out_grad,
    w_query,
    w_key,
    w_value,
    w_out,
    w_up,
    w_down,
    b_query,
    b_value,
    b_out,
    gain_attn,
    shift_attn,
    b_up,
    b_down,
    gain_ffn,
    shift_ffn,
):
    gathered = (
        lax.all_gather(w_query, "group", axis=0, tiled=True),
        lax.all_gather(w_key, "group", axis=0, tiled=True),
        lax.all_gather(w_value, "group", axis=0, tiled=True),
        lax.all_gather(w_out, "group", axis=0, tiled=True),
        lax.all_gather(w_up, "group", axis=0, tiled=True),
        lax.all_gather(w_down, "group", axis=0, tiled=True),
        lax.all_gather(b_query, "group", axis=0, tiled=True),
        lax.all_gather(b_value, "group", axis=0, tiled=True),
        lax.all_gather(b_out, "group", axis=0, tiled=True),
        lax.all_gather(gain_attn, "group", axis=0, tiled=True),
        lax.all_gather(shift_attn, "group", axis=0, tiled=True),
        lax.all_gather(b_up, "group", axis=0, tiled=True),
        lax.all_gather(b_down, "group", axis=0, tiled=True),
        lax.all_gather(gain_ffn, "group", axis=0, tiled=True),
        lax.all_gather(shift_ffn, "group", axis=0, tiled=True),
    )
    (
        query_weight,
        key_weight,
        value_weight,
        out_weight,
        up_weight,
        down_weight,
        query_bias,
        value_bias,
        out_bias,
        attn_gain,
        attn_shift,
        up_bias,
        down_bias,
        ffn_gain,
        ffn_shift,
    ) = gathered
    micros = tokens_in.shape[0]
    outputs = []
    stored = []
    for micro in range(micros):
        inputs = tokens_in[micro]
        segment = doc_ids[micro]
        query = project(inputs, query_weight, query_bias).astype(jnp.bfloat16)
        keys = jnp.dot(inputs, key_weight, preferred_element_type=jnp.float32).astype(jnp.bfloat16)
        values = project(inputs, value_weight, value_bias).astype(jnp.bfloat16)
        keys_all, values_all, seg_all = (
            lax.all_gather(keys, "group", axis=0, tiled=True),
            lax.all_gather(values, "group", axis=0, tiled=True),
            lax.all_gather(segment, "group", axis=0, tiled=True),
        )
        allowed = segment[:, None] == seg_all[None, :]
        attended, log_total = attention_forward(query, keys_all, values_all, allowed)
        attended = attended.astype(jnp.bfloat16)
        resid_one = inputs.astype(jnp.float32) + project(attended, out_weight, out_bias)
        normed = layer_norm(
            resid_one, attn_gain.astype(jnp.float32), attn_shift.astype(jnp.float32)
        )
        hidden = project(normed.astype(jnp.bfloat16), up_weight, up_bias)
        activated = exact_gelu(hidden).astype(jnp.bfloat16)
        resid_two = normed + project(activated, down_weight, down_bias)
        result = layer_norm(resid_two, ffn_gain.astype(jnp.float32), ffn_shift.astype(jnp.float32))
        outputs.append(result.astype(jnp.bfloat16))
        stored.append((query, keys, values, log_total, attended, resid_one, hidden, resid_two))
    gathered = (
        lax.all_gather(w_query, "group", axis=0, tiled=True),
        lax.all_gather(w_key, "group", axis=0, tiled=True),
        lax.all_gather(w_value, "group", axis=0, tiled=True),
        lax.all_gather(w_out, "group", axis=0, tiled=True),
        lax.all_gather(w_up, "group", axis=0, tiled=True),
        lax.all_gather(w_down, "group", axis=0, tiled=True),
        lax.all_gather(b_query, "group", axis=0, tiled=True),
        lax.all_gather(b_value, "group", axis=0, tiled=True),
        lax.all_gather(b_out, "group", axis=0, tiled=True),
        lax.all_gather(gain_attn, "group", axis=0, tiled=True),
        lax.all_gather(shift_attn, "group", axis=0, tiled=True),
        lax.all_gather(b_up, "group", axis=0, tiled=True),
        lax.all_gather(b_down, "group", axis=0, tiled=True),
        lax.all_gather(gain_ffn, "group", axis=0, tiled=True),
        lax.all_gather(shift_ffn, "group", axis=0, tiled=True),
    )
    (
        query_weight,
        key_weight,
        value_weight,
        out_weight,
        up_weight,
        down_weight,
        query_bias,
        value_bias,
        out_bias,
        attn_gain,
        attn_shift,
        up_bias,
        down_bias,
        ffn_gain,
        ffn_shift,
    ) = gathered
    totals = tuple((jnp.zeros(member.shape, jnp.float32) for member in gathered))
    input_grads = []
    for micro in range(micros):
        inputs = tokens_in[micro]
        segment = doc_ids[micro]
        query, keys, values, log_total, attended, resid_one, hidden, resid_two = stored[micro]
        upstream = out_grad[micro].astype(jnp.float32)
        unused_out, (d_resid_two, g_ffn_gain, g_ffn_shift) = norm_pull(
            resid_two, ffn_gain, ffn_shift, upstream
        )
        d_ffn = d_resid_two.astype(jnp.bfloat16)
        activated, gelu_pull = jax.vjp(exact_gelu, hidden)
        activated = activated.astype(jnp.bfloat16)
        g_down_w = contract_rows(activated, d_ffn)
        g_down_b = column_sum(d_ffn)
        d_activated = against_rows(d_ffn, down_weight)
        d_hidden = gelu_pull(d_activated)[0].astype(jnp.bfloat16)
        normed = layer_norm(
            resid_one, attn_gain.astype(jnp.float32), attn_shift.astype(jnp.float32)
        )
        normed_low = normed.astype(jnp.bfloat16)
        g_up_w = contract_rows(normed_low, d_hidden)
        g_up_b = column_sum(d_hidden)
        d_normed = against_rows(d_hidden, up_weight) + d_resid_two
        unused_norm, (d_resid_one, g_attn_gain, g_attn_shift) = norm_pull(
            resid_one, attn_gain, attn_shift, d_normed
        )
        d_branch = d_resid_one.astype(jnp.bfloat16)
        g_out_w = contract_rows(attended, d_branch)
        g_out_b = column_sum(d_branch)
        d_attended = against_rows(d_branch, out_weight).astype(jnp.bfloat16)
        keys_all, values_all, seg_all = (
            lax.all_gather(keys, "group", axis=0, tiled=True),
            lax.all_gather(values, "group", axis=0, tiled=True),
            lax.all_gather(segment, "group", axis=0, tiled=True),
        )
        allowed = segment[:, None] == seg_all[None, :]
        d_query, d_keys_part, d_values_part, row_term = attention_backward(
            query, keys_all, values_all, allowed, log_total, d_attended
        )
        d_keys, d_values = (
            lax.psum_scatter(
                d_keys_part.astype(jnp.bfloat16), "group", scatter_dimension=0, tiled=True
            ).astype(jnp.float32),
            lax.psum_scatter(
                d_values_part.astype(jnp.bfloat16), "group", scatter_dimension=0, tiled=True
            ).astype(jnp.float32),
        )
        d_query = d_query.astype(jnp.bfloat16)
        d_keys = d_keys.astype(jnp.bfloat16)
        d_values = d_values.astype(jnp.bfloat16)
        g_query_w = contract_rows(inputs, d_query)
        g_key_w = contract_rows(inputs, d_keys)
        g_value_w = contract_rows(inputs, d_values)
        g_query_b = column_sum(d_query)
        g_value_b = column_sum(d_values)
        input_grad = (
            d_resid_one
            + against_rows(d_query, query_weight)
            + against_rows(d_keys, key_weight)
            + against_rows(d_values, value_weight)
        )
        input_grads.append(input_grad)
        micro_grads = (
            g_query_w,
            g_key_w,
            g_value_w,
            g_out_w,
            g_up_w,
            g_down_w,
            g_query_b,
            g_value_b,
            g_out_b,
            g_attn_gain,
            g_attn_shift,
            g_up_b,
            g_down_b,
            g_ffn_gain,
            g_ffn_shift,
        )
        totals = jax.tree.map(add_pair, totals, micro_grads)
    totals = tuple(owner_sum(totals))
    summed = (
        lax.psum(totals[0].astype(jnp.bfloat16), "replica").astype(jnp.float32),
        lax.psum(totals[1].astype(jnp.bfloat16), "replica").astype(jnp.float32),
        lax.psum(totals[2].astype(jnp.bfloat16), "replica").astype(jnp.float32),
        lax.psum(totals[3].astype(jnp.bfloat16), "replica").astype(jnp.float32),
        lax.psum(totals[4].astype(jnp.bfloat16), "replica").astype(jnp.float32),
        lax.psum(totals[5].astype(jnp.bfloat16), "replica").astype(jnp.float32),
        lax.psum(totals[6].astype(jnp.bfloat16), "replica").astype(jnp.float32),
        lax.psum(totals[7].astype(jnp.bfloat16), "replica").astype(jnp.float32),
        lax.psum(totals[8].astype(jnp.bfloat16), "replica").astype(jnp.float32),
        lax.psum(totals[9].astype(jnp.bfloat16), "replica").astype(jnp.float32),
        lax.psum(totals[10].astype(jnp.bfloat16), "replica").astype(jnp.float32),
        lax.psum(totals[11].astype(jnp.bfloat16), "replica").astype(jnp.float32),
        lax.psum(totals[12].astype(jnp.bfloat16), "replica").astype(jnp.float32),
        lax.psum(totals[13].astype(jnp.bfloat16), "replica").astype(jnp.float32),
        lax.psum(totals[14].astype(jnp.bfloat16), "replica").astype(jnp.float32),
    )
    layer_out = jnp.stack(outputs)
    grad_input = jnp.stack(input_grads)
    return (
        layer_out,
        grad_input,
        summed[0],
        summed[1],
        summed[2],
        summed[3],
        summed[4],
        summed[5],
        summed[6],
        summed[7],
        summed[8],
        summed[9],
        summed[10],
        summed[11],
        summed[12],
        summed[13],
        summed[14],
    )


def solution(mesh):
    return jax.shard_map(
        shards if not fits(mesh) else fast,
        mesh=mesh,
        in_specs=(
            P("replica", "group", None),
            P("replica", "group"),
            P("replica", "group", None),
            P("group", None),
            P("group", None),
            P("group", None),
            P("group", None),
            P("group", None),
            P("group", None),
            P("group"),
            P("group"),
            P("group"),
            P("group"),
            P("group"),
            P("group"),
            P("group"),
            P("group"),
            P("group"),
        ),
        out_specs=(
            P("replica", "group", None),
            P("replica", "group", None),
            P("group", None),
            P("group", None),
            P("group", None),
            P("group", None),
            P("group", None),
            P("group", None),
            P("group"),
            P("group"),
            P("group"),
            P("group"),
            P("group"),
            P("group"),
            P("group"),
            P("group"),
            P("group"),
        ),
        check_vma=False,
    )
```
